32 devices in a mesh: dp: 4 (over z), row: 4 (over x, core), col: 2 (over y).
Axes of the slice: x: 2, y: 2, z: 4, core: 2. Of those that a mesh axis runs over, the one named last changes fastest.
Arguments:
- inputs: bfloat16 [2048, 4096], P('row', ('dp', 'col')), may hold values from -6 to 6
- cotangent: bfloat16 [2048, 4096], P('row', ('dp', 'col')), may hold values from -6 to 6
- starts: int32 [4096], P(('dp', 'row')), may hold values from 0 to 1, as said below
- x_proj: bfloat16 [2048, 2560], P('row', 'col'), may hold values from -0.125 to 0.125
- y_proj: bfloat16 [2048, 2560], P('row', 'col'), may hold values from -0.125 to 0.125
- out_proj: bfloat16 [2560, 2048], P('col', 'row'), may hold values from -0.15625 to 0.15625
- gate_proj: bfloat16 [2048, 6144], P('row', 'col'), may hold values from -0.125 to 0.125
- up_proj: bfloat16 [2048, 6144], P('row', 'col'), may hold values from -0.125 to 0.125
- down_proj: bfloat16 [2048, 6144], P('row', 'col'), may hold values from -0.15625 to 0.15625
- mix_gain: float32 [2048], P('row'), may hold values from 0.5 to 1.5
- mlp_gain: float32 [2048], P('row'), may hold values from 0.5 to 1.5
- x_bias: float32 [2560], P('col'), may hold values from -3 to 3
- y_bias: float32 [2560], P('col'), may hold values from -3 to 3
- conv_w: float32 [4, 2560], P(None, 'col'), may hold values from -3 to 3
- conv_b: float32 [2560], P('col'), may hold values from -2 to 2
- rec_gate_w: bfloat16 [16, 160, 160], P('col'), may hold values from -0.5 to 0.5
- in_gate_w: bfloat16 [16, 160, 160], P('col'), may hold values from -0.5 to 0.5
- rec_gate_b: float32 [2560], P('col'), may hold values from -3 to 3
- in_gate_b: float32 [2560], P('col'), may hold values from -3 to 3
- decay_param: float32 [2560], P('col'), may hold values from -7 to -2
Outputs:
- output: bfloat16 [2048, 4096], P('row', ('dp', 'col'))
- inputs_grad: float32 [2048, 4096], P('row', ('dp', 'col'))
- x_proj_grad: float32 [2048, 2560], P('row', 'col')
- y_proj_grad: float32 [2048, 2560], P('row', 'col')
- out_proj_grad: float32 [2560, 2048], P('col', 'row')
- gate_proj_grad: float32 [2048, 6144], P('row', 'col')
- up_proj_grad: float32 [2048, 6144], P('row', 'col')
- down_proj_grad: float32 [2048, 6144], P('row', 'col')
- mix_gain_grad: float32 [2048], P('row')
- mlp_gain_grad: float32 [2048], P('row')
- x_bias_grad: float32 [2560], P('col')
- y_bias_grad: float32 [2560], P('col')
- conv_w_grad: float32 [4, 2560], P(None, 'col')
- conv_b_grad: float32 [2560], P('col')
- rec_gate_w_grad: float32 [16, 160, 160], P('col')
- in_gate_w_grad: float32 [16, 160, 160], P('col')
- rec_gate_b_grad: float32 [2560], P('col')
- in_gate_b_grad: float32 [2560], P('col')
- decay_param_grad: float32 [2560], P('col')
The draws below stay inside these ranges and needn't reach their ends.
Inputs may be any that keep to these rules, and one draw needn't show every extreme that they name: `starts`: each packed sequence of 1024 tokens is filled in order with documents of 60 to 800 tokens, the last cut by the sequence's end; every sequence begins with 1.
All inputs are finite; a program needn't handle non-finite values.
Results may differ from the reference program's by a relative error of at most 0.019.
Values may be sent and summed in bfloat16 or wider, within the bound.
A program may use at most 256 MiB of HBM per device.

```python
import math
import jax
import jax.numpy as jnp
from jax import lax

D = 2048
R = 2560
FF = 6144
HEADS = 16
CONV = 4
SEQ_LEN = 1024
HEAD_DIM = 160
TOKENS = 4096
NSEQ = 4
DOC_MIN = 60
DOC_MAX = 800


def draw_starts(key, part):
    piece_count = SEQ_LEN // DOC_MIN + 1
    doc_lengths = jax.random.randint(key, (NSEQ, piece_count), DOC_MIN, DOC_MAX + 1)
    doc_ends = jnp.cumsum(doc_lengths, axis=1, dtype=jnp.int32)
    positions = jnp.arange(SEQ_LEN, dtype=jnp.int32)
    marked = jnp.any(positions[None, :, None] == doc_ends[:, None, :], axis=2)
    first_col = positions[None, :] == 0
    return jnp.where(marked | first_col, 1, 0).astype(jnp.int32).reshape(NSEQ * SEQ_LEN)


def shard_levels(rng, dims, cuts, low, high):
    def one(position, parts):
        heights = jax.random.uniform(jax.random.fold_in(jax.random.fold_in(rng, 6), position), (parts,), jnp.float32, low / len(cuts), high / len(cuts))
        return jnp.repeat(jnp.exp(heights), dims[position] // parts).reshape((-1,) + (1,) * (len(dims) - position - 1))

    gain = one(*cuts[0])
    for cut in cuts[1:]:
        gain = gain * one(*cut)
    return gain


def scatter_about(stream_key, shape, width, reach, cuts=(), kind=jnp.bfloat16):
    values = jax.random.normal(stream_key, shape, jnp.float32) * width
    if len(cuts) > 0:
        values = shard_levels(stream_key, shape, cuts, -0.22, 0.18) * values
    return jnp.clip(values, min=-reach, max=reach).astype(kind)


def setup_inputs(seed: int = 0) -> dict:
    streams_of = jax.random.split(jax.random.key(seed), 21)
    return {
        "inputs": scatter_about(streams_of[0], (D, TOKENS), 1.0, 6.0, ((0, 4), (1, 8))),
        "cotangent": scatter_about(streams_of[1], (D, TOKENS), 1.0, 6.0, ((0, 4), (1, 8))),
        "starts": draw_starts(jax.random.fold_in(streams_of[20], 71), 0),
        "x_proj": scatter_about(streams_of[3], (D, R), D ** -0.5, 0.125, ((0, 4), (1, 2))),
        "y_proj": scatter_about(streams_of[4], (D, R), D ** -0.5, 0.125, ((0, 4), (1, 2))),
        "out_proj": scatter_about(streams_of[5], (R, D), (R // 2) ** -0.5, 0.15625, ((0, 2), (1, 4))),
        "gate_proj": scatter_about(streams_of[6], (D, FF), D ** -0.5, 0.125, ((0, 4), (1, 2))),
        "up_proj": scatter_about(streams_of[7], (D, FF), D ** -0.5, 0.125, ((0, 4), (1, 2))),
        "down_proj": scatter_about(streams_of[8], (D, FF), (FF // 4) ** -0.5, 0.15625, ((0, 4), (1, 2))),
        "mix_gain": jnp.clip(1.0 + 0.1 * jax.random.normal(streams_of[9], (D,), jnp.float32), 0.5, 1.5),
        "mlp_gain": jnp.clip(1.0 + 0.1 * jax.random.normal(streams_of[10], (D,), jnp.float32), 0.5, 1.5),
        "x_bias": scatter_about(streams_of[11], (R,), 0.5, 3.0, ((0, 2),), jnp.float32),
        "y_bias": scatter_about(streams_of[12], (R,), 0.5, 3.0, ((0, 2),), jnp.float32),
        "conv_w": scatter_about(streams_of[13], (CONV, R), 0.5, 3.0, ((1, 2),), jnp.float32),
        "conv_b": scatter_about(streams_of[14], (R,), 0.3, 2.0, ((0, 2),), jnp.float32),
        "rec_gate_w": scatter_about(streams_of[15], (HEADS, HEAD_DIM, HEAD_DIM), HEAD_DIM ** -0.5, 0.5, ((0, 2),)),
        "in_gate_w": scatter_about(streams_of[16], (HEADS, HEAD_DIM, HEAD_DIM), HEAD_DIM ** -0.5, 0.5, ((0, 2),)),
        "rec_gate_b": scatter_about(streams_of[17], (R,), 0.5, 3.0, ((0, 2),), jnp.float32),
        "in_gate_b": scatter_about(streams_of[18], (R,), 0.5, 3.0, ((0, 2),), jnp.float32),
        "decay_param": jnp.clip(-7.0 + 5.0 * jax.random.uniform(streams_of[19], (R,), jnp.float32) ** shard_levels(streams_of[19], (R,), ((0, 2),), -0.2, 0.2), -7.0, -2.0),
    }


@jax.custom_vjp
def low(v):
    return lax.optimization_barrier(v.astype(jnp.bfloat16)).astype(jnp.float32)

@jax.custom_vjp
def low_back(v):
    return v

def low_keep(v):
    return (low(v), None)

def low_pass(kept, grad):
    return (grad,)

def back_keep(v):
    return (v, None)

def back_low(kept, grad):
    return (low(grad),)
low.defvjp(low_keep, low_pass)
low_back.defvjp(back_keep, back_low)
EPS = 1e-06
GATE_C = 8.0

def rms_norm(values, norm_gain):
    inv_rms = lax.rsqrt(lax.optimization_barrier(jnp.mean(values * values, axis=-1, keepdims=True)) + EPS)
    return values * inv_rms * norm_gain

def matmul(left, right):
    return jnp.dot(left, right, precision=lax.Precision.HIGHEST)

def gelu_tanh(values):
    return jax.nn.gelu(values, approximate=True)

def chain(earlier, later):
    return (earlier[0] * later[0], later[0] * earlier[1] + later[1])

def causal_conv(values, conv_w, conv_b, segment_ids):
    result = values * conv_w[0] + conv_b
    for offset in range(1, CONV):
        lagged = jnp.pad(values, ((offset, 0), (0, 0)))[:-offset]
        earlier_ids = jnp.pad(segment_ids, (offset, 0), constant_values=-1)[:-offset]
        result = result + jnp.where((earlier_ids == segment_ids)[:, None], lagged, 0.0) * conv_w[offset]
    return result

def block_gates(conv_vals, gate_w, gate_b):
    token_count = conv_vals.shape[0]
    heads = conv_vals.reshape(token_count, HEADS, HEAD_DIM)
    mixed = jnp.einsum('thk,hkj->thj', heads, gate_w, precision=lax.Precision.HIGHEST)
    return mixed.reshape(token_count, R) + gate_b

def recurrence(rec_pre, in_pre, conv_vals, decay_param, flags):
    rec_gate = jax.nn.sigmoid(rec_pre)
    in_gate = jax.nn.sigmoid(in_pre)
    log_keep = -GATE_C * rec_gate * jax.nn.softplus(decay_param)
    keep_rate = jnp.exp(log_keep)
    fresh = (flags == 1)[:, None]
    multiplier = jnp.where(fresh, 1.0, jnp.sqrt(-jnp.expm1(2.0 * log_keep)))
    driven = conv_vals * in_gate * multiplier
    carried = jnp.where(fresh, 0.0, keep_rate)
    unused, states = lax.associative_scan(chain, (carried, driven), axis=0)
    return states

def layer(values, flags, x_proj, y_proj, out_proj, gate_proj, up_proj, down_proj, mix_gain, mlp_gain, x_bias, y_bias, conv_w, conv_b, rec_gate_w, in_gate_w, rec_gate_b, in_gate_b, decay_param):
    segment_ids = jnp.cumsum(flags, dtype=jnp.int32)
    normed_mix = low(rms_norm(values, mix_gain))
    x_pre = low_back(matmul(normed_mix, x_proj) + x_bias)
    y_pre = low_back(matmul(normed_mix, y_proj) + y_bias)
    conv_out = low(causal_conv(x_pre, conv_w, conv_b, segment_ids))
    rec_pre = low_back(block_gates(conv_out, rec_gate_w, rec_gate_b))
    in_pre = low_back(block_gates(conv_out, in_gate_w, in_gate_b))
    states = recurrence(rec_pre, in_pre, conv_out, decay_param, flags)
    mixed = low(states * gelu_tanh(y_pre))
    resid_mid = values + low_back(matmul(mixed, out_proj))
    normed_mlp = low(rms_norm(resid_mid, mlp_gain))
    gate_vals = low_back(matmul(normed_mlp, gate_proj))
    up_vals = low_back(matmul(normed_mlp, up_proj))
    activ = low(gelu_tanh(gate_vals) * up_vals)
    return resid_mid + matmul(activ, down_proj.T)

def reference(inputs, cotangent, starts, x_proj, y_proj, out_proj, gate_proj, up_proj, down_proj, mix_gain, mlp_gain, x_bias, y_bias, conv_w, conv_b, rec_gate_w, in_gate_w, rec_gate_b, in_gate_b, decay_param):
    params = tuple((item.astype(jnp.float32) for item in (x_proj, y_proj, out_proj, gate_proj, up_proj, down_proj, mix_gain, mlp_gain, x_bias, y_bias, conv_w, conv_b, rec_gate_w, in_gate_w, rec_gate_b, in_gate_b, decay_param)))
    group_size = math.gcd(NSEQ, max(1, 4096 // SEQ_LEN))
    block_count = NSEQ // group_size
    block_rows = group_size * SEQ_LEN
    in_blocks = inputs.astype(jnp.float32).T.reshape(block_count, block_rows, D)
    cot_blocks = cotangent.astype(jnp.float32).T.reshape(block_count, block_rows, D)
    flag_blocks = starts.reshape(block_count, block_rows)

    def visit(totals, block_item):
        block_in, block_cot, block_flags = block_item

        def forward(values, *weights):
            return layer(values, block_flags, *weights)
        result, pullback = jax.vjp(forward, block_in, *params)
        grad_list = pullback(block_cot)
        totals = tuple((acc + part_grad for acc, part_grad in zip(totals, grad_list[1:])))
        return (totals, (result.astype(jnp.bfloat16), grad_list[0]))
    zero_grads = tuple((jnp.zeros_like(item) for item in params))
    totals, (layer_outs, in_grads) = lax.scan(visit, zero_grads, (in_blocks, cot_blocks, flag_blocks))
    return (layer_outs.reshape(TOKENS, D).T, in_grads.reshape(TOKENS, D).T, totals[0], totals[1], totals[2], totals[3], totals[4], totals[5], totals[6], totals[7], totals[8], totals[9], totals[10], totals[11], totals[12], totals[13], totals[14], totals[15], totals[16])
```

```python
import functools

import jax
import jax.numpy as jnp
from jax import lax
from jax.experimental import pallas as pl
from jax.experimental.pallas import tpu as pltpu
from jax.sharding import PartitionSpec as P

MESH = pl.DeviceIdType.MESH

D = 2048


EPS = 1e-06
GATE_C = 8.0
CONTRACT_ROWS = (((0,), (0,)), ((), ()))
CONTRACT_COLS = (((1,), (1,)), ((), ()))
CONTRACT_PLAIN = (((1,), (0,)), ((), ()))


def from_behind(value, axis, by):
    count = lax.axis_size(axis)
    pairs = [(i, i + by) for i in range(count) if 0 <= i + by < count]
    return lax.ppermute(value, axis, pairs)


def carried_in(value, axis, join, neutral, backward):
    count, mine = (lax.axis_size(axis), lax.axis_index(axis))
    pieces = jax.tree.map(lambda part: lax.all_gather(part, axis), value)
    if backward:
        pieces = jax.tree.map(lambda part: part[::-1], pieces)
        mine = count - 1 - mine
    subtotal = jax.tree.map(
        lambda part, zero: jnp.full_like(part, 0) + jnp.asarray(zero, part.dtype), value, neutral
    )

    def hop(position, subtotal):
        longer = join(subtotal, jax.tree.map(lambda part: part[position], pieces))
        return jax.tree.map(lambda new, old: jnp.where(position < mine, new, old), longer, subtotal)

    return lax.fori_loop(0, count - 1, hop, subtotal)


def chain(earlier, later):
    return (earlier[0] * later[0], later[0] * earlier[1] + later[1])


def adjoint_chain(earlier, later):
    return (later[0] * earlier[0], later[1] + later[0] * earlier[1])


def gelu_tanh(values):
    return jax.nn.gelu(values, approximate=True)


def glu_piece(gate_vals, up_vals):
    return gelu_tanh(gate_vals) * up_vals


def causal_conv(values, conv_w, conv_b, segment_ids):
    result = values * conv_w[0] + conv_b
    for offset in range(1, conv_w.shape[0]):
        lagged = jnp.pad(values, ((offset, 0), (0, 0)))[:-offset]
        earlier_ids = jnp.pad(segment_ids, (offset, 0), constant_values=-1)[:-offset]
        result = (
            result + jnp.where((earlier_ids == segment_ids)[:, None], lagged, 0.0) * conv_w[offset]
        )
    return result


def local_recurrence(rec_pre, in_pre, conv_vals, decay_param, flags):
    rec_gate = jax.nn.sigmoid(rec_pre)
    in_gate = jax.nn.sigmoid(in_pre)
    log_keep = -GATE_C * rec_gate * jax.nn.softplus(decay_param)
    keep_rate = jnp.exp(log_keep)
    fresh = (flags == 1)[:, None]
    multiplier = jnp.where(fresh, 1.0, jnp.sqrt(-jnp.expm1(2.0 * log_keep)))
    driven = conv_vals * in_gate * multiplier
    carried = jnp.where(fresh, 0.0, keep_rate)
    cum_keep, states = lax.associative_scan(chain, (carried, driven), axis=0)
    return (cum_keep, states)


def row_sums(values):
    return lax.psum(values, "row")


def norm_forward(values, norm_gain):
    squares = row_sums(jnp.sum(values * values, axis=1))
    inv_rms = lax.rsqrt(squares / D + EPS)
    return (values * inv_rms[:, None] * norm_gain, inv_rms)


def norm_backward(values, inv_rms, norm_gain, incoming):
    scaled = norm_gain * incoming
    dots = row_sums(jnp.sum(scaled * values, axis=1))
    values_grad = inv_rms[:, None] * scaled - values * (inv_rms**3 * dots / D)[:, None]
    gain_grad = jnp.sum(incoming * values * inv_rms[:, None], axis=0)
    return (values_grad, gain_grad)


def gather_edge(values):
    return lax.all_gather(values, "col", axis=0, tiled=True)


def gather_mid(values):
    return lax.all_gather(values, "row", axis=0, tiled=True)


def row_partial(whole, weight, dims):
    return lax.psum_scatter(
        lax.dot_general(whole, weight, dims, preferred_element_type=jnp.float32),
        "row",
        scatter_dimension=0,
        tiled=True,
    )


def col_partial(whole, weight, dims):
    return lax.psum_scatter(
        lax.dot_general(whole, weight, dims, preferred_element_type=jnp.float32),
        "col",
        scatter_dimension=0,
        tiled=True,
    )


def project_in(normed, weight):
    whole = gather_edge(normed)
    result = row_partial(whole, weight, CONTRACT_PLAIN)
    return (result, whole)


def weight_grad(left, right):
    return lax.dot_general(left, right, CONTRACT_ROWS, preferred_element_type=jnp.float32)


def local(
    inputs,
    cotangent,
    starts,
    x_proj,
    y_proj,
    out_proj,
    gate_proj,
    up_proj,
    down_proj,
    mix_gain,
    mlp_gain,
    x_bias,
    y_bias,
    conv_w,
    conv_b,
    rec_gate_w,
    in_gate_w,
    rec_gate_b,
    in_gate_b,
    decay_param,
):
    rows_mid = starts.shape[0]
    rec_width = x_proj.shape[1]
    ff_width = gate_proj.shape[1]
    head_count = rec_gate_w.shape[0]
    margin = conv_w.shape[0] - 1
    mix_weights = jnp.concatenate([x_proj, y_proj], axis=1)
    mlp_weights = jnp.concatenate([gate_proj, up_proj], axis=1)
    cot_rows = cotangent.T
    resid = inputs.astype(jnp.float32).T
    normed_mix, inv_rms_mix = norm_forward(resid, mix_gain)
    normed_mix = normed_mix.astype(jnp.bfloat16)
    pre_both, whole_mix = project_in(normed_mix, mix_weights)
    x_pre = pre_both[:, :rec_width] + x_bias
    y_pre = pre_both[:, rec_width:] + y_bias
    x_tail, flag_tail = from_behind(
        (x_pre[rows_mid - margin :], starts[rows_mid - margin :].astype(jnp.float32)), "row", 1
    )
    ext_flags = jnp.concatenate([flag_tail.astype(jnp.int32), starts])
    ext_ids = jnp.cumsum(ext_flags, dtype=jnp.int32)
    ext_x = jnp.concatenate([x_tail, x_pre], axis=0)

    def conv_piece(values, taps, offsets):
        return causal_conv(values, taps, offsets, ext_ids)[margin:]

    conv_vals, conv_pull = jax.vjp(conv_piece, ext_x, conv_w, conv_b)
    conv_low = conv_vals.astype(jnp.bfloat16)
    conv_heads = conv_low.reshape(rows_mid, head_count, -1)
    rec_pre = (
        jnp.einsum(
            "thk,hkj->thj", conv_heads, rec_gate_w, preferred_element_type=jnp.float32
        ).reshape(rows_mid, rec_width)
        + rec_gate_b
    )
    in_pre = (
        jnp.einsum(
            "thk,hkj->thj", conv_heads, in_gate_w, preferred_element_type=jnp.float32
        ).reshape(rows_mid, rec_width)
        + in_gate_b
    )

    def scan_piece(rec_vals, in_vals, conv_input, decay_vals):
        return local_recurrence(rec_vals, in_vals, conv_input, decay_vals, starts)

    (cum_keep, local_states), scan_pull = jax.vjp(
        scan_piece, rec_pre, in_pre, conv_low.astype(jnp.float32), decay_param
    )
    ones_row = jnp.ones((rec_width,), jnp.float32)
    zeros_row = jnp.zeros((rec_width,), jnp.float32)
    incoming = carried_in(
        (cum_keep[rows_mid - 1], local_states[rows_mid - 1]),
        "row",
        chain,
        (ones_row, zeros_row),
        False,
    )
    state_prev = incoming[1]
    states = local_states + cum_keep * state_prev
    y_act, y_pull = jax.vjp(gelu_tanh, y_pre)
    mixed = (states * y_act).astype(jnp.bfloat16)
    whole_mixed = gather_mid(mixed)
    resid_mid = resid + col_partial(whole_mixed, out_proj, CONTRACT_PLAIN)
    normed_mlp, inv_rms_mlp = norm_forward(resid_mid, mlp_gain)
    normed_mlp = normed_mlp.astype(jnp.bfloat16)
    gate_up, whole_mlp = project_in(normed_mlp, mlp_weights)
    activ, activ_pull = jax.vjp(glu_piece, gate_up[:, :ff_width], gate_up[:, ff_width:])
    activ = activ.astype(jnp.bfloat16)
    whole_activ = gather_mid(activ)
    output = (resid_mid + col_partial(whole_activ, down_proj, CONTRACT_COLS)).astype(jnp.bfloat16)
    cot_whole = gather_edge(cot_rows)
    d_activ = row_partial(cot_whole, down_proj, CONTRACT_PLAIN)
    activ_rows = gather_mid(activ)
    grad_down = weight_grad(cot_whole, activ_rows)
    d_gate, d_up = activ_pull(d_activ)
    d_gate_up = jnp.concatenate([d_gate, d_up], axis=1).astype(jnp.bfloat16)
    d_gate_up_whole = gather_mid(d_gate_up)
    d_normed_mlp = col_partial(d_gate_up_whole, mlp_weights, CONTRACT_COLS)
    mlp_rows = gather_edge(normed_mlp)
    grad_gate_up = weight_grad(mlp_rows, d_gate_up_whole)
    d_norm_mid, grad_mlp_gain = norm_backward(resid_mid, inv_rms_mlp, mlp_gain, d_normed_mlp)
    d_resid_mid = cot_rows.astype(jnp.float32) + d_norm_mid
    d_branch = d_resid_mid.astype(jnp.bfloat16)
    branch_whole = gather_edge(d_branch)
    d_mixed = row_partial(branch_whole, out_proj, CONTRACT_COLS)
    mixed_rows = gather_mid(mixed)
    grad_out = weight_grad(mixed_rows, branch_whole)
    d_state = d_mixed * y_act
    (d_y_pre,) = y_pull(d_mixed * states)
    own_sens = jnp.sum(d_state * cum_keep, axis=0)
    outgoing = carried_in(
        (cum_keep[rows_mid - 1], own_sens), "row", adjoint_chain, (ones_row, zeros_row), True
    )
    d_total = d_state + jnp.pad(outgoing[1][None, :], ((rows_mid - 1, 0), (0, 0)))
    d_rec_pre, d_in_pre, d_conv_direct, grad_decay = scan_pull((d_total * state_prev, d_total))
    d_rec_low = d_rec_pre.astype(jnp.bfloat16)
    d_in_low = d_in_pre.astype(jnp.bfloat16)
    d_rec_heads = d_rec_low.reshape(rows_mid, head_count, -1)
    d_in_heads = d_in_low.reshape(rows_mid, head_count, -1)
    d_conv = d_conv_direct + jnp.einsum(
        "thj,hkj->thk", d_rec_heads, rec_gate_w, preferred_element_type=jnp.float32
    ).reshape(rows_mid, rec_width)
    d_conv = d_conv + jnp.einsum(
        "thj,hkj->thk", d_in_heads, in_gate_w, preferred_element_type=jnp.float32
    ).reshape(rows_mid, rec_width)
    grad_rec_w = jnp.einsum(
        "thk,thj->hkj", conv_heads, d_rec_heads, preferred_element_type=jnp.float32
    )
    grad_in_w = jnp.einsum(
        "thk,thj->hkj", conv_heads, d_in_heads, preferred_element_type=jnp.float32
    )
    grad_rec_b = jnp.sum(d_rec_low.astype(jnp.float32), axis=0)
    grad_in_b = jnp.sum(d_in_low.astype(jnp.float32), axis=0)
    d_ext, grad_conv_w, grad_conv_b = conv_pull(d_conv)
    d_from_next = from_behind(d_ext[:margin], "row", -1)
    d_x_pre = d_ext[margin:] + jnp.pad(d_from_next, ((rows_mid - margin, 0), (0, 0)))
    d_pre = jnp.concatenate([d_x_pre, d_y_pre], axis=1).astype(jnp.bfloat16)
    bias_sums = jnp.sum(d_pre.astype(jnp.float32), axis=0)
    d_pre_whole = gather_mid(d_pre)
    d_normed_mix = col_partial(d_pre_whole, mix_weights, CONTRACT_COLS)
    mix_rows = gather_edge(normed_mix)
    grad_mix = weight_grad(mix_rows, d_pre_whole)
    d_norm_in, grad_mix_gain = norm_backward(resid, inv_rms_mix, mix_gain, d_normed_mix)
    inputs_grad = d_resid_mid + d_norm_in
    grad_mix, grad_out, grad_gate_up, grad_down = (
        lax.psum(grad_mix.astype(jnp.bfloat16), "dp").astype(jnp.float32),
        lax.psum(grad_out.astype(jnp.bfloat16), "dp").astype(jnp.float32),
        lax.psum(grad_gate_up.astype(jnp.bfloat16), "dp").astype(jnp.float32),
        lax.psum(grad_down.astype(jnp.bfloat16), "dp").astype(jnp.float32),
    )
    (
        bias_sums,
        grad_conv_w,
        grad_conv_b,
        grad_rec_w,
        grad_in_w,
        grad_rec_b,
        grad_in_b,
        grad_decay,
    ) = (
        lax.psum(bias_sums.astype(jnp.bfloat16), ("dp", "row")).astype(jnp.float32),
        lax.psum(grad_conv_w.astype(jnp.bfloat16), ("dp", "row")).astype(jnp.float32),
        lax.psum(grad_conv_b.astype(jnp.bfloat16), ("dp", "row")).astype(jnp.float32),
        lax.psum(grad_rec_w.astype(jnp.bfloat16), ("dp", "row")).astype(jnp.float32),
        lax.psum(grad_in_w.astype(jnp.bfloat16), ("dp", "row")).astype(jnp.float32),
        lax.psum(grad_rec_b.astype(jnp.bfloat16), ("dp", "row")).astype(jnp.float32),
        lax.psum(grad_in_b.astype(jnp.bfloat16), ("dp", "row")).astype(jnp.float32),
        lax.psum(grad_decay.astype(jnp.bfloat16), ("dp", "row")).astype(jnp.float32),
    )
    grad_mix_gain, grad_mlp_gain = lax.psum((grad_mix_gain, grad_mlp_gain), ("dp", "col"))
    return (
        output.T,
        inputs_grad.T,
        grad_mix[:, :rec_width],
        grad_mix[:, rec_width:],
        grad_out,
        grad_gate_up[:, :ff_width],
        grad_gate_up[:, ff_width:],
        grad_down,
        grad_mix_gain,
        grad_mlp_gain,
        bias_sums[:rec_width],
        bias_sums[rec_width:],
        grad_conv_w,
        grad_conv_b,
        grad_rec_w,
        grad_in_w,
        grad_rec_b,
        grad_in_b,
        grad_decay,
    )


GATHER_ID, FORWARD_ID, BACKWARD_ID, FINISH_ID, REDUCE_ID = (0, 1, 2, 3, 4)
BLOCK = 128
VMEM_BYTES = 56 << 20


def one_minus_exp(rate):
    series = rate * (1.0 - rate * (0.5 - rate * (1.0 / 6.0 - rate * (1.0 / 24.0 - rate / 120.0))))
    return jnp.where(rate < 0.1, series, 1.0 - jnp.exp(-rate))


GELU_C = 0.7978845608028654


def gelu_both(values):
    squared = values * values
    inner = jnp.tanh(GELU_C * values * (1.0 + 0.044715 * squared))
    value = 0.5 * values * (1.0 + inner)
    slope = 0.5 * (1.0 + inner) + 0.5 * values * (1.0 - inner * inner) * GELU_C * (
        1.0 + 3.0 * 0.044715 * squared
    )
    return (value, slope)


def down_rows(values, by):
    return pltpu.roll(values, by, 0)


def up_rows(values, by):
    return pltpu.roll(values, values.shape[0] - by, 0)


def scan_down(keep, add):
    rows = keep.shape[0]
    position = lax.broadcasted_iota(jnp.int32, keep.shape, 0)
    step = 1
    while step < rows:
        if step < 8:
            inside = position >= step
            before_keep = jnp.where(inside, down_rows(keep, step), 1.0)
            before_add = jnp.where(inside, down_rows(add, step), 0.0)
            add = add + keep * before_add
            keep = keep * before_keep
        else:
            add = jnp.concatenate([add[:step], add[step:] + keep[step:] * add[:-step]], axis=0)
            keep = jnp.concatenate([keep[:step], keep[step:] * keep[:-step]], axis=0)
        step *= 2
    return (keep, add)


def scan_up(keep, add):
    rows = keep.shape[0]
    position = lax.broadcasted_iota(jnp.int32, keep.shape, 0)
    step = 1
    while step < rows:
        if step < 8:
            inside = position < rows - step
            after_keep = jnp.where(inside, up_rows(keep, step), 1.0)
            after_add = jnp.where(inside, up_rows(add, step), 0.0)
            add = add + keep * after_add
            keep = keep * after_keep
        else:
            add = jnp.concatenate([add[:-step] + keep[:-step] * add[step:], add[-step:]], axis=0)
            keep = jnp.concatenate([keep[:-step] * keep[step:], keep[-step:]], axis=0)
        step *= 2
    return (keep, add)


def mixer_forward_kernel(
    pre, masks, vec, rec_w, in_w, mixed, x_pre, conv, rec_gate, in_gate, states, tail, carry
):
    width = x_pre.shape[1]

    @pl.when(pl.program_id(0) == 0)
    def _():
        tail[...] = jnp.zeros_like(tail)
        carry[...] = jnp.zeros_like(carry)

    marks = masks[...]
    x = pre[:, :width] + vec[0:1, :]
    x_pre[...] = x
    longer = jnp.concatenate([tail[...], x], axis=0)
    tail[...] = x[BLOCK - 8 :]
    total = x * vec[2:3, :] + vec[6:7, :]
    for tap in range(1, 4):
        total = total + marks[:, tap : tap + 1] * down_rows(longer, tap)[8:] * vec[
            2 + tap : 3 + tap, :
        ]
    low = total.astype(jnp.bfloat16)
    conv[...] = low
    rec = jax.nn.sigmoid(
        jnp.dot(low, rec_w[...], preferred_element_type=jnp.float32) + vec[7:8, :]
    )
    inn = jax.nn.sigmoid(
        jnp.dot(low, in_w[...], preferred_element_type=jnp.float32) + vec[8:9, :]
    )
    rec_gate[...] = rec
    in_gate[...] = inn
    log_keep = rec * vec[9:10, :]
    fresh = marks[:, 0:1]
    scale = jnp.where(fresh > 0.5, 1.0, jnp.sqrt(one_minus_exp(-2.0 * log_keep)))
    driven = low.astype(jnp.float32) * inn * scale
    keep, add = scan_down(jnp.exp(log_keep) * (1.0 - fresh), driven)
    state = add + keep * carry[0:1, :]
    carry[...] = jnp.broadcast_to(state[BLOCK - 1 :, :], carry.shape)
    states[...] = state
    y = pre[:, width:] + vec[1:2, :]
    mixed[:, :width] = (state * gelu_both(y)[0]).astype(jnp.bfloat16)
    mixed[:, width:] = jnp.zeros((BLOCK, mixed.shape[1] - width), jnp.bfloat16)


def mixer_forward(pre, masks, vec, rec_w, in_w, padded):
    tokens, width = (pre.shape[0], rec_w.shape[0])

    def block(columns):
        return pl.BlockSpec((BLOCK, columns), lambda i: (i, 0))

    def whole(array):
        return pl.BlockSpec(array.shape, lambda i: (0, 0))

    def out(columns, kind):
        return jax.ShapeDtypeStruct((tokens, columns), kind)

    return pl.pallas_call(
        mixer_forward_kernel,
        grid=(tokens // BLOCK,),
        in_specs=[block(2 * width), block(8), whole(vec), whole(rec_w), whole(in_w)],
        out_specs=[block(padded)] + [block(width)] * 5,
        out_shape=[
            out(padded, jnp.bfloat16),
            out(width, jnp.float32),
            out(width, jnp.bfloat16),
            out(width, jnp.float32),
            out(width, jnp.float32),
            out(width, jnp.float32),
        ],
        scratch_shapes=[pltpu.VMEM((8, width), jnp.float32), pltpu.VMEM((8, width), jnp.float32)],
        compiler_params=pltpu.CompilerParams(vmem_limit_bytes=32 << 20),
        name="mixer_forward",
    )(pre, masks, vec, rec_w, in_w)


def mixer_backward_kernel(
    d_mixed,
    pre,
    masks,
    vec,
    rec_w,
    in_w,
    x_pre,
    x_before,
    conv,
    rec_gate,
    in_gate,
    states,
    state_before,
    d_pre,
    d_gates,
    sums,
    edge,
    carry,
):
    width = x_pre.shape[1]

    @pl.when(pl.program_id(0) == 0)
    def _():
        edge[...] = jnp.zeros_like(edge)
        carry[...] = jnp.zeros_like(carry)
        sums[...] = jnp.zeros_like(sums)

    position = lax.broadcasted_iota(jnp.int32, (BLOCK, width), 0)
    marks = masks[...]
    fresh = marks[:, 0:1]
    stale = 1.0 - fresh
    gelu, slope = gelu_both(pre[:, width:] + vec[1:2, :])
    state = states[...]
    incoming = d_mixed[...]
    d_y = (incoming * state * slope).astype(jnp.bfloat16)
    rec, inn = (rec_gate[...], in_gate[...])
    conv_vals = conv[...].astype(jnp.float32)
    log_keep = rec * vec[9:10, :]
    keep_rate = jnp.exp(log_keep)
    scale = jnp.where(fresh > 0.5, 1.0, jnp.sqrt(one_minus_exp(-2.0 * log_keep)))
    carried = keep_rate * stale
    after = jnp.where(position == BLOCK - 1, carry[1:2, :], up_rows(carried, 1))
    keep, add = scan_up(after, incoming * gelu)
    adjoint = add + keep * carry[0:1, :]
    carry[0:1, :] = adjoint[0:1]
    carry[1:2, :] = carried[0:1]
    earlier = jnp.where(position == 0, state_before[7:8, :], down_rows(state, 1))
    drive = adjoint * scale
    d_log = stale * (
        adjoint * earlier * keep_rate
        - adjoint * inn * conv_vals * keep_rate * keep_rate / scale
    )
    d_rec = (d_log * vec[9:10, :] * rec * (1.0 - rec)).astype(jnp.bfloat16)
    d_in = (drive * conv_vals * inn * (1.0 - inn)).astype(jnp.bfloat16)
    d_gates[:, :width] = d_rec
    d_gates[:, width:] = d_in
    d_conv = drive * inn
    d_conv = d_conv + lax.dot_general(
        d_rec, rec_w[...], CONTRACT_COLS, preferred_element_type=jnp.float32
    )
    d_conv = d_conv + lax.dot_general(
        d_in, in_w[...], CONTRACT_COLS, preferred_element_type=jnp.float32
    )
    x = x_pre[...]
    longer = jnp.concatenate([x_before[...], x], axis=0)

    def column(values):
        return jnp.sum(values, axis=0, keepdims=True)

    d_x = d_conv * vec[2:3, :]
    taps = [column(d_conv * x)]
    for tap in range(1, 4):
        part = marks[:, tap : tap + 1] * d_conv
        taps.append(column(part * down_rows(longer, tap)[8:]))
        beyond = jnp.concatenate([part, edge[8 * tap - 8 : 8 * tap, :]], axis=0)
        d_x = d_x + vec[2 + tap : 3 + tap, :] * up_rows(beyond, tap)[:BLOCK]
        edge[8 * tap - 8 : 8 * tap, :] = part[:8]
    d_x = d_x.astype(jnp.bfloat16)
    d_pre[:, :width] = d_x
    d_pre[:, width:] = d_y
    parts = (
        [column(d_x.astype(jnp.float32)), column(d_y.astype(jnp.float32))]
        + taps
        + [
            column(d_conv),
            column(d_rec.astype(jnp.float32)),
            column(d_in.astype(jnp.float32)),
            column(d_log * rec) * vec[10:11, :],
        ]
    )
    for place, part in enumerate(parts):
        sums[place : place + 1, :] += part


def mixer_backward(d_mixed, pre, masks, vec, rec_w, in_w, x_pre, conv, rec_gate, in_gate, states):
    tokens, width = x_pre.shape
    last = tokens // BLOCK - 1

    def block(columns):
        return pl.BlockSpec((BLOCK, columns), lambda i: (last - i, 0))

    def before():
        return pl.BlockSpec(
            (8, width), lambda i: (jnp.maximum((last - i) * (BLOCK // 8) - 1, 0), 0)
        )

    def whole(array):
        return pl.BlockSpec(array.shape, lambda i: (0, 0))

    return pl.pallas_call(
        mixer_backward_kernel,
        grid=(tokens // BLOCK,),
        in_specs=[
            block(width),
            block(2 * width),
            block(8),
            whole(vec),
            whole(rec_w),
            whole(in_w),
            block(width),
            before(),
            block(width),
            block(width),
            block(width),
            block(width),
            before(),
        ],
        out_specs=[block(2 * width), block(2 * width), pl.BlockSpec((16, width), lambda i: (0, 0))],
        out_shape=[
            jax.ShapeDtypeStruct((tokens, 2 * width), jnp.bfloat16),
            jax.ShapeDtypeStruct((tokens, 2 * width), jnp.bfloat16),
            jax.ShapeDtypeStruct((16, width), jnp.float32),
        ],
        scratch_shapes=[pltpu.VMEM((24, width), jnp.float32), pltpu.VMEM((8, width), jnp.float32)],
        compiler_params=pltpu.CompilerParams(vmem_limit_bytes=32 << 20),
        name="mixer_backward",
    )(d_mixed, pre, masks, vec, rec_w, in_w, x_pre, x_pre, conv, rec_gate, in_gate, states, states)


def here():
    return (lax.axis_index("dp"), lax.axis_index("row"), lax.axis_index("col"))


def flip(index):
    return index + 1 - 2 * (index % 2)


def across(row):
    return (row + 2) % 4


def greet(peers):
    barrier = pltpu.get_barrier_semaphore()
    for peer in peers:
        pl.semaphore_signal(barrier, inc=1, device_id=peer, device_id_type=MESH)
    pl.semaphore_wait(barrier, len(peers))


class Copies:
    def __init__(self, send, recv):
        self.send, self.recv, self.used, self.sent = (send, recv, 0, [])

    def make(self, source, target, device):
        place = self.used
        self.used += 1
        if device is None:
            copy = pltpu.make_async_copy(source, target, self.recv.at[place])
        else:
            copy = pltpu.make_async_remote_copy(
                src_ref=source,
                dst_ref=target,
                send_sem=self.send.at[place],
                recv_sem=self.recv.at[place],
                device_id=device,
                device_id_type=MESH,
            )
            self.sent.append(copy)
        return copy

    def go(self, source, target, device):
        copy = self.make(source, target, device)
        copy.start()
        return copy

    def finish(self):
        for copy in self.sent:
            copy.wait_send()


def arrived(copy):
    copy.wait_recv()


def spread(copies, own, place, halves):
    z, r, c = here()
    twin, side, top = ((z, flip(r), c), (z, across(r), c), (z, r, 1 - c))
    to_side = copies.go(own, place(r, c), side)
    to_top = copies.go(own, place(r, c), top)
    to_twin = copies.go(own, place(r, c), twin)
    arrived(to_side)
    from_side = place(across(r), c)
    on_top = copies.go(halves(from_side, 0), halves(from_side, 0), top)
    late = [to_twin, copies.go(from_side, from_side, twin)]
    arrived(to_top)
    from_top = place(r, 1 - c)
    on_side = copies.go(halves(from_top, 1), halves(from_top, 1), side)
    late.append(copies.go(from_top, from_top, twin))
    far = place(across(r), 1 - c)
    for half, copy in enumerate((on_top, on_side)):
        arrived(copy)
        late.append(copies.go(halves(far, half), halves(far, half), twin))
    return late


def gather_kernel(*refs):
    x_in, c_in, s_in, mix_in, out_in, *mlp_in = refs[:8]
    x_all, c_all, s_all, mix_all, out_all, *mlp_all = refs[8:16]
    send, recv = refs[16:]
    z, r, c = here()
    twin, side, cross, top, pair = (
        (z, flip(r), c),
        (z, across(r), c),
        (z, flip(across(r)), c),
        (z, r, 1 - c),
        (flip(z), r, c),
    )
    greet((twin, side, cross, top, pair))
    copies = Copies(send, recv)
    rows, columns = x_in.shape
    depth, width = (mlp_in[0].shape[0], mlp_in[0].shape[1] // 4)
    rec = out_in.shape[0] // 4

    def part(start, size, step):
        return pl.ds(pl.multiple_of(start * step, step), size)

    matrices = [
        (lambda to: mix_in.at[to], lambda of: mix_all.at[part(of, depth, depth), :], depth),
        (
            lambda to: out_in.at[part(to, rec, rec), :],
            lambda of: out_all.at[:, part(of, columns, columns)],
            rec,
        ),
    ] + [
        (
            lambda to, source=source: source.at[:, part(to, width, width)],
            lambda of, target=target: target.at[part(of, depth, depth), :],
            depth,
        )
        for source, target in zip(mlp_in, mlp_all)
    ]

    def half(ref, which, size):
        return ref.at[part(which, size // 2, size // 2), :]

    def block(ref):
        return lambda row, col: ref.at[part(col, rows, rows), part(row, columns, columns)]

    def halves(ref, which):
        return ref.at[pl.ds(which * (rows // 2), rows // 2), :]

    locals_ = [
        copies.go(x_in, block(x_all)(r, c), None),
        copies.go(c_in, block(c_all)(r, c), None),
        copies.go(s_in, s_all.at[r], None),
    ]
    late = []
    for peer in (twin, side, cross):
        late.append(copies.go(s_in, s_all.at[r], peer))
    mine = z % 2
    first = []
    for source, target, size in matrices:
        locals_.append(copies.go(source(r), target(r), None))
        late.append(copies.go(source(flip(r)), target(r), twin))
        for peer in (side, cross):
            first.append(
                copies.make(half(source(peer[1]), mine, size), half(target(r), mine, size), peer)
            )
    for copy in first[:4]:
        copy.start()
    late.extend(spread(copies, x_in, block(x_all), halves))
    for copy in first[4:]:
        copy.start()
    for place, (source, target, size) in enumerate(matrices):
        for which, peer in enumerate((side, cross)):
            arrived(first[2 * place + which])
            piece = half(target(peer[1]), mine, size)
            late.append(copies.go(piece, piece, pair))
    late.extend(spread(copies, c_in, block(c_all), halves))
    for copy in late:
        arrived(copy)
    for copy in locals_:
        copy.wait()
    copies.finish()


def gather(x_in, c_in, s_in, mix_in, out_in, mlp_in):
    rows, columns = x_in.shape
    depth, width = (mlp_in[0].shape[0], mlp_in[0].shape[1] // 4)

    def shape(*dims, kind=jnp.bfloat16):
        return jax.ShapeDtypeStruct(dims, kind)

    outs = [
        shape(2 * rows, 4 * columns),
        shape(2 * rows, 4 * columns),
        shape(4, *s_in.shape, kind=s_in.dtype),
        shape(4 * depth, mix_in.shape[2]),
        shape(out_in.shape[0] // 4, 4 * columns),
    ] + [shape(4 * depth, width)] * 3
    return pl.pallas_call(
        gather_kernel,
        in_specs=[pl.BlockSpec(memory_space=pl.ANY)] * 8,
        out_specs=[pl.BlockSpec(memory_space=pl.ANY)] * 8,
        out_shape=outs,
        scratch_shapes=[pltpu.SemaphoreType.DMA((64,)), pltpu.SemaphoreType.DMA((64,))],
        compiler_params=pltpu.CompilerParams(collective_id=GATHER_ID, has_side_effects=True),
        name="gather",
    )(x_in, c_in, s_in, mix_in, out_in, *mlp_in)


STRIP = 16


def strips(count, body):
    def run(index, nothing):
        body(pl.multiple_of(index * STRIP, STRIP))
        return nothing

    lax.fori_loop(0, count // STRIP, run, 0)


def token_shard(row, col):
    return col * 4 + row


def reduce_shards(copies, parts, twin_in, sums, side_in, top_in, hop_in):
    z, r, c = here()
    twin, side, top = ((z, flip(r), c), (z, across(r), c), (z, r, 1 - c))
    size = side_in.shape[0]
    half = size // 2

    def shard(row, col):
        return pl.multiple_of(token_shard(row, col) * size, size)

    spots = [(across(r), 1 - c), (across(r), c), (r, 1 - c), (r, c)]
    from_twin = [
        copies.go(parts.at[pl.ds(shard(flip(row), col), size), :], twin_in.at[place], twin)
        for place, (row, col) in enumerate(spots)
    ]

    def add_twin(place):
        arrived(from_twin[place])
        start = shard(*spots[place])

        def body(at):
            total = parts[pl.ds(start + at, STRIP), :].astype(jnp.float32) + twin_in[
                place, pl.ds(at, STRIP), :
            ].astype(jnp.float32)
            sums[place, pl.ds(at, STRIP), :] = total.astype(jnp.bfloat16)

        strips(size, body)

    def add_hop(place, which, hop):
        def body(at):
            rows = pl.ds(which * half + at, STRIP)
            total = sums[place, rows, :].astype(jnp.float32) + hop_in[
                hop, pl.ds(at, STRIP), :
            ].astype(jnp.float32)
            sums[place, rows, :] = total.astype(jnp.bfloat16)

        strips(half, body)

    def rows_of(ref, which):
        return ref.at[pl.ds(which * half, half), :]

    add_twin(0)
    hop_side = copies.go(rows_of(sums.at[0], 0), hop_in.at[0], side)
    hop_top = copies.go(rows_of(sums.at[0], 1), hop_in.at[1], top)
    add_twin(1)
    waits = [copies.go(rows_of(sums.at[1], 0), rows_of(side_in, 0), side)]
    add_twin(2)
    waits.append(copies.go(rows_of(sums.at[2], 1), rows_of(top_in, 1), top))
    add_twin(3)
    arrived(hop_top)
    add_hop(1, 1, 1)
    waits.append(copies.go(rows_of(sums.at[1], 1), rows_of(side_in, 1), side))
    arrived(hop_side)
    add_hop(2, 0, 0)
    waits.append(copies.go(rows_of(sums.at[2], 0), rows_of(top_in, 0), top))
    for copy in waits:
        arrived(copy)

    def total(at):
        rows = pl.ds(at, STRIP)
        return (
            sums[3, rows, :].astype(jnp.float32)
            + side_in[rows, :].astype(jnp.float32)
            + top_in[rows, :].astype(jnp.float32)
        )

    return total


def reduce_scratch(size, width):
    return [
        pltpu.VMEM((4, size, width), jnp.bfloat16),
        pltpu.VMEM((4, size, width), jnp.bfloat16),
        pltpu.VMEM((size, width), jnp.bfloat16),
        pltpu.VMEM((size, width), jnp.bfloat16),
        pltpu.VMEM((2, size // 2, width), jnp.bfloat16),
    ]


def near():
    z, r, c = here()
    return ((z, flip(r), c), (z, across(r), c), (z, r, 1 - c))


def spread_rows(copies, mine, full):
    z, r, c = here()
    size = mine.shape[0]
    half = size // 2

    def place(row, col):
        return full.at[pl.ds(pl.multiple_of(token_shard(row, col) * size, size), size), :]

    local = copies.go(mine, place(r, c), None)
    late = spread(
        copies, mine, place, lambda ref, which: ref.at[pl.ds(which * half, half), :]
    )
    for copy in late:
        arrived(copy)
    local.wait()


def forward_kernel(parts, resid, gain, full, resid_mid, *scratch):
    *buffers, mine, send, recv = scratch
    greet(near())
    copies = Copies(send, recv)
    total = reduce_shards(copies, parts, *buffers)

    def body(at):
        rows = pl.ds(at, STRIP)
        values = resid[rows, :].astype(jnp.float32) + total(at)
        resid_mid[rows, :] = values
        scale = lax.rsqrt(jnp.mean(values * values, axis=1, keepdims=True) + EPS)
        mine[rows, :] = (values * scale * gain[...]).astype(jnp.bfloat16)

    strips(mine.shape[0], body)
    spread_rows(copies, mine, full)
    copies.finish()


def norm_pull(values, gain, incoming):
    scale = lax.rsqrt(jnp.mean(values * values, axis=1, keepdims=True) + EPS)
    scaled = gain * incoming
    dots = jnp.sum(scaled * values, axis=1, keepdims=True)
    grad = scale * scaled - values * (scale * scale * scale * dots / values.shape[1])
    return (grad, jnp.sum(incoming * values * scale, axis=0, keepdims=True))


def backward_kernel(parts, resid_mid, cot, gain, full, d_resid, gain_grad, *scratch):
    *buffers, mine, send, recv = scratch
    greet(near())
    copies = Copies(send, recv)
    total = reduce_shards(copies, parts, *buffers)
    gain_grad[...] = jnp.zeros_like(gain_grad)

    def body(at):
        rows = pl.ds(at, STRIP)
        grad, part = norm_pull(resid_mid[rows, :], gain[...], total(at))
        grad = grad + cot[rows, :].astype(jnp.float32)
        gain_grad[...] += part
        d_resid[rows, :] = grad
        mine[rows, :] = grad.astype(jnp.bfloat16)

    strips(mine.shape[0], body)
    spread_rows(copies, mine, full)
    copies.finish()


def finish_kernel(
    parts, out_parts, resid, resid_mid, d_resid, gain, grad, output, gain_grad, *scratch
):
    buffers, more = (scratch[:5], scratch[5:10])
    mine, mine_out, send, recv = scratch[10:]
    z, r, c = here()
    twin, side, top = near()
    cross = (z, flip(across(r)), c)
    greet((twin, side, top, cross))
    copies = Copies(send, recv)
    columns = grad.shape[1]
    size = mine.shape[0]
    gain_grad[...] = jnp.zeros_like(gain_grad)

    def hand_out(source, target):
        def piece(row):
            return source.at[:, pl.ds(pl.multiple_of(row * columns, columns), columns)]

        spot = target.at[pl.ds(pl.multiple_of(r * size, size), size), :]
        waits = [copies.go(piece(peer[1]), spot, peer) for peer in (side, cross, twin)]
        return (copies.go(piece(r), spot, None), waits)

    total = reduce_shards(copies, out_parts, *more)

    def body_out(at):
        rows = pl.ds(at, STRIP)
        mine_out[rows, :] = (resid_mid[rows, :] + total(at)).astype(jnp.bfloat16)

    strips(size, body_out)
    moves = [hand_out(mine_out, output)]
    total_back = reduce_shards(copies, parts, *buffers)

    def body(at):
        rows = pl.ds(at, STRIP)
        values, part = norm_pull(resid[rows, :].astype(jnp.float32), gain[...], total_back(at))
        gain_grad[...] += part
        mine[rows, :] = (d_resid[rows, :] + values).astype(jnp.bfloat16)

    strips(size, body)
    moves.append(hand_out(mine, grad))
    for local, waits in moves:
        for copy in waits:
            arrived(copy)
        local.wait()
    copies.finish()


def vmem_call(kernel, name, place, arrays, outs, spaces, scratch, count):
    return pl.pallas_call(
        kernel,
        in_specs=[pl.BlockSpec(memory_space=pltpu.VMEM)] * len(arrays),
        out_specs=[pl.BlockSpec(memory_space=space) for space in spaces],
        out_shape=outs,
        scratch_shapes=scratch
        + [pltpu.SemaphoreType.DMA((count,)), pltpu.SemaphoreType.DMA((count,))],
        compiler_params=pltpu.CompilerParams(
            collective_id=place, has_side_effects=True, vmem_limit_bytes=VMEM_BYTES
        ),
        name=name,
    )(*arrays)


CHUNK = 16


def reduce_kernel(count, *refs):
    sources, (out, own, left, right, move_send, move_recv) = (refs[:count], refs[count : count + 6])
    end_send, low_recv, high_recv, out_recv, mid_send, first_send, last_send, local, on_send = refs[
        count + 6 :
    ]
    z, r, c = here()
    twin, side, cross = ((z, flip(r), c), (z, across(r), c), (z, flip(across(r)), c))
    is_end = (z == 0) | (z == 3)
    near_z = jnp.where(z == 0, 1, 2)
    end_z = jnp.where(z == 1, 0, 3)
    barrier = pltpu.get_barrier_semaphore()
    for peer in (twin, side, cross):
        pl.semaphore_signal(barrier, inc=1, device_id=peer, device_id_type=MESH)

    @pl.when(is_end)
    def _():
        pl.semaphore_signal(barrier, inc=1, device_id=(near_z, r, c), device_id_type=MESH)
        pl.semaphore_wait(barrier, 4)

    @pl.when(jnp.logical_not(is_end))
    def _():
        pl.semaphore_signal(barrier, inc=1, device_id=(end_z, r, c), device_id_type=MESH)
        pl.semaphore_signal(barrier, inc=1, device_id=(3 - z, r, c), device_id_type=MESH)
        pl.semaphore_wait(barrier, 5)

    rows = own.shape[1]
    half = rows // 2
    per = half // CHUNK
    chunks = 4 * per
    moves = []
    for which, peer in ((1, twin), (2, side), (3, cross)):
        start = 0
        group = []
        for place, source in enumerate(sources):
            width = source.shape[1]
            copy = pltpu.make_async_remote_copy(
                src_ref=source.at[pl.ds(pl.multiple_of(peer[1] * rows, rows), rows), :],
                dst_ref=own.at[r, :, pl.ds(start, width)],
                send_sem=move_send.at[which, place],
                recv_sem=move_recv.at[which, place],
                device_id=peer,
                device_id_type=MESH,
            )
            copy.start()
            group.append(copy)
            start += width
        moves.append(group)
    start = 0
    group = []
    for place, source in enumerate(sources):
        width = source.shape[1]
        copy = pltpu.make_async_copy(
            source.at[pl.ds(pl.multiple_of(r * rows, rows), rows), :],
            own.at[r, :, pl.ds(start, width)],
            move_recv.at[0, place],
        )
        copy.start()
        group.append(copy)
        start += width

    def piece_arrived(index):
        @pl.when(index == 0)
        def _():
            for copy in group:
                copy.wait()

        for which in (1, 2, 3):

            @pl.when(index == which * per)
            def _():
                for copy in moves[which - 1]:
                    copy.wait_recv()

    def slot(index):
        step = index // per
        return (r // 2 + step // 2) % 2 * 2 + (r % 2 + step % 2) % 2

    def strip_of(index):
        return pl.multiple_of(index % per * CHUNK, CHUNK)

    def own_at(index, part):
        return own.at[slot(index), pl.ds(part * half + strip_of(index), CHUNK), :]

    def out_at(index, part):
        return out.at[slot(index), pl.ds(part * half + strip_of(index), CHUNK), :]

    def remote(source, target, sender, receiver, device):
        return pltpu.make_async_remote_copy(
            src_ref=source,
            dst_ref=target,
            send_sem=sender,
            recv_sem=receiver,
            device_id=device,
            device_id_type=MESH,
        )

    def loop(count, body):
        def run(index, nothing):
            body(index)
            return nothing

        lax.fori_loop(0, count, run, 0)

    @pl.when(is_end)
    def _():
        low = z // 3
        peer = (near_z, r, c)

        def send_low(index):
            return remote(
                own_at(index, low),
                left.at[index],
                end_send.at[0, index],
                low_recv.at[index],
                peer,
            )

        def send_high(index):
            return remote(
                own_at(index, 1 - low),
                right.at[1, index],
                end_send.at[1, index],
                high_recv.at[1, index],
                peer,
            )

        def begin(index):
            piece_arrived(index)
            send_low(index).start()
            send_high(index).start()

        def end(index):
            send_low(index).wait_send()
            send_high(index).wait_send()
            for part in (0, 1):
                spot = out_at(index, part)
                remote(
                    spot, spot, end_send.at[0, index], out_recv.at[part, index], peer
                ).wait_recv()

        loop(chunks, begin)
        loop(chunks, end)

    @pl.when(jnp.logical_not(is_end))
    def _():
        low = z - 1
        other, outer = ((3 - z, r, c), (end_z, r, c))

        def to_other(index):
            return remote(
                own_at(index, 1 - low),
                right.at[0, index],
                mid_send.at[index],
                high_recv.at[0, index],
                other,
            )

        def from_outer(index):
            return remote(
                own_at(index, 1 - low),
                right.at[1, index],
                mid_send.at[index],
                high_recv.at[1, index],
                outer,
            )

        def from_low(index):
            return remote(
                own_at(index, low), left.at[index], mid_send.at[index], low_recv.at[index], outer
            )

        def final(index):
            mine = own_at(index, low)
            spot = out_at(index, low)
            return (
                pltpu.make_async_copy(mine, spot, local.at[index]),
                remote(mine, spot, first_send.at[index], out_recv.at[low, index], outer),
                remote(mine, spot, last_send.at[index], out_recv.at[low, index], other),
            )

        def onward(index):
            spot = out_at(index, 1 - low)
            return remote(spot, spot, on_send.at[index], out_recv.at[1 - low, index], outer)

        def rows_at(index, part):
            return pl.ds(pl.multiple_of(part * half + strip_of(index), CHUNK), CHUNK)

        def step(index):
            @pl.when(index < chunks)
            def _():
                piece_arrived(index)
                from_outer(index).wait_recv()
                spot = rows_at(index, 1 - low)
                total = own[slot(index), spot, :].astype(jnp.float32) + right[1, index].astype(
                    jnp.float32
                )
                own[slot(index), spot, :] = total.astype(jnp.bfloat16)
                to_other(index).start()

            @pl.when((index >= 2) & (index < chunks + 2))
            def _():
                back = index - 2
                from_low(back).wait_recv()
                to_other(back).wait_recv()
                spot = rows_at(back, low)
                total = (
                    own[slot(back), spot, :].astype(jnp.float32)
                    + left[back].astype(jnp.float32)
                    + right[0, back].astype(jnp.float32)
                )
                own[slot(back), spot, :] = total.astype(jnp.bfloat16)
                for copy in final(back):
                    copy.start()

            @pl.when(index >= 4)
            def _():
                back = index - 4
                onward(back).wait_recv()
                onward(back).start()

        def end(index):
            to_other(index).wait_send()
            here_copy, first, last = final(index)
            here_copy.wait()
            first.wait_send()
            last.wait_send()
            onward(index).wait_send()

        loop(chunks + 4, step)
        loop(chunks, end)

    for moved in moves:
        for copy in moved:
            copy.wait_send()


def reduce_grads(sources):
    rows = sources[0].shape[0] // 4
    width = sum(source.shape[1] for source in sources)
    chunks = 4 * (rows // 2 // CHUNK)
    dma = pltpu.SemaphoreType.DMA
    count = len(sources)
    return pl.pallas_call(
        functools.partial(reduce_kernel, count),
        in_specs=[pl.BlockSpec(memory_space=pl.ANY)] * count,
        out_specs=pl.BlockSpec(memory_space=pl.ANY),
        out_shape=jax.ShapeDtypeStruct((4, rows, width), jnp.bfloat16),
        scratch_shapes=[
            pltpu.VMEM((4, rows, width), jnp.bfloat16),
            pltpu.VMEM((chunks, CHUNK, width), jnp.bfloat16),
            pltpu.VMEM((2, chunks, CHUNK, width), jnp.bfloat16),
            dma((4, count)),
            dma((4, count)),
            dma((2, chunks)),
            dma((chunks,)),
            dma((2, chunks)),
            dma((2, chunks)),
            dma((chunks,)),
            dma((chunks,)),
            dma((chunks,)),
            dma((chunks,)),
            dma((chunks,)),
        ],
        compiler_params=pltpu.CompilerParams(
            collective_id=REDUCE_ID, has_side_effects=True, vmem_limit_bytes=VMEM_BYTES
        ),
        name="reduce_grads",
    )(*sources)


def dot(left, right, dims, kind=jnp.float32):
    return lax.dot_general(left, right, dims, preferred_element_type=jnp.float32).astype(kind)


def local_plane(
    inputs,
    cotangent,
    starts,
    x_proj,
    y_proj,
    out_proj,
    gate_proj,
    up_proj,
    down_proj,
    mix_gain,
    mlp_gain,
    x_bias,
    y_bias,
    conv_w,
    conv_b,
    rec_gate_w,
    in_gate_w,
    rec_gate_b,
    in_gate_b,
    decay_param,
):
    z, r, c = here()
    depth = x_proj.shape[0]
    rec = x_proj.shape[1] // 4
    width = gate_proj.shape[1] // 4
    heads, head = (rec_gate_w.shape[0] // 4, rec_gate_w.shape[1])
    padded = (rec + 127) // 128 * 128
    low = jnp.bfloat16

    def mine(array, size, axis=0):
        return lax.dynamic_slice_in_dim(array, r * size, size, axis)

    mix_in = jnp.concatenate(
        [x_proj.reshape(depth, 4, rec), y_proj.reshape(depth, 4, rec)], axis=2
    ).transpose(1, 0, 2)
    flags = jnp.pad(starts.astype(jnp.float32).reshape(-1, 128), ((0, 6), (0, 0)))
    x_all, c_all, s_all, mix_w, out_w, gate_w, up_w, down_w = gather(
        inputs.T, cotangent.T, flags, mix_in, out_proj, (gate_proj, up_proj, down_proj)
    )
    tokens, model = x_all.shape
    gain_mix, gain_mlp = (
        lax.all_gather(mix_gain, "row", axis=0, tiled=True)[None, :],
        lax.all_gather(mlp_gain, "row", axis=0, tiled=True)[None, :],
    )
    fresh = s_all[:, :2, :].reshape(tokens)
    stale = 1.0 - fresh
    stale_one = jnp.concatenate([jnp.zeros((1,), jnp.float32), stale[:-1]])
    stale_two = jnp.concatenate([jnp.zeros((2,), jnp.float32), stale[:-2]])
    nothing = jnp.zeros_like(fresh)
    masks = jnp.stack(
        [fresh, stale, stale * stale_one, stale * stale_one * stale_two] + [nothing] * 4, axis=1
    )
    vectors = jnp.concatenate(
        [
            x_bias[None],
            y_bias[None],
            conv_w,
            conv_b[None],
            rec_gate_b[None],
            in_gate_b[None],
            -GATE_C * jax.nn.softplus(decay_param)[None],
            -GATE_C * jax.nn.sigmoid(decay_param)[None],
            jnp.zeros((5, x_bias.shape[0]), jnp.float32),
        ],
        axis=0,
    )
    vec = mine(vectors, rec, 1)

    def diagonal(blocks):
        blocks = mine(blocks, heads)
        rows = [jnp.pad(blocks[i], ((0, 0), (i * head, rec - (i + 1) * head))) for i in range(heads)]
        return jnp.concatenate(rows, axis=0)

    rec_w, in_w = (diagonal(rec_gate_w), diagonal(in_gate_w))
    values = x_all.astype(jnp.float32)
    scale = lax.rsqrt(jnp.mean(values * values, axis=1, keepdims=True) + EPS)
    normed_mix = (values * scale * gain_mix).astype(low)
    pre = dot(normed_mix, mix_w, CONTRACT_PLAIN)
    mixed, x_pre, conv, rec_gate, in_gate, states = mixer_forward(
        pre, masks, vec, rec_w, in_w, padded
    )
    size = tokens // 8
    shard = token_shard(r, c) * size
    resid = lax.dynamic_slice_in_dim(x_all, shard, size, 0)
    cot = lax.dynamic_slice_in_dim(c_all, shard, size, 0)
    full = jax.ShapeDtypeStruct((tokens, model), low)
    part = jax.ShapeDtypeStruct((size, model), jnp.float32)
    line = jax.ShapeDtypeStruct((1, model), jnp.float32)
    piece = pltpu.VMEM((size, model), low)
    block = jax.ShapeDtypeStruct((inputs.shape[1], inputs.shape[0]), low)
    normed_mlp, resid_mid = vmem_call(
        forward_kernel,
        "forward_norm",
        FORWARD_ID,
        (dot(mixed[:, :rec], out_w, CONTRACT_PLAIN, low), resid, gain_mlp),
        [full, part],
        [pl.ANY, pltpu.VMEM],
        reduce_scratch(size, model) + [piece],
        24,
    )
    gate = dot(normed_mlp, gate_w, CONTRACT_PLAIN)
    up = dot(normed_mlp, up_w, CONTRACT_PLAIN)
    d_activ = dot(c_all, down_w, CONTRACT_PLAIN)
    gelu, slope = gelu_both(gate)
    activ = (gelu * up).astype(low)
    d_gate = (d_activ * up * slope).astype(low)
    d_up = (d_activ * gelu).astype(low)
    d_normed = lax.dot_general(
        d_gate, gate_w, CONTRACT_COLS, preferred_element_type=jnp.float32
    ) + lax.dot_general(d_up, up_w, CONTRACT_COLS, preferred_element_type=jnp.float32)
    d_branch, d_resid, grad_mlp_gain = vmem_call(
        backward_kernel,
        "backward_norm",
        BACKWARD_ID,
        (d_normed.astype(low), resid_mid, cot, gain_mlp),
        [full, part, line],
        [pl.ANY, pltpu.VMEM, pltpu.VMEM],
        reduce_scratch(size, model) + [piece],
        24,
    )
    d_mixed = dot(d_branch, out_w, CONTRACT_COLS)
    d_pre, d_gates, sums = mixer_backward(
        d_mixed, pre, masks, vec, rec_w, in_w, x_pre, conv, rec_gate, in_gate, states
    )
    grad_in, output, grad_mix_gain = vmem_call(
        finish_kernel,
        "finish_norm",
        FINISH_ID,
        (
            dot(d_pre, mix_w, CONTRACT_COLS, low),
            dot(activ, down_w, CONTRACT_COLS, low),
            resid,
            resid_mid,
            d_resid,
            gain_mix,
        ),
        [block, block, line],
        [pltpu.VMEM] * 3,
        reduce_scratch(size, model) * 2 + [piece, piece],
        40,
    )
    grads = reduce_grads(
        (
            dot(normed_mlp, d_gate, CONTRACT_ROWS, low),
            dot(normed_mlp, d_up, CONTRACT_ROWS, low),
            dot(c_all, activ, CONTRACT_ROWS, low),
            dot(normed_mix, d_pre, CONTRACT_ROWS, low),
            dot(d_branch, mixed, CONTRACT_ROWS, low),
        )
    )
    gate_grads = dot(conv, d_gates, CONTRACT_ROWS, low)

    def spots(array, axis):
        shape = list(array.shape)
        length = shape[axis]
        shape[axis] = 4 * length
        return lax.dynamic_update_slice_in_dim(
            jnp.zeros(shape, array.dtype), array, r * length, axis
        )

    def blocks(array):
        return jnp.stack(
            [array[i * head : (i + 1) * head, i * head : (i + 1) * head] for i in range(heads)]
        )

    grad_rec_w = spots(blocks(gate_grads[:, :rec]), 0)
    grad_in_w = spots(blocks(gate_grads[:, rec:]), 0)
    vec_sums, grad_rec_w, grad_in_w = (
        item.astype(jnp.float32)
        for item in lax.psum((spots(sums.astype(low), 1), grad_rec_w, grad_in_w), ("dp", "row"))
    )
    gains = lax.psum(
        jnp.concatenate([grad_mix_gain, grad_mlp_gain], axis=0), ("dp", "row", "col")
    )
    gains = lax.dynamic_slice_in_dim(gains, r * depth, depth, 1)

    def columns(first, length):
        piece = grads[:, :, first : first + length].astype(jnp.float32)
        return piece.transpose(1, 0, 2).reshape(depth, 4 * length)

    after = 3 * width
    grad_out = grads[:, :, after + 2 * rec : after + 3 * rec].astype(jnp.float32)
    grad_out = grad_out.transpose(0, 2, 1).reshape(4 * rec, depth)
    return (
        output.T,
        grad_in.astype(jnp.float32).T,
        columns(after, rec),
        columns(after + rec, rec),
        grad_out,
        columns(0, width),
        columns(width, width),
        columns(2 * width, width),
        gains[0],
        gains[1],
        vec_sums[0],
        vec_sums[1],
        vec_sums[2:6],
        vec_sums[6],
        grad_rec_w,
        grad_in_w,
        vec_sums[7],
        vec_sums[8],
        vec_sums[9],
    )


def fits(mesh):
    return mesh.shape["dp"] == 4 and mesh.shape["row"] == 4 and mesh.shape["col"] == 2


def solution(mesh):
    placed = (
        P("row", ("dp", "col")),
        P("row", ("dp", "col")),
        P(("dp", "row")),
        P("row", "col"),
        P("row", "col"),
        P("col", "row"),
        P("row", "col"),
        P("row", "col"),
        P("row", "col"),
        P("row"),
        P("row"),
        P("col"),
        P("col"),
        P(None, "col"),
        P("col"),
        P("col", None, None),
        P("col", None, None),
        P("col"),
        P("col"),
        P("col"),
    )
    return jax.shard_map(
        local_plane if fits(mesh) else local,
        mesh=mesh,
        in_specs=placed,
        out_specs=(
            P("row", ("dp", "col")),
            P("row", ("dp", "col")),
            P("row", "col"),
            P("row", "col"),
            P("col", "row"),
            P("row", "col"),
            P("row", "col"),
            P("row", "col"),
            P("row"),
            P("row"),
            P("col"),
            P("col"),
            P(None, "col"),
            P("col"),
            P("col", None, None),
            P("col", None, None),
            P("col"),
            P("col"),
            P("col"),
        ),
        check_vma=False,
    )
```

```python
import functools

import jax
import jax.numpy as jnp
from jax import lax
from jax.experimental import pallas as pl
from jax.experimental.pallas import tpu as pltpu
from jax.sharding import PartitionSpec as P

MESH = pl.DeviceIdType.MESH

D = 2048


EPS = 1e-06
GATE_C = 8.0
CONTRACT_ROWS = (((0,), (0,)), ((), ()))
CONTRACT_COLS = (((1,), (1,)), ((), ()))
CONTRACT_PLAIN = (((1,), (0,)), ((), ()))


def from_behind(value, axis, by):
    count = lax.axis_size(axis)
    pairs = [(i, i + by) for i in range(count) if 0 <= i + by < count]
    return lax.ppermute(value, axis, pairs)


def carried_in(value, axis, join, neutral, backward):
    count, mine = (lax.axis_size(axis), lax.axis_index(axis))
    pieces = jax.tree.map(lambda part: lax.all_gather(part, axis), value)
    if backward:
        pieces = jax.tree.map(lambda part: part[::-1], pieces)
        mine = count - 1 - mine
    subtotal = jax.tree.map(
        lambda part, zero: jnp.full_like(part, 0) + jnp.asarray(zero, part.dtype), value, neutral
    )

    def hop(position, subtotal):
        longer = join(subtotal, jax.tree.map(lambda part: part[position], pieces))
        return jax.tree.map(lambda new, old: jnp.where(position < mine, new, old), longer, subtotal)

    return lax.fori_loop(0, count - 1, hop, subtotal)


def chain(earlier, later):
    return (earlier[0] * later[0], later[0] * earlier[1] + later[1])


def adjoint_chain(earlier, later):
    return (later[0] * earlier[0], later[1] + later[0] * earlier[1])


def gelu_tanh(values):
    return jax.nn.gelu(values, approximate=True)


def glu_piece(gate_vals, up_vals):
    return gelu_tanh(gate_vals) * up_vals


def causal_conv(values, conv_w, conv_b, segment_ids):
    result = values * conv_w[0] + conv_b
    for offset in range(1, conv_w.shape[0]):
        lagged = jnp.pad(values, ((offset, 0), (0, 0)))[:-offset]
        earlier_ids = jnp.pad(segment_ids, (offset, 0), constant_values=-1)[:-offset]
        result = (
            result + jnp.where((earlier_ids == segment_ids)[:, None], lagged, 0.0) * conv_w[offset]
        )
    return result


def local_recurrence(rec_pre, in_pre, conv_vals, decay_param, flags):
    rec_gate = jax.nn.sigmoid(rec_pre)
    in_gate = jax.nn.sigmoid(in_pre)
    log_keep = -GATE_C * rec_gate * jax.nn.softplus(decay_param)
    keep_rate = jnp.exp(log_keep)
    fresh = (flags == 1)[:, None]
    multiplier = jnp.where(fresh, 1.0, jnp.sqrt(-jnp.expm1(2.0 * log_keep)))
    driven = conv_vals * in_gate * multiplier
    carried = jnp.where(fresh, 0.0, keep_rate)
    cum_keep, states = lax.associative_scan(chain, (carried, driven), axis=0)
    return (cum_keep, states)


def row_sums(values):
    return lax.psum(values, "row")


def norm_forward(values, norm_gain):
    squares = row_sums(jnp.sum(values * values, axis=1))
    inv_rms = lax.rsqrt(squares / D + EPS)
    return (values * inv_rms[:, None] * norm_gain, inv_rms)


def norm_backward(values, inv_rms, norm_gain, incoming):
    scaled = norm_gain * incoming
    dots = row_sums(jnp.sum(scaled * values, axis=1))
    values_grad = inv_rms[:, None] * scaled - values * (inv_rms**3 * dots / D)[:, None]
    gain_grad = jnp.sum(incoming * values * inv_rms[:, None], axis=0)
    return (values_grad, gain_grad)


def gather_edge(values):
    return lax.all_gather(values, "col", axis=0, tiled=True)


def gather_mid(values):
    return lax.all_gather(values, "row", axis=0, tiled=True)


def row_partial(whole, weight, dims):
    return lax.psum_scatter(
        lax.dot_general(whole, weight, dims, preferred_element_type=jnp.float32),
        "row",
        scatter_dimension=0,
        tiled=True,
    )


def col_partial(whole, weight, dims):
    return lax.psum_scatter(
        lax.dot_general(whole, weight, dims, preferred_element_type=jnp.float32),
        "col",
        scatter_dimension=0,
        tiled=True,
    )


def project_in(normed, weight):
    whole = gather_edge(normed)
    result = row_partial(whole, weight, CONTRACT_PLAIN)
    return (result, whole)


def weight_grad(left, right):
    return lax.dot_general(left, right, CONTRACT_ROWS, preferred_element_type=jnp.float32)


def local(
    inputs,
    cotangent,
    starts,
    x_proj,
    y_proj,
    out_proj,
    gate_proj,
    up_proj,
    down_proj,
    mix_gain,
    mlp_gain,
    x_bias,
    y_bias,
    conv_w,
    conv_b,
    rec_gate_w,
    in_gate_w,
    rec_gate_b,
    in_gate_b,
    decay_param,
):
    rows_mid = starts.shape[0]
    rec_width = x_proj.shape[1]
    ff_width = gate_proj.shape[1]
    head_count = rec_gate_w.shape[0]
    margin = conv_w.shape[0] - 1
    mix_weights = jnp.concatenate([x_proj, y_proj], axis=1)
    mlp_weights = jnp.concatenate([gate_proj, up_proj], axis=1)
    cot_rows = cotangent.T
    resid = inputs.astype(jnp.float32).T
    normed_mix, inv_rms_mix = norm_forward(resid, mix_gain)
    normed_mix = normed_mix.astype(jnp.bfloat16)
    pre_both, whole_mix = project_in(normed_mix, mix_weights)
    x_pre = pre_both[:, :rec_width] + x_bias
    y_pre = pre_both[:, rec_width:] + y_bias
    x_tail, flag_tail = from_behind(
        (x_pre[rows_mid - margin :], starts[rows_mid - margin :].astype(jnp.float32)), "row", 1
    )
    ext_flags = jnp.concatenate([flag_tail.astype(jnp.int32), starts])
    ext_ids = jnp.cumsum(ext_flags, dtype=jnp.int32)
    ext_x = jnp.concatenate([x_tail, x_pre], axis=0)

    def conv_piece(values, taps, offsets):
        return causal_conv(values, taps, offsets, ext_ids)[margin:]

    conv_vals, conv_pull = jax.vjp(conv_piece, ext_x, conv_w, conv_b)
    conv_low = conv_vals.astype(jnp.bfloat16)
    conv_heads = conv_low.reshape(rows_mid, head_count, -1)
    rec_pre = (
        jnp.einsum(
            "thk,hkj->thj", conv_heads, rec_gate_w, preferred_element_type=jnp.float32
        ).reshape(rows_mid, rec_width)
        + rec_gate_b
    )
    in_pre = (
        jnp.einsum(
            "thk,hkj->thj", conv_heads, in_gate_w, preferred_element_type=jnp.float32
        ).reshape(rows_mid, rec_width)
        + in_gate_b
    )

    def scan_piece(rec_vals, in_vals, conv_input, decay_vals):
        return local_recurrence(rec_vals, in_vals, conv_input, decay_vals, starts)

    (cum_keep, local_states), scan_pull = jax.vjp(
        scan_piece, rec_pre, in_pre, conv_low.astype(jnp.float32), decay_param
    )
    ones_row = jnp.ones((rec_width,), jnp.float32)
    zeros_row = jnp.zeros((rec_width,), jnp.float32)
    incoming = carried_in(
        (cum_keep[rows_mid - 1], local_states[rows_mid - 1]),
        "row",
        chain,
        (ones_row, zeros_row),
        False,
    )
    state_prev = incoming[1]
    states = local_states + cum_keep * state_prev
    y_act, y_pull = jax.vjp(gelu_tanh, y_pre)
    mixed = (states * y_act).astype(jnp.bfloat16)
    whole_mixed = gather_mid(mixed)
    resid_mid = resid + col_partial(whole_mixed, out_proj, CONTRACT_PLAIN)
    normed_mlp, inv_rms_mlp = norm_forward(resid_mid, mlp_gain)
    normed_mlp = normed_mlp.astype(jnp.bfloat16)
    gate_up, whole_mlp = project_in(normed_mlp, mlp_weights)
    activ, activ_pull = jax.vjp(glu_piece, gate_up[:, :ff_width], gate_up[:, ff_width:])
    activ = activ.astype(jnp.bfloat16)
    whole_activ = gather_mid(activ)
    output = (resid_mid + col_partial(whole_activ, down_proj, CONTRACT_COLS)).astype(jnp.bfloat16)
    cot_whole = gather_edge(cot_rows)
    d_activ = row_partial(cot_whole, down_proj, CONTRACT_PLAIN)
    activ_rows = gather_mid(activ)
    grad_down = weight_grad(cot_whole, activ_rows)
    d_gate, d_up = activ_pull(d_activ)
    d_gate_up = jnp.concatenate([d_gate, d_up], axis=1).astype(jnp.bfloat16)
    d_gate_up_whole = gather_mid(d_gate_up)
    d_normed_mlp = col_partial(d_gate_up_whole, mlp_weights, CONTRACT_COLS)
    mlp_rows = gather_edge(normed_mlp)
    grad_gate_up = weight_grad(mlp_rows, d_gate_up_whole)
    d_norm_mid, grad_mlp_gain = norm_backward(resid_mid, inv_rms_mlp, mlp_gain, d_normed_mlp)
    d_resid_mid = cot_rows.astype(jnp.float32) + d_norm_mid
    d_branch = d_resid_mid.astype(jnp.bfloat16)
    branch_whole = gather_edge(d_branch)
    d_mixed = row_partial(branch_whole, out_proj, CONTRACT_COLS)
    mixed_rows = gather_mid(mixed)
    grad_out = weight_grad(mixed_rows, branch_whole)
    d_state = d_mixed * y_act
    (d_y_pre,) = y_pull(d_mixed * states)
    own_sens = jnp.sum(d_state * cum_keep, axis=0)
    outgoing = carried_in(
        (cum_keep[rows_mid - 1], own_sens), "row", adjoint_chain, (ones_row, zeros_row), True
    )
    d_total = d_state + jnp.pad(outgoing[1][None, :], ((rows_mid - 1, 0), (0, 0)))
    d_rec_pre, d_in_pre, d_conv_direct, grad_decay = scan_pull((d_total * state_prev, d_total))
    d_rec_low = d_rec_pre.astype(jnp.bfloat16)
    d_in_low = d_in_pre.astype(jnp.bfloat16)
    d_rec_heads = d_rec_low.reshape(rows_mid, head_count, -1)
    d_in_heads = d_in_low.reshape(rows_mid, head_count, -1)
    d_conv = d_conv_direct + jnp.einsum(
        "thj,hkj->thk", d_rec_heads, rec_gate_w, preferred_element_type=jnp.float32
    ).reshape(rows_mid, rec_width)
    d_conv = d_conv + jnp.einsum(
        "thj,hkj->thk", d_in_heads, in_gate_w, preferred_element_type=jnp.float32
    ).reshape(rows_mid, rec_width)
    grad_rec_w = jnp.einsum(
        "thk,thj->hkj", conv_heads, d_rec_heads, preferred_element_type=jnp.float32
    )
    grad_in_w = jnp.einsum(
        "thk,thj->hkj", conv_heads, d_in_heads, preferred_element_type=jnp.float32
    )
    grad_rec_b = jnp.sum(d_rec_low.astype(jnp.float32), axis=0)
    grad_in_b = jnp.sum(d_in_low.astype(jnp.float32), axis=0)
    d_ext, grad_conv_w, grad_conv_b = conv_pull(d_conv)
    d_from_next = from_behind(d_ext[:margin], "row", -1)
    d_x_pre = d_ext[margin:] + jnp.pad(d_from_next, ((rows_mid - margin, 0), (0, 0)))
    d_pre = jnp.concatenate([d_x_pre, d_y_pre], axis=1).astype(jnp.bfloat16)
    bias_sums = jnp.sum(d_pre.astype(jnp.float32), axis=0)
    d_pre_whole = gather_mid(d_pre)
    d_normed_mix = col_partial(d_pre_whole, mix_weights, CONTRACT_COLS)
    mix_rows = gather_edge(normed_mix)
    grad_mix = weight_grad(mix_rows, d_pre_whole)
    d_norm_in, grad_mix_gain = norm_backward(resid, inv_rms_mix, mix_gain, d_normed_mix)
    inputs_grad = d_resid_mid + d_norm_in
    grad_mix, grad_out, grad_gate_up, grad_down = (
        lax.psum(grad_mix.astype(jnp.bfloat16), "dp").astype(jnp.float32),
        lax.psum(grad_out.astype(jnp.bfloat16), "dp").astype(jnp.float32),
        lax.psum(grad_gate_up.astype(jnp.bfloat16), "dp").astype(jnp.float32),
        lax.psum(grad_down.astype(jnp.bfloat16), "dp").astype(jnp.float32),
    )
    (
        bias_sums,
        grad_conv_w,
        grad_conv_b,
        grad_rec_w,
        grad_in_w,
        grad_rec_b,
        grad_in_b,
        grad_decay,
    ) = (
        lax.psum(bias_sums.astype(jnp.bfloat16), ("dp", "row")).astype(jnp.float32),
        lax.psum(grad_conv_w.astype(jnp.bfloat16), ("dp", "row")).astype(jnp.float32),
        lax.psum(grad_conv_b.astype(jnp.bfloat16), ("dp", "row")).astype(jnp.float32),
        lax.psum(grad_rec_w.astype(jnp.bfloat16), ("dp", "row")).astype(jnp.float32),
        lax.psum(grad_in_w.astype(jnp.bfloat16), ("dp", "row")).astype(jnp.float32),
        lax.psum(grad_rec_b.astype(jnp.bfloat16), ("dp", "row")).astype(jnp.float32),
        lax.psum(grad_in_b.astype(jnp.bfloat16), ("dp", "row")).astype(jnp.float32),
        lax.psum(grad_decay.astype(jnp.bfloat16), ("dp", "row")).astype(jnp.float32),
    )
    grad_mix_gain, grad_mlp_gain = lax.psum((grad_mix_gain, grad_mlp_gain), ("dp", "col"))
    return (
        output.T,
        inputs_grad.T,
        grad_mix[:, :rec_width],
        grad_mix[:, rec_width:],
        grad_out,
        grad_gate_up[:, :ff_width],
        grad_gate_up[:, ff_width:],
        grad_down,
        grad_mix_gain,
        grad_mlp_gain,
        bias_sums[:rec_width],
        bias_sums[rec_width:],
        grad_conv_w,
        grad_conv_b,
        grad_rec_w,
        grad_in_w,
        grad_rec_b,
        grad_in_b,
        grad_decay,
    )


GATHER_ID, FORWARD_ID, BACKWARD_ID, FINISH_ID, REDUCE_ID = (0, 1, 2, 3, 4)
BLOCK = 128
VMEM_BYTES = 56 << 20


def one_minus_exp(rate):
    series = rate * (1.0 - rate * (0.5 - rate * (1.0 / 6.0 - rate * (1.0 / 24.0 - rate / 120.0))))
    return jnp.where(rate < 0.1, series, 1.0 - jnp.exp(-rate))


GELU_C = 0.7978845608028654


def gelu_both(values):
    squared = values * values
    inner = jnp.tanh(GELU_C * values * (1.0 + 0.044715 * squared))
    value = 0.5 * values * (1.0 + inner)
    slope = 0.5 * (1.0 + inner) + 0.5 * values * (1.0 - inner * inner) * GELU_C * (
        1.0 + 3.0 * 0.044715 * squared
    )
    return (value, slope)


def down_rows(values, by):
    return pltpu.roll(values, by, 0)


def up_rows(values, by):
    return pltpu.roll(values, values.shape[0] - by, 0)


def scan_down(keep, add):
    rows = keep.shape[0]
    position = lax.broadcasted_iota(jnp.int32, keep.shape, 0)
    step = 1
    while step < rows:
        if step < 8:
            inside = position >= step
            before_keep = jnp.where(inside, down_rows(keep, step), 1.0)
            before_add = jnp.where(inside, down_rows(add, step), 0.0)
            add = add + keep * before_add
            keep = keep * before_keep
        else:
            add = jnp.concatenate([add[:step], add[step:] + keep[step:] * add[:-step]], axis=0)
            keep = jnp.concatenate([keep[:step], keep[step:] * keep[:-step]], axis=0)
        step *= 2
    return (keep, add)


def scan_up(keep, add):
    rows = keep.shape[0]
    position = lax.broadcasted_iota(jnp.int32, keep.shape, 0)
    step = 1
    while step < rows:
        if step < 8:
            inside = position < rows - step
            after_keep = jnp.where(inside, up_rows(keep, step), 1.0)
            after_add = jnp.where(inside, up_rows(add, step), 0.0)
            add = add + keep * after_add
            keep = keep * after_keep
        else:
            add = jnp.concatenate([add[:-step] + keep[:-step] * add[step:], add[-step:]], axis=0)
            keep = jnp.concatenate([keep[:-step] * keep[step:], keep[-step:]], axis=0)
        step *= 2
    return (keep, add)


def mixer_forward_step(
    pre, marks, vec, rec_w, in_w, mixed, x_pre, conv, rec_gate, in_gate, states, tail, carry
):
    width = x_pre.shape[1]
    x = pre[:, :width] + vec[0:1, :]
    x_pre[...] = x
    longer = jnp.concatenate([tail[...], x], axis=0)
    tail[...] = x[BLOCK - 8 :]
    total = x * vec[2:3, :] + vec[6:7, :]
    for tap in range(1, 4):
        total = total + marks[:, tap : tap + 1] * down_rows(longer, tap)[8:] * vec[
            2 + tap : 3 + tap, :
        ]
    low = total.astype(jnp.bfloat16)
    conv[...] = low
    rec = jax.nn.sigmoid(
        jnp.dot(low, rec_w[...], preferred_element_type=jnp.float32) + vec[7:8, :]
    )
    inn = jax.nn.sigmoid(
        jnp.dot(low, in_w[...], preferred_element_type=jnp.float32) + vec[8:9, :]
    )
    rec_gate[...] = rec
    in_gate[...] = inn
    log_keep = rec * vec[9:10, :]
    fresh = marks[:, 0:1]
    scale = jnp.where(fresh > 0.5, 1.0, jnp.sqrt(one_minus_exp(-2.0 * log_keep)))
    driven = low.astype(jnp.float32) * inn * scale
    keep, add = scan_down(jnp.exp(log_keep) * (1.0 - fresh), driven)
    state = add + keep * carry[0:1, :]
    carry[...] = jnp.broadcast_to(state[BLOCK - 1 :, :], carry.shape)
    states[...] = state
    y = pre[:, width:] + vec[1:2, :]
    mixed[:, :width] = (state * gelu_both(y)[0]).astype(jnp.bfloat16)
    mixed[:, width:] = jnp.zeros((BLOCK, mixed.shape[1] - width), jnp.bfloat16)


def mixer_backward_kernel(
    d_mixed,
    pre,
    masks,
    vec,
    rec_w,
    in_w,
    x_pre,
    x_before,
    conv,
    rec_gate,
    in_gate,
    states,
    state_before,
    d_pre,
    d_gates,
    sums,
    edge,
    carry,
):
    width = x_pre.shape[1]

    @pl.when(pl.program_id(0) == 0)
    def _():
        edge[...] = jnp.zeros_like(edge)
        carry[...] = jnp.zeros_like(carry)
        sums[...] = jnp.zeros_like(sums)

    position = lax.broadcasted_iota(jnp.int32, (BLOCK, width), 0)
    marks = masks[...]
    fresh = marks[:, 0:1]
    stale = 1.0 - fresh
    gelu, slope = gelu_both(pre[:, width:] + vec[1:2, :])
    state = states[...]
    incoming = d_mixed[...]
    d_y = (incoming * state * slope).astype(jnp.bfloat16)
    rec, inn = (rec_gate[...], in_gate[...])
    conv_vals = conv[...].astype(jnp.float32)
    log_keep = rec * vec[9:10, :]
    keep_rate = jnp.exp(log_keep)
    scale = jnp.where(fresh > 0.5, 1.0, jnp.sqrt(one_minus_exp(-2.0 * log_keep)))
    carried = keep_rate * stale
    after = jnp.where(position == BLOCK - 1, carry[1:2, :], up_rows(carried, 1))
    keep, add = scan_up(after, incoming * gelu)
    adjoint = add + keep * carry[0:1, :]
    carry[0:1, :] = adjoint[0:1]
    carry[1:2, :] = carried[0:1]
    earlier = jnp.where(position == 0, state_before[7:8, :], down_rows(state, 1))
    drive = adjoint * scale
    d_log = stale * (
        adjoint * earlier * keep_rate
        - adjoint * inn * conv_vals * keep_rate * keep_rate / scale
    )
    d_rec = (d_log * vec[9:10, :] * rec * (1.0 - rec)).astype(jnp.bfloat16)
    d_in = (drive * conv_vals * inn * (1.0 - inn)).astype(jnp.bfloat16)
    d_gates[:, :width] = d_rec
    d_gates[:, width:] = d_in
    d_conv = drive * inn
    d_conv = d_conv + lax.dot_general(
        d_rec, rec_w[...], CONTRACT_COLS, preferred_element_type=jnp.float32
    )
    d_conv = d_conv + lax.dot_general(
        d_in, in_w[...], CONTRACT_COLS, preferred_element_type=jnp.float32
    )
    x = x_pre[...]
    longer = jnp.concatenate([x_before[...], x], axis=0)

    def column(values):
        return jnp.sum(values, axis=0, keepdims=True)

    d_x = d_conv * vec[2:3, :]
    taps = [column(d_conv * x)]
    for tap in range(1, 4):
        part = marks[:, tap : tap + 1] * d_conv
        taps.append(column(part * down_rows(longer, tap)[8:]))
        beyond = jnp.concatenate([part, edge[8 * tap - 8 : 8 * tap, :]], axis=0)
        d_x = d_x + vec[2 + tap : 3 + tap, :] * up_rows(beyond, tap)[:BLOCK]
        edge[8 * tap - 8 : 8 * tap, :] = part[:8]
    d_x = d_x.astype(jnp.bfloat16)
    d_pre[:, :width] = d_x
    d_pre[:, width:] = d_y
    parts = (
        [column(d_x.astype(jnp.float32)), column(d_y.astype(jnp.float32))]
        + taps
        + [
            column(d_conv),
            column(d_rec.astype(jnp.float32)),
            column(d_in.astype(jnp.float32)),
            column(d_log * rec) * vec[10:11, :],
        ]
    )
    for place, part in enumerate(parts):
        sums[place : place + 1, :] += part


def mixer_backward(d_mixed, pre, masks, vec, rec_w, in_w, x_pre, conv, rec_gate, in_gate, states):
    tokens, width = x_pre.shape
    last = tokens // BLOCK - 1

    def block(columns):
        return pl.BlockSpec((BLOCK, columns), lambda i: (last - i, 0))

    def before():
        return pl.BlockSpec(
            (8, width), lambda i: (jnp.maximum((last - i) * (BLOCK // 8) - 1, 0), 0)
        )

    def whole(array):
        return pl.BlockSpec(array.shape, lambda i: (0, 0))

    return pl.pallas_call(
        mixer_backward_kernel,
        grid=(tokens // BLOCK,),
        in_specs=[
            block(width),
            block(2 * width),
            block(8),
            whole(vec),
            whole(rec_w),
            whole(in_w),
            block(width),
            before(),
            block(width),
            block(width),
            block(width),
            block(width),
            before(),
        ],
        out_specs=[block(2 * width), block(2 * width), pl.BlockSpec((16, width), lambda i: (0, 0))],
        out_shape=[
            jax.ShapeDtypeStruct((tokens, 2 * width), jnp.bfloat16),
            jax.ShapeDtypeStruct((tokens, 2 * width), jnp.bfloat16),
            jax.ShapeDtypeStruct((16, width), jnp.float32),
        ],
        scratch_shapes=[pltpu.VMEM((24, width), jnp.float32), pltpu.VMEM((8, width), jnp.float32)],
        compiler_params=pltpu.CompilerParams(vmem_limit_bytes=32 << 20),
        name="mixer_backward",
    )(d_mixed, pre, masks, vec, rec_w, in_w, x_pre, x_pre, conv, rec_gate, in_gate, states, states)


def here():
    return (lax.axis_index("dp"), lax.axis_index("row"), lax.axis_index("col"))


def flip(index):
    return index + 1 - 2 * (index % 2)


def across(row):
    return (row + 2) % 4


def greet(peers):
    barrier = pltpu.get_barrier_semaphore()
    for peer in peers:
        pl.semaphore_signal(barrier, inc=1, device_id=peer, device_id_type=MESH)
    pl.semaphore_wait(barrier, len(peers))


class Copies:
    def __init__(self, send, recv):
        self.send, self.recv, self.used, self.sent = (send, recv, 0, [])

    def make(self, source, target, device):
        place = self.used
        self.used += 1
        if device is None:
            copy = pltpu.make_async_copy(source, target, self.recv.at[place])
        else:
            copy = pltpu.make_async_remote_copy(
                src_ref=source,
                dst_ref=target,
                send_sem=self.send.at[place],
                recv_sem=self.recv.at[place],
                device_id=device,
                device_id_type=MESH,
            )
            self.sent.append(copy)
        return copy

    def go(self, source, target, device):
        copy = self.make(source, target, device)
        copy.start()
        return copy

    def finish(self):
        for copy in self.sent:
            copy.wait_send()


def arrived(copy):
    copy.wait_recv()


def spread(copies, own, place, halves, between=lambda: None):
    z, r, c = here()
    twin, side, top = ((z, flip(r), c), (z, across(r), c), (z, r, 1 - c))
    to_side = copies.go(own, place(r, c), side)
    to_top = copies.go(own, place(r, c), top)
    to_twin = copies.go(own, place(r, c), twin)
    between()
    arrived(to_side)
    from_side = place(across(r), c)
    on_top = copies.go(halves(from_side, 0), halves(from_side, 0), top)
    late = [to_twin, copies.go(from_side, from_side, twin)]
    between()
    arrived(to_top)
    from_top = place(r, 1 - c)
    on_side = copies.go(halves(from_top, 1), halves(from_top, 1), side)
    late.append(copies.go(from_top, from_top, twin))
    far = place(across(r), 1 - c)
    between()
    for half, copy in enumerate((on_top, on_side)):
        arrived(copy)
        late.append(copies.go(halves(far, half), halves(far, half), twin))
    return late


def part(start, size, step):
    return pl.ds(pl.multiple_of(start * step, step), size)


class Moves:
    def __init__(self, copies, matrices, cuts):
        self.copies = copies
        z, r, c = here()
        self.mine = z % 2
        self.sides = ((z, across(r), c), (z, flip(across(r)), c))
        self.pair = (flip(z), r, c)
        self.locals, self.late, self.flying = ([], [], [])
        self.groups = [(matrix, cut) for matrix in matrices for cut in range(cuts)]
        self.cuts, self.begun = (cuts, 0)
        for source, target, size in matrices:
            self.locals.append(copies.go(source(r), target(r), None))
            self.late.append(copies.go(source(flip(r)), target(r), (z, flip(r), c)))

    def piece(self, ref, size, cut):
        length = size // 2 // self.cuts
        return ref.at[part(self.mine * self.cuts + cut, length, length), :]

    def step(self):
        if len(self.flying) == 2 or self.begun == len(self.groups):
            if self.flying:
                (source, target, size), cut, group = self.flying.pop(0)
                for peer, copy in zip(self.sides, group):
                    arrived(copy)
                    piece = self.piece(target(peer[1]), size, cut)
                    self.late.append(self.copies.go(piece, piece, self.pair))
        if self.begun < len(self.groups):
            (source, target, size), cut = self.groups[self.begun]
            self.begun += 1
            group = [
                self.copies.go(
                    self.piece(source(peer[1]), size, cut),
                    self.piece(target(here()[1]), size, cut),
                    peer,
                )
                for peer in self.sides
            ]
            self.flying.append(((source, target, size), cut, group))

    def finish(self):
        while self.flying:
            self.step()
        for copy in self.late:
            arrived(copy)
        for copy in self.locals:
            copy.wait()


def block_of(ref, rows, columns):
    return lambda row, col: ref.at[part(col, rows, rows), part(row, columns, columns)]


def halves_of(rows):
    return lambda ref, which: ref.at[pl.ds(which * (rows // 2), rows // 2), :]


def mlp_matrices(sources, targets):
    depth, width = (sources[0].shape[0], sources[0].shape[1] // 4)
    return [
        (
            lambda to, source=source: source.at[:, part(to, width, width)],
            lambda of, target=target: target.at[part(of, depth, depth), :],
            depth,
        )
        for source, target in zip(sources, targets)
    ]


def gather_kernel(x_in, s_in, g_in, mix_in, out_in, x_all, s_all, g_all, mix_all, out_all, send, recv):
    z, r, c = here()
    twin, side, cross, top, pair = (
        (z, flip(r), c),
        (z, across(r), c),
        (z, flip(across(r)), c),
        (z, r, 1 - c),
        (flip(z), r, c),
    )
    greet((twin, side, cross, top, pair))
    copies = Copies(send, recv)
    rows, columns = x_in.shape
    depth, rec = (mix_in.shape[1], out_in.shape[0] // 4)
    matrices = [
        (lambda to: mix_in.at[to], lambda of: mix_all.at[part(of, depth, depth), :], depth),
        (
            lambda to: out_in.at[part(to, rec, rec), :],
            lambda of: out_all.at[:, part(of, columns, columns)],
            rec,
        ),
    ]
    small = g_all.at[:, part(r, depth, depth)]
    locals_ = [
        copies.go(x_in, block_of(x_all, rows, columns)(r, c), None),
        copies.go(s_in, s_all.at[r], None),
        copies.go(g_in, small, None),
    ]
    late = []
    for peer in (twin, side, cross):
        late.append(copies.go(s_in, s_all.at[r], peer))
        late.append(copies.go(g_in, small, peer))
    moves = Moves(copies, matrices, 2)
    moves.step()
    late.extend(
        spread(copies, x_in, block_of(x_all, rows, columns), halves_of(rows), moves.step)
    )
    moves.finish()
    for copy in late:
        arrived(copy)
    for copy in locals_:
        copy.wait()
    copies.finish()


def gather(x_in, s_in, g_in, mix_in, out_in):
    rows, columns = x_in.shape
    depth = mix_in.shape[1]

    def shape(*dims, kind=jnp.bfloat16):
        return jax.ShapeDtypeStruct(dims, kind)

    outs = [
        shape(2 * rows, 4 * columns),
        shape(4, *s_in.shape, kind=s_in.dtype),
        shape(g_in.shape[0], 4 * depth, kind=g_in.dtype),
        shape(4 * depth, mix_in.shape[2]),
        shape(out_in.shape[0] // 4, 4 * columns),
    ]
    return pl.pallas_call(
        gather_kernel,
        in_specs=[pl.BlockSpec(memory_space=pl.ANY)] * 5,
        out_specs=[pl.BlockSpec(memory_space=pl.ANY)] * 5,
        out_shape=outs,
        scratch_shapes=[pltpu.SemaphoreType.DMA((48,)), pltpu.SemaphoreType.DMA((48,))],
        compiler_params=pltpu.CompilerParams(collective_id=GATHER_ID, has_side_effects=True),
        name="gather",
    )(x_in, s_in, g_in, mix_in, out_in)


STRIP = 16


def strips(count, body):
    def run(index, nothing):
        body(pl.multiple_of(index * STRIP, STRIP))
        return nothing

    lax.fori_loop(0, count // STRIP, run, 0)


def token_shard(row, col):
    return col * 4 + row


def reduce_shards(copies, parts, twin_in, sums, side_in, top_in, hop_in, between=lambda: None):
    z, r, c = here()
    twin, side, top = ((z, flip(r), c), (z, across(r), c), (z, r, 1 - c))
    size = side_in.shape[0]
    half = size // 2

    def shard(row, col):
        return pl.multiple_of(token_shard(row, col) * size, size)

    spots = [(across(r), 1 - c), (across(r), c), (r, 1 - c), (r, c)]
    from_twin = [
        copies.go(parts.at[pl.ds(shard(flip(row), col), size), :], twin_in.at[place], twin)
        for place, (row, col) in enumerate(spots)
    ]

    def add_twin(place):
        arrived(from_twin[place])
        start = shard(*spots[place])

        def body(at):
            total = parts[pl.ds(start + at, STRIP), :].astype(jnp.float32) + twin_in[
                place, pl.ds(at, STRIP), :
            ].astype(jnp.float32)
            sums[place, pl.ds(at, STRIP), :] = total.astype(jnp.bfloat16)

        strips(size, body)

    def add_hop(place, which, hop):
        def body(at):
            rows = pl.ds(which * half + at, STRIP)
            total = sums[place, rows, :].astype(jnp.float32) + hop_in[
                hop, pl.ds(at, STRIP), :
            ].astype(jnp.float32)
            sums[place, rows, :] = total.astype(jnp.bfloat16)

        strips(half, body)

    def rows_of(ref, which):
        return ref.at[pl.ds(which * half, half), :]

    add_twin(0)
    hop_side = copies.go(rows_of(sums.at[0], 0), hop_in.at[0], side)
    hop_top = copies.go(rows_of(sums.at[0], 1), hop_in.at[1], top)
    add_twin(1)
    waits = [copies.go(rows_of(sums.at[1], 0), rows_of(side_in, 0), side)]
    add_twin(2)
    waits.append(copies.go(rows_of(sums.at[2], 1), rows_of(top_in, 1), top))
    add_twin(3)
    between()
    arrived(hop_top)
    add_hop(1, 1, 1)
    waits.append(copies.go(rows_of(sums.at[1], 1), rows_of(side_in, 1), side))
    arrived(hop_side)
    add_hop(2, 0, 0)
    waits.append(copies.go(rows_of(sums.at[2], 0), rows_of(top_in, 0), top))
    between()
    for copy in waits:
        arrived(copy)

    def total(at):
        rows = pl.ds(at, STRIP)
        return (
            sums[3, rows, :].astype(jnp.float32)
            + side_in[rows, :].astype(jnp.float32)
            + top_in[rows, :].astype(jnp.float32)
        )

    return total


def reduce_scratch(size, width):
    return [
        pltpu.VMEM((4, size, width), jnp.bfloat16),
        pltpu.VMEM((4, size, width), jnp.bfloat16),
        pltpu.VMEM((size, width), jnp.bfloat16),
        pltpu.VMEM((size, width), jnp.bfloat16),
        pltpu.VMEM((2, size // 2, width), jnp.bfloat16),
    ]


def near():
    z, r, c = here()
    return ((z, flip(r), c), (z, across(r), c), (z, r, 1 - c))


def spread_rows(copies, mine, full, between=lambda: None):
    z, r, c = here()
    size = mine.shape[0]
    half = size // 2

    def place(row, col):
        return full.at[pl.ds(pl.multiple_of(token_shard(row, col) * size, size), size), :]

    local = copies.go(mine, place(r, c), None)
    late = spread(
        copies, mine, place, lambda ref, which: ref.at[pl.ds(which * half, half), :], between
    )
    for copy in late:
        arrived(copy)
    local.wait()


def forward_kernel(x_all, masks, vec, rec_w, in_w, mix_w, out_w, gain_mix, gain, c_in, *refs):
    mlp_in, outs, scratch = (refs[:3], refs[3:17], refs[17:])
    full, resid_mid, c_all = outs[:3]
    mlp_all, kept_out = (outs[3:6], outs[6:])
    kept, (tail, carry, parts), (*buffers, mine, kept_sem, send, recv) = (
        scratch[:8],
        scratch[8:11],
        scratch[11:],
    )
    normed, pre, mixed, *saved = kept
    z, r, c = here()
    greet((*near(), (z, flip(across(r)), c), (flip(z), r, c)))
    copies = Copies(send, recv)
    rows, columns = c_in.shape
    moves = Moves(copies, mlp_matrices(mlp_in, mlp_all), 2)
    moves.step()
    moves.step()
    tail[...] = jnp.zeros_like(tail)
    carry[...] = jnp.zeros_like(carry)

    def block(index, nothing):
        start = pl.multiple_of(index * BLOCK, BLOCK)
        rows = pl.ds(start, BLOCK)

        def norm(at):
            strip = pl.ds(start + at, STRIP)
            values = x_all[strip, :].astype(jnp.float32)
            scale = lax.rsqrt(jnp.mean(values * values, axis=1, keepdims=True) + EPS)
            normed[strip, :] = (values * scale * gain_mix[...]).astype(jnp.bfloat16)

        strips(BLOCK, norm)
        pre[rows, :] = jnp.dot(normed[rows, :], mix_w[...], preferred_element_type=jnp.float32)
        mixer_forward_step(
            pre.at[rows, :],
            masks[rows, :],
            vec,
            rec_w,
            in_w,
            mixed.at[rows, :],
            *[ref.at[rows, :] for ref in saved],
            tail,
            carry,
        )
        width = rec_w.shape[0]
        parts[rows, :] = jnp.dot(
            mixed[rows, :width], out_w[...], preferred_element_type=jnp.float32
        ).astype(jnp.bfloat16)
        return nothing

    lax.fori_loop(0, 3, block, 0)
    moves.step()
    lax.fori_loop(3, 6, block, 0)
    moves.step()
    lax.fori_loop(6, x_all.shape[0] // BLOCK, block, 0)
    keeping = [
        pltpu.make_async_copy(source, target, kept_sem.at[place])
        for place, (source, target) in enumerate(zip(kept, kept_out))
    ]
    for copy in keeping:
        copy.start()
    total = reduce_shards(copies, parts, *buffers, between=moves.step)
    size = mine.shape[0]
    start = pl.multiple_of(token_shard(r, c) * size, size)

    def body(at):
        rows = pl.ds(at, STRIP)
        values = x_all[pl.ds(start + at, STRIP), :].astype(jnp.float32) + total(at)
        resid_mid[rows, :] = values
        scale = lax.rsqrt(jnp.mean(values * values, axis=1, keepdims=True) + EPS)
        mine[rows, :] = (values * scale * gain[...]).astype(jnp.bfloat16)

    strips(size, body)
    spread_rows(copies, mine, full, moves.step)
    local = copies.go(c_in, block_of(c_all, rows, columns)(r, c), None)
    late = spread(copies, c_in, block_of(c_all, rows, columns), halves_of(rows), moves.step)
    for copy in late:
        arrived(copy)
    local.wait()
    moves.finish()
    for copy in keeping:
        copy.wait()
    copies.finish()


def norm_pull(values, gain, incoming):
    scale = lax.rsqrt(jnp.mean(values * values, axis=1, keepdims=True) + EPS)
    scaled = gain * incoming
    dots = jnp.sum(scaled * values, axis=1, keepdims=True)
    grad = scale * scaled - values * (scale * scale * scale * dots / values.shape[1])
    return (grad, jnp.sum(incoming * values * scale, axis=0, keepdims=True))


def backward_kernel(parts, resid_mid, cot, gain, full, d_resid, gain_grad, *scratch):
    *buffers, mine, send, recv = scratch
    greet(near())
    copies = Copies(send, recv)
    total = reduce_shards(copies, parts, *buffers)
    gain_grad[...] = jnp.zeros_like(gain_grad)

    def body(at):
        rows = pl.ds(at, STRIP)
        grad, part = norm_pull(resid_mid[rows, :], gain[...], total(at))
        grad = grad + cot[rows, :].astype(jnp.float32)
        gain_grad[...] += part
        d_resid[rows, :] = grad
        mine[rows, :] = grad.astype(jnp.bfloat16)

    strips(mine.shape[0], body)
    spread_rows(copies, mine, full)
    copies.finish()


def finish_kernel(
    parts, out_parts, resid, resid_mid, d_resid, gain, grad, output, gain_grad, *scratch
):
    buffers, more = (scratch[:5], scratch[5:10])
    mine, mine_out, send, recv = scratch[10:]
    z, r, c = here()
    twin, side, top = near()
    cross = (z, flip(across(r)), c)
    greet((twin, side, top, cross))
    copies = Copies(send, recv)
    columns = grad.shape[1]
    size = mine.shape[0]
    gain_grad[...] = jnp.zeros_like(gain_grad)

    def hand_out(source, target):
        def piece(row):
            return source.at[:, pl.ds(pl.multiple_of(row * columns, columns), columns)]

        spot = target.at[pl.ds(pl.multiple_of(r * size, size), size), :]
        waits = [copies.go(piece(peer[1]), spot, peer) for peer in (side, cross, twin)]
        return (copies.go(piece(r), spot, None), waits)

    total = reduce_shards(copies, out_parts, *more)

    def body_out(at):
        rows = pl.ds(at, STRIP)
        mine_out[rows, :] = (resid_mid[rows, :] + total(at)).astype(jnp.bfloat16)

    strips(size, body_out)
    moves = [hand_out(mine_out, output)]
    total_back = reduce_shards(copies, parts, *buffers)

    def body(at):
        rows = pl.ds(at, STRIP)
        values, part = norm_pull(resid[rows, :].astype(jnp.float32), gain[...], total_back(at))
        gain_grad[...] += part
        mine[rows, :] = (d_resid[rows, :] + values).astype(jnp.bfloat16)

    strips(size, body)
    moves.append(hand_out(mine, grad))
    for local, waits in moves:
        for copy in waits:
            arrived(copy)
        local.wait()
    copies.finish()


def vmem_call(kernel, name, place, arrays, outs, spaces, scratch, count, loose=()):
    return pl.pallas_call(
        kernel,
        in_specs=[pl.BlockSpec(memory_space=pltpu.VMEM)] * len(arrays)
        + [pl.BlockSpec(memory_space=pl.ANY)] * len(loose),
        out_specs=[pl.BlockSpec(memory_space=space) for space in spaces],
        out_shape=outs,
        scratch_shapes=scratch
        + [pltpu.SemaphoreType.DMA((count,)), pltpu.SemaphoreType.DMA((count,))],
        compiler_params=pltpu.CompilerParams(
            collective_id=place, has_side_effects=True, vmem_limit_bytes=VMEM_BYTES
        ),
        name=name,
    )(*arrays, *loose)


CHUNK = 16


def reduce_kernel(count, *refs):
    sources, (gates, vec, gain) = (refs[:count], refs[count : count + 3])
    out, out_gates, out_vec, out_gain = refs[count + 3 : count + 7]
    own, left, right, vec_z, gain_z, vec_sum, gain_sum, vec_in, gain_in = refs[count + 7 : count + 16]
    move_send, move_recv, gate_sem, small_send, small_recv = refs[count + 16 : count + 21]
    end_send, low_recv, high_recv, out_recv, mid_send, first_send, last_send, local, on_send = refs[
        count + 21 :
    ]
    z, r, c = here()
    twin, side, cross = ((z, flip(r), c), (z, across(r), c), (z, flip(across(r)), c))
    is_end = (z == 0) | (z == 3)
    near_z = jnp.where(z == 0, 1, 2)
    end_z = jnp.where(z == 1, 0, 3)
    lines = [((z + step) % 4, r, c) for step in (1, 2, 3)]
    plane = [
        (z, (r + step) % 4, (c + turn) % 2) for turn in (0, 1) for step in range(4) if step or turn
    ]
    greet(lines + plane)

    rows = own.shape[1]
    half = rows // 2
    per = half // CHUNK
    chunks = 4 * per + 1

    def remote(source, target, sender, receiver, device):
        return pltpu.make_async_remote_copy(
            src_ref=source,
            dst_ref=target,
            send_sem=sender,
            recv_sem=receiver,
            device_id=device,
            device_id_type=MESH,
        )

    small = [
        [
            remote(
                source,
                target.at[3 - step],
                small_send.at[kind, step - 1],
                small_recv.at[kind, 3 - step],
                lines[step - 1],
            )
            for step in (1, 2, 3)
        ]
        for kind, (source, target) in enumerate(((vec, vec_z), (gain, gain_z)))
    ]
    for kind in small:
        for copy in kind:
            copy.start()
    packed = []
    width = gates.shape[1]
    for tile in range(gates.shape[0] // CHUNK):
        which, place = (tile // 5, tile % 5)
        copy = pltpu.make_async_copy(
            gates.at[pl.ds(tile * CHUNK, CHUNK), :],
            own.at[4, pl.ds(which * half, CHUNK), pl.ds(place * width, width)],
            gate_sem.at[tile],
        )
        copy.start()
        packed.append(copy)
    moves = []
    for which, peer in ((1, twin), (2, side), (3, cross)):
        start = 0
        group = []
        for place, source in enumerate(sources):
            width = source.shape[1]
            copy = remote(
                source.at[pl.ds(pl.multiple_of(peer[1] * rows, rows), rows), :],
                own.at[r, :, pl.ds(start, width)],
                move_send.at[which, place],
                move_recv.at[which, place],
                peer,
            )
            copy.start()
            group.append(copy)
            start += width
        moves.append(group)
    start = 0
    group = []
    for place, source in enumerate(sources):
        width = source.shape[1]
        copy = pltpu.make_async_copy(
            source.at[pl.ds(pl.multiple_of(r * rows, rows), rows), :],
            own.at[r, :, pl.ds(start, width)],
            move_recv.at[0, place],
        )
        copy.start()
        group.append(copy)
        start += width
    for copy in packed:
        copy.wait()

    def piece_arrived(index):
        @pl.when(index == 1)
        def _():
            for copy in group:
                copy.wait()

        for which in (1, 2, 3):

            @pl.when(index == 1 + which * per)
            def _():
                for copy in moves[which - 1]:
                    copy.wait_recv()

    def slot(index):
        step = (index + per - 1) // per - 1
        turned = (r // 2 + step // 2) % 2 * 2 + (r % 2 + step % 2) % 2
        return jnp.where(index == 0, 4, turned)

    def strip_of(index):
        return pl.multiple_of((index + per - 1) % per * CHUNK * jnp.where(index == 0, 0, 1), CHUNK)

    def own_at(index, part):
        return own.at[slot(index), pl.ds(part * half + strip_of(index), CHUNK), :]

    def out_at(index, part):
        return out.at[slot(index), pl.ds(part * half + strip_of(index), CHUNK), :]

    def loop(first, last, body):
        def run(index, nothing):
            body(index)
            return nothing

        lax.fori_loop(first, last, run, 0)

    spread_out = [
        [
            remote(
                source,
                target.at[6 - step],
                small_send.at[kind, 3 + step],
                small_recv.at[kind, 3 + 6 - step],
                peer,
            )
            for step, peer in enumerate(
                [(z, (r + turn % 4) % 4, (c + turn // 4) % 2) for turn in range(1, 8)]
            )
        ]
        for kind, (source, target) in enumerate(((vec_sum, vec_in), (gain_sum, gain_in)))
    ]

    def small_middle():
        for kind in small:
            for copy in kind:
                copy.wait_recv()
        vec_sum[...] = vec[...] + vec_z[0] + vec_z[1] + vec_z[2]
        gain_sum[...] = gain[...] + gain_z[0] + gain_z[1] + gain_z[2]
        for kind in spread_out:
            for copy in kind:
                copy.start()

    gate_moves = []
    for which, peer in enumerate((twin, side, cross)):
        for part in (0, 1):
            gate_moves.append(
                remote(
                    out.at[4, pl.ds(part * half, CHUNK), :],
                    out_gates.at[r, part],
                    small_send.at[0, 10 + 2 * which + part],
                    small_recv.at[0, 10 + 2 * which + part],
                    peer,
                )
            )
    gate_local = [
        pltpu.make_async_copy(
            out.at[4, pl.ds(part * half, CHUNK), :], out_gates.at[r, part], gate_sem.at[part]
        )
        for part in (0, 1)
    ]

    def gates_out():
        for copy in gate_moves + gate_local:
            copy.start()

    @pl.when(is_end)
    def _():
        low = z // 3
        peer = (near_z, r, c)

        def send_low(index):
            return remote(
                own_at(index, low),
                left.at[index],
                end_send.at[0, index],
                low_recv.at[index],
                peer,
            )

        def send_high(index):
            return remote(
                own_at(index, 1 - low),
                right.at[1, index],
                end_send.at[1, index],
                high_recv.at[1, index],
                peer,
            )

        def begin(index):
            piece_arrived(index)
            send_low(index).start()
            send_high(index).start()

        def end(index):
            send_low(index).wait_send()
            send_high(index).wait_send()
            for part in (0, 1):
                spot = out_at(index, part)
                remote(
                    spot, spot, end_send.at[0, index], out_recv.at[part, index], peer
                ).wait_recv()

        loop(0, chunks, begin)
        small_middle()
        loop(0, 1, end)
        gates_out()
        loop(1, chunks, end)

    @pl.when(jnp.logical_not(is_end))
    def _():
        low = z - 1
        other, outer = ((3 - z, r, c), (end_z, r, c))

        def to_other(index):
            return remote(
                own_at(index, 1 - low),
                right.at[0, index],
                mid_send.at[index],
                high_recv.at[0, index],
                other,
            )

        def from_outer(index):
            return remote(
                own_at(index, 1 - low),
                right.at[1, index],
                mid_send.at[index],
                high_recv.at[1, index],
                outer,
            )

        def from_low(index):
            return remote(
                own_at(index, low), left.at[index], mid_send.at[index], low_recv.at[index], outer
            )

        def final(index):
            mine = own_at(index, low)
            spot = out_at(index, low)
            return (
                pltpu.make_async_copy(mine, spot, local.at[index]),
                remote(mine, spot, first_send.at[index], out_recv.at[low, index], outer),
                remote(mine, spot, last_send.at[index], out_recv.at[low, index], other),
            )

        def onward(index):
            spot = out_at(index, 1 - low)
            return remote(spot, spot, on_send.at[index], out_recv.at[1 - low, index], outer)

        def rows_at(index, part):
            return pl.ds(pl.multiple_of(part * half + strip_of(index), CHUNK), CHUNK)

        def step(index):
            @pl.when(index < chunks)
            def _():
                piece_arrived(index)
                from_outer(index).wait_recv()
                spot = rows_at(index, 1 - low)
                total = own[slot(index), spot, :].astype(jnp.float32) + right[1, index].astype(
                    jnp.float32
                )
                own[slot(index), spot, :] = total.astype(jnp.bfloat16)
                to_other(index).start()

            @pl.when((index >= 2) & (index < chunks + 2))
            def _():
                back = index - 2
                from_low(back).wait_recv()
                to_other(back).wait_recv()
                spot = rows_at(back, low)
                total = (
                    own[slot(back), spot, :].astype(jnp.float32)
                    + left[back].astype(jnp.float32)
                    + right[0, back].astype(jnp.float32)
                )
                own[slot(back), spot, :] = total.astype(jnp.bfloat16)
                for copy in final(back):
                    copy.start()

            @pl.when(index >= 4)
            def _():
                back = index - 4
                onward(back).wait_recv()
                onward(back).start()

        def end(index):
            to_other(index).wait_send()
            _, first, last = final(index)
            first.wait_send()
            last.wait_send()
            onward(index).wait_send()

        def end_local(index):
            final(index)[0].wait()

        loop(0, 32, step)
        small_middle()
        end_local(0)
        gates_out()
        loop(32, chunks + 4, step)
        loop(1, chunks, end_local)
        loop(0, chunks, end)

    for kind in spread_out:
        for copy in kind:
            copy.wait_recv()
    out_gain[...] = (
        gain_sum[...]
        + gain_in[0]
        + gain_in[1]
        + gain_in[2]
        + gain_in[3]
        + gain_in[4]
        + gain_in[5]
        + gain_in[6]
    )
    out_vec[...] = jnp.zeros_like(out_vec)
    out_vec[r] = vec_sum[...]
    for step in (0, 1, 2):
        out_vec[(r + 3 - step) % 4] = vec_in[6 - step]
    for copy in gate_moves:
        copy.wait_recv()
    for copy in gate_local:
        copy.wait()
    for group in small + spread_out + moves + [gate_moves]:
        for copy in group:
            copy.wait_send()


def reduce_grads(sources, gates, vec, gain):
    rows = sources[0].shape[0] // 4
    width = sum(source.shape[1] for source in sources)
    chunks = 4 * (rows // 2 // CHUNK) + 1
    dma = pltpu.SemaphoreType.DMA
    count = len(sources)
    vmem = pl.BlockSpec(memory_space=pltpu.VMEM)
    loose = pl.BlockSpec(memory_space=pl.ANY)
    return pl.pallas_call(
        functools.partial(reduce_kernel, count),
        in_specs=[loose] * (count + 1) + [vmem, vmem],
        out_specs=[loose, loose, vmem, vmem],
        out_shape=[
            jax.ShapeDtypeStruct((5, rows, width), jnp.bfloat16),
            jax.ShapeDtypeStruct((4, 2, CHUNK, width), jnp.bfloat16),
            jax.ShapeDtypeStruct((4, *vec.shape), jnp.float32),
            jax.ShapeDtypeStruct(gain.shape, jnp.float32),
        ],
        scratch_shapes=[
            pltpu.VMEM((5, rows, width), jnp.bfloat16),
            pltpu.VMEM((chunks, CHUNK, width), jnp.bfloat16),
            pltpu.VMEM((2, chunks, CHUNK, width), jnp.bfloat16),
            pltpu.VMEM((3, *vec.shape), jnp.float32),
            pltpu.VMEM((3, *gain.shape), jnp.float32),
            pltpu.VMEM(vec.shape, jnp.float32),
            pltpu.VMEM(gain.shape, jnp.float32),
            pltpu.VMEM((7, *vec.shape), jnp.float32),
            pltpu.VMEM((7, *gain.shape), jnp.float32),
            dma((4, count)),
            dma((4, count)),
            dma((10,)),
            dma((2, 16)),
            dma((2, 16)),
            dma((2, chunks)),
            dma((chunks,)),
            dma((2, chunks)),
            dma((2, chunks)),
            dma((chunks,)),
            dma((chunks,)),
            dma((chunks,)),
            dma((chunks,)),
            dma((chunks,)),
        ],
        compiler_params=pltpu.CompilerParams(
            collective_id=REDUCE_ID, has_side_effects=True, vmem_limit_bytes=VMEM_BYTES
        ),
        name="reduce_grads",
    )(*sources, gates, vec, gain)


def dot(left, right, dims, kind=jnp.float32):
    return lax.dot_general(left, right, dims, preferred_element_type=jnp.float32).astype(kind)


def local_plane(
    inputs,
    cotangent,
    starts,
    x_proj,
    y_proj,
    out_proj,
    gate_proj,
    up_proj,
    down_proj,
    mix_gain,
    mlp_gain,
    x_bias,
    y_bias,
    conv_w,
    conv_b,
    rec_gate_w,
    in_gate_w,
    rec_gate_b,
    in_gate_b,
    decay_param,
):
    z, r, c = here()
    depth = x_proj.shape[0]
    rec = x_proj.shape[1] // 4
    width = gate_proj.shape[1] // 4
    heads, head = (rec_gate_w.shape[0] // 4, rec_gate_w.shape[1])
    padded = (rec + 127) // 128 * 128
    low = jnp.bfloat16

    def mine(array, size, axis=0):
        return lax.dynamic_slice_in_dim(array, r * size, size, axis)

    mix_in = jnp.concatenate(
        [x_proj.reshape(depth, 4, rec), y_proj.reshape(depth, 4, rec)], axis=2
    ).transpose(1, 0, 2)
    flags = jnp.pad(starts.astype(jnp.float32).reshape(-1, 128), ((0, 6), (0, 0)))
    x_all, s_all, g_all, mix_w, out_w = gather(
        inputs.T, flags, jnp.stack([mix_gain, mlp_gain]), mix_in, out_proj
    )
    tokens, model = x_all.shape
    gain_mix, gain_mlp = (g_all[0:1], g_all[1:2])
    fresh = s_all[:, :2, :].reshape(tokens)
    stale = 1.0 - fresh
    stale_one = jnp.concatenate([jnp.zeros((1,), jnp.float32), stale[:-1]])
    stale_two = jnp.concatenate([jnp.zeros((2,), jnp.float32), stale[:-2]])
    nothing = jnp.zeros_like(fresh)
    masks = jnp.stack(
        [fresh, stale, stale * stale_one, stale * stale_one * stale_two] + [nothing] * 4, axis=1
    )
    vectors = jnp.concatenate(
        [
            x_bias[None],
            y_bias[None],
            conv_w,
            conv_b[None],
            rec_gate_b[None],
            in_gate_b[None],
            -GATE_C * jax.nn.softplus(decay_param)[None],
            -GATE_C * jax.nn.sigmoid(decay_param)[None],
            jnp.zeros((5, x_bias.shape[0]), jnp.float32),
        ],
        axis=0,
    )
    vec = mine(vectors, rec, 1)

    def diagonal(blocks):
        blocks = mine(blocks, heads)
        rows = [jnp.pad(blocks[i], ((0, 0), (i * head, rec - (i + 1) * head))) for i in range(heads)]
        return jnp.concatenate(rows, axis=0)

    rec_w, in_w = (diagonal(rec_gate_w), diagonal(in_gate_w))
    size = tokens // 8
    shard = token_shard(r, c) * size
    resid = lax.dynamic_slice_in_dim(x_all, shard, size, 0)
    full = jax.ShapeDtypeStruct((tokens, model), low)
    part = jax.ShapeDtypeStruct((size, model), jnp.float32)
    line = jax.ShapeDtypeStruct((1, model), jnp.float32)
    piece = pltpu.VMEM((size, model), low)
    block = jax.ShapeDtypeStruct((inputs.shape[1], inputs.shape[0]), low)
    weights = (gate_proj, up_proj, down_proj)
    slices = jax.ShapeDtypeStruct((4 * depth, width), low)
    kept = [((tokens, model), low), ((tokens, 2 * rec), jnp.float32), ((tokens, padded), low)]
    kept += [((tokens, rec), kind) for kind in (jnp.float32, low) + (jnp.float32,) * 3]
    row8 = pltpu.VMEM((8, rec), jnp.float32)
    (
        normed_mlp,
        resid_mid,
        c_all,
        gate_w,
        up_w,
        down_w,
        normed_mix,
        pre,
        mixed,
        x_pre,
        conv,
        rec_gate,
        in_gate,
        states,
    ) = vmem_call(
        forward_kernel,
        "forward",
        FORWARD_ID,
        (x_all, masks, vec, rec_w, in_w, mix_w, out_w, gain_mix, gain_mlp),
        [full, part, full] + [slices] * 3 + [jax.ShapeDtypeStruct(*item) for item in kept],
        [pl.ANY, pltpu.VMEM] + [pl.ANY] * 12,
        [pltpu.VMEM(*item) for item in kept]
        + [row8, row8, pltpu.VMEM((tokens, model), low)]
        + reduce_scratch(size, model)
        + [piece, pltpu.SemaphoreType.DMA((8,))],
        80,
        (cotangent.T, *weights),
    )
    cot = lax.dynamic_slice_in_dim(c_all, shard, size, 0)
    gate = dot(normed_mlp, gate_w, CONTRACT_PLAIN)
    up = dot(normed_mlp, up_w, CONTRACT_PLAIN)
    d_activ = dot(c_all, down_w, CONTRACT_PLAIN)
    gelu, slope = gelu_both(gate)
    activ = (gelu * up).astype(low)
    d_gate = (d_activ * up * slope).astype(low)
    d_up = (d_activ * gelu).astype(low)
    d_normed = lax.dot_general(
        d_gate, gate_w, CONTRACT_COLS, preferred_element_type=jnp.float32
    ) + lax.dot_general(d_up, up_w, CONTRACT_COLS, preferred_element_type=jnp.float32)
    d_branch, d_resid, grad_mlp_gain = vmem_call(
        backward_kernel,
        "backward_norm",
        BACKWARD_ID,
        (d_normed.astype(low), resid_mid, cot, gain_mlp),
        [full, part, line],
        [pl.ANY, pltpu.VMEM, pltpu.VMEM],
        reduce_scratch(size, model) + [piece],
        24,
    )
    d_mixed = dot(d_branch, out_w, CONTRACT_COLS)
    d_pre, d_gates, sums = mixer_backward(
        d_mixed, pre, masks, vec, rec_w, in_w, x_pre, conv, rec_gate, in_gate, states
    )
    grad_in, output, grad_mix_gain = vmem_call(
        finish_kernel,
        "finish_norm",
        FINISH_ID,
        (
            dot(d_pre, mix_w, CONTRACT_COLS, low),
            dot(activ, down_w, CONTRACT_COLS, low),
            resid,
            resid_mid,
            d_resid,
            gain_mix,
        ),
        [block, block, line],
        [pltpu.VMEM] * 3,
        reduce_scratch(size, model) * 2 + [piece, piece],
        40,
    )
    gate_grads = dot(conv, d_gates, CONTRACT_ROWS, low)
    gates = jnp.concatenate(
        [
            gate_grads[i * head : (i + 1) * head, first + i * head : first + (i + 1) * head]
            for first in (0, rec)
            for i in range(heads)
        ],
        axis=1,
    )
    grads, gates, vec_sums, gains = reduce_grads(
        (
            dot(normed_mlp, d_gate, CONTRACT_ROWS, low),
            dot(normed_mlp, d_up, CONTRACT_ROWS, low),
            dot(c_all, activ, CONTRACT_ROWS, low),
            dot(normed_mix, d_pre, CONTRACT_ROWS, low),
            dot(d_branch, mixed, CONTRACT_ROWS, low),
        ),
        gates,
        sums,
        jnp.concatenate([grad_mix_gain, grad_mlp_gain], axis=0),
    )
    gates = gates[:, :, :, : 5 * 4 * head].reshape(4, 2, CHUNK, 5, 2, heads, head)
    gates = gates.transpose(4, 0, 5, 1, 3, 2, 6).reshape(2, 4 * heads, head, head)
    gates = gates.astype(jnp.float32)
    vec_sums = vec_sums.transpose(1, 0, 2).reshape(vec_sums.shape[1], 4 * rec)
    gains = lax.dynamic_slice_in_dim(gains, r * depth, depth, 1)

    def columns(first, length):
        return jnp.concatenate(
            [grads[i, :, first : first + length] for i in range(4)], axis=1
        ).astype(jnp.float32)

    after = 3 * width
    grad_out = jnp.concatenate(
        [grads[i, :, after + 2 * rec : after + 3 * rec].T for i in range(4)], axis=0
    ).astype(jnp.float32)
    return (
        output.T,
        grad_in.astype(jnp.float32).T,
        columns(after, rec),
        columns(after + rec, rec),
        grad_out,
        columns(0, width),
        columns(width, width),
        columns(2 * width, width),
        gains[0],
        gains[1],
        vec_sums[0],
        vec_sums[1],
        vec_sums[2:6],
        vec_sums[6],
        gates[0],
        gates[1],
        vec_sums[7],
        vec_sums[8],
        vec_sums[9],
    )


def fits(mesh):
    return mesh.shape["dp"] == 4 and mesh.shape["row"] == 4 and mesh.shape["col"] == 2


def solution(mesh):
    placed = (
        P("row", ("dp", "col")),
        P("row", ("dp", "col")),
        P(("dp", "row")),
        P("row", "col"),
        P("row", "col"),
        P("col", "row"),
        P("row", "col"),
        P("row", "col"),
        P("row", "col"),
        P("row"),
        P("row"),
        P("col"),
        P("col"),
        P(None, "col"),
        P("col"),
        P("col", None, None),
        P("col", None, None),
        P("col"),
        P("col"),
        P("col"),
    )
    return jax.shard_map(
        local_plane if fits(mesh) else local,
        mesh=mesh,
        in_specs=placed,
        out_specs=(
            P("row", ("dp", "col")),
            P("row", ("dp", "col")),
            P("row", "col"),
            P("row", "col"),
            P("col", "row"),
            P("row", "col"),
            P("row", "col"),
            P("row", "col"),
            P("row"),
            P("row"),
            P("col"),
            P("col"),
            P(None, "col"),
            P("col"),
            P("col", None, None),
            P("col", None, None),
            P("col"),
            P("col"),
            P("col"),
        ),
        check_vma=False,
    )
```

```python
import functools

import jax
import jax.numpy as jnp
from jax import lax
from jax.experimental import pallas as pl
from jax.experimental.pallas import tpu as pltpu
from jax.sharding import PartitionSpec as P

MESH = pl.DeviceIdType.MESH

D = 2048


EPS = 1e-06
GATE_C = 8.0
CONTRACT_ROWS = (((0,), (0,)), ((), ()))
CONTRACT_COLS = (((1,), (1,)), ((), ()))
CONTRACT_PLAIN = (((1,), (0,)), ((), ()))


def from_behind(value, axis, by):
    count = lax.axis_size(axis)
    pairs = [(i, i + by) for i in range(count) if 0 <= i + by < count]
    return lax.ppermute(value, axis, pairs)


def carried_in(value, axis, join, neutral, backward):
    count, mine = (lax.axis_size(axis), lax.axis_index(axis))
    pieces = jax.tree.map(lambda part: lax.all_gather(part, axis), value)
    if backward:
        pieces = jax.tree.map(lambda part: part[::-1], pieces)
        mine = count - 1 - mine
    subtotal = jax.tree.map(
        lambda part, zero: jnp.full_like(part, 0) + jnp.asarray(zero, part.dtype), value, neutral
    )

    def hop(position, subtotal):
        longer = join(subtotal, jax.tree.map(lambda part: part[position], pieces))
        return jax.tree.map(lambda new, old: jnp.where(position < mine, new, old), longer, subtotal)

    return lax.fori_loop(0, count - 1, hop, subtotal)


def chain(earlier, later):
    return (earlier[0] * later[0], later[0] * earlier[1] + later[1])


def adjoint_chain(earlier, later):
    return (later[0] * earlier[0], later[1] + later[0] * earlier[1])


def gelu_tanh(values):
    return jax.nn.gelu(values, approximate=True)


def glu_piece(gate_vals, up_vals):
    return gelu_tanh(gate_vals) * up_vals


def causal_conv(values, conv_w, conv_b, segment_ids):
    result = values * conv_w[0] + conv_b
    for offset in range(1, conv_w.shape[0]):
        lagged = jnp.pad(values, ((offset, 0), (0, 0)))[:-offset]
        earlier_ids = jnp.pad(segment_ids, (offset, 0), constant_values=-1)[:-offset]
        result = (
            result + jnp.where((earlier_ids == segment_ids)[:, None], lagged, 0.0) * conv_w[offset]
        )
    return result


def local_recurrence(rec_pre, in_pre, conv_vals, decay_param, flags):
    rec_gate = jax.nn.sigmoid(rec_pre)
    in_gate = jax.nn.sigmoid(in_pre)
    log_keep = -GATE_C * rec_gate * jax.nn.softplus(decay_param)
    keep_rate = jnp.exp(log_keep)
    fresh = (flags == 1)[:, None]
    multiplier = jnp.where(fresh, 1.0, jnp.sqrt(-jnp.expm1(2.0 * log_keep)))
    driven = conv_vals * in_gate * multiplier
    carried = jnp.where(fresh, 0.0, keep_rate)
    cum_keep, states = lax.associative_scan(chain, (carried, driven), axis=0)
    return (cum_keep, states)


def row_sums(values):
    return lax.psum(values, "row")


def norm_forward(values, norm_gain):
    squares = row_sums(jnp.sum(values * values, axis=1))
    inv_rms = lax.rsqrt(squares / D + EPS)
    return (values * inv_rms[:, None] * norm_gain, inv_rms)


def norm_backward(values, inv_rms, norm_gain, incoming):
    scaled = norm_gain * incoming
    dots = row_sums(jnp.sum(scaled * values, axis=1))
    values_grad = inv_rms[:, None] * scaled - values * (inv_rms**3 * dots / D)[:, None]
    gain_grad = jnp.sum(incoming * values * inv_rms[:, None], axis=0)
    return (values_grad, gain_grad)


def gather_edge(values):
    return lax.all_gather(values, "col", axis=0, tiled=True)


def gather_mid(values):
    return lax.all_gather(values, "row", axis=0, tiled=True)


def row_partial(whole, weight, dims):
    return lax.psum_scatter(
        lax.dot_general(whole, weight, dims, preferred_element_type=jnp.float32),
        "row",
        scatter_dimension=0,
        tiled=True,
    )


def col_partial(whole, weight, dims):
    return lax.psum_scatter(
        lax.dot_general(whole, weight, dims, preferred_element_type=jnp.float32),
        "col",
        scatter_dimension=0,
        tiled=True,
    )


def project_in(normed, weight):
    whole = gather_edge(normed)
    result = row_partial(whole, weight, CONTRACT_PLAIN)
    return (result, whole)


def weight_grad(left, right):
    return lax.dot_general(left, right, CONTRACT_ROWS, preferred_element_type=jnp.float32)


def local(
    inputs,
    cotangent,
    starts,
    x_proj,
    y_proj,
    out_proj,
    gate_proj,
    up_proj,
    down_proj,
    mix_gain,
    mlp_gain,
    x_bias,
    y_bias,
    conv_w,
    conv_b,
    rec_gate_w,
    in_gate_w,
    rec_gate_b,
    in_gate_b,
    decay_param,
):
    rows_mid = starts.shape[0]
    rec_width = x_proj.shape[1]
    ff_width = gate_proj.shape[1]
    head_count = rec_gate_w.shape[0]
    margin = conv_w.shape[0] - 1
    mix_weights = jnp.concatenate([x_proj, y_proj], axis=1)
    mlp_weights = jnp.concatenate([gate_proj, up_proj], axis=1)
    cot_rows = cotangent.T
    resid = inputs.astype(jnp.float32).T
    normed_mix, inv_rms_mix = norm_forward(resid, mix_gain)
    normed_mix = normed_mix.astype(jnp.bfloat16)
    pre_both, whole_mix = project_in(normed_mix, mix_weights)
    x_pre = pre_both[:, :rec_width] + x_bias
    y_pre = pre_both[:, rec_width:] + y_bias
    x_tail, flag_tail = from_behind(
        (x_pre[rows_mid - margin :], starts[rows_mid - margin :].astype(jnp.float32)), "row", 1
    )
    ext_flags = jnp.concatenate([flag_tail.astype(jnp.int32), starts])
    ext_ids = jnp.cumsum(ext_flags, dtype=jnp.int32)
    ext_x = jnp.concatenate([x_tail, x_pre], axis=0)

    def conv_piece(values, taps, offsets):
        return causal_conv(values, taps, offsets, ext_ids)[margin:]

    conv_vals, conv_pull = jax.vjp(conv_piece, ext_x, conv_w, conv_b)
    conv_low = conv_vals.astype(jnp.bfloat16)
    conv_heads = conv_low.reshape(rows_mid, head_count, -1)
    rec_pre = (
        jnp.einsum(
            "thk,hkj->thj", conv_heads, rec_gate_w, preferred_element_type=jnp.float32
        ).reshape(rows_mid, rec_width)
        + rec_gate_b
    )
    in_pre = (
        jnp.einsum(
            "thk,hkj->thj", conv_heads, in_gate_w, preferred_element_type=jnp.float32
        ).reshape(rows_mid, rec_width)
        + in_gate_b
    )

    def scan_piece(rec_vals, in_vals, conv_input, decay_vals):
        return local_recurrence(rec_vals, in_vals, conv_input, decay_vals, starts)

    (cum_keep, local_states), scan_pull = jax.vjp(
        scan_piece, rec_pre, in_pre, conv_low.astype(jnp.float32), decay_param
    )
    ones_row = jnp.ones((rec_width,), jnp.float32)
    zeros_row = jnp.zeros((rec_width,), jnp.float32)
    incoming = carried_in(
        (cum_keep[rows_mid - 1], local_states[rows_mid - 1]),
        "row",
        chain,
        (ones_row, zeros_row),
        False,
    )
    state_prev = incoming[1]
    states = local_states + cum_keep * state_prev
    y_act, y_pull = jax.vjp(gelu_tanh, y_pre)
    mixed = (states * y_act).astype(jnp.bfloat16)
    whole_mixed = gather_mid(mixed)
    resid_mid = resid + col_partial(whole_mixed, out_proj, CONTRACT_PLAIN)
    normed_mlp, inv_rms_mlp = norm_forward(resid_mid, mlp_gain)
    normed_mlp = normed_mlp.astype(jnp.bfloat16)
    gate_up, whole_mlp = project_in(normed_mlp, mlp_weights)
    activ, activ_pull = jax.vjp(glu_piece, gate_up[:, :ff_width], gate_up[:, ff_width:])
    activ = activ.astype(jnp.bfloat16)
    whole_activ = gather_mid(activ)
    output = (resid_mid + col_partial(whole_activ, down_proj, CONTRACT_COLS)).astype(jnp.bfloat16)
    cot_whole = gather_edge(cot_rows)
    d_activ = row_partial(cot_whole, down_proj, CONTRACT_PLAIN)
    activ_rows = gather_mid(activ)
    grad_down = weight_grad(cot_whole, activ_rows)
    d_gate, d_up = activ_pull(d_activ)
    d_gate_up = jnp.concatenate([d_gate, d_up], axis=1).astype(jnp.bfloat16)
    d_gate_up_whole = gather_mid(d_gate_up)
    d_normed_mlp = col_partial(d_gate_up_whole, mlp_weights, CONTRACT_COLS)
    mlp_rows = gather_edge(normed_mlp)
    grad_gate_up = weight_grad(mlp_rows, d_gate_up_whole)
    d_norm_mid, grad_mlp_gain = norm_backward(resid_mid, inv_rms_mlp, mlp_gain, d_normed_mlp)
    d_resid_mid = cot_rows.astype(jnp.float32) + d_norm_mid
    d_branch = d_resid_mid.astype(jnp.bfloat16)
    branch_whole = gather_edge(d_branch)
    d_mixed = row_partial(branch_whole, out_proj, CONTRACT_COLS)
    mixed_rows = gather_mid(mixed)
    grad_out = weight_grad(mixed_rows, branch_whole)
    d_state = d_mixed * y_act
    (d_y_pre,) = y_pull(d_mixed * states)
    own_sens = jnp.sum(d_state * cum_keep, axis=0)
    outgoing = carried_in(
        (cum_keep[rows_mid - 1], own_sens), "row", adjoint_chain, (ones_row, zeros_row), True
    )
    d_total = d_state + jnp.pad(outgoing[1][None, :], ((rows_mid - 1, 0), (0, 0)))
    d_rec_pre, d_in_pre, d_conv_direct, grad_decay = scan_pull((d_total * state_prev, d_total))
    d_rec_low = d_rec_pre.astype(jnp.bfloat16)
    d_in_low = d_in_pre.astype(jnp.bfloat16)
    d_rec_heads = d_rec_low.reshape(rows_mid, head_count, -1)
    d_in_heads = d_in_low.reshape(rows_mid, head_count, -1)
    d_conv = d_conv_direct + jnp.einsum(
        "thj,hkj->thk", d_rec_heads, rec_gate_w, preferred_element_type=jnp.float32
    ).reshape(rows_mid, rec_width)
    d_conv = d_conv + jnp.einsum(
        "thj,hkj->thk", d_in_heads, in_gate_w, preferred_element_type=jnp.float32
    ).reshape(rows_mid, rec_width)
    grad_rec_w = jnp.einsum(
        "thk,thj->hkj", conv_heads, d_rec_heads, preferred_element_type=jnp.float32
    )
    grad_in_w = jnp.einsum(
        "thk,thj->hkj", conv_heads, d_in_heads, preferred_element_type=jnp.float32
    )
    grad_rec_b = jnp.sum(d_rec_low.astype(jnp.float32), axis=0)
    grad_in_b = jnp.sum(d_in_low.astype(jnp.float32), axis=0)
    d_ext, grad_conv_w, grad_conv_b = conv_pull(d_conv)
    d_from_next = from_behind(d_ext[:margin], "row", -1)
    d_x_pre = d_ext[margin:] + jnp.pad(d_from_next, ((rows_mid - margin, 0), (0, 0)))
    d_pre = jnp.concatenate([d_x_pre, d_y_pre], axis=1).astype(jnp.bfloat16)
    bias_sums = jnp.sum(d_pre.astype(jnp.float32), axis=0)
    d_pre_whole = gather_mid(d_pre)
    d_normed_mix = col_partial(d_pre_whole, mix_weights, CONTRACT_COLS)
    mix_rows = gather_edge(normed_mix)
    grad_mix = weight_grad(mix_rows, d_pre_whole)
    d_norm_in, grad_mix_gain = norm_backward(resid, inv_rms_mix, mix_gain, d_normed_mix)
    inputs_grad = d_resid_mid + d_norm_in
    grad_mix, grad_out, grad_gate_up, grad_down = (
        lax.psum(grad_mix.astype(jnp.bfloat16), "dp").astype(jnp.float32),
        lax.psum(grad_out.astype(jnp.bfloat16), "dp").astype(jnp.float32),
        lax.psum(grad_gate_up.astype(jnp.bfloat16), "dp").astype(jnp.float32),
        lax.psum(grad_down.astype(jnp.bfloat16), "dp").astype(jnp.float32),
    )
    (
        bias_sums,
        grad_conv_w,
        grad_conv_b,
        grad_rec_w,
        grad_in_w,
        grad_rec_b,
        grad_in_b,
        grad_decay,
    ) = (
        lax.psum(bias_sums.astype(jnp.bfloat16), ("dp", "row")).astype(jnp.float32),
        lax.psum(grad_conv_w.astype(jnp.bfloat16), ("dp", "row")).astype(jnp.float32),
        lax.psum(grad_conv_b.astype(jnp.bfloat16), ("dp", "row")).astype(jnp.float32),
        lax.psum(grad_rec_w.astype(jnp.bfloat16), ("dp", "row")).astype(jnp.float32),
        lax.psum(grad_in_w.astype(jnp.bfloat16), ("dp", "row")).astype(jnp.float32),
        lax.psum(grad_rec_b.astype(jnp.bfloat16), ("dp", "row")).astype(jnp.float32),
        lax.psum(grad_in_b.astype(jnp.bfloat16), ("dp", "row")).astype(jnp.float32),
        lax.psum(grad_decay.astype(jnp.bfloat16), ("dp", "row")).astype(jnp.float32),
    )
    grad_mix_gain, grad_mlp_gain = lax.psum((grad_mix_gain, grad_mlp_gain), ("dp", "col"))
    return (
        output.T,
        inputs_grad.T,
        grad_mix[:, :rec_width],
        grad_mix[:, rec_width:],
        grad_out,
        grad_gate_up[:, :ff_width],
        grad_gate_up[:, ff_width:],
        grad_down,
        grad_mix_gain,
        grad_mlp_gain,
        bias_sums[:rec_width],
        bias_sums[rec_width:],
        grad_conv_w,
        grad_conv_b,
        grad_rec_w,
        grad_in_w,
        grad_rec_b,
        grad_in_b,
        grad_decay,
    )


GATHER_ID, FORWARD_ID, BACKWARD_ID, REDUCE_ID = (0, 1, 2, 3)
BLOCK = 128
VMEM_BYTES = 60 << 20


def one_minus_exp(rate):
    series = rate * (1.0 - rate * (0.5 - rate * (1.0 / 6.0 - rate * (1.0 / 24.0 - rate / 120.0))))
    return jnp.where(rate < 0.1, series, 1.0 - jnp.exp(-rate))


GELU_C = 0.7978845608028654


def gelu_both(values):
    squared = values * values
    inner = jnp.tanh(GELU_C * values * (1.0 + 0.044715 * squared))
    value = 0.5 * values * (1.0 + inner)
    slope = 0.5 * (1.0 + inner) + 0.5 * values * (1.0 - inner * inner) * GELU_C * (
        1.0 + 3.0 * 0.044715 * squared
    )
    return (value, slope)


def down_rows(values, by):
    return pltpu.roll(values, by, 0)


def up_rows(values, by):
    return pltpu.roll(values, values.shape[0] - by, 0)


def scan_down(keep, add):
    rows = keep.shape[0]
    position = lax.broadcasted_iota(jnp.int32, keep.shape, 0)
    step = 1
    while step < rows:
        if step < 8:
            inside = position >= step
            before_keep = jnp.where(inside, down_rows(keep, step), 1.0)
            before_add = jnp.where(inside, down_rows(add, step), 0.0)
            add = add + keep * before_add
            keep = keep * before_keep
        else:
            add = jnp.concatenate([add[:step], add[step:] + keep[step:] * add[:-step]], axis=0)
            keep = jnp.concatenate([keep[:step], keep[step:] * keep[:-step]], axis=0)
        step *= 2
    return (keep, add)


def scan_up(keep, add):
    rows = keep.shape[0]
    position = lax.broadcasted_iota(jnp.int32, keep.shape, 0)
    step = 1
    while step < rows:
        if step < 8:
            inside = position < rows - step
            after_keep = jnp.where(inside, up_rows(keep, step), 1.0)
            after_add = jnp.where(inside, up_rows(add, step), 0.0)
            add = add + keep * after_add
            keep = keep * after_keep
        else:
            add = jnp.concatenate([add[:-step] + keep[:-step] * add[step:], add[-step:]], axis=0)
            keep = jnp.concatenate([keep[:-step] * keep[step:], keep[-step:]], axis=0)
        step *= 2
    return (keep, add)


def mixer_forward_step(
    pre, marks, vec, rec_w, in_w, mixed, x_pre, conv, rec_gate, in_gate, states, tail, carry
):
    width = x_pre.shape[1]
    x = pre[:, :width] + vec[0:1, :]
    x_pre[...] = x
    longer = jnp.concatenate([tail[...], x], axis=0)
    tail[...] = x[BLOCK - 8 :]
    total = x * vec[2:3, :] + vec[6:7, :]
    for tap in range(1, 4):
        total = total + marks[:, tap : tap + 1] * down_rows(longer, tap)[8:] * vec[
            2 + tap : 3 + tap, :
        ]
    low = total.astype(jnp.bfloat16)
    conv[...] = low
    rec = jax.nn.sigmoid(
        jnp.dot(low, rec_w[...], preferred_element_type=jnp.float32) + vec[7:8, :]
    )
    inn = jax.nn.sigmoid(
        jnp.dot(low, in_w[...], preferred_element_type=jnp.float32) + vec[8:9, :]
    )
    rec_gate[...] = rec
    in_gate[...] = inn
    log_keep = rec * vec[9:10, :]
    fresh = marks[:, 0:1]
    scale = jnp.where(fresh > 0.5, 1.0, jnp.sqrt(one_minus_exp(-2.0 * log_keep)))
    driven = low.astype(jnp.float32) * inn * scale
    keep, add = scan_down(jnp.exp(log_keep) * (1.0 - fresh), driven)
    state = add + keep * carry[0:1, :]
    carry[...] = jnp.broadcast_to(state[BLOCK - 1 :, :], carry.shape)
    states[...] = state
    y = pre[:, width:] + vec[1:2, :]
    mixed[:, :width] = (state * gelu_both(y)[0]).astype(jnp.bfloat16)
    mixed[:, width:] = jnp.zeros((BLOCK, mixed.shape[1] - width), jnp.bfloat16)


def mixer_backward_step(
    incoming,
    pre,
    marks,
    vec,
    rec_w,
    in_w,
    x_pre,
    x_before,
    conv,
    rec_gate,
    in_gate,
    states,
    state_before,
    d_pre,
    d_gates,
    sums,
    edge,
    carry,
):
    width = x_pre.shape[1]
    position = lax.broadcasted_iota(jnp.int32, (BLOCK, width), 0)
    fresh = marks[:, 0:1]
    stale = 1.0 - fresh
    gelu, slope = gelu_both(pre[:, width:] + vec[1:2, :])
    state = states[...]
    d_y = (incoming * state * slope).astype(jnp.bfloat16)
    rec, inn = (rec_gate[...], in_gate[...])
    conv_vals = conv[...].astype(jnp.float32)
    log_keep = rec * vec[9:10, :]
    keep_rate = jnp.exp(log_keep)
    scale = jnp.where(fresh > 0.5, 1.0, jnp.sqrt(one_minus_exp(-2.0 * log_keep)))
    carried = keep_rate * stale
    after = jnp.where(position == BLOCK - 1, carry[1:2, :], up_rows(carried, 1))
    keep, add = scan_up(after, incoming * gelu)
    adjoint = add + keep * carry[0:1, :]
    carry[0:1, :] = adjoint[0:1]
    carry[1:2, :] = carried[0:1]
    earlier = jnp.where(position == 0, state_before[7:8, :], down_rows(state, 1))
    drive = adjoint * scale
    d_log = stale * (
        adjoint * earlier * keep_rate
        - adjoint * inn * conv_vals * keep_rate * keep_rate / scale
    )
    d_rec = (d_log * vec[9:10, :] * rec * (1.0 - rec)).astype(jnp.bfloat16)
    d_in = (drive * conv_vals * inn * (1.0 - inn)).astype(jnp.bfloat16)
    d_gates[:, :width] = d_rec
    d_gates[:, width:] = d_in
    d_conv = drive * inn
    d_conv = d_conv + lax.dot_general(
        d_rec, rec_w[...], CONTRACT_COLS, preferred_element_type=jnp.float32
    )
    d_conv = d_conv + lax.dot_general(
        d_in, in_w[...], CONTRACT_COLS, preferred_element_type=jnp.float32
    )
    x = x_pre[...]
    longer = jnp.concatenate([x_before[...], x], axis=0)

    def column(values):
        return jnp.sum(values, axis=0, keepdims=True)

    d_x = d_conv * vec[2:3, :]
    taps = [column(d_conv * x)]
    for tap in range(1, 4):
        piece = marks[:, tap : tap + 1] * d_conv
        taps.append(column(piece * down_rows(longer, tap)[8:]))
        beyond = jnp.concatenate([piece, edge[8 * tap - 8 : 8 * tap, :]], axis=0)
        d_x = d_x + vec[2 + tap : 3 + tap, :] * up_rows(beyond, tap)[:BLOCK]
        edge[8 * tap - 8 : 8 * tap, :] = piece[:8]
    d_x = d_x.astype(jnp.bfloat16)
    d_pre[:, :width] = d_x
    d_pre[:, width:] = d_y
    pieces = (
        [column(d_x.astype(jnp.float32)), column(d_y.astype(jnp.float32))]
        + taps
        + [
            column(d_conv),
            column(d_rec.astype(jnp.float32)),
            column(d_in.astype(jnp.float32)),
            column(d_log * rec) * vec[10:11, :],
        ]
    )
    for place, piece in enumerate(pieces):
        sums[place : place + 1, :] += piece


def here():
    return (lax.axis_index("dp"), lax.axis_index("row"), lax.axis_index("col"))


def flip(index):
    return index + 1 - 2 * (index % 2)


def across(row):
    return (row + 2) % 4


def greet(peers):
    barrier = pltpu.get_barrier_semaphore()
    for peer in peers:
        pl.semaphore_signal(barrier, inc=1, device_id=peer, device_id_type=MESH)
    pl.semaphore_wait(barrier, len(peers))


class Copies:
    def __init__(self, send, recv):
        self.send, self.recv, self.used, self.sent = (send, recv, 0, [])

    def make(self, source, target, device):
        place = self.used
        self.used += 1
        if device is None:
            copy = pltpu.make_async_copy(source, target, self.recv.at[place])
        else:
            copy = pltpu.make_async_remote_copy(
                src_ref=source,
                dst_ref=target,
                send_sem=self.send.at[place],
                recv_sem=self.recv.at[place],
                device_id=device,
                device_id_type=MESH,
            )
            self.sent.append(copy)
        return copy

    def go(self, source, target, device):
        copy = self.make(source, target, device)
        copy.start()
        return copy

    def finish(self):
        for copy in self.sent:
            copy.wait_send()
        self.sent = []


def arrived(copy):
    copy.wait_recv()


def spread(copies, own, place, halves, between=lambda: None):
    z, r, c = here()
    twin, side, top = ((z, flip(r), c), (z, across(r), c), (z, r, 1 - c))
    to_side = copies.go(own, place(r, c), side)
    to_top = copies.go(own, place(r, c), top)
    to_twin = copies.go(own, place(r, c), twin)
    between()
    arrived(to_side)
    from_side = place(across(r), c)
    on_top = copies.go(halves(from_side, 0), halves(from_side, 0), top)
    late = [to_twin, copies.go(from_side, from_side, twin)]
    between()
    arrived(to_top)
    from_top = place(r, 1 - c)
    on_side = copies.go(halves(from_top, 1), halves(from_top, 1), side)
    late.append(copies.go(from_top, from_top, twin))
    far = place(across(r), 1 - c)
    between()
    for half, copy in enumerate((on_top, on_side)):
        arrived(copy)
        late.append(copies.go(halves(far, half), halves(far, half), twin))
    return late


def part(start, size, step):
    return pl.ds(pl.multiple_of(start * step, step), size)


class Moves:
    def __init__(self, copies, matrices, cuts):
        self.copies = copies
        z, r, c = here()
        self.mine = z % 2
        self.sides = ((z, across(r), c), (z, flip(across(r)), c))
        self.pair = (flip(z), r, c)
        self.locals, self.late, self.flying = ([], [], [])
        self.groups = [(matrix, cut) for matrix in matrices for cut in range(cuts)]
        self.cuts, self.begun = (cuts, 0)
        for source, target, size in matrices:
            self.locals.append(copies.go(source(r), target(r), None))
            self.late.append(copies.go(source(flip(r)), target(r), (z, flip(r), c)))

    def piece(self, ref, size, cut):
        length = size // 2 // self.cuts
        return ref.at[part(self.mine * self.cuts + cut, length, length), :]

    def step(self):
        if len(self.flying) == 2 or self.begun == len(self.groups):
            if self.flying:
                (source, target, size), cut, group = self.flying.pop(0)
                for peer, copy in zip(self.sides, group):
                    arrived(copy)
                    piece = self.piece(target(peer[1]), size, cut)
                    self.late.append(self.copies.go(piece, piece, self.pair))
        if self.begun < len(self.groups):
            (source, target, size), cut = self.groups[self.begun]
            self.begun += 1
            group = [
                self.copies.go(
                    self.piece(source(peer[1]), size, cut),
                    self.piece(target(here()[1]), size, cut),
                    peer,
                )
                for peer in self.sides
            ]
            self.flying.append(((source, target, size), cut, group))

    def finish(self):
        while self.flying:
            self.step()
        for copy in self.late:
            arrived(copy)
        for copy in self.locals:
            copy.wait()


def block_of(ref, rows, columns):
    return lambda row, col: ref.at[part(col, rows, rows), part(row, columns, columns)]


def halves_of(rows):
    return lambda ref, which: ref.at[pl.ds(which * (rows // 2), rows // 2), :]


def mlp_matrices(sources, targets):
    depth, width = (sources[0].shape[0], sources[0].shape[1] // 4)
    return [
        (
            lambda to, source=source: source.at[:, part(to, width, width)],
            lambda of, target=target: target.at[part(of, depth, depth), :],
            depth,
        )
        for source, target in zip(sources, targets)
    ]


def gather_kernel(x_in, s_in, g_in, mix_in, out_in, x_all, s_all, g_all, mix_all, out_all, send, recv):
    z, r, c = here()
    twin, side, cross, top, pair = (
        (z, flip(r), c),
        (z, across(r), c),
        (z, flip(across(r)), c),
        (z, r, 1 - c),
        (flip(z), r, c),
    )
    greet((twin, side, cross, top, pair))
    copies = Copies(send, recv)
    rows, columns = x_in.shape
    depth, rec = (mix_in.shape[1], out_in.shape[0] // 4)
    matrices = [
        (lambda to: mix_in.at[to], lambda of: mix_all.at[part(of, depth, depth), :], depth),
        (
            lambda to: out_in.at[part(to, rec, rec), :],
            lambda of: out_all.at[:, part(of, columns, columns)],
            rec,
        ),
    ]
    small = g_all.at[:, part(r, depth, depth)]
    locals_ = [
        copies.go(x_in, block_of(x_all, rows, columns)(r, c), None),
        copies.go(s_in, s_all.at[r], None),
        copies.go(g_in, small, None),
    ]
    late = []
    for peer in (twin, side, cross):
        late.append(copies.go(s_in, s_all.at[r], peer))
        late.append(copies.go(g_in, small, peer))
    moves = Moves(copies, matrices, 2)
    moves.step()
    late.extend(
        spread(copies, x_in, block_of(x_all, rows, columns), halves_of(rows), moves.step)
    )
    moves.finish()
    for copy in late:
        arrived(copy)
    for copy in locals_:
        copy.wait()
    copies.finish()


def gather(x_in, s_in, g_in, mix_in, out_in):
    rows, columns = x_in.shape
    depth = mix_in.shape[1]

    def shape(*dims, kind=jnp.bfloat16):
        return jax.ShapeDtypeStruct(dims, kind)

    outs = [
        shape(2 * rows, 4 * columns),
        shape(4, *s_in.shape, kind=s_in.dtype),
        shape(g_in.shape[0], 4 * depth, kind=g_in.dtype),
        shape(4 * depth, mix_in.shape[2]),
        shape(out_in.shape[0] // 4, 4 * columns),
    ]
    return pl.pallas_call(
        gather_kernel,
        in_specs=[pl.BlockSpec(memory_space=pl.ANY)] * 5,
        out_specs=[pl.BlockSpec(memory_space=pl.ANY)] * 5,
        out_shape=outs,
        scratch_shapes=[pltpu.SemaphoreType.DMA((48,)), pltpu.SemaphoreType.DMA((48,))],
        compiler_params=pltpu.CompilerParams(collective_id=GATHER_ID, has_side_effects=True),
        name="gather",
    )(x_in, s_in, g_in, mix_in, out_in)


STRIP = 16


def strips(count, body):
    def run(index, nothing):
        body(pl.multiple_of(index * STRIP, STRIP))
        return nothing

    lax.fori_loop(0, count // STRIP, run, 0)


def token_shard(row, col):
    return col * 4 + row


def reduce_shards(copies, parts, twin_in, sums, side_in, top_in, hop_in, between=lambda: None):
    z, r, c = here()
    twin, side, top = ((z, flip(r), c), (z, across(r), c), (z, r, 1 - c))
    size = side_in.shape[0]
    half = size // 2

    def shard(row, col):
        return pl.multiple_of(token_shard(row, col) * size, size)

    spots = [(across(r), 1 - c), (across(r), c), (r, 1 - c), (r, c)]
    from_twin = [
        copies.go(parts.at[pl.ds(shard(flip(row), col), size), :], twin_in.at[place], twin)
        for place, (row, col) in enumerate(spots)
    ]

    def add_twin(place):
        arrived(from_twin[place])
        start = shard(*spots[place])

        def body(at):
            total = parts[pl.ds(start + at, STRIP), :].astype(jnp.float32) + twin_in[
                place, pl.ds(at, STRIP), :
            ].astype(jnp.float32)
            sums[place, pl.ds(at, STRIP), :] = total.astype(jnp.bfloat16)

        strips(size, body)

    def add_hop(place, which, hop):
        def body(at):
            rows = pl.ds(which * half + at, STRIP)
            total = sums[place, rows, :].astype(jnp.float32) + hop_in[
                hop, pl.ds(at, STRIP), :
            ].astype(jnp.float32)
            sums[place, rows, :] = total.astype(jnp.bfloat16)

        strips(half, body)

    def rows_of(ref, which):
        return ref.at[pl.ds(which * half, half), :]

    add_twin(0)
    hop_side = copies.go(rows_of(sums.at[0], 0), hop_in.at[0], side)
    hop_top = copies.go(rows_of(sums.at[0], 1), hop_in.at[1], top)
    add_twin(1)
    waits = [copies.go(rows_of(sums.at[1], 0), rows_of(side_in, 0), side)]
    add_twin(2)
    waits.append(copies.go(rows_of(sums.at[2], 1), rows_of(top_in, 1), top))
    add_twin(3)
    between()
    arrived(hop_top)
    add_hop(1, 1, 1)
    waits.append(copies.go(rows_of(sums.at[1], 1), rows_of(side_in, 1), side))
    arrived(hop_side)
    add_hop(2, 0, 0)
    waits.append(copies.go(rows_of(sums.at[2], 0), rows_of(top_in, 0), top))
    between()
    for copy in waits:
        arrived(copy)

    def total(at):
        rows = pl.ds(at, STRIP)
        return (
            sums[3, rows, :].astype(jnp.float32)
            + side_in[rows, :].astype(jnp.float32)
            + top_in[rows, :].astype(jnp.float32)
        )

    return total


def reduce_scratch(size, width):
    return [
        pltpu.VMEM((4, size, width), jnp.bfloat16),
        pltpu.VMEM((4, size, width), jnp.bfloat16),
        pltpu.VMEM((size, width), jnp.bfloat16),
        pltpu.VMEM((size, width), jnp.bfloat16),
        pltpu.VMEM((2, size // 2, width), jnp.bfloat16),
    ]


def near():
    z, r, c = here()
    return ((z, flip(r), c), (z, across(r), c), (z, r, 1 - c))


def spread_rows(copies, mine, full, between=lambda: None):
    z, r, c = here()
    size = mine.shape[0]
    half = size // 2

    def place(row, col):
        return full.at[pl.ds(pl.multiple_of(token_shard(row, col) * size, size), size), :]

    local = copies.go(mine, place(r, c), None)
    late = spread(
        copies, mine, place, lambda ref, which: ref.at[pl.ds(which * half, half), :], between
    )
    for copy in late:
        arrived(copy)
    local.wait()


def forward_kernel(x_all, masks, vec, rec_w, in_w, mix_w, out_w, gain_mix, gain, c_in, *refs):
    mlp_in, outs, scratch = (refs[:3], refs[3:17], refs[17:])
    full, resid_mid, c_all = outs[:3]
    mlp_all, kept_out = (outs[3:6], outs[6:])
    kept, (tail, carry, parts), (*buffers, mine, kept_sem, send, recv) = (
        scratch[:8],
        scratch[8:11],
        scratch[11:],
    )
    normed, pre, mixed, *saved = kept
    z, r, c = here()
    greet((*near(), (z, flip(across(r)), c), (flip(z), r, c)))
    copies = Copies(send, recv)
    rows, columns = c_in.shape
    moves = Moves(copies, mlp_matrices(mlp_in, mlp_all), 2)
    moves.step()
    moves.step()
    tail[...] = jnp.zeros_like(tail)
    carry[...] = jnp.zeros_like(carry)

    def block(index, nothing):
        start = pl.multiple_of(index * BLOCK, BLOCK)
        rows = pl.ds(start, BLOCK)

        def norm(at):
            strip = pl.ds(start + at, STRIP)
            values = x_all[strip, :].astype(jnp.float32)
            scale = lax.rsqrt(jnp.mean(values * values, axis=1, keepdims=True) + EPS)
            normed[strip, :] = (values * scale * gain_mix[...]).astype(jnp.bfloat16)

        strips(BLOCK, norm)
        pre[rows, :] = jnp.dot(normed[rows, :], mix_w[...], preferred_element_type=jnp.float32)
        mixer_forward_step(
            pre.at[rows, :],
            masks[rows, :],
            vec,
            rec_w,
            in_w,
            mixed.at[rows, :],
            *[ref.at[rows, :] for ref in saved],
            tail,
            carry,
        )
        width = rec_w.shape[0]
        parts[rows, :] = jnp.dot(
            mixed[rows, :width], out_w[...], preferred_element_type=jnp.float32
        ).astype(jnp.bfloat16)
        return nothing

    lax.fori_loop(0, 3, block, 0)
    moves.step()
    lax.fori_loop(3, 6, block, 0)
    moves.step()
    lax.fori_loop(6, x_all.shape[0] // BLOCK, block, 0)
    keeping = [
        pltpu.make_async_copy(source, target, kept_sem.at[place])
        for place, (source, target) in enumerate(zip(kept, kept_out))
    ]
    for copy in keeping:
        copy.start()
    total = reduce_shards(copies, parts, *buffers, between=moves.step)
    size = mine.shape[0]
    start = pl.multiple_of(token_shard(r, c) * size, size)

    def body(at):
        rows = pl.ds(at, STRIP)
        values = x_all[pl.ds(start + at, STRIP), :].astype(jnp.float32) + total(at)
        resid_mid[rows, :] = values
        scale = lax.rsqrt(jnp.mean(values * values, axis=1, keepdims=True) + EPS)
        mine[rows, :] = (values * scale * gain[...]).astype(jnp.bfloat16)

    strips(size, body)
    spread_rows(copies, mine, full, moves.step)
    local = copies.go(c_in, block_of(c_all, rows, columns)(r, c), None)
    late = spread(copies, c_in, block_of(c_all, rows, columns), halves_of(rows), moves.step)
    for copy in late:
        arrived(copy)
    local.wait()
    moves.finish()
    for copy in keeping:
        copy.wait()
    copies.finish()


def norm_pull(values, gain, incoming):
    scale = lax.rsqrt(jnp.mean(values * values, axis=1, keepdims=True) + EPS)
    scaled = gain * incoming
    dots = jnp.sum(scaled * values, axis=1, keepdims=True)
    grad = scale * scaled - values * (scale * scale * scale * dots / values.shape[1])
    return (grad, jnp.sum(incoming * values * scale, axis=0, keepdims=True))


def vmem_call(kernel, name, place, arrays, outs, spaces, scratch, count, loose=()):
    return pl.pallas_call(
        kernel,
        in_specs=[pl.BlockSpec(memory_space=pltpu.VMEM)] * len(arrays)
        + [pl.BlockSpec(memory_space=pl.ANY)] * len(loose),
        out_specs=[pl.BlockSpec(memory_space=space) for space in spaces],
        out_shape=outs,
        scratch_shapes=scratch
        + [pltpu.SemaphoreType.DMA((count,)), pltpu.SemaphoreType.DMA((count,))],
        compiler_params=pltpu.CompilerParams(
            collective_id=place, has_side_effects=True, vmem_limit_bytes=VMEM_BYTES
        ),
        name=name,
    )(*arrays, *loose)


AHEAD = 3
DEPTH = 4
HAND_LAG = 4
LAG = 6


def run_loop(first, last, body):
    def run(index, nothing):
        body(index)
        return nothing

    lax.fori_loop(first, last, run, 0)


def remote(source, target, sender, receiver, device):
    return pltpu.make_async_remote_copy(
        src_ref=source,
        dst_ref=target,
        send_sem=sender,
        recv_sem=receiver,
        device_id=device,
        device_id_type=MESH,
    )


class Line:
    def __init__(self, sources, own, left, right, out, sems, lead):
        self.own, self.left, self.right, self.out, self.lead = (own, left, right, out, lead)
        (
            self.load_sem,
            self.end_send,
            self.low_recv,
            self.high_recv,
            self.out_recv,
            self.mid_send,
            self.first_send,
            self.last_send,
            self.hand_send,
            self.on_send,
        ) = sems
        z, r, c = here()
        self.chunk = left.shape[1]
        self.rows = out.shape[1]
        self.half = self.rows // 2
        self.per = self.half // self.chunk
        self.chunks = 4 * self.per + lead
        self.total = self.chunks + LAG
        self.at = 0
        self.ahead = 0
        self.is_end = (z == 0) | (z == 3)
        self.near_z = (jnp.where(z == 0, 1, 2), r, c)
        self.outer = (jnp.where(z == 1, 0, 3), r, c)
        self.other = (3 - z, r, c)
        self.loads = []
        start = 0
        for place, source in enumerate(sources):
            width = source.shape[1]
            self.loads.append(
                pltpu.make_async_copy(
                    source,
                    own.at[pl.ds(0, 4 * self.rows), pl.ds(start, width)],
                    self.load_sem.at[place],
                )
            )
            start += width

    def spot(self, index):
        step = (index - self.lead + self.per) // self.per - 1
        strip = (index - self.lead + self.per) % self.per
        if self.lead:
            strip = strip - jnp.where(step < 0, self.per - self.lead, 0)
        return (step, strip)

    def peer_row(self, index):
        r = here()[1]
        step = jnp.maximum(self.spot(index)[0], 0)
        return (r // 2 + step // 2) % 2 * 2 + (r % 2 + step % 2) % 2

    def stays(self, index):
        return self.spot(index)[0] <= 0

    def span(self, index, which):
        step, strip = self.spot(index)
        start = self.peer_row(index) * self.rows + which * self.half
        if self.lead:
            start = jnp.where(
                step < 0, 4 * self.rows + which * self.lead * self.chunk, start
            )
        return pl.ds(pl.multiple_of(start + strip * self.chunk, self.chunk), self.chunk)

    def own_at(self, index, which):
        return self.own.at[self.span(index, which), :]

    def out_at(self, index, which, row):
        step, strip = self.spot(index)
        if self.lead:
            row = jnp.where(step < 0, 4, row)
        start = pl.multiple_of(which * self.half + strip * self.chunk, self.chunk)
        return self.out.at[row, pl.ds(start, self.chunk), :]

    def end_sends(self, index):
        low = here()[0] // 3
        return (
            remote(
                self.own_at(index, low),
                self.left.at[index],
                self.end_send.at[0, index],
                self.low_recv.at[index],
                self.near_z,
            ),
            remote(
                self.own_at(index, 1 - low),
                self.right.at[1, index],
                self.end_send.at[1, index],
                self.high_recv.at[1, index],
                self.near_z,
            ),
        )

    def to_other(self, index):
        low = here()[0] - 1
        return remote(
            self.own_at(index, 1 - low),
            self.right.at[0, index],
            self.mid_send.at[index],
            self.high_recv.at[0, index],
            self.other,
        )

    def from_outer(self, index):
        low = here()[0] - 1
        return (
            remote(
                self.own_at(index, low),
                self.left.at[index],
                self.mid_send.at[index],
                self.low_recv.at[index],
                self.outer,
            ),
            remote(
                self.own_at(index, 1 - low),
                self.right.at[1, index],
                self.mid_send.at[index],
                self.high_recv.at[1, index],
                self.outer,
            ),
        )

    def hand(self, index):
        z, r, c = here()
        low = z - 1
        mine, spot = (self.own_at(index, low), self.out_at(index, low, r))
        return (
            pltpu.make_async_copy(mine, spot, self.out_recv.at[low, index]),
            remote(
                mine,
                spot,
                self.hand_send.at[index],
                self.out_recv.at[low, index],
                (z, self.peer_row(index), c),
            ),
        )

    def along(self, index):
        low = here()[0] - 1
        spot = self.out_at(index, low, self.peer_row(index))
        return (
            remote(
                spot, spot, self.first_send.at[index], self.out_recv.at[low, index], self.outer
            ),
            remote(spot, spot, self.last_send.at[index], self.out_recv.at[low, index], self.other),
        )

    def onward(self, index):
        low = here()[0] - 1
        spot = self.out_at(index, 1 - low, self.peer_row(index))
        return remote(
            spot, spot, self.on_send.at[index], self.out_recv.at[1 - low, index], self.outer
        )

    def end_step(self, index):
        @pl.when(index < self.chunks)
        def _():
            @pl.when(index >= DEPTH)
            def _():
                for copy in self.end_sends(index - DEPTH):
                    copy.wait_send()

            for copy in self.end_sends(index):
                copy.start()

    def mid_step(self, index):
        own, left, right, low = (self.own, self.left, self.right, here()[0] - 1)

        @pl.when(index < self.chunks)
        def _():
            self.from_outer(index)[1].wait_recv()
            span = self.span(index, 1 - low)
            total = own[span, :].astype(jnp.float32) + right[1, index].astype(jnp.float32)
            own[span, :] = total.astype(jnp.bfloat16)
            self.to_other(index).start()

        @pl.when((index >= 2) & (index < self.chunks + 2))
        def _():
            back = index - 2
            self.from_outer(back)[0].wait_recv()
            self.to_other(back).wait_recv()
            span = self.span(back, low)
            total = (
                own[span, :].astype(jnp.float32)
                + left[back].astype(jnp.float32)
                + right[0, back].astype(jnp.float32)
            )
            own[span, :] = total.astype(jnp.bfloat16)

            @pl.when(self.stays(back))
            def _():
                self.hand(back)[0].start()

            @pl.when(jnp.logical_not(self.stays(back)))
            def _():
                self.hand(back)[1].start()

        @pl.when((index >= HAND_LAG) & (index < self.chunks + HAND_LAG))
        def _():
            back = index - HAND_LAG

            @pl.when(self.stays(back))
            def _():
                self.hand(back)[0].wait()

            @pl.when(jnp.logical_not(self.stays(back)))
            def _():
                self.hand(back)[1].wait_recv()

            for copy in self.along(back):
                copy.start()

        @pl.when(index >= LAG)
        def _():
            copy = self.onward(index - LAG)
            copy.wait_recv()
            copy.start()

    def begin(self):
        for copy in self.loads:
            copy.start()

    def ready(self):
        for copy in self.loads:
            copy.wait()

    def advance(self, count):
        first, last = (self.at, min(self.at + count, self.total))
        self.at = last
        if first == last:
            return

        @pl.when(self.is_end)
        def _():
            run_loop(self.ahead, last + AHEAD, self.end_step)

        self.ahead = last + AHEAD

        @pl.when(jnp.logical_not(self.is_end))
        def _():
            run_loop(first, last, self.mid_step)

    def one(self, index):
        @pl.when(self.is_end)
        def _():
            self.end_step(index + AHEAD)

        @pl.when(jnp.logical_not(self.is_end))
        def _():
            self.mid_step(index)

    def skip(self, count):
        self.at += count
        self.ahead += count

    def end_done(self, index):
        @pl.when(index >= self.chunks - DEPTH)
        def _():
            for copy in self.end_sends(index):
                copy.wait_send()

        for which in (0, 1):
            spot = self.out_at(index, which, self.peer_row(index))
            remote(
                spot, spot, self.end_send.at[0, index], self.out_recv.at[which, index], self.near_z
            ).wait_recv()

    def mid_done(self, index):
        self.to_other(index).wait_send()

        @pl.when(jnp.logical_not(self.stays(index)))
        def _():
            self.hand(index)[1].wait_send()

        for copy in self.along(index):
            copy.wait_send()
        self.onward(index).wait_send()

    def settle(self, first, last):
        @pl.when(self.is_end)
        def _():
            run_loop(first, last, self.end_done)

        @pl.when(jnp.logical_not(self.is_end))
        def _():
            run_loop(first, last, self.mid_done)

    def finish(self, first):
        self.advance(self.total)
        self.settle(first, self.chunks)


def line_scratch(count, rows, width, chunk, lead):
    dma = pltpu.SemaphoreType.DMA
    chunks = 4 * (rows // 2 // chunk) + lead
    return [
        pltpu.VMEM((4 * rows + 2 * lead * chunk, width), jnp.bfloat16),
        pltpu.VMEM((chunks, chunk, width), jnp.bfloat16),
        pltpu.VMEM((2, chunks, chunk, width), jnp.bfloat16),
        dma((count,)),
        dma((2, chunks)),
        dma((chunks,)),
        dma((2, chunks)),
        dma((2, chunks)),
        dma((chunks,)),
        dma((chunks,)),
        dma((chunks,)),
        dma((chunks,)),
        dma((chunks,)),
    ]


LINE_REFS = 13
PACK = 32
BACK_CHUNK = 32
LAST_CHUNK = 16


def z_peers():
    z, r, c = here()
    return [((z + step) % 4, r, c) for step in (1, 2, 3)]


def plane_peers():
    z, r, c = here()
    return [(z, (r + turn % 4) % 4, (c + turn // 4) % 2) for turn in range(1, 8)]


def hand_out(copies, source, target):
    z, r, c = here()
    twin, side, _ = near()
    cross = (z, flip(across(r)), c)
    columns = target.shape[1]
    size = source.shape[0]

    def piece(row):
        return source.at[:, part(row, columns, columns)]

    spot = target.at[part(r, size, size), :]
    waits = [copies.go(piece(peer[1]), spot, peer) for peer in (side, cross, twin)]
    local = copies.go(piece(r), spot, None)

    def done():
        for copy in waits:
            arrived(copy)
        local.wait()

    return done


def backward_kernel(resid_mid, gain, gain_mix, masks, vec, rec_w, in_w, mix_w, out_w, *refs):
    parts_in, c_all, x_all, *kept_in = refs[:9]
    sources, outs, scratch = (refs[9:11], refs[11:19], refs[19:])
    branch_out, d_pre_out, d_gates_out, grad, grads, sums, gain_grad, gain_mix_grad = outs
    line_refs, scratch = (scratch[:LINE_REFS], scratch[LINE_REFS:])
    parts, cot, resid, branch, d_resid, d_pre, d_gates, edge, carry = scratch[:9]
    kept, scratch = (scratch[9:15], scratch[15:])
    *buffers, mine, load_sem, send, recv = scratch
    pre, x_pre, conv, rec_gate, in_gate, states = kept
    z, r, c = here()
    greet([*near(), (z, flip(across(r)), c), *z_peers()])
    copies = Copies(send, recv)
    size = mine.shape[0]
    shard = part(token_shard(r, c), size, size)
    loads = [
        pltpu.make_async_copy(source, target, load_sem.at[place])
        for place, (source, target) in enumerate(
            zip(
                [parts_in, c_all.at[shard, :], x_all.at[shard, :], *kept_in],
                [parts, cot, resid, *kept],
            )
        )
    ]
    loads[0].start()
    line = Line(sources, *line_refs[:3], grads, line_refs[3:], 0)
    line.begin()
    for copy in loads[1:]:
        copy.start()
    gain_grad[...] = jnp.zeros_like(gain_grad)
    gain_mix_grad[...] = jnp.zeros_like(gain_mix_grad)
    sums[...] = jnp.zeros_like(sums)
    edge[...] = jnp.zeros_like(edge)
    carry[...] = jnp.zeros_like(carry)
    loads[0].wait()
    line.ready()
    pace = iter((4, 4, 4, 2, 2, 2, 4))

    def between():
        line.advance(next(pace))

    total = reduce_shards(copies, parts, *buffers, between=between)
    for copy in loads[1:]:
        copy.wait()

    def body(at):
        rows = pl.ds(at, STRIP)
        values, piece = norm_pull(resid_mid[rows, :], gain[...], total(at))
        values = values + cot[rows, :].astype(jnp.float32)
        gain_grad[...] += piece
        d_resid[rows, :] = values
        mine[rows, :] = values.astype(jnp.bfloat16)

    strips(size, body)
    spread_rows(copies, mine, branch, between)
    copies.finish()
    last = branch.shape[0] // BLOCK - 1
    width = x_pre.shape[1]

    def block(index, base):
        start = pl.multiple_of((last - index) * BLOCK, BLOCK)
        rows = pl.ds(start, BLOCK)
        before = pl.ds(pl.multiple_of(jnp.maximum(start - 8, 0), 8), 8)
        mixer_backward_step(
            lax.dot_general(
                branch[rows, :], out_w[...], CONTRACT_COLS, preferred_element_type=jnp.float32
            ),
            pre.at[rows, :],
            masks[rows, :],
            vec,
            rec_w,
            in_w,
            x_pre.at[rows, :],
            x_pre.at[before, :],
            conv.at[rows, :],
            rec_gate.at[rows, :],
            in_gate.at[rows, :],
            states.at[rows, :],
            states.at[before, :],
            d_pre.at[rows, :],
            d_gates.at[rows, :],
            sums,
            edge,
            carry,
        )
        parts[rows, :] = lax.dot_general(
            d_pre[rows, :], mix_w[...], CONTRACT_COLS, preferred_element_type=jnp.float32
        ).astype(jnp.bfloat16)

        line.one(base + index)
        return base

    lax.fori_loop(0, last + 1, block, line.at)
    line.skip(last + 1)
    keeping = [
        pltpu.make_async_copy(source, target, load_sem.at[place])
        for place, (source, target) in enumerate(
            ((branch, branch_out), (d_pre, d_pre_out), (d_gates, d_gates_out))
        )
    ]
    for copy in keeping:
        copy.start()
    total_back = reduce_shards(copies, parts, *buffers, between=between)

    def body_back(at):
        rows = pl.ds(at, STRIP)
        values, piece = norm_pull(
            resid[rows, :].astype(jnp.float32), gain_mix[...], total_back(at)
        )
        gain_mix_grad[...] += piece
        mine[rows, :] = (d_resid[rows, :] + values).astype(jnp.bfloat16)

    strips(size, body_back)
    done = hand_out(copies, mine, grad)
    line.finish(0)
    done()
    for copy in keeping:
        copy.wait()
    copies.finish()


def gate_tiles(width):
    tiles = []
    for tile in range(5):
        first, rest = (0, width)
        if tile < 4:
            tiles.append((tile, 0, width, tile // 2, tile % 2 * width))
        else:
            tiles.append((tile, 0, 512, 0, 2 * width))
            tiles.append((tile, 512, width - 512, 1, 2 * width))
    return tiles


def reduce_kernel(count, resid_mid, vec, gain, *refs):
    parts_in, gates, sources = (refs[0], refs[1], refs[2 : 2 + count])
    out, out_gates, output, out_vec, out_gain = refs[2 + count : 7 + count]
    scratch = refs[7 + count :]
    line_refs, scratch = (scratch[:LINE_REFS], scratch[LINE_REFS:])
    vec_z, gain_z, vec_sum, gain_sum, vec_in, gain_in, parts = scratch[:7]
    *buffers, mine, gate_sem, small_send, small_recv, send, recv = scratch[7:]
    z, r, c = here()
    twin, side, top = near()
    cross = (z, flip(across(r)), c)
    lines, plane = (z_peers(), plane_peers())
    greet(lines + plane)
    copies = Copies(send, recv)
    load = pltpu.make_async_copy(parts_in, parts, gate_sem.at[8])
    load.start()
    line = Line(sources, *line_refs[:3], out, line_refs[3:], PACK // LAST_CHUNK)
    half = line.half
    packed = []
    for place, (tile, first, width, which, spot) in enumerate(gate_tiles(gates.shape[1])):
        copy = pltpu.make_async_copy(
            gates.at[pl.ds(tile * PACK, PACK), pl.ds(first, width)],
            line.own.at[pl.ds(8 * half + which * PACK, PACK), pl.ds(spot, width)],
            gate_sem.at[place],
        )
        copy.start()
        packed.append(copy)
    small = [
        [
            remote(
                source,
                target.at[3 - step],
                small_send.at[kind, step - 1],
                small_recv.at[kind, 3 - step],
                lines[step - 1],
            )
            for step in (1, 2, 3)
        ]
        for kind, (source, target) in enumerate(((vec, vec_z), (gain, gain_z)))
    ]
    for kind in small:
        for copy in kind:
            copy.start()
    line.begin()
    for copy in packed:
        copy.wait()
    line.ready()
    spread_out = [
        [
            remote(
                source,
                target.at[6 - step],
                small_send.at[kind, 3 + step],
                small_recv.at[kind, 3 + 6 - step],
                peer,
            )
            for step, peer in enumerate(plane)
        ]
        for kind, (source, target) in enumerate(((vec_sum, vec_in), (gain_sum, gain_in)))
    ]
    gate_moves = [
        remote(
            out.at[4, pl.ds(which * half, PACK), :],
            out_gates.at[r, which],
            small_send.at[0, 10 + 2 * place + which],
            small_recv.at[0, 10 + 2 * place + which],
            peer,
        )
        for place, peer in enumerate((twin, side, cross))
        for which in (0, 1)
    ]
    gate_local = [
        pltpu.make_async_copy(
            out.at[4, pl.ds(which * half, PACK), :], out_gates.at[r, which], gate_sem.at[which]
        )
        for which in (0, 1)
    ]
    load.wait()
    pace = iter((4, 6))
    total = reduce_shards(
        copies, parts, *buffers, between=lambda: line.advance(next(pace))
    )
    size = mine.shape[0]

    def body(at):
        rows = pl.ds(at, STRIP)
        mine[rows, :] = (resid_mid[rows, :] + total(at)).astype(jnp.bfloat16)

    strips(size, body)
    done = hand_out(copies, mine, output)
    line.advance(6)
    for kind in small:
        for copy in kind:
            copy.wait_recv()
    vec_sum[...] = vec[...] + vec_z[0] + vec_z[1] + vec_z[2]
    gain_sum[...] = gain[...] + gain_z[0] + gain_z[1] + gain_z[2]
    for kind in spread_out:
        for copy in kind:
            copy.start()
    line.advance(16)
    line.settle(0, line.lead)
    for copy in gate_moves + gate_local:
        copy.start()
    line.finish(line.lead)
    done()
    for kind in spread_out:
        for copy in kind:
            copy.wait_recv()
    gains = gain_sum[...]
    for place in range(7):
        gains = gains + gain_in[place]
    out_gain[...] = gains
    out_vec[r] = vec_sum[...]
    for step in (0, 1, 2):
        out_vec[(r + 3 - step) % 4] = vec_in[6 - step]
    for copy in gate_moves:
        copy.wait_recv()
    for copy in gate_local:
        copy.wait()
    for group in small + spread_out + [gate_moves]:
        for copy in group:
            copy.wait_send()
    copies.finish()


def dot(left, right, dims, kind=jnp.float32):
    return lax.dot_general(left, right, dims, preferred_element_type=jnp.float32).astype(kind)


def local_plane(
    inputs,
    cotangent,
    starts,
    x_proj,
    y_proj,
    out_proj,
    gate_proj,
    up_proj,
    down_proj,
    mix_gain,
    mlp_gain,
    x_bias,
    y_bias,
    conv_w,
    conv_b,
    rec_gate_w,
    in_gate_w,
    rec_gate_b,
    in_gate_b,
    decay_param,
):
    z, r, c = here()
    depth = x_proj.shape[0]
    rec = x_proj.shape[1] // 4
    width = gate_proj.shape[1] // 4
    heads, head = (rec_gate_w.shape[0] // 4, rec_gate_w.shape[1])
    padded = (rec + 127) // 128 * 128
    low = jnp.bfloat16

    def mine(array, size, axis=0):
        return lax.dynamic_slice_in_dim(array, r * size, size, axis)

    mix_in = jnp.concatenate(
        [x_proj.reshape(depth, 4, rec), y_proj.reshape(depth, 4, rec)], axis=2
    ).transpose(1, 0, 2)
    flags = jnp.pad(starts.astype(jnp.float32).reshape(-1, 128), ((0, 6), (0, 0)))
    x_all, s_all, g_all, mix_w, out_w = gather(
        inputs.T, flags, jnp.stack([mix_gain, mlp_gain]), mix_in, out_proj
    )
    tokens, model = x_all.shape
    gain_mix, gain_mlp = (g_all[0:1], g_all[1:2])
    fresh = s_all[:, :2, :].reshape(tokens)
    stale = 1.0 - fresh
    stale_one = jnp.concatenate([jnp.zeros((1,), jnp.float32), stale[:-1]])
    stale_two = jnp.concatenate([jnp.zeros((2,), jnp.float32), stale[:-2]])
    nothing = jnp.zeros_like(fresh)
    masks = jnp.stack(
        [fresh, stale, stale * stale_one, stale * stale_one * stale_two] + [nothing] * 4, axis=1
    )
    vectors = jnp.concatenate(
        [
            x_bias[None],
            y_bias[None],
            conv_w,
            conv_b[None],
            rec_gate_b[None],
            in_gate_b[None],
            -GATE_C * jax.nn.softplus(decay_param)[None],
            -GATE_C * jax.nn.sigmoid(decay_param)[None],
            jnp.zeros((5, x_bias.shape[0]), jnp.float32),
        ],
        axis=0,
    )
    vec = mine(vectors, rec, 1)

    def diagonal(blocks):
        blocks = mine(blocks, heads)
        rows = [jnp.pad(blocks[i], ((0, 0), (i * head, rec - (i + 1) * head))) for i in range(heads)]
        return jnp.concatenate(rows, axis=0)

    rec_w, in_w = (diagonal(rec_gate_w), diagonal(in_gate_w))
    size = tokens // 8
    full = jax.ShapeDtypeStruct((tokens, model), low)
    part = jax.ShapeDtypeStruct((size, model), jnp.float32)
    line = jax.ShapeDtypeStruct((1, model), jnp.float32)
    piece = pltpu.VMEM((size, model), low)
    block = jax.ShapeDtypeStruct((inputs.shape[1], inputs.shape[0]), low)
    weights = (gate_proj, up_proj, down_proj)
    slices = jax.ShapeDtypeStruct((4 * depth, width), low)
    kept = [((tokens, model), low), ((tokens, 2 * rec), jnp.float32), ((tokens, padded), low)]
    kept += [((tokens, rec), kind) for kind in (jnp.float32, low) + (jnp.float32,) * 3]
    row8 = pltpu.VMEM((8, rec), jnp.float32)
    (
        normed_mlp,
        resid_mid,
        c_all,
        gate_w,
        up_w,
        down_w,
        normed_mix,
        pre,
        mixed,
        x_pre,
        conv,
        rec_gate,
        in_gate,
        states,
    ) = vmem_call(
        forward_kernel,
        "forward",
        FORWARD_ID,
        (x_all, masks, vec, rec_w, in_w, mix_w, out_w, gain_mix, gain_mlp),
        [full, part, full] + [slices] * 3 + [jax.ShapeDtypeStruct(*item) for item in kept],
        [pl.ANY, pltpu.VMEM] + [pl.ANY] * 12,
        [pltpu.VMEM(*item) for item in kept]
        + [row8, row8, pltpu.VMEM((tokens, model), low)]
        + reduce_scratch(size, model)
        + [piece, pltpu.SemaphoreType.DMA((8,))],
        80,
        (cotangent.T, *weights),
    )
    gate = dot(normed_mlp, gate_w, CONTRACT_PLAIN)
    up = dot(normed_mlp, up_w, CONTRACT_PLAIN)
    d_activ = dot(c_all, down_w, CONTRACT_PLAIN)
    gelu, slope = gelu_both(gate)
    activ = (gelu * up).astype(low)
    d_gate = (d_activ * up * slope).astype(low)
    d_up = (d_activ * gelu).astype(low)
    d_normed = lax.dot_general(
        d_gate, gate_w, CONTRACT_COLS, preferred_element_type=jnp.float32
    ) + lax.dot_general(d_up, up_w, CONTRACT_COLS, preferred_element_type=jnp.float32)
    def kind_of(array):
        return pltpu.VMEM(array.shape, array.dtype)

    def like(array):
        return jax.ShapeDtypeStruct(array.shape, array.dtype)

    both = jax.ShapeDtypeStruct((tokens, 2 * rec), low)
    held = (pre, x_pre, conv, rec_gate, in_gate, states)
    d_branch, d_pre, d_gates, grad_in, grads_mlp, sums, grad_mlp_gain, grad_mix_gain = vmem_call(
        backward_kernel,
        "backward",
        BACKWARD_ID,
        (resid_mid, gain_mlp, gain_mix, masks, vec, rec_w, in_w, mix_w, out_w),
        [
            full,
            both,
            both,
            block,
            jax.ShapeDtypeStruct((4, depth, 2 * width), low),
            jax.ShapeDtypeStruct((16, rec), jnp.float32),
            line,
            line,
        ],
        [pl.ANY] * 5 + [pltpu.VMEM] * 3,
        line_scratch(2, depth, 2 * width, BACK_CHUNK, 0)
        + [
            kind_of(full),
            piece,
            piece,
            kind_of(full),
            kind_of(part),
            kind_of(both),
            kind_of(both),
            pltpu.VMEM((24, rec), jnp.float32),
            row8,
        ]
        + [kind_of(item) for item in held]
        + reduce_scratch(size, model)
        + [piece, pltpu.SemaphoreType.DMA((9,))],
        60,
        (
            d_normed.astype(low),
            c_all,
            x_all,
            *held,
            dot(normed_mlp, d_gate, CONTRACT_ROWS, low),
            dot(normed_mlp, d_up, CONTRACT_ROWS, low),
        ),
    )
    gate_grads = dot(conv, d_gates, CONTRACT_ROWS, low)
    gates = jnp.concatenate(
        [
            gate_grads[i * head : (i + 1) * head, first + i * head : first + (i + 1) * head]
            for first in (0, rec)
            for i in range(heads)
        ],
        axis=1,
    )
    gain_grads = jnp.concatenate([grad_mix_gain, grad_mlp_gain], axis=0)
    final_width = width + 2 * rec + padded
    dma = pltpu.SemaphoreType.DMA
    grads, gates, output, vec_sums, gains = vmem_call(
        functools.partial(reduce_kernel, 3),
        "reduce_grads",
        REDUCE_ID,
        (resid_mid, sums, gain_grads),
        [
            jax.ShapeDtypeStruct((5, depth, final_width), low),
            jax.ShapeDtypeStruct((4, 2, PACK, final_width), low),
            block,
            jax.ShapeDtypeStruct((4, *sums.shape), jnp.float32),
            like(gain_grads),
        ],
        [pl.ANY] * 3 + [pltpu.VMEM] * 2,
        line_scratch(3, depth, final_width, LAST_CHUNK, PACK // LAST_CHUNK)
        + [
            pltpu.VMEM((3, *sums.shape), jnp.float32),
            pltpu.VMEM((3, *gain_grads.shape), jnp.float32),
            kind_of(sums),
            kind_of(gain_grads),
            pltpu.VMEM((7, *sums.shape), jnp.float32),
            pltpu.VMEM((7, *gain_grads.shape), jnp.float32),
            kind_of(full),
        ]
        + reduce_scratch(size, model)
        + [piece, dma((9,)), dma((2, 16)), dma((2, 16))],
        40,
        (
            dot(activ, down_w, CONTRACT_COLS, low),
            gates,
            dot(c_all, activ, CONTRACT_ROWS, low),
            dot(normed_mix, d_pre, CONTRACT_ROWS, low),
            dot(d_branch, mixed, CONTRACT_ROWS, low),
        ),
    )
    tiles = [[], [], [], [], []]
    for tile, first, length, which, spot in gate_tiles(2 * heads * head):
        tiles[tile].append(gates[:, which, :, spot : spot + length])
    gates = jnp.concatenate([jnp.concatenate(item, axis=2) for item in tiles], axis=1)
    gates = gates.reshape(4, head, 2, heads, head).transpose(2, 0, 3, 1, 4)
    gates = gates.reshape(2, 4 * heads, head, head).astype(jnp.float32)
    vec_sums = vec_sums.transpose(1, 0, 2).reshape(vec_sums.shape[1], 4 * rec)
    gains = lax.dynamic_slice_in_dim(gains, r * depth, depth, 1)

    def columns(array, first, length):
        return jnp.concatenate(
            [array[i, :, first : first + length] for i in range(4)], axis=1
        ).astype(jnp.float32)

    after = width
    grad_out = jnp.concatenate(
        [grads[i, :, after + 2 * rec : after + 3 * rec].T for i in range(4)], axis=0
    ).astype(jnp.float32)
    return (
        output.T,
        grad_in.astype(jnp.float32).T,
        columns(grads, after, rec),
        columns(grads, after + rec, rec),
        grad_out,
        columns(grads_mlp, 0, width),
        columns(grads_mlp, width, width),
        columns(grads, 0, width),
        gains[0],
        gains[1],
        vec_sums[0],
        vec_sums[1],
        vec_sums[2:6],
        vec_sums[6],
        gates[0],
        gates[1],
        vec_sums[7],
        vec_sums[8],
        vec_sums[9],
    )


def fits(mesh):
    return mesh.shape["dp"] == 4 and mesh.shape["row"] == 4 and mesh.shape["col"] == 2


def solution(mesh):
    placed = (
        P("row", ("dp", "col")),
        P("row", ("dp", "col")),
        P(("dp", "row")),
        P("row", "col"),
        P("row", "col"),
        P("col", "row"),
        P("row", "col"),
        P("row", "col"),
        P("row", "col"),
        P("row"),
        P("row"),
        P("col"),
        P("col"),
        P(None, "col"),
        P("col"),
        P("col", None, None),
        P("col", None, None),
        P("col"),
        P("col"),
        P("col"),
    )
    return jax.shard_map(
        local_plane if fits(mesh) else local,
        mesh=mesh,
        in_specs=placed,
        out_specs=(
            P("row", ("dp", "col")),
            P("row", ("dp", "col")),
            P("row", "col"),
            P("row", "col"),
            P("col", "row"),
            P("row", "col"),
            P("row", "col"),
            P("row", "col"),
            P("row"),
            P("row"),
            P("col"),
            P("col"),
            P(None, "col"),
            P("col"),
            P("col", None, None),
            P("col", None, None),
            P("col"),
            P("col"),
            P("col"),
        ),
        check_vma=False,
    )
```

```python
import functools

import jax
import jax.numpy as jnp
from jax import lax
from jax.experimental import pallas as pl
from jax.experimental.pallas import tpu as pltpu
from jax.sharding import PartitionSpec as P

MESH = pl.DeviceIdType.MESH

D = 2048


EPS = 1e-06
GATE_C = 8.0
CONTRACT_ROWS = (((0,), (0,)), ((), ()))
CONTRACT_COLS = (((1,), (1,)), ((), ()))
CONTRACT_PLAIN = (((1,), (0,)), ((), ()))


def from_behind(value, axis, by):
    count = lax.axis_size(axis)
    pairs = [(i, i + by) for i in range(count) if 0 <= i + by < count]
    return lax.ppermute(value, axis, pairs)


def carried_in(value, axis, join, neutral, backward):
    count, mine = (lax.axis_size(axis), lax.axis_index(axis))
    pieces = jax.tree.map(lambda part: lax.all_gather(part, axis), value)
    if backward:
        pieces = jax.tree.map(lambda part: part[::-1], pieces)
        mine = count - 1 - mine
    subtotal = jax.tree.map(
        lambda part, zero: jnp.full_like(part, 0) + jnp.asarray(zero, part.dtype), value, neutral
    )

    def hop(position, subtotal):
        longer = join(subtotal, jax.tree.map(lambda part: part[position], pieces))
        return jax.tree.map(lambda new, old: jnp.where(position < mine, new, old), longer, subtotal)

    return lax.fori_loop(0, count - 1, hop, subtotal)


def chain(earlier, later):
    return (earlier[0] * later[0], later[0] * earlier[1] + later[1])


def adjoint_chain(earlier, later):
    return (later[0] * earlier[0], later[1] + later[0] * earlier[1])


def gelu_tanh(values):
    return jax.nn.gelu(values, approximate=True)


def glu_piece(gate_vals, up_vals):
    return gelu_tanh(gate_vals) * up_vals


def causal_conv(values, conv_w, conv_b, segment_ids):
    result = values * conv_w[0] + conv_b
    for offset in range(1, conv_w.shape[0]):
        lagged = jnp.pad(values, ((offset, 0), (0, 0)))[:-offset]
        earlier_ids = jnp.pad(segment_ids, (offset, 0), constant_values=-1)[:-offset]
        result = (
            result + jnp.where((earlier_ids == segment_ids)[:, None], lagged, 0.0) * conv_w[offset]
        )
    return result


def local_recurrence(rec_pre, in_pre, conv_vals, decay_param, flags):
    rec_gate = jax.nn.sigmoid(rec_pre)
    in_gate = jax.nn.sigmoid(in_pre)
    log_keep = -GATE_C * rec_gate * jax.nn.softplus(decay_param)
    keep_rate = jnp.exp(log_keep)
    fresh = (flags == 1)[:, None]
    multiplier = jnp.where(fresh, 1.0, jnp.sqrt(-jnp.expm1(2.0 * log_keep)))
    driven = conv_vals * in_gate * multiplier
    carried = jnp.where(fresh, 0.0, keep_rate)
    cum_keep, states = lax.associative_scan(chain, (carried, driven), axis=0)
    return (cum_keep, states)


def row_sums(values):
    return lax.psum(values, "row")


def norm_forward(values, norm_gain):
    squares = row_sums(jnp.sum(values * values, axis=1))
    inv_rms = lax.rsqrt(squares / D + EPS)
    return (values * inv_rms[:, None] * norm_gain, inv_rms)


def norm_backward(values, inv_rms, norm_gain, incoming):
    scaled = norm_gain * incoming
    dots = row_sums(jnp.sum(scaled * values, axis=1))
    values_grad = inv_rms[:, None] * scaled - values * (inv_rms**3 * dots / D)[:, None]
    gain_grad = jnp.sum(incoming * values * inv_rms[:, None], axis=0)
    return (values_grad, gain_grad)


def gather_edge(values):
    return lax.all_gather(values, "col", axis=0, tiled=True)


def gather_mid(values):
    return lax.all_gather(values, "row", axis=0, tiled=True)


def row_partial(whole, weight, dims):
    return lax.psum_scatter(
        lax.dot_general(whole, weight, dims, preferred_element_type=jnp.float32),
        "row",
        scatter_dimension=0,
        tiled=True,
    )


def col_partial(whole, weight, dims):
    return lax.psum_scatter(
        lax.dot_general(whole, weight, dims, preferred_element_type=jnp.float32),
        "col",
        scatter_dimension=0,
        tiled=True,
    )


def project_in(normed, weight):
    whole = gather_edge(normed)
    result = row_partial(whole, weight, CONTRACT_PLAIN)
    return (result, whole)


def weight_grad(left, right):
    return lax.dot_general(left, right, CONTRACT_ROWS, preferred_element_type=jnp.float32)


def local(
    inputs,
    cotangent,
    starts,
    x_proj,
    y_proj,
    out_proj,
    gate_proj,
    up_proj,
    down_proj,
    mix_gain,
    mlp_gain,
    x_bias,
    y_bias,
    conv_w,
    conv_b,
    rec_gate_w,
    in_gate_w,
    rec_gate_b,
    in_gate_b,
    decay_param,
):
    rows_mid = starts.shape[0]
    rec_width = x_proj.shape[1]
    ff_width = gate_proj.shape[1]
    head_count = rec_gate_w.shape[0]
    margin = conv_w.shape[0] - 1
    mix_weights = jnp.concatenate([x_proj, y_proj], axis=1)
    mlp_weights = jnp.concatenate([gate_proj, up_proj], axis=1)
    cot_rows = cotangent.T
    resid = inputs.astype(jnp.float32).T
    normed_mix, inv_rms_mix = norm_forward(resid, mix_gain)
    normed_mix = normed_mix.astype(jnp.bfloat16)
    pre_both, whole_mix = project_in(normed_mix, mix_weights)
    x_pre = pre_both[:, :rec_width] + x_bias
    y_pre = pre_both[:, rec_width:] + y_bias
    x_tail, flag_tail = from_behind(
        (x_pre[rows_mid - margin :], starts[rows_mid - margin :].astype(jnp.float32)), "row", 1
    )
    ext_flags = jnp.concatenate([flag_tail.astype(jnp.int32), starts])
    ext_ids = jnp.cumsum(ext_flags, dtype=jnp.int32)
    ext_x = jnp.concatenate([x_tail, x_pre], axis=0)

    def conv_piece(values, taps, offsets):
        return causal_conv(values, taps, offsets, ext_ids)[margin:]

    conv_vals, conv_pull = jax.vjp(conv_piece, ext_x, conv_w, conv_b)
    conv_low = conv_vals.astype(jnp.bfloat16)
    conv_heads = conv_low.reshape(rows_mid, head_count, -1)
    rec_pre = (
        jnp.einsum(
            "thk,hkj->thj", conv_heads, rec_gate_w, preferred_element_type=jnp.float32
        ).reshape(rows_mid, rec_width)
        + rec_gate_b
    )
    in_pre = (
        jnp.einsum(
            "thk,hkj->thj", conv_heads, in_gate_w, preferred_element_type=jnp.float32
        ).reshape(rows_mid, rec_width)
        + in_gate_b
    )

    def scan_piece(rec_vals, in_vals, conv_input, decay_vals):
        return local_recurrence(rec_vals, in_vals, conv_input, decay_vals, starts)

    (cum_keep, local_states), scan_pull = jax.vjp(
        scan_piece, rec_pre, in_pre, conv_low.astype(jnp.float32), decay_param
    )
    ones_row = jnp.ones((rec_width,), jnp.float32)
    zeros_row = jnp.zeros((rec_width,), jnp.float32)
    incoming = carried_in(
        (cum_keep[rows_mid - 1], local_states[rows_mid - 1]),
        "row",
        chain,
        (ones_row, zeros_row),
        False,
    )
    state_prev = incoming[1]
    states = local_states + cum_keep * state_prev
    y_act, y_pull = jax.vjp(gelu_tanh, y_pre)
    mixed = (states * y_act).astype(jnp.bfloat16)
    whole_mixed = gather_mid(mixed)
    resid_mid = resid + col_partial(whole_mixed, out_proj, CONTRACT_PLAIN)
    normed_mlp, inv_rms_mlp = norm_forward(resid_mid, mlp_gain)
    normed_mlp = normed_mlp.astype(jnp.bfloat16)
    gate_up, whole_mlp = project_in(normed_mlp, mlp_weights)
    activ, activ_pull = jax.vjp(glu_piece, gate_up[:, :ff_width], gate_up[:, ff_width:])
    activ = activ.astype(jnp.bfloat16)
    whole_activ = gather_mid(activ)
    output = (resid_mid + col_partial(whole_activ, down_proj, CONTRACT_COLS)).astype(jnp.bfloat16)
    cot_whole = gather_edge(cot_rows)
    d_activ = row_partial(cot_whole, down_proj, CONTRACT_PLAIN)
    activ_rows = gather_mid(activ)
    grad_down = weight_grad(cot_whole, activ_rows)
    d_gate, d_up = activ_pull(d_activ)
    d_gate_up = jnp.concatenate([d_gate, d_up], axis=1).astype(jnp.bfloat16)
    d_gate_up_whole = gather_mid(d_gate_up)
    d_normed_mlp = col_partial(d_gate_up_whole, mlp_weights, CONTRACT_COLS)
    mlp_rows = gather_edge(normed_mlp)
    grad_gate_up = weight_grad(mlp_rows, d_gate_up_whole)
    d_norm_mid, grad_mlp_gain = norm_backward(resid_mid, inv_rms_mlp, mlp_gain, d_normed_mlp)
    d_resid_mid = cot_rows.astype(jnp.float32) + d_norm_mid
    d_branch = d_resid_mid.astype(jnp.bfloat16)
    branch_whole = gather_edge(d_branch)
    d_mixed = row_partial(branch_whole, out_proj, CONTRACT_COLS)
    mixed_rows = gather_mid(mixed)
    grad_out = weight_grad(mixed_rows, branch_whole)
    d_state = d_mixed * y_act
    (d_y_pre,) = y_pull(d_mixed * states)
    own_sens = jnp.sum(d_state * cum_keep, axis=0)
    outgoing = carried_in(
        (cum_keep[rows_mid - 1], own_sens), "row", adjoint_chain, (ones_row, zeros_row), True
    )
    d_total = d_state + jnp.pad(outgoing[1][None, :], ((rows_mid - 1, 0), (0, 0)))
    d_rec_pre, d_in_pre, d_conv_direct, grad_decay = scan_pull((d_total * state_prev, d_total))
    d_rec_low = d_rec_pre.astype(jnp.bfloat16)
    d_in_low = d_in_pre.astype(jnp.bfloat16)
    d_rec_heads = d_rec_low.reshape(rows_mid, head_count, -1)
    d_in_heads = d_in_low.reshape(rows_mid, head_count, -1)
    d_conv = d_conv_direct + jnp.einsum(
        "thj,hkj->thk", d_rec_heads, rec_gate_w, preferred_element_type=jnp.float32
    ).reshape(rows_mid, rec_width)
    d_conv = d_conv + jnp.einsum(
        "thj,hkj->thk", d_in_heads, in_gate_w, preferred_element_type=jnp.float32
    ).reshape(rows_mid, rec_width)
    grad_rec_w = jnp.einsum(
        "thk,thj->hkj", conv_heads, d_rec_heads, preferred_element_type=jnp.float32
    )
    grad_in_w = jnp.einsum(
        "thk,thj->hkj", conv_heads, d_in_heads, preferred_element_type=jnp.float32
    )
    grad_rec_b = jnp.sum(d_rec_low.astype(jnp.float32), axis=0)
    grad_in_b = jnp.sum(d_in_low.astype(jnp.float32), axis=0)
    d_ext, grad_conv_w, grad_conv_b = conv_pull(d_conv)
    d_from_next = from_behind(d_ext[:margin], "row", -1)
    d_x_pre = d_ext[margin:] + jnp.pad(d_from_next, ((rows_mid - margin, 0), (0, 0)))
    d_pre = jnp.concatenate([d_x_pre, d_y_pre], axis=1).astype(jnp.bfloat16)
    bias_sums = jnp.sum(d_pre.astype(jnp.float32), axis=0)
    d_pre_whole = gather_mid(d_pre)
    d_normed_mix = col_partial(d_pre_whole, mix_weights, CONTRACT_COLS)
    mix_rows = gather_edge(normed_mix)
    grad_mix = weight_grad(mix_rows, d_pre_whole)
    d_norm_in, grad_mix_gain = norm_backward(resid, inv_rms_mix, mix_gain, d_normed_mix)
    inputs_grad = d_resid_mid + d_norm_in
    grad_mix, grad_out, grad_gate_up, grad_down = (
        lax.psum(grad_mix.astype(jnp.bfloat16), "dp").astype(jnp.float32),
        lax.psum(grad_out.astype(jnp.bfloat16), "dp").astype(jnp.float32),
        lax.psum(grad_gate_up.astype(jnp.bfloat16), "dp").astype(jnp.float32),
        lax.psum(grad_down.astype(jnp.bfloat16), "dp").astype(jnp.float32),
    )
    (
        bias_sums,
        grad_conv_w,
        grad_conv_b,
        grad_rec_w,
        grad_in_w,
        grad_rec_b,
        grad_in_b,
        grad_decay,
    ) = (
        lax.psum(bias_sums.astype(jnp.bfloat16), ("dp", "row")).astype(jnp.float32),
        lax.psum(grad_conv_w.astype(jnp.bfloat16), ("dp", "row")).astype(jnp.float32),
        lax.psum(grad_conv_b.astype(jnp.bfloat16), ("dp", "row")).astype(jnp.float32),
        lax.psum(grad_rec_w.astype(jnp.bfloat16), ("dp", "row")).astype(jnp.float32),
        lax.psum(grad_in_w.astype(jnp.bfloat16), ("dp", "row")).astype(jnp.float32),
        lax.psum(grad_rec_b.astype(jnp.bfloat16), ("dp", "row")).astype(jnp.float32),
        lax.psum(grad_in_b.astype(jnp.bfloat16), ("dp", "row")).astype(jnp.float32),
        lax.psum(grad_decay.astype(jnp.bfloat16), ("dp", "row")).astype(jnp.float32),
    )
    grad_mix_gain, grad_mlp_gain = lax.psum((grad_mix_gain, grad_mlp_gain), ("dp", "col"))
    return (
        output.T,
        inputs_grad.T,
        grad_mix[:, :rec_width],
        grad_mix[:, rec_width:],
        grad_out,
        grad_gate_up[:, :ff_width],
        grad_gate_up[:, ff_width:],
        grad_down,
        grad_mix_gain,
        grad_mlp_gain,
        bias_sums[:rec_width],
        bias_sums[rec_width:],
        grad_conv_w,
        grad_conv_b,
        grad_rec_w,
        grad_in_w,
        grad_rec_b,
        grad_in_b,
        grad_decay,
    )


GATHER_ID, FORWARD_ID, BACKWARD_ID = (0, 1, 2)
BLOCK = 128
VMEM_BYTES = 60 << 20


def one_minus_exp(rate):
    series = rate * (1.0 - rate * (0.5 - rate * (1.0 / 6.0 - rate * (1.0 / 24.0 - rate / 120.0))))
    return jnp.where(rate < 0.1, series, 1.0 - jnp.exp(-rate))


GELU_C = 0.7978845608028654


def gelu_both(values):
    squared = values * values
    inner = jnp.tanh(GELU_C * values * (1.0 + 0.044715 * squared))
    value = 0.5 * values * (1.0 + inner)
    slope = 0.5 * (1.0 + inner) + 0.5 * values * (1.0 - inner * inner) * GELU_C * (
        1.0 + 3.0 * 0.044715 * squared
    )
    return (value, slope)


def down_rows(values, by):
    return pltpu.roll(values, by, 0)


def up_rows(values, by):
    return pltpu.roll(values, values.shape[0] - by, 0)


def scan_down(keep, add):
    rows = keep.shape[0]
    position = lax.broadcasted_iota(jnp.int32, keep.shape, 0)
    step = 1
    while step < rows:
        if step < 8:
            inside = position >= step
            before_keep = jnp.where(inside, down_rows(keep, step), 1.0)
            before_add = jnp.where(inside, down_rows(add, step), 0.0)
            add = add + keep * before_add
            keep = keep * before_keep
        else:
            add = jnp.concatenate([add[:step], add[step:] + keep[step:] * add[:-step]], axis=0)
            keep = jnp.concatenate([keep[:step], keep[step:] * keep[:-step]], axis=0)
        step *= 2
    return (keep, add)


def scan_up(keep, add):
    rows = keep.shape[0]
    position = lax.broadcasted_iota(jnp.int32, keep.shape, 0)
    step = 1
    while step < rows:
        if step < 8:
            inside = position < rows - step
            after_keep = jnp.where(inside, up_rows(keep, step), 1.0)
            after_add = jnp.where(inside, up_rows(add, step), 0.0)
            add = add + keep * after_add
            keep = keep * after_keep
        else:
            add = jnp.concatenate([add[:-step] + keep[:-step] * add[step:], add[-step:]], axis=0)
            keep = jnp.concatenate([keep[:-step] * keep[step:], keep[-step:]], axis=0)
        step *= 2
    return (keep, add)


def mixer_forward_step(
    pre, marks, vec, rec_w, in_w, mixed, x_pre, conv, rec_gate, in_gate, states, tail, carry
):
    width = x_pre.shape[1]
    x = pre[:, :width] + vec[0:1, :]
    x_pre[...] = x
    longer = jnp.concatenate([tail[...], x], axis=0)
    tail[...] = x[BLOCK - 8 :]
    total = x * vec[2:3, :] + vec[6:7, :]
    for tap in range(1, 4):
        total = total + marks[:, tap : tap + 1] * down_rows(longer, tap)[8:] * vec[
            2 + tap : 3 + tap, :
        ]
    low = total.astype(jnp.bfloat16)
    conv[...] = low
    rec = jax.nn.sigmoid(
        jnp.dot(low, rec_w[...], preferred_element_type=jnp.float32) + vec[7:8, :]
    )
    inn = jax.nn.sigmoid(
        jnp.dot(low, in_w[...], preferred_element_type=jnp.float32) + vec[8:9, :]
    )
    rec_gate[...] = rec
    in_gate[...] = inn
    log_keep = rec * vec[9:10, :]
    fresh = marks[:, 0:1]
    scale = jnp.where(fresh > 0.5, 1.0, jnp.sqrt(one_minus_exp(-2.0 * log_keep)))
    driven = low.astype(jnp.float32) * inn * scale
    keep, add = scan_down(jnp.exp(log_keep) * (1.0 - fresh), driven)
    state = add + keep * carry[0:1, :]
    carry[...] = jnp.broadcast_to(state[BLOCK - 1 :, :], carry.shape)
    states[...] = state
    y = pre[:, width:] + vec[1:2, :]
    mixed[:, :width] = (state * gelu_both(y)[0]).astype(jnp.bfloat16)
    mixed[:, width:] = jnp.zeros((BLOCK, mixed.shape[1] - width), jnp.bfloat16)


def mixer_backward_step(
    incoming,
    pre,
    marks,
    vec,
    rec_w,
    in_w,
    x_pre,
    x_before,
    conv,
    rec_gate,
    in_gate,
    states,
    state_before,
    d_pre,
    d_gates,
    sums,
    edge,
    carry,
):
    width = x_pre.shape[1]
    position = lax.broadcasted_iota(jnp.int32, (BLOCK, width), 0)
    fresh = marks[:, 0:1]
    stale = 1.0 - fresh
    gelu, slope = gelu_both(pre[:, width:] + vec[1:2, :])
    state = states[...]
    d_y = (incoming * state * slope).astype(jnp.bfloat16)
    rec, inn = (rec_gate[...], in_gate[...])
    conv_vals = conv[...].astype(jnp.float32)
    log_keep = rec * vec[9:10, :]
    keep_rate = jnp.exp(log_keep)
    scale = jnp.where(fresh > 0.5, 1.0, jnp.sqrt(one_minus_exp(-2.0 * log_keep)))
    carried = keep_rate * stale
    after = jnp.where(position == BLOCK - 1, carry[1:2, :], up_rows(carried, 1))
    keep, add = scan_up(after, incoming * gelu)
    adjoint = add + keep * carry[0:1, :]
    carry[0:1, :] = adjoint[0:1]
    carry[1:2, :] = carried[0:1]
    earlier = jnp.where(position == 0, state_before[7:8, :], down_rows(state, 1))
    drive = adjoint * scale
    d_log = stale * (
        adjoint * earlier * keep_rate
        - adjoint * inn * conv_vals * keep_rate * keep_rate / scale
    )
    d_rec = (d_log * vec[9:10, :] * rec * (1.0 - rec)).astype(jnp.bfloat16)
    d_in = (drive * conv_vals * inn * (1.0 - inn)).astype(jnp.bfloat16)
    d_gates[:, :width] = d_rec
    d_gates[:, width:] = d_in
    d_conv = drive * inn
    d_conv = d_conv + lax.dot_general(
        d_rec, rec_w[...], CONTRACT_COLS, preferred_element_type=jnp.float32
    )
    d_conv = d_conv + lax.dot_general(
        d_in, in_w[...], CONTRACT_COLS, preferred_element_type=jnp.float32
    )
    x = x_pre[...]
    longer = jnp.concatenate([x_before[...], x], axis=0)

    def column(values):
        return jnp.sum(values, axis=0, keepdims=True)

    d_x = d_conv * vec[2:3, :]
    taps = [column(d_conv * x)]
    for tap in range(1, 4):
        piece = marks[:, tap : tap + 1] * d_conv
        taps.append(column(piece * down_rows(longer, tap)[8:]))
        beyond = jnp.concatenate([piece, edge[8 * tap - 8 : 8 * tap, :]], axis=0)
        d_x = d_x + vec[2 + tap : 3 + tap, :] * up_rows(beyond, tap)[:BLOCK]
        edge[8 * tap - 8 : 8 * tap, :] = piece[:8]
    d_x = d_x.astype(jnp.bfloat16)
    d_pre[:, :width] = d_x
    d_pre[:, width:] = d_y
    pieces = (
        [column(d_x.astype(jnp.float32)), column(d_y.astype(jnp.float32))]
        + taps
        + [
            column(d_conv),
            column(d_rec.astype(jnp.float32)),
            column(d_in.astype(jnp.float32)),
            column(d_log * rec) * vec[10:11, :],
        ]
    )
    for place, piece in enumerate(pieces):
        sums[place : place + 1, :] += piece


def here():
    return (lax.axis_index("dp"), lax.axis_index("row"), lax.axis_index("col"))


def flip(index):
    return index + 1 - 2 * (index % 2)


def across(row):
    return (row + 2) % 4


def greet(peers):
    barrier = pltpu.get_barrier_semaphore()
    for peer in peers:
        pl.semaphore_signal(barrier, inc=1, device_id=peer, device_id_type=MESH)
    pl.semaphore_wait(barrier, len(peers))


class Copies:
    def __init__(self, send, recv):
        self.send, self.recv, self.used, self.sent = (send, recv, 0, [])

    def make(self, source, target, device):
        place = self.used
        self.used += 1
        if device is None:
            copy = pltpu.make_async_copy(source, target, self.recv.at[place])
        else:
            copy = pltpu.make_async_remote_copy(
                src_ref=source,
                dst_ref=target,
                send_sem=self.send.at[place],
                recv_sem=self.recv.at[place],
                device_id=device,
                device_id_type=MESH,
            )
            self.sent.append(copy)
        return copy

    def go(self, source, target, device):
        copy = self.make(source, target, device)
        copy.start()
        return copy

    def finish(self):
        for copy in self.sent:
            copy.wait_send()
        self.sent = []


def arrived(copy):
    copy.wait_recv()


def spread(copies, own, place, halves, between=lambda: None):
    z, r, c = here()
    twin, side, top = ((z, flip(r), c), (z, across(r), c), (z, r, 1 - c))
    to_side = copies.go(own, place(r, c), side)
    to_top = copies.go(own, place(r, c), top)
    to_twin = copies.go(own, place(r, c), twin)
    between()
    arrived(to_side)
    from_side = place(across(r), c)
    on_top = copies.go(halves(from_side, 0), halves(from_side, 0), top)
    late = [to_twin, copies.go(from_side, from_side, twin)]
    between()
    arrived(to_top)
    from_top = place(r, 1 - c)
    on_side = copies.go(halves(from_top, 1), halves(from_top, 1), side)
    late.append(copies.go(from_top, from_top, twin))
    far = place(across(r), 1 - c)
    between()
    for half, copy in enumerate((on_top, on_side)):
        arrived(copy)
        late.append(copies.go(halves(far, half), halves(far, half), twin))
    return late


def part(start, size, step):
    return pl.ds(pl.multiple_of(start * step, step), size)


class Moves:
    def __init__(self, copies, matrices, cuts):
        self.copies = copies
        z, r, c = here()
        self.mine = z % 2
        self.sides = ((z, across(r), c), (z, flip(across(r)), c))
        self.pair = (flip(z), r, c)
        self.locals, self.late, self.flying = ([], [], [])
        self.groups = [(matrix, cut) for matrix in matrices for cut in range(cuts)]
        self.cuts, self.begun = (cuts, 0)
        for source, target, size in matrices:
            self.locals.append(copies.go(source(r), target(r), None))
            self.late.append(copies.go(source(flip(r)), target(r), (z, flip(r), c)))

    def piece(self, ref, size, cut):
        length = size // 2 // self.cuts
        return ref.at[part(self.mine * self.cuts + cut, length, length), :]

    def step(self):
        if len(self.flying) == 2 or self.begun == len(self.groups):
            if self.flying:
                (source, target, size), cut, group = self.flying.pop(0)
                for peer, copy in zip(self.sides, group):
                    arrived(copy)
                    piece = self.piece(target(peer[1]), size, cut)
                    self.late.append(self.copies.go(piece, piece, self.pair))
        if self.begun < len(self.groups):
            (source, target, size), cut = self.groups[self.begun]
            self.begun += 1
            group = [
                self.copies.go(
                    self.piece(source(peer[1]), size, cut),
                    self.piece(target(here()[1]), size, cut),
                    peer,
                )
                for peer in self.sides
            ]
            self.flying.append(((source, target, size), cut, group))

    def finish(self):
        while self.flying:
            self.step()
        for copy in self.late:
            arrived(copy)
        for copy in self.locals:
            copy.wait()


def block_of(ref, rows, columns):
    return lambda row, col: ref.at[part(col, rows, rows), part(row, columns, columns)]


def halves_of(rows):
    return lambda ref, which: ref.at[pl.ds(which * (rows // 2), rows // 2), :]


def mlp_matrices(sources, targets):
    depth, width = (sources[0].shape[0], sources[0].shape[1] // 4)
    return [
        (
            lambda to, source=source: source.at[:, part(to, width, width)],
            lambda of, target=target: target.at[part(of, depth, depth), :],
            depth,
        )
        for source, target in zip(sources, targets)
    ]


def gather_kernel(x_in, s_in, g_in, mix_in, out_in, x_all, s_all, g_all, mix_all, out_all, send, recv):
    z, r, c = here()
    twin, side, cross, top, pair = (
        (z, flip(r), c),
        (z, across(r), c),
        (z, flip(across(r)), c),
        (z, r, 1 - c),
        (flip(z), r, c),
    )
    greet((twin, side, cross, top, pair))
    copies = Copies(send, recv)
    rows, columns = x_in.shape
    depth, rec = (mix_in.shape[1], out_in.shape[0] // 4)
    matrices = [
        (lambda to: mix_in.at[to], lambda of: mix_all.at[part(of, depth, depth), :], depth),
        (
            lambda to: out_in.at[part(to, rec, rec), :],
            lambda of: out_all.at[:, part(of, columns, columns)],
            rec,
        ),
    ]
    small = g_all.at[:, part(r, depth, depth)]
    locals_ = [
        copies.go(x_in, block_of(x_all, rows, columns)(r, c), None),
        copies.go(s_in, s_all.at[r], None),
        copies.go(g_in, small, None),
    ]
    late = []
    for peer in (twin, side, cross):
        late.append(copies.go(s_in, s_all.at[r], peer))
        late.append(copies.go(g_in, small, peer))
    moves = Moves(copies, matrices, 2)
    moves.step()
    late.extend(
        spread(copies, x_in, block_of(x_all, rows, columns), halves_of(rows), moves.step)
    )
    moves.finish()
    for copy in late:
        arrived(copy)
    for copy in locals_:
        copy.wait()
    copies.finish()


def gather(x_in, s_in, g_in, mix_in, out_in):
    rows, columns = x_in.shape
    depth = mix_in.shape[1]

    def shape(*dims, kind=jnp.bfloat16):
        return jax.ShapeDtypeStruct(dims, kind)

    outs = [
        shape(2 * rows, 4 * columns),
        shape(4, *s_in.shape, kind=s_in.dtype),
        shape(g_in.shape[0], 4 * depth, kind=g_in.dtype),
        shape(4 * depth, mix_in.shape[2]),
        shape(out_in.shape[0] // 4, 4 * columns),
    ]
    return pl.pallas_call(
        gather_kernel,
        in_specs=[pl.BlockSpec(memory_space=pl.ANY)] * 5,
        out_specs=[pl.BlockSpec(memory_space=pl.ANY)] * 5,
        out_shape=outs,
        scratch_shapes=[pltpu.SemaphoreType.DMA((48,)), pltpu.SemaphoreType.DMA((48,))],
        compiler_params=pltpu.CompilerParams(collective_id=GATHER_ID, has_side_effects=True),
        name="gather",
    )(x_in, s_in, g_in, mix_in, out_in)


STRIP = 16


def strips(count, body):
    def run(index, nothing):
        body(pl.multiple_of(index * STRIP, STRIP))
        return nothing

    lax.fori_loop(0, count // STRIP, run, 0)


def token_shard(row, col):
    return col * 4 + row


def reduce_shards(copies, parts, twin_in, sums, side_in, top_in, hop_in, between=lambda: None):
    z, r, c = here()
    twin, side, top = ((z, flip(r), c), (z, across(r), c), (z, r, 1 - c))
    size = side_in.shape[0]
    half = size // 2

    def shard(row, col):
        return pl.multiple_of(token_shard(row, col) * size, size)

    spots = [(across(r), 1 - c), (across(r), c), (r, 1 - c), (r, c)]
    from_twin = [
        copies.go(parts.at[pl.ds(shard(flip(row), col), size), :], twin_in.at[place], twin)
        for place, (row, col) in enumerate(spots)
    ]

    def add_twin(place):
        arrived(from_twin[place])
        start = shard(*spots[place])

        def body(at):
            total = parts[pl.ds(start + at, STRIP), :].astype(jnp.float32) + twin_in[
                place, pl.ds(at, STRIP), :
            ].astype(jnp.float32)
            sums[place, pl.ds(at, STRIP), :] = total.astype(jnp.bfloat16)

        strips(size, body)

    def add_hop(place, which, hop):
        def body(at):
            rows = pl.ds(which * half + at, STRIP)
            total = sums[place, rows, :].astype(jnp.float32) + hop_in[
                hop, pl.ds(at, STRIP), :
            ].astype(jnp.float32)
            sums[place, rows, :] = total.astype(jnp.bfloat16)

        strips(half, body)

    def rows_of(ref, which):
        return ref.at[pl.ds(which * half, half), :]

    add_twin(0)
    hop_side = copies.go(rows_of(sums.at[0], 0), hop_in.at[0], side)
    hop_top = copies.go(rows_of(sums.at[0], 1), hop_in.at[1], top)
    add_twin(1)
    waits = [copies.go(rows_of(sums.at[1], 0), rows_of(side_in, 0), side)]
    add_twin(2)
    waits.append(copies.go(rows_of(sums.at[2], 1), rows_of(top_in, 1), top))
    add_twin(3)
    between()
    arrived(hop_top)
    add_hop(1, 1, 1)
    waits.append(copies.go(rows_of(sums.at[1], 1), rows_of(side_in, 1), side))
    arrived(hop_side)
    add_hop(2, 0, 0)
    waits.append(copies.go(rows_of(sums.at[2], 0), rows_of(top_in, 0), top))
    between()
    for copy in waits:
        arrived(copy)

    def total(at):
        rows = pl.ds(at, STRIP)
        return (
            sums[3, rows, :].astype(jnp.float32)
            + side_in[rows, :].astype(jnp.float32)
            + top_in[rows, :].astype(jnp.float32)
        )

    return total


def reduce_scratch(size, width):
    return [
        pltpu.VMEM((4, size, width), jnp.bfloat16),
        pltpu.VMEM((4, size, width), jnp.bfloat16),
        pltpu.VMEM((size, width), jnp.bfloat16),
        pltpu.VMEM((size, width), jnp.bfloat16),
        pltpu.VMEM((2, size // 2, width), jnp.bfloat16),
    ]


def near():
    z, r, c = here()
    return ((z, flip(r), c), (z, across(r), c), (z, r, 1 - c))


def spread_rows(copies, mine, full, between=lambda: None):
    z, r, c = here()
    size = mine.shape[0]
    half = size // 2

    def place(row, col):
        return full.at[pl.ds(pl.multiple_of(token_shard(row, col) * size, size), size), :]

    local = copies.go(mine, place(r, c), None)
    late = spread(
        copies, mine, place, lambda ref, which: ref.at[pl.ds(which * half, half), :], between
    )
    for copy in late:
        arrived(copy)
    local.wait()


def forward_kernel(x_all, masks, vec, rec_w, in_w, mix_w, out_w, gain_mix, gain, c_in, *refs):
    mlp_in, outs, scratch = (refs[:3], refs[3:17], refs[17:])
    full, resid_mid, c_all = outs[:3]
    mlp_all, kept_out = (outs[3:6], outs[6:])
    kept, (tail, carry, parts), (*buffers, mine, kept_sem, send, recv) = (
        scratch[:8],
        scratch[8:11],
        scratch[11:],
    )
    normed, pre, mixed, *saved = kept
    z, r, c = here()
    greet((*near(), (z, flip(across(r)), c), (flip(z), r, c)))
    copies = Copies(send, recv)
    rows, columns = c_in.shape
    moves = Moves(copies, mlp_matrices(mlp_in, mlp_all), 2)
    moves.step()
    moves.step()
    tail[...] = jnp.zeros_like(tail)
    carry[...] = jnp.zeros_like(carry)

    def block(index, nothing):
        start = pl.multiple_of(index * BLOCK, BLOCK)
        rows = pl.ds(start, BLOCK)

        def norm(at):
            strip = pl.ds(start + at, STRIP)
            values = x_all[strip, :].astype(jnp.float32)
            scale = lax.rsqrt(jnp.mean(values * values, axis=1, keepdims=True) + EPS)
            normed[strip, :] = (values * scale * gain_mix[...]).astype(jnp.bfloat16)

        strips(BLOCK, norm)
        pre[rows, :] = jnp.dot(normed[rows, :], mix_w[...], preferred_element_type=jnp.float32)
        mixer_forward_step(
            pre.at[rows, :],
            masks[rows, :],
            vec,
            rec_w,
            in_w,
            mixed.at[rows, :],
            *[ref.at[rows, :] for ref in saved],
            tail,
            carry,
        )
        width = rec_w.shape[0]
        parts[rows, :] = jnp.dot(
            mixed[rows, :width], out_w[...], preferred_element_type=jnp.float32
        ).astype(jnp.bfloat16)
        return nothing

    lax.fori_loop(0, 3, block, 0)
    moves.step()
    lax.fori_loop(3, 6, block, 0)
    moves.step()
    lax.fori_loop(6, x_all.shape[0] // BLOCK, block, 0)
    keeping = [
        pltpu.make_async_copy(source, target, kept_sem.at[place])
        for place, (source, target) in enumerate(zip(kept, kept_out))
    ]
    for copy in keeping:
        copy.start()
    total = reduce_shards(copies, parts, *buffers, between=moves.step)
    size = mine.shape[0]
    start = pl.multiple_of(token_shard(r, c) * size, size)

    def body(at):
        rows = pl.ds(at, STRIP)
        values = x_all[pl.ds(start + at, STRIP), :].astype(jnp.float32) + total(at)
        resid_mid[rows, :] = values
        scale = lax.rsqrt(jnp.mean(values * values, axis=1, keepdims=True) + EPS)
        mine[rows, :] = (values * scale * gain[...]).astype(jnp.bfloat16)

    strips(size, body)
    spread_rows(copies, mine, full, moves.step)
    local = copies.go(c_in, block_of(c_all, rows, columns)(r, c), None)
    late = spread(copies, c_in, block_of(c_all, rows, columns), halves_of(rows), moves.step)
    for copy in late:
        arrived(copy)
    local.wait()
    moves.finish()
    for copy in keeping:
        copy.wait()
    copies.finish()


def norm_pull(values, gain, incoming):
    scale = lax.rsqrt(jnp.mean(values * values, axis=1, keepdims=True) + EPS)
    scaled = gain * incoming
    dots = jnp.sum(scaled * values, axis=1, keepdims=True)
    grad = scale * scaled - values * (scale * scale * scale * dots / values.shape[1])
    return (grad, jnp.sum(incoming * values * scale, axis=0, keepdims=True))


def vmem_call(kernel, name, place, arrays, outs, spaces, scratch, count, loose=()):
    return pl.pallas_call(
        kernel,
        in_specs=[pl.BlockSpec(memory_space=pltpu.VMEM)] * len(arrays)
        + [pl.BlockSpec(memory_space=pl.ANY)] * len(loose),
        out_specs=[pl.BlockSpec(memory_space=space) for space in spaces],
        out_shape=outs,
        scratch_shapes=scratch
        + [pltpu.SemaphoreType.DMA((count,)), pltpu.SemaphoreType.DMA((count,))],
        compiler_params=pltpu.CompilerParams(
            collective_id=place, has_side_effects=True, vmem_limit_bytes=VMEM_BYTES
        ),
        name=name,
    )(*arrays, *loose)


AHEAD = 3
DEPTH = 4
HAND_LAG = 4
LAG = 6
RING = 16
SEGMENTS = 2


def run_loop(first, last, body):
    def run(index, nothing):
        body(index)
        return nothing

    lax.fori_loop(first, last, run, 0)


def remote(source, target, sender, receiver, device):
    return pltpu.make_async_remote_copy(
        src_ref=source,
        dst_ref=target,
        send_sem=sender,
        recv_sem=receiver,
        device_id=device,
        device_id_type=MESH,
    )


class Line:
    def __init__(self, own, left, right, out, sems, lead):
        self.own, self.left, self.right, self.out, self.lead = (own, left, right, out, lead)
        (
            self.end_send,
            self.low_recv,
            self.high_recv,
            self.out_recv,
            self.mid_send,
            self.first_send,
            self.last_send,
            self.hand_send,
            self.on_send,
        ) = sems
        z, r, c = here()
        self.chunk = left.shape[1]
        self.rows = out.shape[1]
        self.half = self.rows // 2
        self.per = self.half // self.chunk
        self.first = 4 * self.per
        self.chunks = 4 * SEGMENTS * self.per + lead
        self.total = self.chunks + LAG
        self.at = 0
        self.ahead = 0
        self.is_end = (z == 0) | (z == 3)
        self.near_z = (jnp.where(z == 0, 1, 2), r, c)
        self.outer = (jnp.where(z == 1, 0, 3), r, c)
        self.other = (3 - z, r, c)

    def extra(self, index):
        return (index >= self.first) & (index < self.first + self.lead)

    def spot(self, index):
        later = index >= self.first + self.lead
        plain = index - jnp.where(later, self.lead, 0)
        step = jnp.where(self.extra(index), 0, plain // self.per)
        strip = jnp.where(self.extra(index), index - self.first, plain % self.per)
        return (step // 4, step % 4, strip)

    def peer_row(self, index):
        r = here()[1]
        step = self.spot(index)[1]
        return (r // 2 + step // 2) % 2 * 2 + (r % 2 + step % 2) % 2

    def stays(self, index):
        return self.spot(index)[1] == 0

    def span(self, index, which):
        segment, _, strip = self.spot(index)
        start = (segment * 4 + self.peer_row(index)) * self.rows + which * self.half
        outside = SEGMENTS * 4 * self.rows + which * self.lead * self.chunk
        start = jnp.where(self.extra(index), outside, start)
        return pl.ds(pl.multiple_of(start + strip * self.chunk, self.chunk), self.chunk)

    def own_at(self, index, which):
        return self.own.at[self.span(index, which), :]

    def out_at(self, index, which, row):
        segment, _, strip = self.spot(index)
        place = jnp.where(self.extra(index), 4 * SEGMENTS, segment * 4 + row)
        start = pl.multiple_of(which * self.half + strip * self.chunk, self.chunk)
        return self.out.at[place, pl.ds(start, self.chunk), :]

    def end_sends(self, index):
        low = here()[0] // 3
        return (
            remote(
                self.own_at(index, low),
                self.left.at[index % RING],
                self.end_send.at[0, index],
                self.low_recv.at[index],
                self.near_z,
            ),
            remote(
                self.own_at(index, 1 - low),
                self.right.at[1, index % RING],
                self.end_send.at[1, index],
                self.high_recv.at[1, index],
                self.near_z,
            ),
        )

    def to_other(self, index):
        low = here()[0] - 1
        return remote(
            self.own_at(index, 1 - low),
            self.right.at[0, index % RING],
            self.mid_send.at[index],
            self.high_recv.at[0, index],
            self.other,
        )

    def from_outer(self, index):
        low = here()[0] - 1
        return (
            remote(
                self.own_at(index, low),
                self.left.at[index % RING],
                self.mid_send.at[index],
                self.low_recv.at[index],
                self.outer,
            ),
            remote(
                self.own_at(index, 1 - low),
                self.right.at[1, index % RING],
                self.mid_send.at[index],
                self.high_recv.at[1, index],
                self.outer,
            ),
        )

    def hand(self, index):
        z, r, c = here()
        low = z - 1
        mine, spot = (self.own_at(index, low), self.out_at(index, low, r))
        return (
            pltpu.make_async_copy(mine, spot, self.out_recv.at[low, index]),
            remote(
                mine,
                spot,
                self.hand_send.at[index],
                self.out_recv.at[low, index],
                (z, self.peer_row(index), c),
            ),
        )

    def along(self, index):
        low = here()[0] - 1
        spot = self.out_at(index, low, self.peer_row(index))
        return (
            remote(
                spot, spot, self.first_send.at[index], self.out_recv.at[low, index], self.outer
            ),
            remote(spot, spot, self.last_send.at[index], self.out_recv.at[low, index], self.other),
        )

    def onward(self, index):
        low = here()[0] - 1
        spot = self.out_at(index, 1 - low, self.peer_row(index))
        return remote(
            spot, spot, self.on_send.at[index], self.out_recv.at[1 - low, index], self.outer
        )

    def came_back(self, index):
        for which in (0, 1):
            spot = self.out_at(index, which, self.peer_row(index))
            remote(
                spot, spot, self.end_send.at[0, index], self.out_recv.at[which, index], self.near_z
            ).wait_recv()

    def end_step(self, index):
        @pl.when(index < self.chunks)
        def _():
            @pl.when(index >= DEPTH)
            def _():
                for copy in self.end_sends(index - DEPTH):
                    copy.wait_send()

            @pl.when(index >= RING)
            def _():
                self.came_back(index - RING)

            for copy in self.end_sends(index):
                copy.start()

    def mid_step(self, index):
        own, left, right, low = (self.own, self.left, self.right, here()[0] - 1)

        @pl.when(index < self.chunks)
        def _():
            self.from_outer(index)[1].wait_recv()
            span = self.span(index, 1 - low)
            total = own[span, :].astype(jnp.float32) + right[1, index % RING].astype(jnp.float32)
            own[span, :] = total.astype(jnp.bfloat16)
            self.to_other(index).start()

        @pl.when((index >= 2) & (index < self.chunks + 2))
        def _():
            back = index - 2
            self.from_outer(back)[0].wait_recv()
            self.to_other(back).wait_recv()
            span = self.span(back, low)
            total = (
                own[span, :].astype(jnp.float32)
                + left[back % RING].astype(jnp.float32)
                + right[0, back % RING].astype(jnp.float32)
            )
            own[span, :] = total.astype(jnp.bfloat16)

            @pl.when(self.stays(back))
            def _():
                self.hand(back)[0].start()

            @pl.when(jnp.logical_not(self.stays(back)))
            def _():
                self.hand(back)[1].start()

        @pl.when((index >= HAND_LAG) & (index < self.chunks + HAND_LAG))
        def _():
            back = index - HAND_LAG

            @pl.when(self.stays(back))
            def _():
                self.hand(back)[0].wait()

            @pl.when(jnp.logical_not(self.stays(back)))
            def _():
                self.hand(back)[1].wait_recv()

            for copy in self.along(back):
                copy.start()

        @pl.when(index >= LAG)
        def _():
            copy = self.onward(index - LAG)
            copy.wait_recv()
            copy.start()

    def advance(self, count):
        first, last = (self.at, min(self.at + count, self.total))
        self.at = last
        if first == last:
            return

        @pl.when(self.is_end)
        def _():
            run_loop(self.ahead, last + AHEAD, self.end_step)

        self.ahead = last + AHEAD

        @pl.when(jnp.logical_not(self.is_end))
        def _():
            run_loop(first, last, self.mid_step)

    def one(self, index):
        @pl.when(self.is_end)
        def _():
            self.end_step(index + AHEAD)

        @pl.when(jnp.logical_not(self.is_end))
        def _():
            self.mid_step(index)

    def skip(self, count):
        self.at += count
        self.ahead += count

    def end_done(self, index):
        @pl.when(index >= self.chunks - DEPTH)
        def _():
            for copy in self.end_sends(index):
                copy.wait_send()

        @pl.when(index >= self.chunks - RING)
        def _():
            self.came_back(index)

    def mid_done(self, index):
        self.to_other(index).wait_send()

        @pl.when(jnp.logical_not(self.stays(index)))
        def _():
            self.hand(index)[1].wait_send()

        for copy in self.along(index):
            copy.wait_send()
        self.onward(index).wait_send()

    def finish(self):
        self.advance(self.total)

        @pl.when(self.is_end)
        def _():
            run_loop(0, self.chunks, self.end_done)

        @pl.when(jnp.logical_not(self.is_end))
        def _():
            run_loop(0, self.chunks, self.mid_done)


def line_scratch(rows, width, chunk, lead):
    dma = pltpu.SemaphoreType.DMA
    chunks = 4 * SEGMENTS * (rows // 2 // chunk) + lead
    return [
        pltpu.VMEM((4 * SEGMENTS * rows + 2 * lead * chunk, width), jnp.bfloat16),
        pltpu.VMEM((RING, chunk, width), jnp.bfloat16),
        pltpu.VMEM((2, RING, chunk, width), jnp.bfloat16),
        dma((2, chunks)),
        dma((chunks,)),
        dma((2, chunks)),
        dma((2, chunks)),
        dma((chunks,)),
        dma((chunks,)),
        dma((chunks,)),
        dma((chunks,)),
        dma((chunks,)),
    ]


LINE_REFS = 12
PACK = 32
CHUNK = 16
PACE = (6, 6, 6, 2, 2, 4, 6, 6, 8)
BLOCK_STEPS = 2


def z_peers():
    z, r, c = here()
    return [((z + step) % 4, r, c) for step in (1, 2, 3)]


def plane_peers():
    z, r, c = here()
    return [(z, (r + turn % 4) % 4, (c + turn // 4) % 2) for turn in range(1, 8)]


def hand_out(copies, source, target):
    z, r, c = here()
    twin, side, _ = near()
    cross = (z, flip(across(r)), c)
    columns = target.shape[1]
    size = source.shape[0]

    def piece(row):
        return source.at[:, part(row, columns, columns)]

    spot = target.at[part(r, size, size), :]
    waits = [copies.go(piece(peer[1]), spot, peer) for peer in (side, cross, twin)]
    local = copies.go(piece(r), spot, None)

    def done():
        for copy in waits:
            arrived(copy)
        local.wait()

    return done


def gate_tiles(width):
    tiles = []
    for tile in range(5):
        first, rest = (0, width)
        if tile < 4:
            tiles.append((tile, 0, width, tile // 2, tile % 2 * width))
        else:
            tiles.append((tile, 0, 384, 0, 2 * width))
            tiles.append((tile, 384, width - 384, 1, 2 * width))
    return tiles


def backward_kernel(resid_mid, gain, gain_mix, masks, vec, rec_w, in_w, mix_w, out_w, *refs):
    parts_in, out_parts, c_all, x_all, *kept_in = refs[:12]
    gate_grad, up_grad, down_grad = refs[12:15]
    grad, output, grads, out_gates, out_vec, out_gain = refs[15:21]
    scratch = refs[21:]
    line_refs, scratch = (scratch[:LINE_REFS], scratch[LINE_REFS:])
    parts, cot, resid, branch, d_resid, d_pre, d_gates, edge, carry = scratch[:9]
    kept, scratch = (scratch[9:17], scratch[17:])
    sums, gains, vec_z, gain_z, vec_sum, gain_sum, vec_in, gain_in = scratch[:8]
    *buffers, mine, mine_out, load_sem, gate_sem, small_send, small_recv, free, send, recv = scratch[8:]
    normed, pre, mixed, x_pre, conv, rec_gate, in_gate, states = kept
    z, r, c = here()
    twin, side, top = near()
    cross = (z, flip(across(r)), c)
    lines, plane = (z_peers(), plane_peers())
    greet(lines + plane)
    copies = Copies(send, recv)
    line = Line(*line_refs[:3], grads, line_refs[3:], PACK // CHUNK)
    own, half, rows_all = (line.own, line.half, 4 * line.rows)
    size = mine.shape[0]
    shard = part(token_shard(r, c), size, size)
    width, ff = (x_pre.shape[1], gate_grad.shape[1])
    head, rest = (own.shape[1] - 2 * ff, 3 * ff - own.shape[1])
    first, second = (pl.ds(0, rows_all), pl.ds(rows_all, rows_all))
    loads = [
        pltpu.make_async_copy(source, target, load_sem.at[place])
        for place, (source, target) in enumerate(
            zip(
                [
                    parts_in,
                    gate_grad,
                    up_grad,
                    down_grad.at[:, pl.ds(0, head)],
                    down_grad.at[:, pl.ds(head, rest)],
                    c_all.at[shard, :],
                    x_all.at[shard, :],
                    *kept_in,
                ],
                [
                    parts,
                    own.at[first, pl.ds(0, ff)],
                    own.at[first, pl.ds(ff, ff)],
                    own.at[first, pl.ds(2 * ff, head)],
                    own.at[second, pl.ds(0, rest)],
                    cot,
                    resid,
                    *kept,
                ],
            )
        )
    ]
    for copy in loads:
        copy.start()
    for ref in (gains, sums, edge, carry):
        ref[...] = jnp.zeros_like(ref)
    for copy in loads[:4]:
        copy.wait()
    pace = iter(PACE)

    def between():
        line.advance(next(pace))

    total = reduce_shards(copies, parts, *buffers, between=between)
    for copy in loads[4:]:
        copy.wait()

    def body(at):
        rows = pl.ds(at, STRIP)
        values, piece = norm_pull(resid_mid[rows, :], gain[...], total(at))
        values = values + cot[rows, :].astype(jnp.float32)
        gains[1:2, :] += piece
        d_resid[rows, :] = values
        mine[rows, :] = values.astype(jnp.bfloat16)

    strips(size, body)
    spread_rows(copies, mine, branch, between)
    copies.finish()
    last = branch.shape[0] // BLOCK - 1

    def block(index, base):
        start = pl.multiple_of((last - index) * BLOCK, BLOCK)
        rows = pl.ds(start, BLOCK)
        before = pl.ds(pl.multiple_of(jnp.maximum(start - 8, 0), 8), 8)
        mixer_backward_step(
            lax.dot_general(
                branch[rows, :], out_w[...], CONTRACT_COLS, preferred_element_type=jnp.float32
            ),
            pre.at[rows, :],
            masks[rows, :],
            vec,
            rec_w,
            in_w,
            x_pre.at[rows, :],
            x_pre.at[before, :],
            conv.at[rows, :],
            rec_gate.at[rows, :],
            in_gate.at[rows, :],
            states.at[rows, :],
            states.at[before, :],
            d_pre.at[rows, :],
            d_gates.at[rows, :],
            sums,
            edge,
            carry,
        )
        parts[rows, :] = lax.dot_general(
            d_pre[rows, :], mix_w[...], CONTRACT_COLS, preferred_element_type=jnp.float32
        ).astype(jnp.bfloat16)
        for step in range(BLOCK_STEPS):
            line.one(base + BLOCK_STEPS * index + step)
        return base

    lax.fori_loop(0, last + 1, block, line.at)
    line.skip(BLOCK_STEPS * (last + 1))
    total_back = reduce_shards(copies, parts, *buffers, between=between)

    def body_back(at):
        rows = pl.ds(at, STRIP)
        values, piece = norm_pull(
            resid[rows, :].astype(jnp.float32), gain_mix[...], total_back(at)
        )
        gains[0:1, :] += piece
        mine[rows, :] = (d_resid[rows, :] + values).astype(jnp.bfloat16)

    strips(size, body_back)
    for peer in (twin, side, top):
        pl.semaphore_signal(free, inc=1, device_id=peer, device_id_type=MESH)
    copies.finish()
    load = pltpu.make_async_copy(out_parts, parts, load_sem.at[0])
    load.start()
    grad_done = hand_out(copies, mine, grad)
    small = [
        [
            remote(
                source,
                target.at[3 - step],
                small_send.at[kind, step - 1],
                small_recv.at[kind, 3 - step],
                lines[step - 1],
            )
            for step in (1, 2, 3)
        ]
        for kind, (source, target) in enumerate(((sums, vec_z), (gains, gain_z)))
    ]
    for kind in small:
        for copy in kind:
            copy.start()
    blocks = lax.dot_general(conv[...], d_gates[...], CONTRACT_ROWS, preferred_element_type=jnp.float32)
    rows_half = width // 2
    lane = lax.broadcasted_iota(jnp.int32, (rows_half, 2 * width), 1)
    mingled = jnp.where(
        lane // rows_half % 2 == 0, blocks[:rows_half], blocks[rows_half:]
    ).astype(jnp.bfloat16)
    for tile, begin, length, which, spot in gate_tiles(2 * width):
        own[pl.ds(2 * rows_all + which * PACK, PACK), spot : spot + length] = mingled[
            tile * PACK : (tile + 1) * PACK, begin : begin + length
        ]

    def weights(index, base):
        columns = pl.ds(pl.multiple_of(index * 256, 256), 256)
        rows = pl.ds(pl.multiple_of(rows_all + index * 256, 256), 256)
        own[rows, rest : rest + 2 * width] = lax.dot_general(
            normed[:, columns], d_pre[...], CONTRACT_ROWS, preferred_element_type=jnp.float32
        ).astype(jnp.bfloat16)
        own[rows, rest + 2 * width :] = lax.dot_general(
            branch[:, columns], mixed[...], CONTRACT_ROWS, preferred_element_type=jnp.float32
        ).astype(jnp.bfloat16)
        line.one(base + index)
        return base

    lax.fori_loop(0, rows_all // 256, weights, line.at)
    line.skip(rows_all // 256)
    load.wait()
    pl.semaphore_wait(free, 3)
    total_out = reduce_shards(copies, parts, *buffers, between=between)

    def body_out(at):
        rows = pl.ds(at, STRIP)
        mine_out[rows, :] = (resid_mid[rows, :] + total_out(at)).astype(jnp.bfloat16)

    strips(size, body_out)
    output_done = hand_out(copies, mine_out, output)
    spread_out = [
        [
            remote(
                source,
                target.at[6 - step],
                small_send.at[kind, 3 + step],
                small_recv.at[kind, 3 + 6 - step],
                peer,
            )
            for step, peer in enumerate(plane)
        ]
        for kind, (source, target) in enumerate(((vec_sum, vec_in), (gain_sum, gain_in)))
    ]
    for kind in small:
        for copy in kind:
            copy.wait_recv()
    vec_sum[...] = sums[...] + vec_z[0] + vec_z[1] + vec_z[2]
    gain_sum[...] = gains[...] + gain_z[0] + gain_z[1] + gain_z[2]
    for kind in spread_out:
        for copy in kind:
            copy.start()
    line.advance(max(line.first + line.lead + RING + 2 - line.at, 0))
    gate_moves = [
        remote(
            grads.at[4 * SEGMENTS, pl.ds(which * half, PACK), :],
            out_gates.at[r, which],
            small_send.at[0, 10 + 2 * place + which],
            small_recv.at[0, 10 + 2 * place + which],
            peer,
        )
        for place, peer in enumerate((twin, side, cross))
        for which in (0, 1)
    ]
    gate_local = [
        pltpu.make_async_copy(
            grads.at[4 * SEGMENTS, pl.ds(which * half, PACK), :],
            out_gates.at[r, which],
            gate_sem.at[which],
        )
        for which in (0, 1)
    ]
    for copy in gate_moves + gate_local:
        copy.start()
    for kind in spread_out:
        for copy in kind:
            copy.wait_recv()
    all_gains = gain_sum[...]
    for place in range(7):
        all_gains = all_gains + gain_in[place]
    out_gain[...] = all_gains
    out_vec[r] = vec_sum[...]
    for step in (0, 1, 2):
        out_vec[(r + 3 - step) % 4] = vec_in[6 - step]
    line.finish()
    grad_done()
    output_done()
    for copy in gate_moves:
        copy.wait_recv()
    for copy in gate_local:
        copy.wait()
    for group in small + spread_out + [gate_moves]:
        for copy in group:
            copy.wait_send()
    copies.finish()


def dot(left, right, dims, kind=jnp.float32):
    return lax.dot_general(left, right, dims, preferred_element_type=jnp.float32).astype(kind)


def local_plane(
    inputs,
    cotangent,
    starts,
    x_proj,
    y_proj,
    out_proj,
    gate_proj,
    up_proj,
    down_proj,
    mix_gain,
    mlp_gain,
    x_bias,
    y_bias,
    conv_w,
    conv_b,
    rec_gate_w,
    in_gate_w,
    rec_gate_b,
    in_gate_b,
    decay_param,
):
    z, r, c = here()
    depth = x_proj.shape[0]
    rec = x_proj.shape[1] // 4
    width = gate_proj.shape[1] // 4
    heads, head = (rec_gate_w.shape[0] // 4, rec_gate_w.shape[1])
    padded = (rec + 127) // 128 * 128
    low = jnp.bfloat16

    def mine(array, size, axis=0):
        return lax.dynamic_slice_in_dim(array, r * size, size, axis)

    mix_in = jnp.concatenate(
        [x_proj.reshape(depth, 4, rec), y_proj.reshape(depth, 4, rec)], axis=2
    ).transpose(1, 0, 2)
    flags = jnp.pad(starts.astype(jnp.float32).reshape(-1, 128), ((0, 6), (0, 0)))
    x_all, s_all, g_all, mix_w, out_w = gather(
        inputs.T, flags, jnp.stack([mix_gain, mlp_gain]), mix_in, out_proj
    )
    tokens, model = x_all.shape
    gain_mix, gain_mlp = (g_all[0:1], g_all[1:2])
    fresh = s_all[:, :2, :].reshape(tokens)
    stale = 1.0 - fresh
    stale_one = jnp.concatenate([jnp.zeros((1,), jnp.float32), stale[:-1]])
    stale_two = jnp.concatenate([jnp.zeros((2,), jnp.float32), stale[:-2]])
    nothing = jnp.zeros_like(fresh)
    masks = jnp.stack(
        [fresh, stale, stale * stale_one, stale * stale_one * stale_two] + [nothing] * 4, axis=1
    )
    vectors = jnp.concatenate(
        [
            x_bias[None],
            y_bias[None],
            conv_w,
            conv_b[None],
            rec_gate_b[None],
            in_gate_b[None],
            -GATE_C * jax.nn.softplus(decay_param)[None],
            -GATE_C * jax.nn.sigmoid(decay_param)[None],
            jnp.zeros((5, x_bias.shape[0]), jnp.float32),
        ],
        axis=0,
    )
    vec = mine(vectors, rec, 1)

    def diagonal(blocks):
        blocks = mine(blocks, heads)
        rows = [jnp.pad(blocks[i], ((0, 0), (i * head, rec - (i + 1) * head))) for i in range(heads)]
        return jnp.concatenate(rows, axis=0)

    rec_w, in_w = (diagonal(rec_gate_w), diagonal(in_gate_w))
    size = tokens // 8
    full = jax.ShapeDtypeStruct((tokens, model), low)
    part = jax.ShapeDtypeStruct((size, model), jnp.float32)
    piece = pltpu.VMEM((size, model), low)
    block = jax.ShapeDtypeStruct((inputs.shape[1], inputs.shape[0]), low)
    weights = (gate_proj, up_proj, down_proj)
    slices = jax.ShapeDtypeStruct((4 * depth, width), low)
    kept = [((tokens, model), low), ((tokens, 2 * rec), jnp.float32), ((tokens, padded), low)]
    kept += [((tokens, rec), kind) for kind in (jnp.float32, low) + (jnp.float32,) * 3]
    row8 = pltpu.VMEM((8, rec), jnp.float32)
    (
        normed_mlp,
        resid_mid,
        c_all,
        gate_w,
        up_w,
        down_w,
        normed_mix,
        pre,
        mixed,
        x_pre,
        conv,
        rec_gate,
        in_gate,
        states,
    ) = vmem_call(
        forward_kernel,
        "forward",
        FORWARD_ID,
        (x_all, masks, vec, rec_w, in_w, mix_w, out_w, gain_mix, gain_mlp),
        [full, part, full] + [slices] * 3 + [jax.ShapeDtypeStruct(*item) for item in kept],
        [pl.ANY, pltpu.VMEM] + [pl.ANY] * 12,
        [pltpu.VMEM(*item) for item in kept]
        + [row8, row8, pltpu.VMEM((tokens, model), low)]
        + reduce_scratch(size, model)
        + [piece, pltpu.SemaphoreType.DMA((8,))],
        80,
        (cotangent.T, *weights),
    )
    gate = dot(normed_mlp, gate_w, CONTRACT_PLAIN)
    up = dot(normed_mlp, up_w, CONTRACT_PLAIN)
    d_activ = dot(c_all, down_w, CONTRACT_PLAIN)
    gelu, slope = gelu_both(gate)
    activ = (gelu * up).astype(low)
    d_gate = (d_activ * up * slope).astype(low)
    d_up = (d_activ * gelu).astype(low)
    d_normed = lax.dot_general(
        d_gate, gate_w, CONTRACT_COLS, preferred_element_type=jnp.float32
    ) + lax.dot_general(d_up, up_w, CONTRACT_COLS, preferred_element_type=jnp.float32)
    def kind_of(array):
        return pltpu.VMEM(array.shape, array.dtype)

    def like(array):
        return jax.ShapeDtypeStruct(array.shape, array.dtype)

    both = jax.ShapeDtypeStruct((tokens, 2 * rec), low)
    held = (normed_mix, pre, mixed, x_pre, conv, rec_gate, in_gate, states)
    wide = (3 * width + 2 * rec + padded) // SEGMENTS
    sums = pltpu.VMEM((16, rec), jnp.float32)
    lines = pltpu.VMEM((2, model), jnp.float32)
    dma = pltpu.SemaphoreType.DMA

    def several(count, kind):
        return pltpu.VMEM((count, *kind.shape), kind.dtype)

    grad_in, output, grads, gates, vec_sums, gains = vmem_call(
        backward_kernel,
        "backward",
        BACKWARD_ID,
        (resid_mid, gain_mlp, gain_mix, masks, vec, rec_w, in_w, mix_w, out_w),
        [
            block,
            block,
            jax.ShapeDtypeStruct((4 * SEGMENTS + 1, depth, wide), low),
            jax.ShapeDtypeStruct((4, 2, PACK, wide), low),
            jax.ShapeDtypeStruct((4, 16, rec), jnp.float32),
            jax.ShapeDtypeStruct((2, model), jnp.float32),
        ],
        [pl.ANY] * 4 + [pltpu.VMEM] * 2,
        line_scratch(depth, wide, CHUNK, PACK // CHUNK)
        + [
            kind_of(full),
            piece,
            piece,
            kind_of(full),
            kind_of(part),
            kind_of(both),
            kind_of(both),
            pltpu.VMEM((24, rec), jnp.float32),
            row8,
        ]
        + [kind_of(item) for item in held]
        + [
            sums,
            lines,
            several(3, sums),
            several(3, lines),
            sums,
            lines,
            several(7, sums),
            several(7, lines),
        ]
        + reduce_scratch(size, model)
        + [
            piece,
            piece,
            dma((15,)),
            dma((2,)),
            dma((2, 16)),
            dma((2, 16)),
            pltpu.SemaphoreType.REGULAR,
        ],
        80,
        (
            d_normed.astype(low),
            dot(activ, down_w, CONTRACT_COLS, low),
            c_all,
            x_all,
            *held,
            dot(normed_mlp, d_gate, CONTRACT_ROWS, low),
            dot(normed_mlp, d_up, CONTRACT_ROWS, low),
            dot(c_all, activ, CONTRACT_ROWS, low),
        ),
    )
    tiles = [[], [], [], [], []]
    for tile, first, length, which, spot in gate_tiles(2 * heads * head):
        tiles[tile].append(gates[:, which, :, spot : spot + length])
    gates = jnp.concatenate([jnp.concatenate(item, axis=2) for item in tiles], axis=1)
    gates = gates.reshape(4, head, 2, heads, head).transpose(2, 0, 3, 1, 4)
    gates = gates.reshape(2, 4 * heads, head, head).astype(jnp.float32)
    vec_sums = vec_sums.transpose(1, 0, 2).reshape(vec_sums.shape[1], 4 * rec)
    gains = lax.dynamic_slice_in_dim(gains, r * depth, depth, 1)

    def columns(*spans):
        return jnp.concatenate(
            [grads[4 * seg + i, :, a : a + n] for i in range(4) for seg, a, n in spans], axis=1
        ).astype(jnp.float32)

    head_width = wide - 2 * width
    after = width - head_width
    grad_out = jnp.concatenate(
        [grads[4 + i, :, after + 2 * rec : after + 3 * rec].T for i in range(4)], axis=0
    ).astype(jnp.float32)
    return (
        output.T,
        grad_in.astype(jnp.float32).T,
        columns((1, after, rec)),
        columns((1, after + rec, rec)),
        grad_out,
        columns((0, 0, width)),
        columns((0, width, width)),
        columns((0, 2 * width, head_width), (1, 0, after)),
        gains[0],
        gains[1],
        vec_sums[0],
        vec_sums[1],
        vec_sums[2:6],
        vec_sums[6],
        gates[0],
        gates[1],
        vec_sums[7],
        vec_sums[8],
        vec_sums[9],
    )


def fits(mesh):
    return mesh.shape["dp"] == 4 and mesh.shape["row"] == 4 and mesh.shape["col"] == 2


def solution(mesh):
    placed = (
        P("row", ("dp", "col")),
        P("row", ("dp", "col")),
        P(("dp", "row")),
        P("row", "col"),
        P("row", "col"),
        P("col", "row"),
        P("row", "col"),
        P("row", "col"),
        P("row", "col"),
        P("row"),
        P("row"),
        P("col"),
        P("col"),
        P(None, "col"),
        P("col"),
        P("col", None, None),
        P("col", None, None),
        P("col"),
        P("col"),
        P("col"),
    )
    return jax.shard_map(
        local_plane if fits(mesh) else local,
        mesh=mesh,
        in_specs=placed,
        out_specs=(
            P("row", ("dp", "col")),
            P("row", ("dp", "col")),
            P("row", "col"),
            P("row", "col"),
            P("col", "row"),
            P("row", "col"),
            P("row", "col"),
            P("row", "col"),
            P("row"),
            P("row"),
            P("col"),
            P("col"),
            P(None, "col"),
            P("col"),
            P("col", None, None),
            P("col", None, None),
            P("col"),
            P("col"),
            P("col"),
        ),
        check_vma=False,
    )
```

```python
import functools

import jax
import jax.numpy as jnp
from jax import lax
from jax.experimental import pallas as pl
from jax.experimental.pallas import tpu as pltpu
from jax.sharding import PartitionSpec as P

MESH = pl.DeviceIdType.MESH

D = 2048


EPS = 1e-06
GATE_C = 8.0
CONTRACT_ROWS = (((0,), (0,)), ((), ()))
CONTRACT_COLS = (((1,), (1,)), ((), ()))
CONTRACT_PLAIN = (((1,), (0,)), ((), ()))


def from_behind(value, axis, by):
    count = lax.axis_size(axis)
    pairs = [(i, i + by) for i in range(count) if 0 <= i + by < count]
    return lax.ppermute(value, axis, pairs)


def carried_in(value, axis, join, neutral, backward):
    count, mine = (lax.axis_size(axis), lax.axis_index(axis))
    pieces = jax.tree.map(lambda part: lax.all_gather(part, axis), value)
    if backward:
        pieces = jax.tree.map(lambda part: part[::-1], pieces)
        mine = count - 1 - mine
    subtotal = jax.tree.map(
        lambda part, zero: jnp.full_like(part, 0) + jnp.asarray(zero, part.dtype), value, neutral
    )

    def hop(position, subtotal):
        longer = join(subtotal, jax.tree.map(lambda part: part[position], pieces))
        return jax.tree.map(lambda new, old: jnp.where(position < mine, new, old), longer, subtotal)

    return lax.fori_loop(0, count - 1, hop, subtotal)


def chain(earlier, later):
    return (earlier[0] * later[0], later[0] * earlier[1] + later[1])


def adjoint_chain(earlier, later):
    return (later[0] * earlier[0], later[1] + later[0] * earlier[1])


def gelu_tanh(values):
    return jax.nn.gelu(values, approximate=True)


def glu_piece(gate_vals, up_vals):
    return gelu_tanh(gate_vals) * up_vals


def causal_conv(values, conv_w, conv_b, segment_ids):
    result = values * conv_w[0] + conv_b
    for offset in range(1, conv_w.shape[0]):
        lagged = jnp.pad(values, ((offset, 0), (0, 0)))[:-offset]
        earlier_ids = jnp.pad(segment_ids, (offset, 0), constant_values=-1)[:-offset]
        result = (
            result + jnp.where((earlier_ids == segment_ids)[:, None], lagged, 0.0) * conv_w[offset]
        )
    return result


def local_recurrence(rec_pre, in_pre, conv_vals, decay_param, flags):
    rec_gate = jax.nn.sigmoid(rec_pre)
    in_gate = jax.nn.sigmoid(in_pre)
    log_keep = -GATE_C * rec_gate * jax.nn.softplus(decay_param)
    keep_rate = jnp.exp(log_keep)
    fresh = (flags == 1)[:, None]
    multiplier = jnp.where(fresh, 1.0, jnp.sqrt(-jnp.expm1(2.0 * log_keep)))
    driven = conv_vals * in_gate * multiplier
    carried = jnp.where(fresh, 0.0, keep_rate)
    cum_keep, states = lax.associative_scan(chain, (carried, driven), axis=0)
    return (cum_keep, states)


def row_sums(values):
    return lax.psum(values, "row")


def norm_forward(values, norm_gain):
    squares = row_sums(jnp.sum(values * values, axis=1))
    inv_rms = lax.rsqrt(squares / D + EPS)
    return (values * inv_rms[:, None] * norm_gain, inv_rms)


def norm_backward(values, inv_rms, norm_gain, incoming):
    scaled = norm_gain * incoming
    dots = row_sums(jnp.sum(scaled * values, axis=1))
    values_grad = inv_rms[:, None] * scaled - values * (inv_rms**3 * dots / D)[:, None]
    gain_grad = jnp.sum(incoming * values * inv_rms[:, None], axis=0)
    return (values_grad, gain_grad)


def gather_edge(values):
    return lax.all_gather(values, "col", axis=0, tiled=True)


def gather_mid(values):
    return lax.all_gather(values, "row", axis=0, tiled=True)


def row_partial(whole, weight, dims):
    return lax.psum_scatter(
        lax.dot_general(whole, weight, dims, preferred_element_type=jnp.float32),
        "row",
        scatter_dimension=0,
        tiled=True,
    )


def col_partial(whole, weight, dims):
    return lax.psum_scatter(
        lax.dot_general(whole, weight, dims, preferred_element_type=jnp.float32),
        "col",
        scatter_dimension=0,
        tiled=True,
    )


def project_in(normed, weight):
    whole = gather_edge(normed)
    result = row_partial(whole, weight, CONTRACT_PLAIN)
    return (result, whole)


def weight_grad(left, right):
    return lax.dot_general(left, right, CONTRACT_ROWS, preferred_element_type=jnp.float32)


def local(
    inputs,
    cotangent,
    starts,
    x_proj,
    y_proj,
    out_proj,
    gate_proj,
    up_proj,
    down_proj,
    mix_gain,
    mlp_gain,
    x_bias,
    y_bias,
    conv_w,
    conv_b,
    rec_gate_w,
    in_gate_w,
    rec_gate_b,
    in_gate_b,
    decay_param,
):
    rows_mid = starts.shape[0]
    rec_width = x_proj.shape[1]
    ff_width = gate_proj.shape[1]
    head_count = rec_gate_w.shape[0]
    margin = conv_w.shape[0] - 1
    mix_weights = jnp.concatenate([x_proj, y_proj], axis=1)
    mlp_weights = jnp.concatenate([gate_proj, up_proj], axis=1)
    cot_rows = cotangent.T
    resid = inputs.astype(jnp.float32).T
    normed_mix, inv_rms_mix = norm_forward(resid, mix_gain)
    normed_mix = normed_mix.astype(jnp.bfloat16)
    pre_both, whole_mix = project_in(normed_mix, mix_weights)
    x_pre = pre_both[:, :rec_width] + x_bias
    y_pre = pre_both[:, rec_width:] + y_bias
    x_tail, flag_tail = from_behind(
        (x_pre[rows_mid - margin :], starts[rows_mid - margin :].astype(jnp.float32)), "row", 1
    )
    ext_flags = jnp.concatenate([flag_tail.astype(jnp.int32), starts])
    ext_ids = jnp.cumsum(ext_flags, dtype=jnp.int32)
    ext_x = jnp.concatenate([x_tail, x_pre], axis=0)

    def conv_piece(values, taps, offsets):
        return causal_conv(values, taps, offsets, ext_ids)[margin:]

    conv_vals, conv_pull = jax.vjp(conv_piece, ext_x, conv_w, conv_b)
    conv_low = conv_vals.astype(jnp.bfloat16)
    conv_heads = conv_low.reshape(rows_mid, head_count, -1)
    rec_pre = (
        jnp.einsum(
            "thk,hkj->thj", conv_heads, rec_gate_w, preferred_element_type=jnp.float32
        ).reshape(rows_mid, rec_width)
        + rec_gate_b
    )
    in_pre = (
        jnp.einsum(
            "thk,hkj->thj", conv_heads, in_gate_w, preferred_element_type=jnp.float32
        ).reshape(rows_mid, rec_width)
        + in_gate_b
    )

    def scan_piece(rec_vals, in_vals, conv_input, decay_vals):
        return local_recurrence(rec_vals, in_vals, conv_input, decay_vals, starts)

    (cum_keep, local_states), scan_pull = jax.vjp(
        scan_piece, rec_pre, in_pre, conv_low.astype(jnp.float32), decay_param
    )
    ones_row = jnp.ones((rec_width,), jnp.float32)
    zeros_row = jnp.zeros((rec_width,), jnp.float32)
    incoming = carried_in(
        (cum_keep[rows_mid - 1], local_states[rows_mid - 1]),
        "row",
        chain,
        (ones_row, zeros_row),
        False,
    )
    state_prev = incoming[1]
    states = local_states + cum_keep * state_prev
    y_act, y_pull = jax.vjp(gelu_tanh, y_pre)
    mixed = (states * y_act).astype(jnp.bfloat16)
    whole_mixed = gather_mid(mixed)
    resid_mid = resid + col_partial(whole_mixed, out_proj, CONTRACT_PLAIN)
    normed_mlp, inv_rms_mlp = norm_forward(resid_mid, mlp_gain)
    normed_mlp = normed_mlp.astype(jnp.bfloat16)
    gate_up, whole_mlp = project_in(normed_mlp, mlp_weights)
    activ, activ_pull = jax.vjp(glu_piece, gate_up[:, :ff_width], gate_up[:, ff_width:])
    activ = activ.astype(jnp.bfloat16)
    whole_activ = gather_mid(activ)
    output = (resid_mid + col_partial(whole_activ, down_proj, CONTRACT_COLS)).astype(jnp.bfloat16)
    cot_whole = gather_edge(cot_rows)
    d_activ = row_partial(cot_whole, down_proj, CONTRACT_PLAIN)
    activ_rows = gather_mid(activ)
    grad_down = weight_grad(cot_whole, activ_rows)
    d_gate, d_up = activ_pull(d_activ)
    d_gate_up = jnp.concatenate([d_gate, d_up], axis=1).astype(jnp.bfloat16)
    d_gate_up_whole = gather_mid(d_gate_up)
    d_normed_mlp = col_partial(d_gate_up_whole, mlp_weights, CONTRACT_COLS)
    mlp_rows = gather_edge(normed_mlp)
    grad_gate_up = weight_grad(mlp_rows, d_gate_up_whole)
    d_norm_mid, grad_mlp_gain = norm_backward(resid_mid, inv_rms_mlp, mlp_gain, d_normed_mlp)
    d_resid_mid = cot_rows.astype(jnp.float32) + d_norm_mid
    d_branch = d_resid_mid.astype(jnp.bfloat16)
    branch_whole = gather_edge(d_branch)
    d_mixed = row_partial(branch_whole, out_proj, CONTRACT_COLS)
    mixed_rows = gather_mid(mixed)
    grad_out = weight_grad(mixed_rows, branch_whole)
    d_state = d_mixed * y_act
    (d_y_pre,) = y_pull(d_mixed * states)
    own_sens = jnp.sum(d_state * cum_keep, axis=0)
    outgoing = carried_in(
        (cum_keep[rows_mid - 1], own_sens), "row", adjoint_chain, (ones_row, zeros_row), True
    )
    d_total = d_state + jnp.pad(outgoing[1][None, :], ((rows_mid - 1, 0), (0, 0)))
    d_rec_pre, d_in_pre, d_conv_direct, grad_decay = scan_pull((d_total * state_prev, d_total))
    d_rec_low = d_rec_pre.astype(jnp.bfloat16)
    d_in_low = d_in_pre.astype(jnp.bfloat16)
    d_rec_heads = d_rec_low.reshape(rows_mid, head_count, -1)
    d_in_heads = d_in_low.reshape(rows_mid, head_count, -1)
    d_conv = d_conv_direct + jnp.einsum(
        "thj,hkj->thk", d_rec_heads, rec_gate_w, preferred_element_type=jnp.float32
    ).reshape(rows_mid, rec_width)
    d_conv = d_conv + jnp.einsum(
        "thj,hkj->thk", d_in_heads, in_gate_w, preferred_element_type=jnp.float32
    ).reshape(rows_mid, rec_width)
    grad_rec_w = jnp.einsum(
        "thk,thj->hkj", conv_heads, d_rec_heads, preferred_element_type=jnp.float32
    )
    grad_in_w = jnp.einsum(
        "thk,thj->hkj", conv_heads, d_in_heads, preferred_element_type=jnp.float32
    )
    grad_rec_b = jnp.sum(d_rec_low.astype(jnp.float32), axis=0)
    grad_in_b = jnp.sum(d_in_low.astype(jnp.float32), axis=0)
    d_ext, grad_conv_w, grad_conv_b = conv_pull(d_conv)
    d_from_next = from_behind(d_ext[:margin], "row", -1)
    d_x_pre = d_ext[margin:] + jnp.pad(d_from_next, ((rows_mid - margin, 0), (0, 0)))
    d_pre = jnp.concatenate([d_x_pre, d_y_pre], axis=1).astype(jnp.bfloat16)
    bias_sums = jnp.sum(d_pre.astype(jnp.float32), axis=0)
    d_pre_whole = gather_mid(d_pre)
    d_normed_mix = col_partial(d_pre_whole, mix_weights, CONTRACT_COLS)
    mix_rows = gather_edge(normed_mix)
    grad_mix = weight_grad(mix_rows, d_pre_whole)
    d_norm_in, grad_mix_gain = norm_backward(resid, inv_rms_mix, mix_gain, d_normed_mix)
    inputs_grad = d_resid_mid + d_norm_in
    grad_mix, grad_out, grad_gate_up, grad_down = (
        lax.psum(grad_mix.astype(jnp.bfloat16), "dp").astype(jnp.float32),
        lax.psum(grad_out.astype(jnp.bfloat16), "dp").astype(jnp.float32),
        lax.psum(grad_gate_up.astype(jnp.bfloat16), "dp").astype(jnp.float32),
        lax.psum(grad_down.astype(jnp.bfloat16), "dp").astype(jnp.float32),
    )
    (
        bias_sums,
        grad_conv_w,
        grad_conv_b,
        grad_rec_w,
        grad_in_w,
        grad_rec_b,
        grad_in_b,
        grad_decay,
    ) = (
        lax.psum(bias_sums.astype(jnp.bfloat16), ("dp", "row")).astype(jnp.float32),
        lax.psum(grad_conv_w.astype(jnp.bfloat16), ("dp", "row")).astype(jnp.float32),
        lax.psum(grad_conv_b.astype(jnp.bfloat16), ("dp", "row")).astype(jnp.float32),
        lax.psum(grad_rec_w.astype(jnp.bfloat16), ("dp", "row")).astype(jnp.float32),
        lax.psum(grad_in_w.astype(jnp.bfloat16), ("dp", "row")).astype(jnp.float32),
        lax.psum(grad_rec_b.astype(jnp.bfloat16), ("dp", "row")).astype(jnp.float32),
        lax.psum(grad_in_b.astype(jnp.bfloat16), ("dp", "row")).astype(jnp.float32),
        lax.psum(grad_decay.astype(jnp.bfloat16), ("dp", "row")).astype(jnp.float32),
    )
    grad_mix_gain, grad_mlp_gain = lax.psum((grad_mix_gain, grad_mlp_gain), ("dp", "col"))
    return (
        output.T,
        inputs_grad.T,
        grad_mix[:, :rec_width],
        grad_mix[:, rec_width:],
        grad_out,
        grad_gate_up[:, :ff_width],
        grad_gate_up[:, ff_width:],
        grad_down,
        grad_mix_gain,
        grad_mlp_gain,
        bias_sums[:rec_width],
        bias_sums[rec_width:],
        grad_conv_w,
        grad_conv_b,
        grad_rec_w,
        grad_in_w,
        grad_rec_b,
        grad_in_b,
        grad_decay,
    )


GATHER_ID, FORWARD_ID, BACKWARD_ID = (0, 1, 2)
BLOCK = 128
VMEM_BYTES = 60 << 20


def one_minus_exp(rate):
    series = rate * (1.0 - rate * (0.5 - rate * (1.0 / 6.0 - rate * (1.0 / 24.0 - rate / 120.0))))
    return jnp.where(rate < 0.1, series, 1.0 - jnp.exp(-rate))


GELU_C = 0.7978845608028654


def gelu_both(values):
    squared = values * values
    inner = jnp.tanh(GELU_C * values * (1.0 + 0.044715 * squared))
    value = 0.5 * values * (1.0 + inner)
    slope = 0.5 * (1.0 + inner) + 0.5 * values * (1.0 - inner * inner) * GELU_C * (
        1.0 + 3.0 * 0.044715 * squared
    )
    return (value, slope)


def down_rows(values, by):
    return pltpu.roll(values, by, 0)


def up_rows(values, by):
    return pltpu.roll(values, values.shape[0] - by, 0)


def scan_down(keep, add):
    rows = keep.shape[0]
    position = lax.broadcasted_iota(jnp.int32, keep.shape, 0)
    step = 1
    while step < rows:
        if step < 8:
            inside = position >= step
            before_keep = jnp.where(inside, down_rows(keep, step), 1.0)
            before_add = jnp.where(inside, down_rows(add, step), 0.0)
            add = add + keep * before_add
            keep = keep * before_keep
        else:
            add = jnp.concatenate([add[:step], add[step:] + keep[step:] * add[:-step]], axis=0)
            keep = jnp.concatenate([keep[:step], keep[step:] * keep[:-step]], axis=0)
        step *= 2
    return (keep, add)


def scan_up(keep, add):
    rows = keep.shape[0]
    position = lax.broadcasted_iota(jnp.int32, keep.shape, 0)
    step = 1
    while step < rows:
        if step < 8:
            inside = position < rows - step
            after_keep = jnp.where(inside, up_rows(keep, step), 1.0)
            after_add = jnp.where(inside, up_rows(add, step), 0.0)
            add = add + keep * after_add
            keep = keep * after_keep
        else:
            add = jnp.concatenate([add[:-step] + keep[:-step] * add[step:], add[-step:]], axis=0)
            keep = jnp.concatenate([keep[:-step] * keep[step:], keep[-step:]], axis=0)
        step *= 2
    return (keep, add)


def mixer_forward_step(
    pre, marks, vec, rec_w, in_w, mixed, x_pre, conv, rec_gate, in_gate, states, tail, carry
):
    width = x_pre.shape[1]
    x = pre[:, :width] + vec[0:1, :]
    x_pre[...] = x
    longer = jnp.concatenate([tail[...], x], axis=0)
    tail[...] = x[BLOCK - 8 :]
    total = x * vec[2:3, :] + vec[6:7, :]
    for tap in range(1, 4):
        total = total + marks[:, tap : tap + 1] * down_rows(longer, tap)[8:] * vec[
            2 + tap : 3 + tap, :
        ]
    low = total.astype(jnp.bfloat16)
    conv[...] = low
    rec = jax.nn.sigmoid(
        jnp.dot(low, rec_w[...], preferred_element_type=jnp.float32) + vec[7:8, :]
    )
    inn = jax.nn.sigmoid(
        jnp.dot(low, in_w[...], preferred_element_type=jnp.float32) + vec[8:9, :]
    )
    rec_gate[...] = rec
    in_gate[...] = inn
    log_keep = rec * vec[9:10, :]
    fresh = marks[:, 0:1]
    scale = jnp.where(fresh > 0.5, 1.0, jnp.sqrt(one_minus_exp(-2.0 * log_keep)))
    driven = low.astype(jnp.float32) * inn * scale
    keep, add = scan_down(jnp.exp(log_keep) * (1.0 - fresh), driven)
    state = add + keep * carry[0:1, :]
    carry[...] = jnp.broadcast_to(state[BLOCK - 1 :, :], carry.shape)
    states[...] = state
    y = pre[:, width:] + vec[1:2, :]
    mixed[:, :width] = (state * gelu_both(y)[0]).astype(jnp.bfloat16)
    mixed[:, width:] = jnp.zeros((BLOCK, mixed.shape[1] - width), jnp.bfloat16)


def mixer_backward_step(
    incoming,
    pre,
    marks,
    vec,
    rec_w,
    in_w,
    x_pre,
    x_before,
    conv,
    rec_gate,
    in_gate,
    states,
    state_before,
    d_pre,
    d_gates,
    sums,
    edge,
    carry,
):
    width = x_pre.shape[1]
    position = lax.broadcasted_iota(jnp.int32, (BLOCK, width), 0)
    fresh = marks[:, 0:1]
    stale = 1.0 - fresh
    gelu, slope = gelu_both(pre[:, width:] + vec[1:2, :])
    state = states[...]
    d_y = (incoming * state * slope).astype(jnp.bfloat16)
    rec, inn = (rec_gate[...], in_gate[...])
    conv_vals = conv[...].astype(jnp.float32)
    log_keep = rec * vec[9:10, :]
    keep_rate = jnp.exp(log_keep)
    scale = jnp.where(fresh > 0.5, 1.0, jnp.sqrt(one_minus_exp(-2.0 * log_keep)))
    carried = keep_rate * stale
    after = jnp.where(position == BLOCK - 1, carry[1:2, :], up_rows(carried, 1))
    keep, add = scan_up(after, incoming * gelu)
    adjoint = add + keep * carry[0:1, :]
    carry[0:1, :] = adjoint[0:1]
    carry[1:2, :] = carried[0:1]
    earlier = jnp.where(position == 0, state_before[7:8, :], down_rows(state, 1))
    drive = adjoint * scale
    d_log = stale * (
        adjoint * earlier * keep_rate
        - adjoint * inn * conv_vals * keep_rate * keep_rate / scale
    )
    d_rec = (d_log * vec[9:10, :] * rec * (1.0 - rec)).astype(jnp.bfloat16)
    d_in = (drive * conv_vals * inn * (1.0 - inn)).astype(jnp.bfloat16)
    d_gates[:, :width] = d_rec
    d_gates[:, width:] = d_in
    d_conv = drive * inn
    d_conv = d_conv + lax.dot_general(
        d_rec, rec_w[...], CONTRACT_COLS, preferred_element_type=jnp.float32
    )
    d_conv = d_conv + lax.dot_general(
        d_in, in_w[...], CONTRACT_COLS, preferred_element_type=jnp.float32
    )
    x = x_pre[...]
    longer = jnp.concatenate([x_before[...], x], axis=0)

    def column(values):
        return jnp.sum(values, axis=0, keepdims=True)

    d_x = d_conv * vec[2:3, :]
    taps = [column(d_conv * x)]
    for tap in range(1, 4):
        piece = marks[:, tap : tap + 1] * d_conv
        taps.append(column(piece * down_rows(longer, tap)[8:]))
        beyond = jnp.concatenate([piece, edge[8 * tap - 8 : 8 * tap, :]], axis=0)
        d_x = d_x + vec[2 + tap : 3 + tap, :] * up_rows(beyond, tap)[:BLOCK]
        edge[8 * tap - 8 : 8 * tap, :] = piece[:8]
    d_x = d_x.astype(jnp.bfloat16)
    d_pre[:, :width] = d_x
    d_pre[:, width:] = d_y
    pieces = (
        [column(d_x.astype(jnp.float32)), column(d_y.astype(jnp.float32))]
        + taps
        + [
            column(d_conv),
            column(d_rec.astype(jnp.float32)),
            column(d_in.astype(jnp.float32)),
            column(d_log * rec) * vec[10:11, :],
        ]
    )
    for place, piece in enumerate(pieces):
        sums[place : place + 1, :] += piece


def here():
    return (lax.axis_index("dp"), lax.axis_index("row"), lax.axis_index("col"))


def flip(index):
    return index + 1 - 2 * (index % 2)


def across(row):
    return (row + 2) % 4


def greet(peers):
    barrier = pltpu.get_barrier_semaphore()
    for peer in peers:
        pl.semaphore_signal(barrier, inc=1, device_id=peer, device_id_type=MESH)
    pl.semaphore_wait(barrier, len(peers))


class Copies:
    def __init__(self, send, recv):
        self.send, self.recv, self.used, self.sent = (send, recv, 0, [])

    def make(self, source, target, device):
        place = self.used
        self.used += 1
        if device is None:
            copy = pltpu.make_async_copy(source, target, self.recv.at[place])
        else:
            copy = pltpu.make_async_remote_copy(
                src_ref=source,
                dst_ref=target,
                send_sem=self.send.at[place],
                recv_sem=self.recv.at[place],
                device_id=device,
                device_id_type=MESH,
            )
            self.sent.append(copy)
        return copy

    def go(self, source, target, device):
        copy = self.make(source, target, device)
        copy.start()
        return copy

    def finish(self):
        for copy in self.sent:
            copy.wait_send()
        self.sent = []


def arrived(copy):
    copy.wait_recv()


def spread(copies, own, place, halves, between=lambda: None):
    z, r, c = here()
    twin, side, top = ((z, flip(r), c), (z, across(r), c), (z, r, 1 - c))
    to_side = copies.go(own, place(r, c), side)
    to_top = copies.go(own, place(r, c), top)
    to_twin = copies.go(own, place(r, c), twin)
    between()
    arrived(to_side)
    from_side = place(across(r), c)
    on_top = copies.go(halves(from_side, 0), halves(from_side, 0), top)
    late = [to_twin, copies.go(from_side, from_side, twin)]
    between()
    arrived(to_top)
    from_top = place(r, 1 - c)
    on_side = copies.go(halves(from_top, 1), halves(from_top, 1), side)
    late.append(copies.go(from_top, from_top, twin))
    far = place(across(r), 1 - c)
    between()
    for half, copy in enumerate((on_top, on_side)):
        arrived(copy)
        late.append(copies.go(halves(far, half), halves(far, half), twin))
    return late


def spread_tall(copies, own, place, between=lambda: None):
    z, r, c = here()
    twin, side, top = ((z, flip(r), c), (z, across(r), c), (z, r, 1 - c))
    to_side = copies.go(own, place(r, c), side)
    to_top = copies.go(own, place(r, c), top)
    late = [copies.go(own, place(r, c), twin)]
    between()
    arrived(to_side)
    from_side = place(across(r), c)
    on_top = copies.go(from_side, from_side, top)
    late.append(copies.go(from_side, from_side, twin))
    between()
    arrived(to_top)
    from_top = place(r, 1 - c)
    late.append(copies.go(from_top, from_top, twin))
    between()
    arrived(on_top)
    far = place(across(r), 1 - c)
    late.append(copies.go(far, far, twin))
    return late


def part(start, size, step):
    return pl.ds(pl.multiple_of(start * step, step), size)


class Moves:
    def __init__(self, copies, matrices, cuts):
        z, r, c = here()
        mine = z % 2
        sides = ((z, across(r), c), (z, flip(across(r)), c))
        pair = (flip(z), r, c)
        self.groups, self.locals, self.late = ([], [], [])
        self.begun, self.ended = (0, 0)

        def piece(ref, size, cut):
            length = size // 2 // cuts
            return ref.at[part(mine * cuts + cut, length, length), :]

        for source, target, size in matrices:
            for cut in range(cuts):
                group = []
                for peer in sides:
                    spot = piece(target(peer[1]), size, cut)
                    group.append(
                        (
                            copies.make(
                                piece(source(peer[1]), size, cut), piece(target(r), size, cut), peer
                            ),
                            copies.make(spot, spot, pair),
                        )
                    )
                self.groups.append(group)
        for source, target, size in matrices:
            self.locals.append(copies.go(source(r), target(r), None))
            self.late.append(copies.go(source(flip(r)), target(r), (z, flip(r), c)))

    def step(self):
        if self.begun - self.ended == 2 or self.begun == len(self.groups):
            if self.ended < self.begun:
                for first, second in self.groups[self.ended]:
                    arrived(first)
                    second.start()
                self.ended += 1
        if self.begun < len(self.groups):
            for first, _ in self.groups[self.begun]:
                first.start()
            self.begun += 1

    def finish(self):
        while self.ended < len(self.groups):
            self.step()
        for group in self.groups:
            for _, second in group:
                arrived(second)
        for copy in self.late:
            arrived(copy)
        for copy in self.locals:
            copy.wait()


def block_of(ref, rows, columns):
    return lambda row, col: ref.at[part(col, rows, rows), part(row, columns, columns)]


def halves_of(rows):
    return lambda ref, which: ref.at[pl.ds(which * (rows // 2), rows // 2), :]


def mlp_matrices(sources, targets):
    depth, width = (sources[0].shape[0], sources[0].shape[1] // 4)
    return [
        (
            lambda to, source=source: source.at[:, part(to, width, width)],
            lambda of, target=target: target.at[part(of, depth, depth), :],
            depth,
        )
        for source, target in zip(sources, targets)
    ]


def gather_kernel(
    x_in,
    c_in,
    s_in,
    g_in,
    x_proj,
    y_proj,
    out_in,
    x_all,
    c_all,
    s_all,
    g_all,
    mix_all,
    out_all,
    x_here,
    y_here,
    mix_in,
    load_sem,
    send,
    recv,
):
    z, r, c = here()
    twin, side, cross, top, pair = (
        (z, flip(r), c),
        (z, across(r), c),
        (z, flip(across(r)), c),
        (z, r, 1 - c),
        (flip(z), r, c),
    )
    loads = [
        pltpu.make_async_copy(source, target, load_sem.at[place])
        for place, (source, target) in enumerate(((x_proj, x_here), (y_proj, y_here)))
    ]
    for copy in loads:
        copy.start()
    greet((twin, side, cross, top, pair))
    copies = Copies(send, recv)
    rows, columns = x_in.shape
    depth, rec = (mix_in.shape[1], out_in.shape[0] // 4)
    matrices = [
        (lambda to: mix_in.at[to], lambda of: mix_all.at[part(of, depth, depth), :], depth),
        (
            lambda to: out_in.at[part(to, rec, rec), :],
            lambda of: out_all.at[:, part(of, columns, columns)],
            rec,
        ),
    ]
    moves = []

    def between():
        if not moves:
            for copy in loads:
                copy.wait()

            def body(at):
                strip = pl.ds(at, STRIP)
                x, y = (x_here[strip, :], y_here[strip, :])
                for to in range(4):
                    span = slice(to * rec, (to + 1) * rec)
                    mix_in[to, strip, :] = jnp.concatenate([x[:, span], y[:, span]], axis=1)

            strips(depth, body)
            moves.append(Moves(copies, matrices, 2))
        moves[0].step()

    small = g_all.at[:, part(r, depth, depth)]
    late = spread_tall(copies, x_in, block_of(x_all, rows, columns), between)
    locals_ = [
        copies.go(x_in, block_of(x_all, rows, columns)(r, c), None),
        copies.go(c_in, block_of(c_all, rows, columns)(r, c), None),
        copies.go(s_in, s_all.at[r], None),
        copies.go(g_in, small, None),
    ]
    for peer in (twin, side, cross):
        late.append(copies.go(s_in, s_all.at[r], peer))
        late.append(copies.go(g_in, small, peer))
    late.extend(spread_tall(copies, c_in, block_of(c_all, rows, columns), between))
    moves[0].finish()
    for copy in late:
        arrived(copy)
    for copy in locals_:
        copy.wait()
    copies.finish()


def gather(x_in, c_in, s_in, g_in, x_proj, y_proj, out_in):
    rows, columns = x_in.shape
    depth, wide = x_proj.shape

    def shape(*dims, kind=jnp.bfloat16):
        return jax.ShapeDtypeStruct(dims, kind)

    outs = [
        shape(2 * rows, 4 * columns),
        shape(2 * rows, 4 * columns),
        shape(4, *s_in.shape, kind=s_in.dtype),
        shape(g_in.shape[0], 4 * depth, kind=g_in.dtype),
        shape(4 * depth, wide // 2),
        shape(out_in.shape[0] // 4, 4 * columns),
    ]
    dma = pltpu.SemaphoreType.DMA
    return pl.pallas_call(
        gather_kernel,
        in_specs=[pl.BlockSpec(memory_space=pltpu.HBM)] * 7,
        out_specs=[pl.BlockSpec(memory_space=pltpu.HBM)] * 6,
        out_shape=outs,
        scratch_shapes=[
            pltpu.VMEM((depth, wide), jnp.bfloat16),
            pltpu.VMEM((depth, wide), jnp.bfloat16),
            pltpu.VMEM((4, depth, wide // 2), jnp.bfloat16),
            dma((2,)),
            dma((64,)),
            dma((64,)),
        ],
        compiler_params=pltpu.CompilerParams(
            collective_id=GATHER_ID, has_side_effects=True, vmem_limit_bytes=60 << 20
        ),
        name="gather",
    )(x_in, c_in, s_in, g_in, x_proj, y_proj, out_in)


STRIP = 16


def strips(count, body):
    def run(index, nothing):
        body(pl.multiple_of(index * STRIP, STRIP))
        return nothing

    lax.fori_loop(0, count // STRIP, run, 0)


def token_shard(row, col):
    return col * 4 + row


def reduce_shards(
    copies, parts, twin_in, sums, side_in, top_in, hop_in, between=lambda: None, tall=False
):
    z, r, c = here()
    twin, side, top = ((z, flip(r), c), (z, across(r), c), (z, r, 1 - c))
    size = side_in.shape[0]
    half = size // 2

    def shard(row, col):
        return pl.multiple_of(token_shard(row, col) * size, size)

    spots = [(across(r), 1 - c), (across(r), c), (r, 1 - c), (r, c)]
    from_twin = [
        copies.go(parts.at[pl.ds(shard(flip(row), col), size), :], twin_in.at[place], twin)
        for place, (row, col) in enumerate(spots)
    ]

    def add_twin(place):
        arrived(from_twin[place])
        start = shard(*spots[place])

        def body(at):
            total = parts[pl.ds(start + at, STRIP), :].astype(jnp.float32) + twin_in[
                place, pl.ds(at, STRIP), :
            ].astype(jnp.float32)
            sums[place, pl.ds(at, STRIP), :] = total.astype(jnp.bfloat16)

        strips(size, body)

    def add_hop(place, which, hop):
        def body(at):
            rows = pl.ds(which * half + at, STRIP)
            total = sums[place, rows, :].astype(jnp.float32) + hop_in[
                hop, pl.ds(at, STRIP), :
            ].astype(jnp.float32)
            sums[place, rows, :] = total.astype(jnp.bfloat16)

        strips(half, body)

    def rows_of(ref, which):
        return ref.at[pl.ds(which * half, half), :]

    def total(at):
        rows = pl.ds(at, STRIP)
        return (
            sums[3, rows, :].astype(jnp.float32)
            + side_in[rows, :].astype(jnp.float32)
            + top_in[rows, :].astype(jnp.float32)
        )

    add_twin(0)
    if tall:
        hops = [copies.go(rows_of(sums.at[0], k), hop_in.at[k], top) for k in (0, 1)]
        add_twin(2)
        to_top = copies.go(sums.at[2], top_in, top)
        add_twin(1)
        add_twin(3)
        between()
        to_side = []
        for k in (0, 1):
            arrived(hops[k])
            add_hop(1, k, k)
            to_side.append(copies.go(rows_of(sums.at[1], k), rows_of(side_in, k), side))
        between()
        for copy in [to_top, *to_side]:
            arrived(copy)
        return total
    hop_side = copies.go(rows_of(sums.at[0], 0), hop_in.at[0], side)
    hop_top = copies.go(rows_of(sums.at[0], 1), hop_in.at[1], top)
    add_twin(1)
    waits = [copies.go(rows_of(sums.at[1], 0), rows_of(side_in, 0), side)]
    add_twin(2)
    waits.append(copies.go(rows_of(sums.at[2], 1), rows_of(top_in, 1), top))
    add_twin(3)
    between()
    arrived(hop_top)
    add_hop(1, 1, 1)
    waits.append(copies.go(rows_of(sums.at[1], 1), rows_of(side_in, 1), side))
    arrived(hop_side)
    add_hop(2, 0, 0)
    waits.append(copies.go(rows_of(sums.at[2], 0), rows_of(top_in, 0), top))
    between()
    for copy in waits:
        arrived(copy)
    return total


def reduce_scratch(size, width):
    return [
        pltpu.VMEM((4, size, width), jnp.bfloat16),
        pltpu.VMEM((4, size, width), jnp.bfloat16),
        pltpu.VMEM((size, width), jnp.bfloat16),
        pltpu.VMEM((size, width), jnp.bfloat16),
        pltpu.VMEM((2, size // 2, width), jnp.bfloat16),
    ]


def near():
    z, r, c = here()
    return ((z, flip(r), c), (z, across(r), c), (z, r, 1 - c))


def spread_rows(copies, mine, full, between=lambda: None, tall=False):
    z, r, c = here()
    size = mine.shape[0]
    half = size // 2

    def place(row, col):
        return full.at[pl.ds(pl.multiple_of(token_shard(row, col) * size, size), size), :]

    local = copies.go(mine, place(r, c), None)
    if tall:
        late = spread_tall(copies, mine, place, between)
    else:
        late = spread(
            copies, mine, place, lambda ref, which: ref.at[pl.ds(which * half, half), :], between
        )
    for copy in late:
        arrived(copy)
    local.wait()


def mark_rows(flags, tail):
    stale = 1.0 - flags
    longer = jnp.concatenate([tail[...], stale], axis=0)
    tail[...] = stale[BLOCK - 8 :]
    pair = stale * down_rows(longer, 1)[8:]
    triple = pair * down_rows(longer, 2)[8:]
    lane = lax.broadcasted_iota(jnp.int32, flags.shape, 1)
    return jnp.where(lane == 0, flags, jnp.where(lane == 1, stale, jnp.where(lane == 2, pair, triple)))


def forward_kernel(vec, rec_w, in_w, gains, *refs):
    x_in, s_in, mix_in, out_in = refs[:4]
    mlp_in, outs, scratch = (refs[4:7], refs[7:21], refs[21:])
    full, resid_mid = outs[:2]
    mlp_all, kept_out = (outs[2:5], outs[5:])
    kept, (tail, carry, parts), (*buffers, mine, kept_sem, send, recv) = (
        scratch[:9],
        scratch[9:12],
        scratch[12:],
    )
    x_all, flags, mix_w, out_w, mark_tail, load_sem, *buffers = buffers
    normed, pre, mixed, *saved, masks = kept
    loads = [
        pltpu.make_async_copy(source, target, load_sem.at[8 + place])
        for place, (source, target) in enumerate(
            ((mix_in, mix_w), (s_in, flags), (out_in, out_w))
        )
    ]

    def load_rows(index):
        rows = pl.ds(pl.multiple_of(index * BLOCK, BLOCK), BLOCK)
        return pltpu.make_async_copy(x_in.at[rows, :], x_all.at[rows, :], load_sem.at[index])

    load_rows(0).start()
    for copy in loads:
        copy.start()
    for index in range(1, x_all.shape[0] // BLOCK):
        load_rows(index).start()
    z, r, c = here()
    greet((*near(), (z, flip(across(r)), c), (flip(z), r, c)))
    copies = Copies(send, recv)
    moves = Moves(copies, mlp_matrices(mlp_in, mlp_all), 2)
    moves.step()
    moves.step()
    for copy in loads:
        copy.wait()
    mark_tail[...] = jnp.zeros_like(mark_tail)
    tail[...] = jnp.zeros_like(tail)
    carry[...] = jnp.zeros_like(carry)

    def block(index, nothing):
        start = pl.multiple_of(index * BLOCK, BLOCK)
        rows = pl.ds(start, BLOCK)
        for turn in (3, 6):

            @pl.when(index == turn)
            def _():
                moves.step()

        load_rows(index).wait()
        marks = mark_rows(flags[rows, :8], mark_tail)
        masks[rows, :] = marks

        def norm(at):
            strip = pl.ds(start + at, STRIP)
            values = x_all[strip, :].astype(jnp.float32)
            scale = lax.rsqrt(jnp.mean(values * values, axis=1, keepdims=True) + EPS)
            normed[strip, :] = (values * scale * gains[0:1, :]).astype(jnp.bfloat16)

        strips(BLOCK, norm)
        pre[rows, :] = jnp.dot(normed[rows, :], mix_w[...], preferred_element_type=jnp.float32)
        mixer_forward_step(
            pre.at[rows, :],
            marks,
            vec,
            rec_w,
            in_w,
            mixed.at[rows, :],
            *[ref.at[rows, :] for ref in saved],
            tail,
            carry,
        )
        width = rec_w.shape[0]
        parts[rows, :] = jnp.dot(
            mixed[rows, :width], out_w[...], preferred_element_type=jnp.float32
        ).astype(jnp.bfloat16)
        return nothing

    lax.fori_loop(0, x_all.shape[0] // BLOCK, block, 0)
    keeping = [
        pltpu.make_async_copy(source, target, kept_sem.at[place])
        for place, (source, target) in enumerate(zip(kept, kept_out))
    ]
    for copy in keeping:
        copy.start()
    total = reduce_shards(copies, parts, *buffers, between=moves.step, tall=True)
    size = mine.shape[0]
    start = pl.multiple_of(token_shard(r, c) * size, size)

    def body(at):
        rows = pl.ds(at, STRIP)
        values = x_all[pl.ds(start + at, STRIP), :].astype(jnp.float32) + total(at)
        resid_mid[rows, :] = values
        scale = lax.rsqrt(jnp.mean(values * values, axis=1, keepdims=True) + EPS)
        mine[rows, :] = (values * scale * gains[1:2, :]).astype(jnp.bfloat16)

    strips(size, body)
    spread_rows(copies, mine, full, moves.step, tall=True)
    moves.finish()
    for copy in keeping:
        copy.wait()
    copies.finish()


def norm_pull(values, gain, incoming):
    scale = lax.rsqrt(jnp.mean(values * values, axis=1, keepdims=True) + EPS)
    scaled = gain * incoming
    dots = jnp.sum(scaled * values, axis=1, keepdims=True)
    grad = scale * scaled - values * (scale * scale * scale * dots / values.shape[1])
    return (grad, jnp.sum(incoming * values * scale, axis=0, keepdims=True))


def vmem_call(kernel, name, place, arrays, outs, spaces, scratch, count, loose=()):
    return pl.pallas_call(
        kernel,
        in_specs=[pl.BlockSpec(memory_space=pltpu.VMEM)] * len(arrays)
        + [pl.BlockSpec(memory_space=pltpu.HBM)] * len(loose),
        out_specs=[pl.BlockSpec(memory_space=space) for space in spaces],
        out_shape=outs,
        scratch_shapes=scratch
        + [pltpu.SemaphoreType.DMA((count,)), pltpu.SemaphoreType.DMA((count,))],
        compiler_params=pltpu.CompilerParams(
            collective_id=place, has_side_effects=True, vmem_limit_bytes=VMEM_BYTES
        ),
        name=name,
    )(*arrays, *loose)


AHEAD = 3
DEPTH = 4
SUM_LAG = 1
HAND_LAG = 3
LAG = 4
RING = 9
SEGMENTS = 2


def run_loop(first, last, body):
    def run(index, nothing):
        body(index)
        return nothing

    lax.fori_loop(first, last, run, 0)


def remote(source, target, sender, receiver, device):
    return pltpu.make_async_remote_copy(
        src_ref=source,
        dst_ref=target,
        send_sem=sender,
        recv_sem=receiver,
        device_id=device,
        device_id_type=MESH,
    )


class Line:
    def __init__(self, own, left, right, out, sems, lead):
        self.own, self.left, self.right, self.out, self.lead = (own, left, right, out, lead)
        (
            self.end_send,
            self.low_recv,
            self.high_recv,
            self.out_recv,
            self.mid_send,
            self.first_send,
            self.last_send,
            self.hand_send,
            self.on_send,
        ) = sems
        z, r, c = here()
        self.chunk = left.shape[1]
        self.rows = out.shape[1]
        self.half = self.rows // 2
        self.per = self.half // self.chunk
        self.first = 4 * self.per
        self.chunks = 4 * SEGMENTS * self.per + lead
        self.total = self.chunks + LAG
        self.at = 0
        self.ahead = 0
        self.is_end = (z == 0) | (z == 3)
        self.near_z = (jnp.where(z == 0, 1, 2), r, c)
        self.outer = (jnp.where(z == 1, 0, 3), r, c)
        self.other = (3 - z, r, c)

    def extra(self, index):
        return (index >= self.first) & (index < self.first + self.lead)

    def spot(self, index):
        later = index >= self.first + self.lead
        plain = index - jnp.where(later, self.lead, 0)
        step = jnp.where(self.extra(index), 0, plain // self.per)
        strip = jnp.where(self.extra(index), index - self.first, plain % self.per)
        return (step // 4, step % 4, strip)

    def peer_row(self, index):
        r = here()[1]
        step = self.spot(index)[1]
        return (r // 2 + step // 2) % 2 * 2 + (r % 2 + step % 2) % 2

    def stays(self, index):
        return self.spot(index)[1] == 0

    def span(self, index, which):
        segment, _, strip = self.spot(index)
        start = (segment * 4 + self.peer_row(index)) * self.rows + which * self.half
        outside = SEGMENTS * 4 * self.rows + which * self.lead * self.chunk
        start = jnp.where(self.extra(index), outside, start)
        return pl.ds(pl.multiple_of(start + strip * self.chunk, self.chunk), self.chunk)

    def own_at(self, index, which):
        return self.own.at[self.span(index, which), :]

    def out_at(self, index, which, row):
        segment, _, strip = self.spot(index)
        place = jnp.where(self.extra(index), 4 * SEGMENTS, segment * 4 + row)
        start = pl.multiple_of(which * self.half + strip * self.chunk, self.chunk)
        return self.out.at[place, pl.ds(start, self.chunk), :]

    def end_sends(self, index):
        low = here()[0] // 3
        return (
            remote(
                self.own_at(index, low),
                self.left.at[index % RING],
                self.end_send.at[0, index],
                self.low_recv.at[index],
                self.near_z,
            ),
            remote(
                self.own_at(index, 1 - low),
                self.right.at[1, index % RING],
                self.end_send.at[1, index],
                self.high_recv.at[1, index],
                self.near_z,
            ),
        )

    def to_other(self, index):
        low = here()[0] - 1
        return remote(
            self.own_at(index, 1 - low),
            self.right.at[0, index % RING],
            self.mid_send.at[index],
            self.high_recv.at[0, index],
            self.other,
        )

    def from_outer(self, index):
        low = here()[0] - 1
        return (
            remote(
                self.own_at(index, low),
                self.left.at[index % RING],
                self.mid_send.at[index],
                self.low_recv.at[index],
                self.outer,
            ),
            remote(
                self.own_at(index, 1 - low),
                self.right.at[1, index % RING],
                self.mid_send.at[index],
                self.high_recv.at[1, index],
                self.outer,
            ),
        )

    def hand(self, index):
        z, r, c = here()
        low = z - 1
        mine, spot = (self.own_at(index, low), self.out_at(index, low, r))
        return (
            pltpu.make_async_copy(mine, spot, self.out_recv.at[low, index]),
            remote(
                mine,
                spot,
                self.hand_send.at[index],
                self.out_recv.at[low, index],
                (z, self.peer_row(index), c),
            ),
        )

    def along(self, index):
        low = here()[0] - 1
        spot = self.out_at(index, low, self.peer_row(index))
        return (
            remote(
                spot, spot, self.first_send.at[index], self.out_recv.at[low, index], self.outer
            ),
            remote(spot, spot, self.last_send.at[index], self.out_recv.at[low, index], self.other),
        )

    def onward(self, index):
        low = here()[0] - 1
        spot = self.out_at(index, 1 - low, self.peer_row(index))
        return remote(
            spot, spot, self.on_send.at[index], self.out_recv.at[1 - low, index], self.outer
        )

    def came_back(self, index):
        for which in (0, 1):
            spot = self.out_at(index, which, self.peer_row(index))
            remote(
                spot, spot, self.end_send.at[0, index], self.out_recv.at[which, index], self.near_z
            ).wait_recv()

    def end_step(self, index):
        @pl.when(index < self.chunks)
        def _():
            @pl.when(index >= DEPTH)
            def _():
                for copy in self.end_sends(index - DEPTH):
                    copy.wait_send()

            @pl.when(index >= RING)
            def _():
                self.came_back(index - RING)

            for copy in self.end_sends(index):
                copy.start()

    def mid_step(self, index):
        own, left, right, low = (self.own, self.left, self.right, here()[0] - 1)

        @pl.when(index < self.chunks)
        def _():
            self.from_outer(index)[1].wait_recv()
            span = self.span(index, 1 - low)
            total = own[span, :].astype(jnp.float32) + right[1, index % RING].astype(jnp.float32)
            own[span, :] = total.astype(jnp.bfloat16)
            self.to_other(index).start()

        @pl.when((index >= SUM_LAG) & (index < self.chunks + SUM_LAG))
        def _():
            back = index - SUM_LAG
            self.from_outer(back)[0].wait_recv()
            self.to_other(back).wait_recv()
            span = self.span(back, low)
            total = (
                own[span, :].astype(jnp.float32)
                + left[back % RING].astype(jnp.float32)
                + right[0, back % RING].astype(jnp.float32)
            )
            own[span, :] = total.astype(jnp.bfloat16)

            @pl.when(self.stays(back))
            def _():
                self.hand(back)[0].start()

            @pl.when(jnp.logical_not(self.stays(back)))
            def _():
                self.hand(back)[1].start()

        @pl.when((index >= HAND_LAG) & (index < self.chunks + HAND_LAG))
        def _():
            back = index - HAND_LAG

            @pl.when(self.stays(back))
            def _():
                self.hand(back)[0].wait()

            @pl.when(jnp.logical_not(self.stays(back)))
            def _():
                self.hand(back)[1].wait_recv()

            for copy in self.along(back):
                copy.start()

        @pl.when(index >= LAG)
        def _():
            copy = self.onward(index - LAG)
            copy.wait_recv()
            copy.start()

    def prime(self):
        @pl.when(self.is_end)
        def _():
            run_loop(0, AHEAD, self.end_step)

        self.ahead = AHEAD

    def advance(self, count):
        first, last = (self.at, min(self.at + count, self.total))
        self.at = last
        if first == last:
            return

        @pl.when(self.is_end)
        def _():
            run_loop(self.ahead, last + AHEAD, self.end_step)

        self.ahead = last + AHEAD

        @pl.when(jnp.logical_not(self.is_end))
        def _():
            run_loop(first, last, self.mid_step)

    def one(self, index):
        @pl.when(self.is_end)
        def _():
            self.end_step(index + AHEAD)

        @pl.when(jnp.logical_not(self.is_end))
        def _():
            self.mid_step(index)

    def skip(self, count):
        self.at += count
        self.ahead += count

    def end_done(self, index):
        @pl.when(index >= self.chunks - DEPTH)
        def _():
            for copy in self.end_sends(index):
                copy.wait_send()

        @pl.when(index >= self.chunks - RING)
        def _():
            self.came_back(index)

    def mid_done(self, index):
        self.to_other(index).wait_send()

        @pl.when(jnp.logical_not(self.stays(index)))
        def _():
            self.hand(index)[1].wait_send()

        for copy in self.along(index):
            copy.wait_send()
        self.onward(index).wait_send()

    def finish(self):
        self.advance(self.total)

        @pl.when(self.is_end)
        def _():
            run_loop(0, self.chunks, self.end_done)

        @pl.when(jnp.logical_not(self.is_end))
        def _():
            run_loop(0, self.chunks, self.mid_done)


def line_scratch(rows, width, chunk, lead):
    dma = pltpu.SemaphoreType.DMA
    chunks = 4 * SEGMENTS * (rows // 2 // chunk) + lead
    return [
        pltpu.VMEM((4 * SEGMENTS * rows + 2 * lead * chunk, width), jnp.bfloat16),
        pltpu.VMEM((RING, chunk, width), jnp.bfloat16),
        pltpu.VMEM((2, RING, chunk, width), jnp.bfloat16),
        dma((2, chunks)),
        dma((chunks,)),
        dma((2, chunks)),
        dma((2, chunks)),
        dma((chunks,)),
        dma((chunks,)),
        dma((chunks,)),
        dma((chunks,)),
        dma((chunks,)),
    ]


LINE_REFS = 12
PACK = 32
CHUNK = 32
PACE = (2, 3, 3, 1, 1, 1, 2, 5, 6)
BLOCK_STEPS = 1


def z_peers():
    z, r, c = here()
    return [((z + step) % 4, r, c) for step in (1, 2, 3)]


def plane_peers():
    z, r, c = here()
    return [(z, (r + turn % 4) % 4, (c + turn // 4) % 2) for turn in range(1, 8)]


def hand_out(copies, source, target):
    z, r, c = here()
    twin, side, _ = near()
    cross = (z, flip(across(r)), c)
    columns = target.shape[1]
    size = source.shape[0]

    def piece(row):
        return source.at[:, part(row, columns, columns)]

    spot = target.at[part(r, size, size), :]
    waits = [copies.go(piece(peer[1]), spot, peer) for peer in (side, cross, twin)]
    local = copies.go(piece(r), spot, None)

    def done():
        for copy in waits:
            arrived(copy)
        local.wait()

    return done


def gate_tiles(width):
    tiles = []
    for tile in range(5):
        first, rest = (0, width)
        if tile < 4:
            tiles.append((tile, 0, width, tile // 2, tile % 2 * width))
        else:
            tiles.append((tile, 0, 384, 0, 2 * width))
            tiles.append((tile, 384, width - 384, 1, 2 * width))
    return tiles


def backward_kernel(resid_mid, both_gains, masks, vec, rec_w, in_w, mix_w, out_w, *refs):
    parts_in, out_parts, c_all, x_all, *kept_in = refs[:12]
    gate_grad, up_grad, down_grad = refs[12:15]
    grad, output, grads, out_gates, out_vec, out_gain = refs[15:21]
    scratch = refs[21:]
    line_refs, scratch = (scratch[:LINE_REFS], scratch[LINE_REFS:])
    parts, cot, resid, branch, d_resid, d_pre, d_gates, edge, carry = scratch[:9]
    kept, scratch = (scratch[9:17], scratch[17:])
    sums, gains, vec_z, gain_z, vec_sum, gain_sum, vec_in, gain_in = scratch[:8]
    *buffers, mine, mine_out, load_sem, gate_sem, small_send, small_recv, free, send, recv = scratch[8:]
    normed, pre, mixed, x_pre, conv, rec_gate, in_gate, states = kept
    z, r, c = here()
    twin, side, top = near()
    cross = (z, flip(across(r)), c)
    lines, plane = (z_peers(), plane_peers())
    greet(lines + plane)
    copies = Copies(send, recv)
    line = Line(*line_refs[:3], grads, line_refs[3:], PACK // CHUNK)
    own, half, rows_all = (line.own, line.half, 4 * line.rows)
    size = mine.shape[0]
    shard = part(token_shard(r, c), size, size)
    width, ff = (x_pre.shape[1], gate_grad.shape[1])
    head, rest = (own.shape[1] - 2 * ff, 3 * ff - own.shape[1])
    first, second = (pl.ds(0, rows_all), pl.ds(rows_all, rows_all))
    loads = [
        pltpu.make_async_copy(source, target, load_sem.at[place])
        for place, (source, target) in enumerate(
            zip(
                [
                    gate_grad,
                    up_grad,
                    down_grad.at[:, pl.ds(0, head)],
                    parts_in,
                    down_grad.at[:, pl.ds(head, rest)],
                    c_all.at[shard, :],
                    x_all.at[shard, :],
                    *kept_in,
                ],
                [
                    own.at[first, pl.ds(0, ff)],
                    own.at[first, pl.ds(ff, ff)],
                    own.at[first, pl.ds(2 * ff, head)],
                    parts,
                    own.at[second, pl.ds(0, rest)],
                    cot,
                    resid,
                    *kept,
                ],
            )
        )
    ]
    for copy in loads:
        copy.start()
    for ref in (gains, sums, edge, carry):
        ref[...] = jnp.zeros_like(ref)
    for copy in loads[:3]:
        copy.wait()
    line.prime()
    loads[3].wait()
    pace = iter(PACE)

    def between():
        line.advance(next(pace))

    total = reduce_shards(copies, parts, *buffers, between=between)
    for copy in loads[4:]:
        copy.wait()

    def body(at):
        rows = pl.ds(at, STRIP)
        values, piece = norm_pull(resid_mid[rows, :], both_gains[1:2, :], total(at))
        values = values + cot[rows, :].astype(jnp.float32)
        gains[1:2, :] += piece
        d_resid[rows, :] = values
        mine[rows, :] = values.astype(jnp.bfloat16)

    strips(size, body)
    spread_rows(copies, mine, branch, between)
    copies.finish()
    last = branch.shape[0] // BLOCK - 1

    def block(index, base):
        start = pl.multiple_of((last - index) * BLOCK, BLOCK)
        rows = pl.ds(start, BLOCK)
        before = pl.ds(pl.multiple_of(jnp.maximum(start - 8, 0), 8), 8)
        mixer_backward_step(
            lax.dot_general(
                branch[rows, :], out_w[...], CONTRACT_COLS, preferred_element_type=jnp.float32
            ),
            pre.at[rows, :],
            masks[rows, :],
            vec,
            rec_w,
            in_w,
            x_pre.at[rows, :],
            x_pre.at[before, :],
            conv.at[rows, :],
            rec_gate.at[rows, :],
            in_gate.at[rows, :],
            states.at[rows, :],
            states.at[before, :],
            d_pre.at[rows, :],
            d_gates.at[rows, :],
            sums,
            edge,
            carry,
        )
        parts[rows, :] = lax.dot_general(
            d_pre[rows, :], mix_w[...], CONTRACT_COLS, preferred_element_type=jnp.float32
        ).astype(jnp.bfloat16)
        for step in range(BLOCK_STEPS):
            line.one(base + BLOCK_STEPS * index + step)
        return base

    lax.fori_loop(0, last + 1, block, line.at)
    line.skip(BLOCK_STEPS * (last + 1))
    total_back = reduce_shards(copies, parts, *buffers, between=between)

    def body_back(at):
        rows = pl.ds(at, STRIP)
        values, piece = norm_pull(
            resid[rows, :].astype(jnp.float32), both_gains[0:1, :], total_back(at)
        )
        gains[0:1, :] += piece
        mine[rows, :] = (d_resid[rows, :] + values).astype(jnp.bfloat16)

    strips(size, body_back)
    for peer in (twin, side, top):
        pl.semaphore_signal(free, inc=1, device_id=peer, device_id_type=MESH)
    copies.finish()
    load = pltpu.make_async_copy(out_parts, parts, load_sem.at[0])
    load.start()
    grad_done = hand_out(copies, mine, grad)
    small = [
        [
            remote(
                source,
                target.at[3 - step],
                small_send.at[kind, step - 1],
                small_recv.at[kind, 3 - step],
                lines[step - 1],
            )
            for step in (1, 2, 3)
        ]
        for kind, (source, target) in enumerate(((sums, vec_z), (gains, gain_z)))
    ]
    for kind in small:
        for copy in kind:
            copy.start()
    blocks = lax.dot_general(conv[...], d_gates[...], CONTRACT_ROWS, preferred_element_type=jnp.float32)
    rows_half = width // 2
    lane = lax.broadcasted_iota(jnp.int32, (rows_half, 2 * width), 1)
    mingled = jnp.where(
        lane // rows_half % 2 == 0, blocks[:rows_half], blocks[rows_half:]
    ).astype(jnp.bfloat16)
    for tile, begin, length, which, spot in gate_tiles(2 * width):
        own[pl.ds(2 * rows_all + which * PACK, PACK), spot : spot + length] = mingled[
            tile * PACK : (tile + 1) * PACK, begin : begin + length
        ]

    def weights(index, base):
        columns = pl.ds(pl.multiple_of(index * 256, 256), 256)
        rows = pl.ds(pl.multiple_of(rows_all + index * 256, 256), 256)
        own[rows, rest : rest + 2 * width] = lax.dot_general(
            normed[:, columns], d_pre[...], CONTRACT_ROWS, preferred_element_type=jnp.float32
        ).astype(jnp.bfloat16)
        own[rows, rest + 2 * width :] = lax.dot_general(
            branch[:, columns], mixed[...], CONTRACT_ROWS, preferred_element_type=jnp.float32
        ).astype(jnp.bfloat16)
        line.one(base + index)
        return base

    lax.fori_loop(0, rows_all // 256, weights, line.at)
    line.skip(rows_all // 256)
    assert line.at + AHEAD <= line.first + line.lead
    load.wait()
    pl.semaphore_wait(free, 3)
    total_out = reduce_shards(copies, parts, *buffers, between=between)

    def body_out(at):
        rows = pl.ds(at, STRIP)
        mine_out[rows, :] = (resid_mid[rows, :] + total_out(at)).astype(jnp.bfloat16)

    strips(size, body_out)
    output_done = hand_out(copies, mine_out, output)
    spread_out = [
        [
            remote(
                source,
                target.at[6 - step],
                small_send.at[kind, 3 + step],
                small_recv.at[kind, 3 + 6 - step],
                peer,
            )
            for step, peer in enumerate(plane)
        ]
        for kind, (source, target) in enumerate(((vec_sum, vec_in), (gain_sum, gain_in)))
    ]
    for kind in small:
        for copy in kind:
            copy.wait_recv()
    vec_sum[...] = sums[...] + vec_z[0] + vec_z[1] + vec_z[2]
    gain_sum[...] = gains[...] + gain_z[0] + gain_z[1] + gain_z[2]
    for kind in spread_out:
        for copy in kind:
            copy.start()
    line.advance(max(line.first + line.lead + RING + 2 - line.at, 0))
    gate_moves = [
        remote(
            grads.at[4 * SEGMENTS, pl.ds(which * half, PACK), :],
            out_gates.at[r, which],
            small_send.at[0, 10 + 2 * place + which],
            small_recv.at[0, 10 + 2 * place + which],
            peer,
        )
        for place, peer in enumerate((twin, side, cross))
        for which in (0, 1)
    ]
    gate_local = [
        pltpu.make_async_copy(
            grads.at[4 * SEGMENTS, pl.ds(which * half, PACK), :],
            out_gates.at[r, which],
            gate_sem.at[which],
        )
        for which in (0, 1)
    ]
    for copy in gate_moves + gate_local:
        copy.start()
    for kind in spread_out:
        for copy in kind:
            copy.wait_recv()
    all_gains = gain_sum[...]
    for place in range(7):
        all_gains = all_gains + gain_in[place]
    gain_z[0] = all_gains
    out_gain[...] = gain_z[0, :, part(r, out_gain.shape[1], out_gain.shape[1])]
    out_vec[r] = vec_sum[...]
    for step in (0, 1, 2):
        out_vec[(r + 3 - step) % 4] = vec_in[6 - step]
    line.finish()
    grad_done()
    output_done()
    for copy in gate_moves:
        copy.wait_recv()
    for copy in gate_local:
        copy.wait()
    for group in small + spread_out + [gate_moves]:
        for copy in group:
            copy.wait_send()
    copies.finish()


def unpack_kernel(grads, gates, vec, output, grad_in, *outs):
    out_t, grad_t, x_grad, y_grad, out_grad, gate_grad, up_grad, down_grad, rec_w, in_w = outs[:10]
    wide, ff, rec = (grads.shape[2], gate_grad.shape[1] // 4, x_grad.shape[1] // 4)
    head = wide - 2 * ff
    rest = ff - head
    out_t[...] = output[...].astype(jnp.float32).T.astype(out_t.dtype)
    grad_t[...] = grad_in[...].astype(jnp.float32).T
    for row in range(4):
        wide_span, span = (slice(row * ff, (row + 1) * ff), slice(row * rec, (row + 1) * rec))

        def body(at):
            rows = pl.ds(at, STRIP)
            early = grads[row, rows, :].astype(jnp.float32)
            late = grads[4 + row, rows, :].astype(jnp.float32)
            gate_grad[rows, wide_span] = early[:, :ff]
            up_grad[rows, wide_span] = early[:, ff : 2 * ff]
            down_grad[rows, row * ff : row * ff + head] = early[:, 2 * ff :]
            down_grad[rows, row * ff + head : (row + 1) * ff] = late[:, :rest]
            x_grad[rows, span] = late[:, rest : rest + rec]
            y_grad[rows, span] = late[:, rest + rec : rest + 2 * rec]

        strips(BLOCK, body)
        last = grads[4 + row, :, rest + 2 * rec : rest + 3 * rec]
        out_grad[span, :] = last.astype(jnp.float32).T
    heads, width = (rec_w.shape[0], rec_w.shape[1])
    for tile in range(5):
        spots = [item for item in gate_tiles(2 * rec) if item[0] == tile]
        values = jnp.concatenate(
            [gates[0, which, :, spot : spot + length] for _, _, length, which, spot in spots],
            axis=1,
        ).astype(jnp.float32)
        rows = slice(tile * PACK, (tile + 1) * PACK)
        for place in range(heads):
            rec_w[place, rows, :] = values[:, place * width : (place + 1) * width]
            in_w[place, rows, :] = values[:, rec + place * width : rec + (place + 1) * width]
    line = 0
    for ref in outs[10:]:
        for row in range(ref.shape[0]):
            ref[row : row + 1, :] = jnp.concatenate(
                [vec[place, line : line + 1, :] for place in range(4)], axis=1
            )
            line += 1


def unpack(grads, gates, vec, output, grad_in, rec, ff, heads):
    depth, wide = grads.shape[1:]
    tokens, head = (output.shape[0], rec // heads)

    def out(*dims, kind=jnp.float32):
        return jax.ShapeDtypeStruct(dims, kind)

    def rows(columns):
        return pl.BlockSpec((BLOCK, columns), lambda i: (i, 0))

    def columns(length):
        return pl.BlockSpec((length, BLOCK), lambda i: (0, i))

    def whole(*dims):
        return pl.BlockSpec(dims, lambda i: (0,) * len(dims))

    blocks = pl.BlockSpec((heads, head, head), lambda i: (i, 0, 0))
    lines = (1, 1, 4, 1, 1, 1, 1)
    return pl.pallas_call(
        unpack_kernel,
        grid=(depth // BLOCK,),
        in_specs=[
            pl.BlockSpec((8, BLOCK, wide), lambda i: (0, i, 0)),
            pl.BlockSpec((1, 2, PACK, wide), lambda i: (i, 0, 0, 0)),
            whole(*vec.shape),
            columns(tokens),
            columns(tokens),
        ],
        out_specs=[rows(tokens), rows(tokens), rows(4 * rec), rows(4 * rec), columns(4 * rec)]
        + [rows(4 * ff)] * 3
        + [blocks] * 2
        + [whole(count, 4 * rec) for count in lines],
        out_shape=[
            out(depth, tokens, kind=output.dtype),
            out(depth, tokens),
            out(depth, 4 * rec),
            out(depth, 4 * rec),
            out(4 * rec, depth),
        ]
        + [out(depth, 4 * ff)] * 3
        + [out(4 * heads, head, head)] * 2
        + [out(count, 4 * rec) for count in lines],
        compiler_params=pltpu.CompilerParams(vmem_limit_bytes=60 << 20),
        name="unpack",
    )(grads, gates, vec, output, grad_in)


def dot(left, right, dims, kind=jnp.float32):
    return lax.dot_general(left, right, dims, preferred_element_type=jnp.float32).astype(kind)


def local_plane(
    inputs,
    cotangent,
    starts,
    x_proj,
    y_proj,
    out_proj,
    gate_proj,
    up_proj,
    down_proj,
    mix_gain,
    mlp_gain,
    x_bias,
    y_bias,
    conv_w,
    conv_b,
    rec_gate_w,
    in_gate_w,
    rec_gate_b,
    in_gate_b,
    decay_param,
):
    z, r, c = here()
    depth = x_proj.shape[0]
    rec = x_proj.shape[1] // 4
    width = gate_proj.shape[1] // 4
    heads, head = (rec_gate_w.shape[0] // 4, rec_gate_w.shape[1])
    padded = (rec + 127) // 128 * 128
    low = jnp.bfloat16

    def mine(array, size, axis=0):
        return lax.dynamic_slice_in_dim(array, r * size, size, axis)

    flags = jnp.broadcast_to(starts.astype(jnp.float32)[:, None], (starts.shape[0], 128))
    x_all, c_all, s_all, g_all, mix_w, out_w = gather(
        inputs.T,
        cotangent.T,
        flags,
        jnp.stack([mix_gain, mlp_gain]),
        x_proj,
        y_proj,
        out_proj,
    )
    tokens, model = x_all.shape
    vectors = jnp.concatenate(
        [
            x_bias[None],
            y_bias[None],
            conv_w,
            conv_b[None],
            rec_gate_b[None],
            in_gate_b[None],
            -GATE_C * jax.nn.softplus(decay_param)[None],
            -GATE_C * jax.nn.sigmoid(decay_param)[None],
            jnp.zeros((5, x_bias.shape[0]), jnp.float32),
        ],
        axis=0,
    )
    vec = mine(vectors, rec, 1)

    def diagonal(blocks):
        blocks = mine(blocks, heads)
        rows = [jnp.pad(blocks[i], ((0, 0), (i * head, rec - (i + 1) * head))) for i in range(heads)]
        return jnp.concatenate(rows, axis=0)

    rec_w, in_w = (diagonal(rec_gate_w), diagonal(in_gate_w))
    size = tokens // 8
    full = jax.ShapeDtypeStruct((tokens, model), low)
    part = jax.ShapeDtypeStruct((size, model), jnp.float32)
    piece = pltpu.VMEM((size, model), low)
    block = jax.ShapeDtypeStruct((inputs.shape[1], inputs.shape[0]), low)
    weights = (gate_proj, up_proj, down_proj)
    slices = jax.ShapeDtypeStruct((4 * depth, width), low)
    kept = [((tokens, model), low), ((tokens, 2 * rec), jnp.float32), ((tokens, padded), low)]
    kept += [((tokens, rec), kind) for kind in (jnp.float32, low) + (jnp.float32,) * 3]
    kept.append(((tokens, 8), jnp.float32))
    row8 = pltpu.VMEM((8, rec), jnp.float32)
    (
        normed_mlp,
        resid_mid,
        gate_w,
        up_w,
        down_w,
        normed_mix,
        pre,
        mixed,
        x_pre,
        conv,
        rec_gate,
        in_gate,
        states,
        masks,
    ) = vmem_call(
        forward_kernel,
        "forward",
        FORWARD_ID,
        (vec, rec_w, in_w, g_all),
        [full, part] + [slices] * 3 + [jax.ShapeDtypeStruct(*item) for item in kept],
        [pl.ANY, pltpu.VMEM] + [pl.ANY] * 12,
        [pltpu.VMEM(*item) for item in kept]
        + [row8, row8, pltpu.VMEM((tokens, model), low)]
        + [
            pltpu.VMEM((tokens, model), low),
            pltpu.VMEM((tokens, 128), jnp.float32),
            pltpu.VMEM(mix_w.shape, low),
            pltpu.VMEM(out_w.shape, low),
            pltpu.VMEM((8, 8), jnp.float32),
            pltpu.SemaphoreType.DMA((11,)),
        ]
        + reduce_scratch(size, model)
        + [piece, pltpu.SemaphoreType.DMA((9,))],
        80,
        (x_all, s_all.reshape(tokens, 128), mix_w, out_w, *weights),
    )
    gate = dot(normed_mlp, gate_w, CONTRACT_PLAIN)
    up = dot(normed_mlp, up_w, CONTRACT_PLAIN)
    d_activ = dot(c_all, down_w, CONTRACT_PLAIN)
    gelu, slope = gelu_both(gate)
    activ = (gelu * up).astype(low)
    d_gate = (d_activ * up * slope).astype(low)
    d_up = (d_activ * gelu).astype(low)
    d_normed = lax.dot_general(
        d_gate, gate_w, CONTRACT_COLS, preferred_element_type=jnp.float32
    ) + lax.dot_general(d_up, up_w, CONTRACT_COLS, preferred_element_type=jnp.float32)
    def kind_of(array):
        return pltpu.VMEM(array.shape, array.dtype)

    def like(array):
        return jax.ShapeDtypeStruct(array.shape, array.dtype)

    both = jax.ShapeDtypeStruct((tokens, 2 * rec), low)
    held = (normed_mix, pre, mixed, x_pre, conv, rec_gate, in_gate, states)
    wide = (3 * width + 2 * rec + padded) // SEGMENTS
    sums = pltpu.VMEM((16, rec), jnp.float32)
    lines = pltpu.VMEM((2, model), jnp.float32)
    dma = pltpu.SemaphoreType.DMA

    def several(count, kind):
        return pltpu.VMEM((count, *kind.shape), kind.dtype)

    grad_in, output, grads, gates, vec_sums, gains = vmem_call(
        backward_kernel,
        "backward",
        BACKWARD_ID,
        (resid_mid, g_all, masks, vec, rec_w, in_w, mix_w, out_w),
        [
            block,
            block,
            jax.ShapeDtypeStruct((4 * SEGMENTS + 1, depth, wide), low),
            jax.ShapeDtypeStruct((4, 2, PACK, wide), low),
            jax.ShapeDtypeStruct((4, 16, rec), jnp.float32),
            jax.ShapeDtypeStruct((2, depth), jnp.float32),
        ],
        [pl.ANY] * 4 + [pltpu.VMEM] * 2,
        line_scratch(depth, wide, CHUNK, PACK // CHUNK)
        + [
            kind_of(full),
            piece,
            piece,
            kind_of(full),
            kind_of(part),
            kind_of(both),
            kind_of(both),
            pltpu.VMEM((24, rec), jnp.float32),
            row8,
        ]
        + [kind_of(item) for item in held]
        + [
            sums,
            lines,
            several(3, sums),
            several(3, lines),
            sums,
            lines,
            several(7, sums),
            several(7, lines),
        ]
        + reduce_scratch(size, model)
        + [
            piece,
            piece,
            dma((15,)),
            dma((2,)),
            dma((2, 16)),
            dma((2, 16)),
            pltpu.SemaphoreType.REGULAR,
        ],
        80,
        (
            d_normed.astype(low),
            dot(activ, down_w, CONTRACT_COLS, low),
            c_all,
            x_all,
            *held,
            dot(normed_mlp, d_gate, CONTRACT_ROWS, low),
            dot(normed_mlp, d_up, CONTRACT_ROWS, low),
            dot(c_all, activ, CONTRACT_ROWS, low),
        ),
    )
    done = unpack(grads, gates, vec_sums, output, grad_in, rec, width, heads)
    lines = [item if item.shape[0] > 1 else item[0] for item in done[10:]]
    return (*done[:8], gains[0], gains[1], *lines[:4], *done[8:10], *lines[4:])


def fits(mesh):
    return mesh.shape["dp"] == 4 and mesh.shape["row"] == 4 and mesh.shape["col"] == 2


def solution(mesh):
    placed = (
        P("row", ("dp", "col")),
        P("row", ("dp", "col")),
        P(("dp", "row")),
        P("row", "col"),
        P("row", "col"),
        P("col", "row"),
        P("row", "col"),
        P("row", "col"),
        P("row", "col"),
        P("row"),
        P("row"),
        P("col"),
        P("col"),
        P(None, "col"),
        P("col"),
        P("col", None, None),
        P("col", None, None),
        P("col"),
        P("col"),
        P("col"),
    )
    return jax.shard_map(
        local_plane if fits(mesh) else local,
        mesh=mesh,
        in_specs=placed,
        out_specs=(
            P("row", ("dp", "col")),
            P("row", ("dp", "col")),
            P("row", "col"),
            P("row", "col"),
            P("col", "row"),
            P("row", "col"),
            P("row", "col"),
            P("row", "col"),
            P("row"),
            P("row"),
            P("col"),
            P("col"),
            P(None, "col"),
            P("col"),
            P("col", None, None),
            P("col", None, None),
            P("col"),
            P("col"),
            P("col"),
        ),
        check_vma=False,
    )
```

```python
import functools

import jax
import jax.numpy as jnp
from jax import lax
from jax.experimental import pallas as pl
from jax.experimental.pallas import tpu as pltpu
from jax.sharding import PartitionSpec as P

MESH = pl.DeviceIdType.MESH

D = 2048


EPS = 1e-06
GATE_C = 8.0
CONTRACT_ROWS = (((0,), (0,)), ((), ()))
CONTRACT_COLS = (((1,), (1,)), ((), ()))
CONTRACT_PLAIN = (((1,), (0,)), ((), ()))


def from_behind(value, axis, by):
    count = lax.axis_size(axis)
    pairs = [(i, i + by) for i in range(count) if 0 <= i + by < count]
    return lax.ppermute(value, axis, pairs)


def carried_in(value, axis, join, neutral, backward):
    count, mine = (lax.axis_size(axis), lax.axis_index(axis))
    pieces = jax.tree.map(lambda part: lax.all_gather(part, axis), value)
    if backward:
        pieces = jax.tree.map(lambda part: part[::-1], pieces)
        mine = count - 1 - mine
    subtotal = jax.tree.map(
        lambda part, zero: jnp.full_like(part, 0) + jnp.asarray(zero, part.dtype), value, neutral
    )

    def hop(position, subtotal):
        longer = join(subtotal, jax.tree.map(lambda part: part[position], pieces))
        return jax.tree.map(lambda new, old: jnp.where(position < mine, new, old), longer, subtotal)

    return lax.fori_loop(0, count - 1, hop, subtotal)


def chain(earlier, later):
    return (earlier[0] * later[0], later[0] * earlier[1] + later[1])


def adjoint_chain(earlier, later):
    return (later[0] * earlier[0], later[1] + later[0] * earlier[1])


def gelu_tanh(values):
    return jax.nn.gelu(values, approximate=True)


def glu_piece(gate_vals, up_vals):
    return gelu_tanh(gate_vals) * up_vals


def causal_conv(values, conv_w, conv_b, segment_ids):
    result = values * conv_w[0] + conv_b
    for offset in range(1, conv_w.shape[0]):
        lagged = jnp.pad(values, ((offset, 0), (0, 0)))[:-offset]
        earlier_ids = jnp.pad(segment_ids, (offset, 0), constant_values=-1)[:-offset]
        result = (
            result + jnp.where((earlier_ids == segment_ids)[:, None], lagged, 0.0) * conv_w[offset]
        )
    return result


def local_recurrence(rec_pre, in_pre, conv_vals, decay_param, flags):
    rec_gate = jax.nn.sigmoid(rec_pre)
    in_gate = jax.nn.sigmoid(in_pre)
    log_keep = -GATE_C * rec_gate * jax.nn.softplus(decay_param)
    keep_rate = jnp.exp(log_keep)
    fresh = (flags == 1)[:, None]
    multiplier = jnp.where(fresh, 1.0, jnp.sqrt(-jnp.expm1(2.0 * log_keep)))
    driven = conv_vals * in_gate * multiplier
    carried = jnp.where(fresh, 0.0, keep_rate)
    cum_keep, states = lax.associative_scan(chain, (carried, driven), axis=0)
    return (cum_keep, states)


def row_sums(values):
    return lax.psum(values, "row")


def norm_forward(values, norm_gain):
    squares = row_sums(jnp.sum(values * values, axis=1))
    inv_rms = lax.rsqrt(squares / D + EPS)
    return (values * inv_rms[:, None] * norm_gain, inv_rms)


def norm_backward(values, inv_rms, norm_gain, incoming):
    scaled = norm_gain * incoming
    dots = row_sums(jnp.sum(scaled * values, axis=1))
    values_grad = inv_rms[:, None] * scaled - values * (inv_rms**3 * dots / D)[:, None]
    gain_grad = jnp.sum(incoming * values * inv_rms[:, None], axis=0)
    return (values_grad, gain_grad)


def gather_edge(values):
    return lax.all_gather(values, "col", axis=0, tiled=True)


def gather_mid(values):
    return lax.all_gather(values, "row", axis=0, tiled=True)


def row_partial(whole, weight, dims):
    return lax.psum_scatter(
        lax.dot_general(whole, weight, dims, preferred_element_type=jnp.float32),
        "row",
        scatter_dimension=0,
        tiled=True,
    )


def col_partial(whole, weight, dims):
    return lax.psum_scatter(
        lax.dot_general(whole, weight, dims, preferred_element_type=jnp.float32),
        "col",
        scatter_dimension=0,
        tiled=True,
    )


def project_in(normed, weight):
    whole = gather_edge(normed)
    result = row_partial(whole, weight, CONTRACT_PLAIN)
    return (result, whole)


def weight_grad(left, right):
    return lax.dot_general(left, right, CONTRACT_ROWS, preferred_element_type=jnp.float32)


def local(
    inputs,
    cotangent,
    starts,
    x_proj,
    y_proj,
    out_proj,
    gate_proj,
    up_proj,
    down_proj,
    mix_gain,
    mlp_gain,
    x_bias,
    y_bias,
    conv_w,
    conv_b,
    rec_gate_w,
    in_gate_w,
    rec_gate_b,
    in_gate_b,
    decay_param,
):
    rows_mid = starts.shape[0]
    rec_width = x_proj.shape[1]
    ff_width = gate_proj.shape[1]
    head_count = rec_gate_w.shape[0]
    margin = conv_w.shape[0] - 1
    mix_weights = jnp.concatenate([x_proj, y_proj], axis=1)
    mlp_weights = jnp.concatenate([gate_proj, up_proj], axis=1)
    cot_rows = cotangent.T
    resid = inputs.astype(jnp.float32).T
    normed_mix, inv_rms_mix = norm_forward(resid, mix_gain)
    normed_mix = normed_mix.astype(jnp.bfloat16)
    pre_both, whole_mix = project_in(normed_mix, mix_weights)
    x_pre = pre_both[:, :rec_width] + x_bias
    y_pre = pre_both[:, rec_width:] + y_bias
    x_tail, flag_tail = from_behind(
        (x_pre[rows_mid - margin :], starts[rows_mid - margin :].astype(jnp.float32)), "row", 1
    )
    ext_flags = jnp.concatenate([flag_tail.astype(jnp.int32), starts])
    ext_ids = jnp.cumsum(ext_flags, dtype=jnp.int32)
    ext_x = jnp.concatenate([x_tail, x_pre], axis=0)

    def conv_piece(values, taps, offsets):
        return causal_conv(values, taps, offsets, ext_ids)[margin:]

    conv_vals, conv_pull = jax.vjp(conv_piece, ext_x, conv_w, conv_b)
    conv_low = conv_vals.astype(jnp.bfloat16)
    conv_heads = conv_low.reshape(rows_mid, head_count, -1)
    rec_pre = (
        jnp.einsum(
            "thk,hkj->thj", conv_heads, rec_gate_w, preferred_element_type=jnp.float32
        ).reshape(rows_mid, rec_width)
        + rec_gate_b
    )
    in_pre = (
        jnp.einsum(
            "thk,hkj->thj", conv_heads, in_gate_w, preferred_element_type=jnp.float32
        ).reshape(rows_mid, rec_width)
        + in_gate_b
    )

    def scan_piece(rec_vals, in_vals, conv_input, decay_vals):
        return local_recurrence(rec_vals, in_vals, conv_input, decay_vals, starts)

    (cum_keep, local_states), scan_pull = jax.vjp(
        scan_piece, rec_pre, in_pre, conv_low.astype(jnp.float32), decay_param
    )
    ones_row = jnp.ones((rec_width,), jnp.float32)
    zeros_row = jnp.zeros((rec_width,), jnp.float32)
    incoming = carried_in(
        (cum_keep[rows_mid - 1], local_states[rows_mid - 1]),
        "row",
        chain,
        (ones_row, zeros_row),
        False,
    )
    state_prev = incoming[1]
    states = local_states + cum_keep * state_prev
    y_act, y_pull = jax.vjp(gelu_tanh, y_pre)
    mixed = (states * y_act).astype(jnp.bfloat16)
    whole_mixed = gather_mid(mixed)
    resid_mid = resid + col_partial(whole_mixed, out_proj, CONTRACT_PLAIN)
    normed_mlp, inv_rms_mlp = norm_forward(resid_mid, mlp_gain)
    normed_mlp = normed_mlp.astype(jnp.bfloat16)
    gate_up, whole_mlp = project_in(normed_mlp, mlp_weights)
    activ, activ_pull = jax.vjp(glu_piece, gate_up[:, :ff_width], gate_up[:, ff_width:])
    activ = activ.astype(jnp.bfloat16)
    whole_activ = gather_mid(activ)
    output = (resid_mid + col_partial(whole_activ, down_proj, CONTRACT_COLS)).astype(jnp.bfloat16)
    cot_whole = gather_edge(cot_rows)
    d_activ = row_partial(cot_whole, down_proj, CONTRACT_PLAIN)
    activ_rows = gather_mid(activ)
    grad_down = weight_grad(cot_whole, activ_rows)
    d_gate, d_up = activ_pull(d_activ)
    d_gate_up = jnp.concatenate([d_gate, d_up], axis=1).astype(jnp.bfloat16)
    d_gate_up_whole = gather_mid(d_gate_up)
    d_normed_mlp = col_partial(d_gate_up_whole, mlp_weights, CONTRACT_COLS)
    mlp_rows = gather_edge(normed_mlp)
    grad_gate_up = weight_grad(mlp_rows, d_gate_up_whole)
    d_norm_mid, grad_mlp_gain = norm_backward(resid_mid, inv_rms_mlp, mlp_gain, d_normed_mlp)
    d_resid_mid = cot_rows.astype(jnp.float32) + d_norm_mid
    d_branch = d_resid_mid.astype(jnp.bfloat16)
    branch_whole = gather_edge(d_branch)
    d_mixed = row_partial(branch_whole, out_proj, CONTRACT_COLS)
    mixed_rows = gather_mid(mixed)
    grad_out = weight_grad(mixed_rows, branch_whole)
    d_state = d_mixed * y_act
    (d_y_pre,) = y_pull(d_mixed * states)
    own_sens = jnp.sum(d_state * cum_keep, axis=0)
    outgoing = carried_in(
        (cum_keep[rows_mid - 1], own_sens), "row", adjoint_chain, (ones_row, zeros_row), True
    )
    d_total = d_state + jnp.pad(outgoing[1][None, :], ((rows_mid - 1, 0), (0, 0)))
    d_rec_pre, d_in_pre, d_conv_direct, grad_decay = scan_pull((d_total * state_prev, d_total))
    d_rec_low = d_rec_pre.astype(jnp.bfloat16)
    d_in_low = d_in_pre.astype(jnp.bfloat16)
    d_rec_heads = d_rec_low.reshape(rows_mid, head_count, -1)
    d_in_heads = d_in_low.reshape(rows_mid, head_count, -1)
    d_conv = d_conv_direct + jnp.einsum(
        "thj,hkj->thk", d_rec_heads, rec_gate_w, preferred_element_type=jnp.float32
    ).reshape(rows_mid, rec_width)
    d_conv = d_conv + jnp.einsum(
        "thj,hkj->thk", d_in_heads, in_gate_w, preferred_element_type=jnp.float32
    ).reshape(rows_mid, rec_width)
    grad_rec_w = jnp.einsum(
        "thk,thj->hkj", conv_heads, d_rec_heads, preferred_element_type=jnp.float32
    )
    grad_in_w = jnp.einsum(
        "thk,thj->hkj", conv_heads, d_in_heads, preferred_element_type=jnp.float32
    )
    grad_rec_b = jnp.sum(d_rec_low.astype(jnp.float32), axis=0)
    grad_in_b = jnp.sum(d_in_low.astype(jnp.float32), axis=0)
    d_ext, grad_conv_w, grad_conv_b = conv_pull(d_conv)
    d_from_next = from_behind(d_ext[:margin], "row", -1)
    d_x_pre = d_ext[margin:] + jnp.pad(d_from_next, ((rows_mid - margin, 0), (0, 0)))
    d_pre = jnp.concatenate([d_x_pre, d_y_pre], axis=1).astype(jnp.bfloat16)
    bias_sums = jnp.sum(d_pre.astype(jnp.float32), axis=0)
    d_pre_whole = gather_mid(d_pre)
    d_normed_mix = col_partial(d_pre_whole, mix_weights, CONTRACT_COLS)
    mix_rows = gather_edge(normed_mix)
    grad_mix = weight_grad(mix_rows, d_pre_whole)
    d_norm_in, grad_mix_gain = norm_backward(resid, inv_rms_mix, mix_gain, d_normed_mix)
    inputs_grad = d_resid_mid + d_norm_in
    grad_mix, grad_out, grad_gate_up, grad_down = (
        lax.psum(grad_mix.astype(jnp.bfloat16), "dp").astype(jnp.float32),
        lax.psum(grad_out.astype(jnp.bfloat16), "dp").astype(jnp.float32),
        lax.psum(grad_gate_up.astype(jnp.bfloat16), "dp").astype(jnp.float32),
        lax.psum(grad_down.astype(jnp.bfloat16), "dp").astype(jnp.float32),
    )
    (
        bias_sums,
        grad_conv_w,
        grad_conv_b,
        grad_rec_w,
        grad_in_w,
        grad_rec_b,
        grad_in_b,
        grad_decay,
    ) = (
        lax.psum(bias_sums.astype(jnp.bfloat16), ("dp", "row")).astype(jnp.float32),
        lax.psum(grad_conv_w.astype(jnp.bfloat16), ("dp", "row")).astype(jnp.float32),
        lax.psum(grad_conv_b.astype(jnp.bfloat16), ("dp", "row")).astype(jnp.float32),
        lax.psum(grad_rec_w.astype(jnp.bfloat16), ("dp", "row")).astype(jnp.float32),
        lax.psum(grad_in_w.astype(jnp.bfloat16), ("dp", "row")).astype(jnp.float32),
        lax.psum(grad_rec_b.astype(jnp.bfloat16), ("dp", "row")).astype(jnp.float32),
        lax.psum(grad_in_b.astype(jnp.bfloat16), ("dp", "row")).astype(jnp.float32),
        lax.psum(grad_decay.astype(jnp.bfloat16), ("dp", "row")).astype(jnp.float32),
    )
    grad_mix_gain, grad_mlp_gain = lax.psum((grad_mix_gain, grad_mlp_gain), ("dp", "col"))
    return (
        output.T,
        inputs_grad.T,
        grad_mix[:, :rec_width],
        grad_mix[:, rec_width:],
        grad_out,
        grad_gate_up[:, :ff_width],
        grad_gate_up[:, ff_width:],
        grad_down,
        grad_mix_gain,
        grad_mlp_gain,
        bias_sums[:rec_width],
        bias_sums[rec_width:],
        grad_conv_w,
        grad_conv_b,
        grad_rec_w,
        grad_in_w,
        grad_rec_b,
        grad_in_b,
        grad_decay,
    )


GATHER_ID, FORWARD_ID, BACKWARD_ID = (0, 1, 2)
BLOCK = 128
VMEM_BYTES = 60 << 20


def one_minus_exp(rate):
    series = rate * (1.0 - rate * (0.5 - rate * (1.0 / 6.0 - rate * (1.0 / 24.0 - rate / 120.0))))
    return jnp.where(rate < 0.1, series, 1.0 - jnp.exp(-rate))


GELU_C = 0.7978845608028654


def gelu_both(values):
    squared = values * values
    inner = jnp.tanh(GELU_C * values * (1.0 + 0.044715 * squared))
    value = 0.5 * values * (1.0 + inner)
    slope = 0.5 * (1.0 + inner) + 0.5 * values * (1.0 - inner * inner) * GELU_C * (
        1.0 + 3.0 * 0.044715 * squared
    )
    return (value, slope)


def down_rows(values, by):
    return pltpu.roll(values, by, 0)


def up_rows(values, by):
    return pltpu.roll(values, values.shape[0] - by, 0)


def scan_down(keep, add):
    rows = keep.shape[0]
    position = lax.broadcasted_iota(jnp.int32, keep.shape, 0)
    step = 1
    while step < rows:
        if step < 8:
            inside = position >= step
            before_keep = jnp.where(inside, down_rows(keep, step), 1.0)
            before_add = jnp.where(inside, down_rows(add, step), 0.0)
            add = add + keep * before_add
            keep = keep * before_keep
        else:
            add = jnp.concatenate([add[:step], add[step:] + keep[step:] * add[:-step]], axis=0)
            keep = jnp.concatenate([keep[:step], keep[step:] * keep[:-step]], axis=0)
        step *= 2
    return (keep, add)


def scan_up(keep, add):
    rows = keep.shape[0]
    position = lax.broadcasted_iota(jnp.int32, keep.shape, 0)
    step = 1
    while step < rows:
        if step < 8:
            inside = position < rows - step
            after_keep = jnp.where(inside, up_rows(keep, step), 1.0)
            after_add = jnp.where(inside, up_rows(add, step), 0.0)
            add = add + keep * after_add
            keep = keep * after_keep
        else:
            add = jnp.concatenate([add[:-step] + keep[:-step] * add[step:], add[-step:]], axis=0)
            keep = jnp.concatenate([keep[:-step] * keep[step:], keep[-step:]], axis=0)
        step *= 2
    return (keep, add)


def mixer_forward_step(
    pre, marks, vec, rec_w, in_w, mixed, x_pre, conv, rec_gate, in_gate, states, tail, carry
):
    width = x_pre.shape[1]
    x = pre[:, :width] + vec[0:1, :]
    x_pre[...] = x
    longer = jnp.concatenate([tail[...], x], axis=0)
    tail[...] = x[BLOCK - 8 :]
    total = x * vec[2:3, :] + vec[6:7, :]
    for tap in range(1, 4):
        total = total + marks[:, tap : tap + 1] * down_rows(longer, tap)[8:] * vec[
            2 + tap : 3 + tap, :
        ]
    low = total.astype(jnp.bfloat16)
    conv[...] = low
    rec = jax.nn.sigmoid(
        jnp.dot(low, rec_w[...], preferred_element_type=jnp.float32) + vec[7:8, :]
    )
    inn = jax.nn.sigmoid(
        jnp.dot(low, in_w[...], preferred_element_type=jnp.float32) + vec[8:9, :]
    )
    rec_gate[...] = rec
    in_gate[...] = inn
    log_keep = rec * vec[9:10, :]
    fresh = marks[:, 0:1]
    scale = jnp.where(fresh > 0.5, 1.0, jnp.sqrt(one_minus_exp(-2.0 * log_keep)))
    driven = low.astype(jnp.float32) * inn * scale
    keep, add = scan_down(jnp.exp(log_keep) * (1.0 - fresh), driven)
    state = add + keep * carry[0:1, :]
    carry[...] = jnp.broadcast_to(state[BLOCK - 1 :, :], carry.shape)
    states[...] = state
    y = pre[:, width:] + vec[1:2, :]
    mixed[:, :width] = (state * gelu_both(y)[0]).astype(jnp.bfloat16)
    mixed[:, width:] = jnp.zeros((BLOCK, mixed.shape[1] - width), jnp.bfloat16)


def mixer_backward_step(
    incoming,
    pre,
    marks,
    vec,
    rec_w,
    in_w,
    x_pre,
    x_before,
    conv,
    rec_gate,
    in_gate,
    states,
    state_before,
    d_pre,
    d_gates,
    sums,
    edge,
    carry,
):
    width = x_pre.shape[1]
    position = lax.broadcasted_iota(jnp.int32, (BLOCK, width), 0)
    fresh = marks[:, 0:1]
    stale = 1.0 - fresh
    gelu, slope = gelu_both(pre[:, width:] + vec[1:2, :])
    state = states[...]
    d_y = (incoming * state * slope).astype(jnp.bfloat16)
    rec, inn = (rec_gate[...], in_gate[...])
    conv_vals = conv[...].astype(jnp.float32)
    log_keep = rec * vec[9:10, :]
    keep_rate = jnp.exp(log_keep)
    scale = jnp.where(fresh > 0.5, 1.0, jnp.sqrt(one_minus_exp(-2.0 * log_keep)))
    carried = keep_rate * stale
    after = jnp.where(position == BLOCK - 1, carry[1:2, :], up_rows(carried, 1))
    keep, add = scan_up(after, incoming * gelu)
    adjoint = add + keep * carry[0:1, :]
    carry[0:1, :] = adjoint[0:1]
    carry[1:2, :] = carried[0:1]
    earlier = jnp.where(position == 0, state_before[7:8, :], down_rows(state, 1))
    drive = adjoint * scale
    d_log = stale * (
        adjoint * earlier * keep_rate
        - adjoint * inn * conv_vals * keep_rate * keep_rate / scale
    )
    d_rec = (d_log * vec[9:10, :] * rec * (1.0 - rec)).astype(jnp.bfloat16)
    d_in = (drive * conv_vals * inn * (1.0 - inn)).astype(jnp.bfloat16)
    d_gates[:, :width] = d_rec
    d_gates[:, width:] = d_in
    d_conv = drive * inn
    d_conv = d_conv + lax.dot_general(
        d_rec, rec_w[...], CONTRACT_COLS, preferred_element_type=jnp.float32
    )
    d_conv = d_conv + lax.dot_general(
        d_in, in_w[...], CONTRACT_COLS, preferred_element_type=jnp.float32
    )
    x = x_pre[...]
    longer = jnp.concatenate([x_before[...], x], axis=0)

    def column(values):
        return jnp.sum(values, axis=0, keepdims=True)

    d_x = d_conv * vec[2:3, :]
    taps = [column(d_conv * x)]
    for tap in range(1, 4):
        piece = marks[:, tap : tap + 1] * d_conv
        taps.append(column(piece * down_rows(longer, tap)[8:]))
        beyond = jnp.concatenate([piece, edge[8 * tap - 8 : 8 * tap, :]], axis=0)
        d_x = d_x + vec[2 + tap : 3 + tap, :] * up_rows(beyond, tap)[:BLOCK]
        edge[8 * tap - 8 : 8 * tap, :] = piece[:8]
    d_x = d_x.astype(jnp.bfloat16)
    d_pre[:, :width] = d_x
    d_pre[:, width:] = d_y
    pieces = (
        [column(d_x.astype(jnp.float32)), column(d_y.astype(jnp.float32))]
        + taps
        + [
            column(d_conv),
            column(d_rec.astype(jnp.float32)),
            column(d_in.astype(jnp.float32)),
            column(d_log * rec) * vec[10:11, :],
        ]
    )
    for place, piece in enumerate(pieces):
        sums[place : place + 1, :] += piece


def here():
    return (lax.axis_index("dp"), lax.axis_index("row"), lax.axis_index("col"))


def flip(index):
    return index + 1 - 2 * (index % 2)


def across(row):
    return (row + 2) % 4


def greet(peers):
    barrier = pltpu.get_barrier_semaphore()
    for peer in peers:
        pl.semaphore_signal(barrier, inc=1, device_id=peer, device_id_type=MESH)
    pl.semaphore_wait(barrier, len(peers))


class Copies:
    def __init__(self, send, recv):
        self.send, self.recv, self.used, self.sent = (send, recv, 0, [])

    def make(self, source, target, device):
        place = self.used
        self.used += 1
        if device is None:
            copy = pltpu.make_async_copy(source, target, self.recv.at[place])
        else:
            copy = pltpu.make_async_remote_copy(
                src_ref=source,
                dst_ref=target,
                send_sem=self.send.at[place],
                recv_sem=self.recv.at[place],
                device_id=device,
                device_id_type=MESH,
            )
            self.sent.append(copy)
        return copy

    def go(self, source, target, device):
        copy = self.make(source, target, device)
        copy.start()
        return copy

    def finish(self):
        for copy in self.sent:
            copy.wait_send()
        self.sent = []


def arrived(copy):
    copy.wait_recv()


def spread(copies, own, place, halves, between=lambda: None):
    z, r, c = here()
    twin, side, top = ((z, flip(r), c), (z, across(r), c), (z, r, 1 - c))
    to_side = copies.go(own, place(r, c), side)
    to_top = copies.go(own, place(r, c), top)
    to_twin = copies.go(own, place(r, c), twin)
    between()
    arrived(to_side)
    from_side = place(across(r), c)
    on_top = copies.go(halves(from_side, 0), halves(from_side, 0), top)
    late = [to_twin, copies.go(from_side, from_side, twin)]
    between()
    arrived(to_top)
    from_top = place(r, 1 - c)
    on_side = copies.go(halves(from_top, 1), halves(from_top, 1), side)
    late.append(copies.go(from_top, from_top, twin))
    far = place(across(r), 1 - c)
    between()
    for half, copy in enumerate((on_top, on_side)):
        arrived(copy)
        late.append(copies.go(halves(far, half), halves(far, half), twin))
    return late


def spread_tall(copies, own, place, between=lambda: None):
    z, r, c = here()
    twin, side, top = ((z, flip(r), c), (z, across(r), c), (z, r, 1 - c))
    to_side = copies.go(own, place(r, c), side)
    to_top = copies.go(own, place(r, c), top)
    late = [copies.go(own, place(r, c), twin)]
    between()
    arrived(to_side)
    from_side = place(across(r), c)
    on_top = copies.go(from_side, from_side, top)
    late.append(copies.go(from_side, from_side, twin))
    between()
    arrived(to_top)
    from_top = place(r, 1 - c)
    late.append(copies.go(from_top, from_top, twin))
    between()
    arrived(on_top)
    far = place(across(r), 1 - c)
    late.append(copies.go(far, far, twin))
    return late


def part(start, size, step):
    return pl.ds(pl.multiple_of(start * step, step), size)


class Moves:
    def __init__(self, copies, matrices, cuts):
        z, r, c = here()
        mine = z % 2
        sides = ((z, across(r), c), (z, flip(across(r)), c))
        pair = (flip(z), r, c)
        self.groups, self.locals, self.late = ([], [], [])
        self.begun, self.ended = (0, 0)

        def piece(ref, size, cut):
            length = size // 2 // cuts
            return ref.at[part(mine * cuts + cut, length, length), :]

        for source, target, size in matrices:
            for cut in range(cuts):
                group = []
                for peer in sides:
                    spot = piece(target(peer[1]), size, cut)
                    group.append(
                        (
                            copies.make(
                                piece(source(peer[1]), size, cut), piece(target(r), size, cut), peer
                            ),
                            copies.make(spot, spot, pair),
                        )
                    )
                self.groups.append(group)
        for source, target, size in matrices:
            self.locals.append(copies.go(source(r), target(r), None))
            self.late.append(copies.go(source(flip(r)), target(r), (z, flip(r), c)))

    def step(self):
        if self.begun - self.ended == 2 or self.begun == len(self.groups):
            if self.ended < self.begun:
                for first, second in self.groups[self.ended]:
                    arrived(first)
                    second.start()
                self.ended += 1
        if self.begun < len(self.groups):
            for first, _ in self.groups[self.begun]:
                first.start()
            self.begun += 1

    def finish(self):
        while self.ended < len(self.groups):
            self.step()
        for group in self.groups:
            for _, second in group:
                arrived(second)
        for copy in self.late:
            arrived(copy)
        for copy in self.locals:
            copy.wait()


def block_of(ref, rows, columns):
    return lambda row, col: ref.at[part(col, rows, rows), part(row, columns, columns)]


def halves_of(rows):
    return lambda ref, which: ref.at[pl.ds(which * (rows // 2), rows // 2), :]


def mlp_matrices(sources, targets):
    depth, width = (sources[0].shape[0], sources[0].shape[1] // 4)
    return [
        (
            lambda to, source=source: source.at[:, part(to, width, width)],
            lambda of, target=target: target.at[part(of, depth, depth), :],
            depth,
        )
        for source, target in zip(sources, targets)
    ]


def gather_kernel(
    x_in,
    c_in,
    s_in,
    g_in,
    x_proj,
    y_proj,
    out_in,
    x_all,
    c_all,
    s_all,
    g_all,
    mix_all,
    out_all,
    x_here,
    y_here,
    mix_in,
    load_sem,
    send,
    recv,
):
    z, r, c = here()
    twin, side, cross, top, pair = (
        (z, flip(r), c),
        (z, across(r), c),
        (z, flip(across(r)), c),
        (z, r, 1 - c),
        (flip(z), r, c),
    )
    loads = [
        pltpu.make_async_copy(source, target, load_sem.at[place])
        for place, (source, target) in enumerate(((x_proj, x_here), (y_proj, y_here)))
    ]
    for copy in loads:
        copy.start()
    greet((twin, side, cross, top, pair))
    copies = Copies(send, recv)
    rows, columns = x_in.shape
    depth, rec = (mix_in.shape[1], out_in.shape[0] // 4)
    matrices = [
        (lambda to: mix_in.at[to], lambda of: mix_all.at[part(of, depth, depth), :], depth),
        (
            lambda to: out_in.at[part(to, rec, rec), :],
            lambda of: out_all.at[:, part(of, columns, columns)],
            rec,
        ),
    ]
    moves = []

    def between():
        if not moves:
            for copy in loads:
                copy.wait()

            def body(at):
                strip = pl.ds(at, STRIP)
                x, y = (x_here[strip, :], y_here[strip, :])
                for to in range(4):
                    span = slice(to * rec, (to + 1) * rec)
                    mix_in[to, strip, :] = jnp.concatenate([x[:, span], y[:, span]], axis=1)

            strips(depth, body)
            moves.append(Moves(copies, matrices, 2))
        moves[0].step()

    small = g_all.at[:, part(r, depth, depth)]
    late = spread_tall(copies, x_in, block_of(x_all, rows, columns), between)
    locals_ = [
        copies.go(x_in, block_of(x_all, rows, columns)(r, c), None),
        copies.go(c_in, block_of(c_all, rows, columns)(r, c), None),
        copies.go(s_in, s_all.at[r], None),
        copies.go(g_in, small, None),
    ]
    for peer in (twin, side, cross):
        late.append(copies.go(g_in, small, peer))
    flags_side = copies.go(s_in, s_all.at[r], side)
    late.append(copies.go(s_in, s_all.at[r], twin))
    late.extend(spread_tall(copies, c_in, block_of(c_all, rows, columns), between))
    arrived(flags_side)
    late.append(copies.go(s_all.at[across(r)], s_all.at[across(r)], twin))
    moves[0].finish()
    for copy in late:
        arrived(copy)
    for copy in locals_:
        copy.wait()
    copies.finish()


def gather(x_in, c_in, s_in, g_in, x_proj, y_proj, out_in):
    rows, columns = x_in.shape
    depth, wide = x_proj.shape

    def shape(*dims, kind=jnp.bfloat16):
        return jax.ShapeDtypeStruct(dims, kind)

    outs = [
        shape(2 * rows, 4 * columns),
        shape(2 * rows, 4 * columns),
        shape(4, *s_in.shape, kind=s_in.dtype),
        shape(g_in.shape[0], 4 * depth, kind=g_in.dtype),
        shape(4 * depth, wide // 2),
        shape(out_in.shape[0] // 4, 4 * columns),
    ]
    dma = pltpu.SemaphoreType.DMA
    return pl.pallas_call(
        gather_kernel,
        in_specs=[pl.BlockSpec(memory_space=pltpu.HBM)] * 7,
        out_specs=[pl.BlockSpec(memory_space=pltpu.HBM)] * 6,
        out_shape=outs,
        scratch_shapes=[
            pltpu.VMEM((depth, wide), jnp.bfloat16),
            pltpu.VMEM((depth, wide), jnp.bfloat16),
            pltpu.VMEM((4, depth, wide // 2), jnp.bfloat16),
            dma((2,)),
            dma((64,)),
            dma((64,)),
        ],
        compiler_params=pltpu.CompilerParams(
            collective_id=GATHER_ID, has_side_effects=True, vmem_limit_bytes=60 << 20
        ),
        name="gather",
    )(x_in, c_in, s_in, g_in, x_proj, y_proj, out_in)


STRIP = 16


def strips(count, body):
    def run(index, nothing):
        body(pl.multiple_of(index * STRIP, STRIP))
        return nothing

    lax.fori_loop(0, count // STRIP, run, 0)


def token_shard(row, col):
    return col * 4 + row


def reduce_shards(
    copies, parts, twin_in, sums, side_in, top_in, hop_in, between=lambda: None, tall=False
):
    z, r, c = here()
    twin, side, top = ((z, flip(r), c), (z, across(r), c), (z, r, 1 - c))
    size = side_in.shape[0]
    half = size // 2

    def shard(row, col):
        return pl.multiple_of(token_shard(row, col) * size, size)

    spots = [(across(r), 1 - c), (across(r), c), (r, 1 - c), (r, c)]
    from_twin = [
        copies.go(parts.at[pl.ds(shard(flip(row), col), size), :], twin_in.at[place], twin)
        for place, (row, col) in enumerate(spots)
    ]

    def add_twin(place):
        arrived(from_twin[place])
        start = shard(*spots[place])

        def body(at):
            total = parts[pl.ds(start + at, STRIP), :].astype(jnp.float32) + twin_in[
                place, pl.ds(at, STRIP), :
            ].astype(jnp.float32)
            sums[place, pl.ds(at, STRIP), :] = total.astype(jnp.bfloat16)

        strips(size, body)

    def add_hop(place, which, hop):
        def body(at):
            rows = pl.ds(which * half + at, STRIP)
            total = sums[place, rows, :].astype(jnp.float32) + hop_in[
                hop, pl.ds(at, STRIP), :
            ].astype(jnp.float32)
            sums[place, rows, :] = total.astype(jnp.bfloat16)

        strips(half, body)

    def rows_of(ref, which):
        return ref.at[pl.ds(which * half, half), :]

    def total(at):
        rows = pl.ds(at, STRIP)
        return (
            sums[3, rows, :].astype(jnp.float32)
            + side_in[rows, :].astype(jnp.float32)
            + top_in[rows, :].astype(jnp.float32)
        )

    add_twin(0)
    if tall:
        hops = [copies.go(rows_of(sums.at[0], k), hop_in.at[k], top) for k in (0, 1)]
        add_twin(2)
        to_top = copies.go(sums.at[2], top_in, top)
        add_twin(1)
        add_twin(3)
        between()
        to_side = []
        for k in (0, 1):
            arrived(hops[k])
            add_hop(1, k, k)
            to_side.append(copies.go(rows_of(sums.at[1], k), rows_of(side_in, k), side))
        between()
        for copy in [to_top, *to_side]:
            arrived(copy)
        return total
    hop_side = copies.go(rows_of(sums.at[0], 0), hop_in.at[0], side)
    hop_top = copies.go(rows_of(sums.at[0], 1), hop_in.at[1], top)
    add_twin(1)
    waits = [copies.go(rows_of(sums.at[1], 0), rows_of(side_in, 0), side)]
    add_twin(2)
    waits.append(copies.go(rows_of(sums.at[2], 1), rows_of(top_in, 1), top))
    add_twin(3)
    between()
    arrived(hop_top)
    add_hop(1, 1, 1)
    waits.append(copies.go(rows_of(sums.at[1], 1), rows_of(side_in, 1), side))
    arrived(hop_side)
    add_hop(2, 0, 0)
    waits.append(copies.go(rows_of(sums.at[2], 0), rows_of(top_in, 0), top))
    between()
    for copy in waits:
        arrived(copy)
    return total


def reduce_scratch(size, width):
    return [
        pltpu.VMEM((4, size, width), jnp.bfloat16),
        pltpu.VMEM((4, size, width), jnp.bfloat16),
        pltpu.VMEM((size, width), jnp.bfloat16),
        pltpu.VMEM((size, width), jnp.bfloat16),
        pltpu.VMEM((2, size // 2, width), jnp.bfloat16),
    ]


def near():
    z, r, c = here()
    return ((z, flip(r), c), (z, across(r), c), (z, r, 1 - c))


def spread_rows(copies, mine, full, between=lambda: None, tall=False):
    z, r, c = here()
    size = mine.shape[0]
    half = size // 2

    def place(row, col):
        return full.at[pl.ds(pl.multiple_of(token_shard(row, col) * size, size), size), :]

    local = copies.go(mine, place(r, c), None)
    if tall:
        late = spread_tall(copies, mine, place, between)
    else:
        late = spread(
            copies, mine, place, lambda ref, which: ref.at[pl.ds(which * half, half), :], between
        )
    for copy in late:
        arrived(copy)
    local.wait()


def mark_rows(flags, tail):
    stale = 1.0 - flags
    longer = jnp.concatenate([tail[...], stale], axis=0)
    tail[...] = stale[BLOCK - 8 :]
    pair = stale * down_rows(longer, 1)[8:]
    triple = pair * down_rows(longer, 2)[8:]
    lane = lax.broadcasted_iota(jnp.int32, flags.shape, 1)
    return jnp.where(lane == 0, flags, jnp.where(lane == 1, stale, jnp.where(lane == 2, pair, triple)))


def forward_kernel(vec, rec_w, in_w, gains, *refs):
    x_in, s_in, mix_in, out_in = refs[:4]
    mlp_in, outs, scratch = (refs[4:7], refs[7:21], refs[21:])
    full, resid_mid = outs[:2]
    mlp_all, kept_out = (outs[2:5], outs[5:])
    kept, (tail, carry, parts), (*buffers, mine, kept_sem, send, recv) = (
        scratch[:9],
        scratch[9:12],
        scratch[12:],
    )
    x_all, flags, mix_w, out_w, mark_tail, load_sem, *buffers = buffers
    normed, pre, mixed, *saved, masks = kept
    loads = [
        pltpu.make_async_copy(source, target, load_sem.at[8 + place])
        for place, (source, target) in enumerate(
            ((mix_in, mix_w), (s_in, flags), (out_in, out_w))
        )
    ]

    def load_rows(index):
        rows = pl.ds(pl.multiple_of(index * BLOCK, BLOCK), BLOCK)
        return pltpu.make_async_copy(x_in.at[rows, :], x_all.at[rows, :], load_sem.at[index])

    load_rows(0).start()
    for copy in loads:
        copy.start()
    for index in range(1, x_all.shape[0] // BLOCK):
        load_rows(index).start()
    z, r, c = here()
    greet((*near(), (z, flip(across(r)), c), (flip(z), r, c)))
    copies = Copies(send, recv)
    moves = Moves(copies, mlp_matrices(mlp_in, mlp_all), 2)
    moves.step()
    moves.step()
    for copy in loads:
        copy.wait()
    mark_tail[...] = jnp.zeros_like(mark_tail)
    tail[...] = jnp.zeros_like(tail)
    carry[...] = jnp.zeros_like(carry)

    def block(index, nothing):
        start = pl.multiple_of(index * BLOCK, BLOCK)
        rows = pl.ds(start, BLOCK)
        for turn in (3, 6):

            @pl.when(index == turn)
            def _():
                moves.step()

        load_rows(index).wait()
        marks = mark_rows(flags[rows, :8].astype(jnp.float32), mark_tail)
        masks[rows, :] = marks

        def norm(at):
            strip = pl.ds(start + at, STRIP)
            values = x_all[strip, :].astype(jnp.float32)
            scale = lax.rsqrt(jnp.mean(values * values, axis=1, keepdims=True) + EPS)
            normed[strip, :] = (values * scale * gains[0:1, :]).astype(jnp.bfloat16)

        strips(BLOCK, norm)
        pre[rows, :] = jnp.dot(normed[rows, :], mix_w[...], preferred_element_type=jnp.float32)
        mixer_forward_step(
            pre.at[rows, :],
            marks,
            vec,
            rec_w,
            in_w,
            mixed.at[rows, :],
            *[ref.at[rows, :] for ref in saved],
            tail,
            carry,
        )
        width = rec_w.shape[0]
        parts[rows, :] = jnp.dot(
            mixed[rows, :width], out_w[...], preferred_element_type=jnp.float32
        ).astype(jnp.bfloat16)
        return nothing

    lax.fori_loop(0, x_all.shape[0] // BLOCK, block, 0)
    keeping = [
        pltpu.make_async_copy(source, target, kept_sem.at[place])
        for place, (source, target) in enumerate(zip(kept, kept_out))
    ]
    for copy in keeping:
        copy.start()
    total = reduce_shards(copies, parts, *buffers, between=moves.step, tall=True)
    size = mine.shape[0]
    start = pl.multiple_of(token_shard(r, c) * size, size)

    def body(at):
        rows = pl.ds(at, STRIP)
        values = x_all[pl.ds(start + at, STRIP), :].astype(jnp.float32) + total(at)
        resid_mid[rows, :] = values
        scale = lax.rsqrt(jnp.mean(values * values, axis=1, keepdims=True) + EPS)
        mine[rows, :] = (values * scale * gains[1:2, :]).astype(jnp.bfloat16)

    strips(size, body)
    spread_rows(copies, mine, full, moves.step, tall=True)
    moves.finish()
    for copy in keeping:
        copy.wait()
    copies.finish()


def norm_pull(values, gain, incoming):
    scale = lax.rsqrt(jnp.mean(values * values, axis=1, keepdims=True) + EPS)
    scaled = gain * incoming
    dots = jnp.sum(scaled * values, axis=1, keepdims=True)
    grad = scale * scaled - values * (scale * scale * scale * dots / values.shape[1])
    return (grad, jnp.sum(incoming * values * scale, axis=0, keepdims=True))


def vmem_call(kernel, name, place, arrays, outs, spaces, scratch, count, loose=()):
    return pl.pallas_call(
        kernel,
        in_specs=[pl.BlockSpec(memory_space=pltpu.VMEM)] * len(arrays)
        + [pl.BlockSpec(memory_space=pltpu.HBM)] * len(loose),
        out_specs=[pl.BlockSpec(memory_space=space) for space in spaces],
        out_shape=outs,
        scratch_shapes=scratch
        + [pltpu.SemaphoreType.DMA((count,)), pltpu.SemaphoreType.DMA((count,))],
        compiler_params=pltpu.CompilerParams(
            collective_id=place, has_side_effects=True, vmem_limit_bytes=VMEM_BYTES
        ),
        name=name,
    )(*arrays, *loose)


AHEAD = 3
DEPTH = 4
SUM_LAG = 1
HAND_LAG = 3
LAG = 4
RING = 9
SEGMENTS = 2


def run_loop(first, last, body):
    def run(index, nothing):
        body(index)
        return nothing

    lax.fori_loop(first, last, run, 0)


def remote(source, target, sender, receiver, device):
    return pltpu.make_async_remote_copy(
        src_ref=source,
        dst_ref=target,
        send_sem=sender,
        recv_sem=receiver,
        device_id=device,
        device_id_type=MESH,
    )


class Line:
    def __init__(self, own, left, right, out, sems, lead):
        self.own, self.left, self.right, self.out, self.lead = (own, left, right, out, lead)
        (
            self.end_send,
            self.low_recv,
            self.high_recv,
            self.out_recv,
            self.mid_send,
            self.first_send,
            self.last_send,
            self.hand_send,
            self.on_send,
        ) = sems
        z, r, c = here()
        self.chunk = left.shape[1]
        self.rows = out.shape[1]
        self.half = self.rows // 2
        self.per = self.half // self.chunk
        self.first = 4 * self.per
        self.chunks = 4 * SEGMENTS * self.per + lead
        self.total = self.chunks + LAG
        self.at = 0
        self.ahead = 0
        self.is_end = (z == 0) | (z == 3)
        self.near_z = (jnp.where(z == 0, 1, 2), r, c)
        self.outer = (jnp.where(z == 1, 0, 3), r, c)
        self.other = (3 - z, r, c)

    def extra(self, index):
        return (index >= self.first) & (index < self.first + self.lead)

    def spot(self, index):
        later = index >= self.first + self.lead
        plain = index - jnp.where(later, self.lead, 0)
        step = jnp.where(self.extra(index), 0, plain // self.per)
        strip = jnp.where(self.extra(index), index - self.first, plain % self.per)
        return (step // 4, step % 4, strip)

    def peer_row(self, index):
        r = here()[1]
        step = self.spot(index)[1]
        return (r // 2 + step // 2) % 2 * 2 + (r % 2 + step % 2) % 2

    def stays(self, index):
        return self.spot(index)[1] == 0

    def span(self, index, which):
        segment, _, strip = self.spot(index)
        start = (segment * 4 + self.peer_row(index)) * self.rows + which * self.half
        outside = SEGMENTS * 4 * self.rows + which * self.lead * self.chunk
        start = jnp.where(self.extra(index), outside, start)
        return pl.ds(pl.multiple_of(start + strip * self.chunk, self.chunk), self.chunk)

    def own_at(self, index, which):
        return self.own.at[self.span(index, which), :]

    def out_at(self, index, which, row):
        segment, _, strip = self.spot(index)
        place = jnp.where(self.extra(index), 4 * SEGMENTS, segment * 4 + row)
        start = pl.multiple_of(which * self.half + strip * self.chunk, self.chunk)
        return self.out.at[place, pl.ds(start, self.chunk), :]

    def end_sends(self, index):
        low = here()[0] // 3
        return (
            remote(
                self.own_at(index, low),
                self.left.at[index % RING],
                self.end_send.at[0, index],
                self.low_recv.at[index],
                self.near_z,
            ),
            remote(
                self.own_at(index, 1 - low),
                self.right.at[1, index % RING],
                self.end_send.at[1, index],
                self.high_recv.at[1, index],
                self.near_z,
            ),
        )

    def to_other(self, index):
        low = here()[0] - 1
        return remote(
            self.own_at(index, 1 - low),
            self.right.at[0, index % RING],
            self.mid_send.at[index],
            self.high_recv.at[0, index],
            self.other,
        )

    def from_outer(self, index):
        low = here()[0] - 1
        return (
            remote(
                self.own_at(index, low),
                self.left.at[index % RING],
                self.mid_send.at[index],
                self.low_recv.at[index],
                self.outer,
            ),
            remote(
                self.own_at(index, 1 - low),
                self.right.at[1, index % RING],
                self.mid_send.at[index],
                self.high_recv.at[1, index],
                self.outer,
            ),
        )

    def hand(self, index):
        z, r, c = here()
        low = z - 1
        mine, spot = (self.own_at(index, low), self.out_at(index, low, r))
        return (
            pltpu.make_async_copy(mine, spot, self.out_recv.at[low, index]),
            remote(
                mine,
                spot,
                self.hand_send.at[index],
                self.out_recv.at[low, index],
                (z, self.peer_row(index), c),
            ),
        )

    def along(self, index):
        low = here()[0] - 1
        spot = self.out_at(index, low, self.peer_row(index))
        return (
            remote(
                spot, spot, self.first_send.at[index], self.out_recv.at[low, index], self.outer
            ),
            remote(spot, spot, self.last_send.at[index], self.out_recv.at[low, index], self.other),
        )

    def onward(self, index):
        low = here()[0] - 1
        spot = self.out_at(index, 1 - low, self.peer_row(index))
        return remote(
            spot, spot, self.on_send.at[index], self.out_recv.at[1 - low, index], self.outer
        )

    def came_back(self, index):
        for which in (0, 1):
            spot = self.out_at(index, which, self.peer_row(index))
            remote(
                spot, spot, self.end_send.at[0, index], self.out_recv.at[which, index], self.near_z
            ).wait_recv()

    def end_step(self, index):
        @pl.when(index < self.chunks)
        def _():
            @pl.when(index >= DEPTH)
            def _():
                for copy in self.end_sends(index - DEPTH):
                    copy.wait_send()

            @pl.when(index >= RING)
            def _():
                self.came_back(index - RING)

            for copy in self.end_sends(index):
                copy.start()

    def mid_step(self, index):
        own, left, right, low = (self.own, self.left, self.right, here()[0] - 1)

        @pl.when(index < self.chunks)
        def _():
            self.from_outer(index)[1].wait_recv()
            span = self.span(index, 1 - low)
            total = own[span, :].astype(jnp.float32) + right[1, index % RING].astype(jnp.float32)
            own[span, :] = total.astype(jnp.bfloat16)
            self.to_other(index).start()

        @pl.when((index >= SUM_LAG) & (index < self.chunks + SUM_LAG))
        def _():
            back = index - SUM_LAG
            self.from_outer(back)[0].wait_recv()
            self.to_other(back).wait_recv()
            span = self.span(back, low)
            total = (
                own[span, :].astype(jnp.float32)
                + left[back % RING].astype(jnp.float32)
                + right[0, back % RING].astype(jnp.float32)
            )
            own[span, :] = total.astype(jnp.bfloat16)

            @pl.when(self.stays(back))
            def _():
                self.hand(back)[0].start()

            @pl.when(jnp.logical_not(self.stays(back)))
            def _():
                self.hand(back)[1].start()

        @pl.when((index >= HAND_LAG) & (index < self.chunks + HAND_LAG))
        def _():
            back = index - HAND_LAG

            @pl.when(self.stays(back))
            def _():
                self.hand(back)[0].wait()

            @pl.when(jnp.logical_not(self.stays(back)))
            def _():
                self.hand(back)[1].wait_recv()

            for copy in self.along(back):
                copy.start()

        @pl.when(index >= LAG)
        def _():
            copy = self.onward(index - LAG)
            copy.wait_recv()
            copy.start()

    def prime(self):
        @pl.when(self.is_end)
        def _():
            run_loop(0, AHEAD, self.end_step)

        self.ahead = AHEAD

    def advance(self, count):
        first, last = (self.at, min(self.at + count, self.total))
        self.at = last
        if first == last:
            return

        @pl.when(self.is_end)
        def _():
            run_loop(self.ahead, last + AHEAD, self.end_step)

        self.ahead = last + AHEAD

        @pl.when(jnp.logical_not(self.is_end))
        def _():
            run_loop(first, last, self.mid_step)

    def one(self, index):
        @pl.when(self.is_end)
        def _():
            self.end_step(index + AHEAD)

        @pl.when(jnp.logical_not(self.is_end))
        def _():
            self.mid_step(index)

    def skip(self, count):
        self.at += count
        self.ahead += count

    def end_done(self, index):
        @pl.when(index >= self.chunks - DEPTH)
        def _():
            for copy in self.end_sends(index):
                copy.wait_send()

        @pl.when(index >= self.chunks - RING)
        def _():
            self.came_back(index)

    def mid_done(self, index):
        self.to_other(index).wait_send()

        @pl.when(jnp.logical_not(self.stays(index)))
        def _():
            self.hand(index)[1].wait_send()

        for copy in self.along(index):
            copy.wait_send()
        self.onward(index).wait_send()

    def finish(self):
        self.advance(self.total)

        @pl.when(self.is_end)
        def _():
            run_loop(0, self.chunks, self.end_done)

        @pl.when(jnp.logical_not(self.is_end))
        def _():
            run_loop(0, self.chunks, self.mid_done)


def line_scratch(rows, width, chunk, lead):
    dma = pltpu.SemaphoreType.DMA
    chunks = 4 * SEGMENTS * (rows // 2 // chunk) + lead
    return [
        pltpu.VMEM((4 * SEGMENTS * rows + 2 * lead * chunk, width), jnp.bfloat16),
        pltpu.VMEM((RING, chunk, width), jnp.bfloat16),
        pltpu.VMEM((2, RING, chunk, width), jnp.bfloat16),
        dma((2, chunks)),
        dma((chunks,)),
        dma((2, chunks)),
        dma((2, chunks)),
        dma((chunks,)),
        dma((chunks,)),
        dma((chunks,)),
        dma((chunks,)),
        dma((chunks,)),
    ]


LINE_REFS = 12
PACK = 32
CHUNK = 32
PACE = (2, 3, 3, 1, 1, 2, 2, 3, 3)
BLOCK_STEPS = 1


def z_peers():
    z, r, c = here()
    return [((z + step) % 4, r, c) for step in (1, 2, 3)]


def plane_peers():
    z, r, c = here()
    return [(z, (r + turn % 4) % 4, (c + turn // 4) % 2) for turn in range(1, 8)]


def hand_out(copies, source, target):
    z, r, c = here()
    twin, side, _ = near()
    cross = (z, flip(across(r)), c)
    columns = target.shape[1]
    size = source.shape[0]

    def piece(row):
        return source.at[:, part(row, columns, columns)]

    spot = target.at[part(r, size, size), :]
    waits = [copies.go(piece(peer[1]), spot, peer) for peer in (side, cross, twin)]
    local = copies.go(piece(r), spot, None)

    def done():
        for copy in waits:
            arrived(copy)
        local.wait()

    return done


def gate_tiles(width):
    tiles = []
    for tile in range(5):
        first, rest = (0, width)
        if tile < 4:
            tiles.append((tile, 0, width, tile // 2, tile % 2 * width))
        else:
            tiles.append((tile, 0, 384, 0, 2 * width))
            tiles.append((tile, 384, width - 384, 1, 2 * width))
    return tiles


def backward_kernel(resid_mid, both_gains, masks, vec, rec_w, in_w, mix_w, out_w, *refs):
    parts_in, out_parts, c_all, x_all, *kept_in = refs[:12]
    gate_grad, up_grad, down_grad = refs[12:15]
    grad, output, grads, out_gates, out_vec, out_gain = refs[15:21]
    scratch = refs[21:]
    line_refs, scratch = (scratch[:LINE_REFS], scratch[LINE_REFS:])
    parts, cot, resid, branch, d_resid, d_pre, d_gates, edge, carry = scratch[:9]
    kept, scratch = (scratch[9:17], scratch[17:])
    sums, gains, vec_z, gain_z, vec_sum, gain_sum, vec_in, gain_in = scratch[:8]
    *buffers, mine, mine_out, load_sem, gate_sem, small_send, small_recv, free, send, recv = scratch[8:]
    normed, pre, mixed, x_pre, conv, rec_gate, in_gate, states = kept
    z, r, c = here()
    twin, side, top = near()
    cross = (z, flip(across(r)), c)
    lines, plane = (z_peers(), plane_peers())
    greet(lines + plane)
    copies = Copies(send, recv)
    line = Line(*line_refs[:3], grads, line_refs[3:], PACK // CHUNK)
    own, half, rows_all = (line.own, line.half, 4 * line.rows)
    size = mine.shape[0]
    shard = part(token_shard(r, c), size, size)
    width, ff = (x_pre.shape[1], gate_grad.shape[1])
    head, rest = (own.shape[1] - 2 * ff, 3 * ff - own.shape[1])
    first, second = (pl.ds(0, rows_all), pl.ds(rows_all, rows_all))
    loads = [
        pltpu.make_async_copy(source, target, load_sem.at[place])
        for place, (source, target) in enumerate(
            zip(
                [
                    gate_grad,
                    up_grad,
                    down_grad.at[:, pl.ds(0, head)],
                    parts_in,
                    down_grad.at[:, pl.ds(head, rest)],
                    c_all.at[shard, :],
                    x_all.at[shard, :],
                    *kept_in,
                ],
                [
                    own.at[first, pl.ds(0, ff)],
                    own.at[first, pl.ds(ff, ff)],
                    own.at[first, pl.ds(2 * ff, head)],
                    parts,
                    own.at[second, pl.ds(0, rest)],
                    cot,
                    resid,
                    *kept,
                ],
            )
        )
    ]
    for copy in loads:
        copy.start()
    for ref in (gains, sums, edge, carry):
        ref[...] = jnp.zeros_like(ref)
    for copy in loads[:3]:
        copy.wait()
    line.prime()
    loads[3].wait()
    pace = iter(PACE)

    def between():
        line.advance(next(pace))

    total = reduce_shards(copies, parts, *buffers, between=between)
    for copy in loads[4:]:
        copy.wait()

    def body(at):
        rows = pl.ds(at, STRIP)
        values, piece = norm_pull(resid_mid[rows, :], both_gains[1:2, :], total(at))
        values = values + cot[rows, :].astype(jnp.float32)
        gains[1:2, :] += piece
        d_resid[rows, :] = values
        mine[rows, :] = values.astype(jnp.bfloat16)

    strips(size, body)
    spread_rows(copies, mine, branch, between)
    copies.finish()
    last = branch.shape[0] // BLOCK - 1

    def block(index, base):
        start = pl.multiple_of((last - index) * BLOCK, BLOCK)
        rows = pl.ds(start, BLOCK)
        before = pl.ds(pl.multiple_of(jnp.maximum(start - 8, 0), 8), 8)
        mixer_backward_step(
            lax.dot_general(
                branch[rows, :], out_w[...], CONTRACT_COLS, preferred_element_type=jnp.float32
            ),
            pre.at[rows, :],
            masks[rows, :],
            vec,
            rec_w,
            in_w,
            x_pre.at[rows, :],
            x_pre.at[before, :],
            conv.at[rows, :],
            rec_gate.at[rows, :],
            in_gate.at[rows, :],
            states.at[rows, :],
            states.at[before, :],
            d_pre.at[rows, :],
            d_gates.at[rows, :],
            sums,
            edge,
            carry,
        )
        parts[rows, :] = lax.dot_general(
            d_pre[rows, :], mix_w[...], CONTRACT_COLS, preferred_element_type=jnp.float32
        ).astype(jnp.bfloat16)
        for step in range(BLOCK_STEPS):
            line.one(base + BLOCK_STEPS * index + step)
        return base

    lax.fori_loop(0, last + 1, block, line.at)
    line.skip(BLOCK_STEPS * (last + 1))
    total_back = reduce_shards(copies, parts, *buffers, between=between)

    def body_back(at):
        rows = pl.ds(at, STRIP)
        values, piece = norm_pull(
            resid[rows, :].astype(jnp.float32), both_gains[0:1, :], total_back(at)
        )
        gains[0:1, :] += piece
        mine[rows, :] = (d_resid[rows, :] + values).astype(jnp.bfloat16)

    strips(size, body_back)
    for peer in (twin, side, top):
        pl.semaphore_signal(free, inc=1, device_id=peer, device_id_type=MESH)
    copies.finish()
    load = pltpu.make_async_copy(out_parts, parts, load_sem.at[0])
    load.start()
    grad_done = hand_out(copies, mine, grad)
    small = [
        [
            remote(
                source,
                target.at[3 - step],
                small_send.at[kind, step - 1],
                small_recv.at[kind, 3 - step],
                lines[step - 1],
            )
            for step in (1, 2, 3)
        ]
        for kind, (source, target) in enumerate(((sums, vec_z), (gains, gain_z)))
    ]
    for kind in small:
        for copy in kind:
            copy.start()
    blocks = lax.dot_general(conv[...], d_gates[...], CONTRACT_ROWS, preferred_element_type=jnp.float32)
    rows_half = width // 2
    lane = lax.broadcasted_iota(jnp.int32, (rows_half, 2 * width), 1)
    mingled = jnp.where(
        lane // rows_half % 2 == 0, blocks[:rows_half], blocks[rows_half:]
    ).astype(jnp.bfloat16)
    for tile, begin, length, which, spot in gate_tiles(2 * width):
        own[pl.ds(2 * rows_all + which * PACK, PACK), spot : spot + length] = mingled[
            tile * PACK : (tile + 1) * PACK, begin : begin + length
        ]

    def weights(index, base):
        columns = pl.ds(pl.multiple_of(index * 256, 256), 256)
        rows = pl.ds(pl.multiple_of(rows_all + index * 256, 256), 256)
        own[rows, rest : rest + 2 * width] = lax.dot_general(
            normed[:, columns], d_pre[...], CONTRACT_ROWS, preferred_element_type=jnp.float32
        ).astype(jnp.bfloat16)
        own[rows, rest + 2 * width :] = lax.dot_general(
            branch[:, columns], mixed[...], CONTRACT_ROWS, preferred_element_type=jnp.float32
        ).astype(jnp.bfloat16)
        line.one(base + index)
        return base

    lax.fori_loop(0, rows_all // 256, weights, line.at)
    line.skip(rows_all // 256)
    assert line.at + AHEAD <= line.first + line.lead
    load.wait()
    pl.semaphore_wait(free, 3)
    total_out = reduce_shards(copies, parts, *buffers, between=between)

    def body_out(at):
        rows = pl.ds(at, STRIP)
        mine_out[rows, :] = (resid_mid[rows, :] + total_out(at)).astype(jnp.bfloat16)

    strips(size, body_out)
    output_done = hand_out(copies, mine_out, output)
    spread_out = [
        [
            remote(
                source,
                target.at[6 - step],
                small_send.at[kind, 3 + step],
                small_recv.at[kind, 3 + 6 - step],
                peer,
            )
            for step, peer in enumerate(plane)
        ]
        for kind, (source, target) in enumerate(((vec_sum, vec_in), (gain_sum, gain_in)))
    ]
    for kind in small:
        for copy in kind:
            copy.wait_recv()
    vec_sum[...] = sums[...] + vec_z[0] + vec_z[1] + vec_z[2]
    gain_sum[...] = gains[...] + gain_z[0] + gain_z[1] + gain_z[2]
    for kind in spread_out:
        for copy in kind:
            copy.start()
    line.advance(max(line.first + line.lead + RING + 2 - line.at, 0))
    gate_moves = [
        remote(
            grads.at[4 * SEGMENTS, pl.ds(which * half, PACK), :],
            out_gates.at[r, which],
            small_send.at[0, 10 + 2 * place + which],
            small_recv.at[0, 10 + 2 * place + which],
            peer,
        )
        for place, peer in enumerate((twin, side, cross))
        for which in (0, 1)
    ]
    gate_local = [
        pltpu.make_async_copy(
            grads.at[4 * SEGMENTS, pl.ds(which * half, PACK), :],
            out_gates.at[r, which],
            gate_sem.at[which],
        )
        for which in (0, 1)
    ]
    for copy in gate_moves + gate_local:
        copy.start()
    for kind in spread_out:
        for copy in kind:
            copy.wait_recv()
    all_gains = gain_sum[...]
    for place in range(7):
        all_gains = all_gains + gain_in[place]
    gain_z[0] = all_gains
    out_gain[...] = gain_z[0, :, part(r, out_gain.shape[1], out_gain.shape[1])]
    out_vec[r] = vec_sum[...]
    for step in (0, 1, 2):
        out_vec[(r + 3 - step) % 4] = vec_in[6 - step]
    line.finish()
    grad_done()
    output_done()
    for copy in gate_moves:
        copy.wait_recv()
    for copy in gate_local:
        copy.wait()
    for group in small + spread_out + [gate_moves]:
        for copy in group:
            copy.wait_send()
    copies.finish()


def unpack_kernel(grads, gates, vec, output, grad_in, *outs):
    out_t, grad_t, x_grad, y_grad, out_grad, gate_grad, up_grad, down_grad, rec_w, in_w = outs[:10]
    wide, ff, rec = (grads.shape[2], gate_grad.shape[1] // 4, x_grad.shape[1] // 4)
    head = wide - 2 * ff
    rest = ff - head
    out_t[...] = output[...].astype(jnp.float32).T.astype(out_t.dtype)
    grad_t[...] = grad_in[...].astype(jnp.float32).T
    for row in range(4):
        wide_span, span = (slice(row * ff, (row + 1) * ff), slice(row * rec, (row + 1) * rec))

        def body(at):
            rows = pl.ds(at, 64)
            early = grads[row, rows, :].astype(jnp.float32)
            late = grads[4 + row, rows, :].astype(jnp.float32)
            gate_grad[rows, wide_span] = early[:, :ff]
            up_grad[rows, wide_span] = early[:, ff : 2 * ff]
            down_grad[rows, row * ff : row * ff + head] = early[:, 2 * ff :]
            down_grad[rows, row * ff + head : (row + 1) * ff] = late[:, :rest]
            x_grad[rows, span] = late[:, rest : rest + rec]
            y_grad[rows, span] = late[:, rest + rec : rest + 2 * rec]

        body(0)
        body(64)
        last = grads[4 + row, :, rest + 2 * rec : rest + 3 * rec]
        out_grad[span, :] = last.astype(jnp.float32).T
    heads, width = (rec_w.shape[0], rec_w.shape[1])
    for tile in range(5):
        spots = [item for item in gate_tiles(2 * rec) if item[0] == tile]
        values = jnp.concatenate(
            [gates[0, which, :, spot : spot + length] for _, _, length, which, spot in spots],
            axis=1,
        ).astype(jnp.float32)
        rows = slice(tile * PACK, (tile + 1) * PACK)
        for place in range(heads):
            rec_w[place, rows, :] = values[:, place * width : (place + 1) * width]
            in_w[place, rows, :] = values[:, rec + place * width : rec + (place + 1) * width]
    line = 0
    for ref in outs[10:]:
        for row in range(ref.shape[0]):
            ref[row : row + 1, :] = jnp.concatenate(
                [vec[place, line : line + 1, :] for place in range(4)], axis=1
            )
            line += 1


def unpack(grads, gates, vec, output, grad_in, rec, ff, heads):
    depth, wide = grads.shape[1:]
    tokens, head = (output.shape[0], rec // heads)

    def out(*dims, kind=jnp.float32):
        return jax.ShapeDtypeStruct(dims, kind)

    def rows(columns):
        return pl.BlockSpec((BLOCK, columns), lambda i: (i, 0))

    def columns(length):
        return pl.BlockSpec((length, BLOCK), lambda i: (0, i))

    def whole(*dims):
        return pl.BlockSpec(dims, lambda i: (0,) * len(dims))

    blocks = pl.BlockSpec((heads, head, head), lambda i: (i, 0, 0))
    lines = (1, 1, 4, 1, 1, 1, 1)
    return pl.pallas_call(
        unpack_kernel,
        grid=(depth // BLOCK,),
        in_specs=[
            pl.BlockSpec((8, BLOCK, wide), lambda i: (0, i, 0)),
            pl.BlockSpec((1, 2, PACK, wide), lambda i: (i, 0, 0, 0)),
            whole(*vec.shape),
            columns(tokens),
            columns(tokens),
        ],
        out_specs=[rows(tokens), rows(tokens), rows(4 * rec), rows(4 * rec), columns(4 * rec)]
        + [rows(4 * ff)] * 3
        + [blocks] * 2
        + [whole(count, 4 * rec) for count in lines],
        out_shape=[
            out(depth, tokens, kind=output.dtype),
            out(depth, tokens),
            out(depth, 4 * rec),
            out(depth, 4 * rec),
            out(4 * rec, depth),
        ]
        + [out(depth, 4 * ff)] * 3
        + [out(4 * heads, head, head)] * 2
        + [out(count, 4 * rec) for count in lines],
        compiler_params=pltpu.CompilerParams(vmem_limit_bytes=60 << 20),
        name="unpack",
    )(grads, gates, vec, output, grad_in)


def dot(left, right, dims, kind=jnp.float32):
    return lax.dot_general(left, right, dims, preferred_element_type=jnp.float32).astype(kind)


def local_plane(
    inputs,
    cotangent,
    starts,
    x_proj,
    y_proj,
    out_proj,
    gate_proj,
    up_proj,
    down_proj,
    mix_gain,
    mlp_gain,
    x_bias,
    y_bias,
    conv_w,
    conv_b,
    rec_gate_w,
    in_gate_w,
    rec_gate_b,
    in_gate_b,
    decay_param,
):
    z, r, c = here()
    depth = x_proj.shape[0]
    rec = x_proj.shape[1] // 4
    width = gate_proj.shape[1] // 4
    heads, head = (rec_gate_w.shape[0] // 4, rec_gate_w.shape[1])
    padded = (rec + 127) // 128 * 128
    low = jnp.bfloat16

    def mine(array, size, axis=0):
        return lax.dynamic_slice_in_dim(array, r * size, size, axis)

    flags = jnp.broadcast_to(starts.astype(low)[:, None], (starts.shape[0], 128))
    x_all, c_all, s_all, g_all, mix_w, out_w = gather(
        inputs.T,
        cotangent.T,
        flags,
        jnp.stack([mix_gain, mlp_gain]),
        x_proj,
        y_proj,
        out_proj,
    )
    tokens, model = x_all.shape
    vectors = jnp.concatenate(
        [
            x_bias[None],
            y_bias[None],
            conv_w,
            conv_b[None],
            rec_gate_b[None],
            in_gate_b[None],
            -GATE_C * jax.nn.softplus(decay_param)[None],
            -GATE_C * jax.nn.sigmoid(decay_param)[None],
            jnp.zeros((5, x_bias.shape[0]), jnp.float32),
        ],
        axis=0,
    )
    vec = mine(vectors, rec, 1)

    def diagonal(blocks):
        blocks = mine(blocks, heads)
        rows = [jnp.pad(blocks[i], ((0, 0), (i * head, rec - (i + 1) * head))) for i in range(heads)]
        return jnp.concatenate(rows, axis=0)

    rec_w, in_w = (diagonal(rec_gate_w), diagonal(in_gate_w))
    size = tokens // 8
    full = jax.ShapeDtypeStruct((tokens, model), low)
    part = jax.ShapeDtypeStruct((size, model), jnp.float32)
    piece = pltpu.VMEM((size, model), low)
    block = jax.ShapeDtypeStruct((inputs.shape[1], inputs.shape[0]), low)
    weights = (gate_proj, up_proj, down_proj)
    slices = jax.ShapeDtypeStruct((4 * depth, width), low)
    kept = [((tokens, model), low), ((tokens, 2 * rec), jnp.float32), ((tokens, padded), low)]
    kept += [((tokens, rec), kind) for kind in (jnp.float32, low) + (jnp.float32,) * 3]
    kept.append(((tokens, 8), jnp.float32))
    row8 = pltpu.VMEM((8, rec), jnp.float32)
    (
        normed_mlp,
        resid_mid,
        gate_w,
        up_w,
        down_w,
        normed_mix,
        pre,
        mixed,
        x_pre,
        conv,
        rec_gate,
        in_gate,
        states,
        masks,
    ) = vmem_call(
        forward_kernel,
        "forward",
        FORWARD_ID,
        (vec, rec_w, in_w, g_all),
        [full, part] + [slices] * 3 + [jax.ShapeDtypeStruct(*item) for item in kept],
        [pl.ANY, pltpu.VMEM] + [pl.ANY] * 12,
        [pltpu.VMEM(*item) for item in kept]
        + [row8, row8, pltpu.VMEM((tokens, model), low)]
        + [
            pltpu.VMEM((tokens, model), low),
            pltpu.VMEM((tokens, 128), low),
            pltpu.VMEM(mix_w.shape, low),
            pltpu.VMEM(out_w.shape, low),
            pltpu.VMEM((8, 8), jnp.float32),
            pltpu.SemaphoreType.DMA((11,)),
        ]
        + reduce_scratch(size, model)
        + [piece, pltpu.SemaphoreType.DMA((9,))],
        80,
        (x_all, s_all.reshape(tokens, 128), mix_w, out_w, *weights),
    )
    gate = dot(normed_mlp, gate_w, CONTRACT_PLAIN)
    up = dot(normed_mlp, up_w, CONTRACT_PLAIN)
    d_activ = dot(c_all, down_w, CONTRACT_PLAIN)
    gelu, slope = gelu_both(gate)
    activ = (gelu * up).astype(low)
    d_gate = (d_activ * up * slope).astype(low)
    d_up = (d_activ * gelu).astype(low)
    d_normed = lax.dot_general(
        d_gate, gate_w, CONTRACT_COLS, preferred_element_type=jnp.float32
    ) + lax.dot_general(d_up, up_w, CONTRACT_COLS, preferred_element_type=jnp.float32)
    def kind_of(array):
        return pltpu.VMEM(array.shape, array.dtype)

    def like(array):
        return jax.ShapeDtypeStruct(array.shape, array.dtype)

    both = jax.ShapeDtypeStruct((tokens, 2 * rec), low)
    held = (normed_mix, pre, mixed, x_pre, conv, rec_gate, in_gate, states)
    wide = (3 * width + 2 * rec + padded) // SEGMENTS
    sums = pltpu.VMEM((16, rec), jnp.float32)
    lines = pltpu.VMEM((2, model), jnp.float32)
    dma = pltpu.SemaphoreType.DMA

    def several(count, kind):
        return pltpu.VMEM((count, *kind.shape), kind.dtype)

    grad_in, output, grads, gates, vec_sums, gains = vmem_call(
        backward_kernel,
        "backward",
        BACKWARD_ID,
        (resid_mid, g_all, masks, vec, rec_w, in_w, mix_w, out_w),
        [
            block,
            block,
            jax.ShapeDtypeStruct((4 * SEGMENTS + 1, depth, wide), low),
            jax.ShapeDtypeStruct((4, 2, PACK, wide), low),
            jax.ShapeDtypeStruct((4, 16, rec), jnp.float32),
            jax.ShapeDtypeStruct((2, depth), jnp.float32),
        ],
        [pl.ANY] * 4 + [pltpu.VMEM] * 2,
        line_scratch(depth, wide, CHUNK, PACK // CHUNK)
        + [
            kind_of(full),
            piece,
            piece,
            kind_of(full),
            kind_of(part),
            kind_of(both),
            kind_of(both),
            pltpu.VMEM((24, rec), jnp.float32),
            row8,
        ]
        + [kind_of(item) for item in held]
        + [
            sums,
            lines,
            several(3, sums),
            several(3, lines),
            sums,
            lines,
            several(7, sums),
            several(7, lines),
        ]
        + reduce_scratch(size, model)
        + [
            piece,
            piece,
            dma((15,)),
            dma((2,)),
            dma((2, 16)),
            dma((2, 16)),
            pltpu.SemaphoreType.REGULAR,
        ],
        80,
        (
            d_normed.astype(low),
            dot(activ, down_w, CONTRACT_COLS, low),
            c_all,
            x_all,
            *held,
            dot(normed_mlp, d_gate, CONTRACT_ROWS, low),
            dot(normed_mlp, d_up, CONTRACT_ROWS, low),
            dot(c_all, activ, CONTRACT_ROWS, low),
        ),
    )
    done = unpack(grads, gates, vec_sums, output, grad_in, rec, width, heads)
    lines = [item if item.shape[0] > 1 else item[0] for item in done[10:]]
    return (*done[:8], gains[0], gains[1], *lines[:4], *done[8:10], *lines[4:])


def fits(mesh):
    return mesh.shape["dp"] == 4 and mesh.shape["row"] == 4 and mesh.shape["col"] == 2


def solution(mesh):
    placed = (
        P("row", ("dp", "col")),
        P("row", ("dp", "col")),
        P(("dp", "row")),
        P("row", "col"),
        P("row", "col"),
        P("col", "row"),
        P("row", "col"),
        P("row", "col"),
        P("row", "col"),
        P("row"),
        P("row"),
        P("col"),
        P("col"),
        P(None, "col"),
        P("col"),
        P("col", None, None),
        P("col", None, None),
        P("col"),
        P("col"),
        P("col"),
    )
    return jax.shard_map(
        local_plane if fits(mesh) else local,
        mesh=mesh,
        in_specs=placed,
        out_specs=(
            P("row", ("dp", "col")),
            P("row", ("dp", "col")),
            P("row", "col"),
            P("row", "col"),
            P("col", "row"),
            P("row", "col"),
            P("row", "col"),
            P("row", "col"),
            P("row"),
            P("row"),
            P("col"),
            P("col"),
            P(None, "col"),
            P("col"),
            P("col", None, None),
            P("col", None, None),
            P("col"),
            P("col"),
            P("col"),
        ),
        check_vma=False,
    )
```

```python
import functools

import jax
import jax.numpy as jnp
from jax import lax
from jax.experimental import pallas as pl
from jax.experimental.pallas import tpu as pltpu
from jax.sharding import PartitionSpec as P

MESH = pl.DeviceIdType.MESH

D = 2048


EPS = 1e-06
GATE_C = 8.0
CONTRACT_ROWS = (((0,), (0,)), ((), ()))
CONTRACT_COLS = (((1,), (1,)), ((), ()))
CONTRACT_PLAIN = (((1,), (0,)), ((), ()))


def from_behind(value, axis, by):
    count = lax.axis_size(axis)
    pairs = [(i, i + by) for i in range(count) if 0 <= i + by < count]
    return lax.ppermute(value, axis, pairs)


def carried_in(value, axis, join, neutral, backward):
    count, mine = (lax.axis_size(axis), lax.axis_index(axis))
    pieces = jax.tree.map(lambda part: lax.all_gather(part, axis), value)
    if backward:
        pieces = jax.tree.map(lambda part: part[::-1], pieces)
        mine = count - 1 - mine
    subtotal = jax.tree.map(
        lambda part, zero: jnp.full_like(part, 0) + jnp.asarray(zero, part.dtype), value, neutral
    )

    def hop(position, subtotal):
        longer = join(subtotal, jax.tree.map(lambda part: part[position], pieces))
        return jax.tree.map(lambda new, old: jnp.where(position < mine, new, old), longer, subtotal)

    return lax.fori_loop(0, count - 1, hop, subtotal)


def chain(earlier, later):
    return (earlier[0] * later[0], later[0] * earlier[1] + later[1])


def adjoint_chain(earlier, later):
    return (later[0] * earlier[0], later[1] + later[0] * earlier[1])


def gelu_tanh(values):
    return jax.nn.gelu(values, approximate=True)


def glu_piece(gate_vals, up_vals):
    return gelu_tanh(gate_vals) * up_vals


def causal_conv(values, conv_w, conv_b, segment_ids):
    result = values * conv_w[0] + conv_b
    for offset in range(1, conv_w.shape[0]):
        lagged = jnp.pad(values, ((offset, 0), (0, 0)))[:-offset]
        earlier_ids = jnp.pad(segment_ids, (offset, 0), constant_values=-1)[:-offset]
        result = (
            result + jnp.where((earlier_ids == segment_ids)[:, None], lagged, 0.0) * conv_w[offset]
        )
    return result


def local_recurrence(rec_pre, in_pre, conv_vals, decay_param, flags):
    rec_gate = jax.nn.sigmoid(rec_pre)
    in_gate = jax.nn.sigmoid(in_pre)
    log_keep = -GATE_C * rec_gate * jax.nn.softplus(decay_param)
    keep_rate = jnp.exp(log_keep)
    fresh = (flags == 1)[:, None]
    multiplier = jnp.where(fresh, 1.0, jnp.sqrt(-jnp.expm1(2.0 * log_keep)))
    driven = conv_vals * in_gate * multiplier
    carried = jnp.where(fresh, 0.0, keep_rate)
    cum_keep, states = lax.associative_scan(chain, (carried, driven), axis=0)
    return (cum_keep, states)


def row_sums(values):
    return lax.psum(values, "row")


def norm_forward(values, norm_gain):
    squares = row_sums(jnp.sum(values * values, axis=1))
    inv_rms = lax.rsqrt(squares / D + EPS)
    return (values * inv_rms[:, None] * norm_gain, inv_rms)


def norm_backward(values, inv_rms, norm_gain, incoming):
    scaled = norm_gain * incoming
    dots = row_sums(jnp.sum(scaled * values, axis=1))
    values_grad = inv_rms[:, None] * scaled - values * (inv_rms**3 * dots / D)[:, None]
    gain_grad = jnp.sum(incoming * values * inv_rms[:, None], axis=0)
    return (values_grad, gain_grad)


def gather_edge(values):
    return lax.all_gather(values, "col", axis=0, tiled=True)


def gather_mid(values):
    return lax.all_gather(values, "row", axis=0, tiled=True)


def row_partial(whole, weight, dims):
    return lax.psum_scatter(
        lax.dot_general(whole, weight, dims, preferred_element_type=jnp.float32),
        "row",
        scatter_dimension=0,
        tiled=True,
    )


def col_partial(whole, weight, dims):
    return lax.psum_scatter(
        lax.dot_general(whole, weight, dims, preferred_element_type=jnp.float32),
        "col",
        scatter_dimension=0,
        tiled=True,
    )


def project_in(normed, weight):
    whole = gather_edge(normed)
    result = row_partial(whole, weight, CONTRACT_PLAIN)
    return (result, whole)


def weight_grad(left, right):
    return lax.dot_general(left, right, CONTRACT_ROWS, preferred_element_type=jnp.float32)


def local(
    inputs,
    cotangent,
    starts,
    x_proj,
    y_proj,
    out_proj,
    gate_proj,
    up_proj,
    down_proj,
    mix_gain,
    mlp_gain,
    x_bias,
    y_bias,
    conv_w,
    conv_b,
    rec_gate_w,
    in_gate_w,
    rec_gate_b,
    in_gate_b,
    decay_param,
):
    rows_mid = starts.shape[0]
    rec_width = x_proj.shape[1]
    ff_width = gate_proj.shape[1]
    head_count = rec_gate_w.shape[0]
    margin = conv_w.shape[0] - 1
    mix_weights = jnp.concatenate([x_proj, y_proj], axis=1)
    mlp_weights = jnp.concatenate([gate_proj, up_proj], axis=1)
    cot_rows = cotangent.T
    resid = inputs.astype(jnp.float32).T
    normed_mix, inv_rms_mix = norm_forward(resid, mix_gain)
    normed_mix = normed_mix.astype(jnp.bfloat16)
    pre_both, whole_mix = project_in(normed_mix, mix_weights)
    x_pre = pre_both[:, :rec_width] + x_bias
    y_pre = pre_both[:, rec_width:] + y_bias
    x_tail, flag_tail = from_behind(
        (x_pre[rows_mid - margin :], starts[rows_mid - margin :].astype(jnp.float32)), "row", 1
    )
    ext_flags = jnp.concatenate([flag_tail.astype(jnp.int32), starts])
    ext_ids = jnp.cumsum(ext_flags, dtype=jnp.int32)
    ext_x = jnp.concatenate([x_tail, x_pre], axis=0)

    def conv_piece(values, taps, offsets):
        return causal_conv(values, taps, offsets, ext_ids)[margin:]

    conv_vals, conv_pull = jax.vjp(conv_piece, ext_x, conv_w, conv_b)
    conv_low = conv_vals.astype(jnp.bfloat16)
    conv_heads = conv_low.reshape(rows_mid, head_count, -1)
    rec_pre = (
        jnp.einsum(
            "thk,hkj->thj", conv_heads, rec_gate_w, preferred_element_type=jnp.float32
        ).reshape(rows_mid, rec_width)
        + rec_gate_b
    )
    in_pre = (
        jnp.einsum(
            "thk,hkj->thj", conv_heads, in_gate_w, preferred_element_type=jnp.float32
        ).reshape(rows_mid, rec_width)
        + in_gate_b
    )

    def scan_piece(rec_vals, in_vals, conv_input, decay_vals):
        return local_recurrence(rec_vals, in_vals, conv_input, decay_vals, starts)

    (cum_keep, local_states), scan_pull = jax.vjp(
        scan_piece, rec_pre, in_pre, conv_low.astype(jnp.float32), decay_param
    )
    ones_row = jnp.ones((rec_width,), jnp.float32)
    zeros_row = jnp.zeros((rec_width,), jnp.float32)
    incoming = carried_in(
        (cum_keep[rows_mid - 1], local_states[rows_mid - 1]),
        "row",
        chain,
        (ones_row, zeros_row),
        False,
    )
    state_prev = incoming[1]
    states = local_states + cum_keep * state_prev
    y_act, y_pull = jax.vjp(gelu_tanh, y_pre)
    mixed = (states * y_act).astype(jnp.bfloat16)
    whole_mixed = gather_mid(mixed)
    resid_mid = resid + col_partial(whole_mixed, out_proj, CONTRACT_PLAIN)
    normed_mlp, inv_rms_mlp = norm_forward(resid_mid, mlp_gain)
    normed_mlp = normed_mlp.astype(jnp.bfloat16)
    gate_up, whole_mlp = project_in(normed_mlp, mlp_weights)
    activ, activ_pull = jax.vjp(glu_piece, gate_up[:, :ff_width], gate_up[:, ff_width:])
    activ = activ.astype(jnp.bfloat16)
    whole_activ = gather_mid(activ)
    output = (resid_mid + col_partial(whole_activ, down_proj, CONTRACT_COLS)).astype(jnp.bfloat16)
    cot_whole = gather_edge(cot_rows)
    d_activ = row_partial(cot_whole, down_proj, CONTRACT_PLAIN)
    activ_rows = gather_mid(activ)
    grad_down = weight_grad(cot_whole, activ_rows)
    d_gate, d_up = activ_pull(d_activ)
    d_gate_up = jnp.concatenate([d_gate, d_up], axis=1).astype(jnp.bfloat16)
    d_gate_up_whole = gather_mid(d_gate_up)
    d_normed_mlp = col_partial(d_gate_up_whole, mlp_weights, CONTRACT_COLS)
    mlp_rows = gather_edge(normed_mlp)
    grad_gate_up = weight_grad(mlp_rows, d_gate_up_whole)
    d_norm_mid, grad_mlp_gain = norm_backward(resid_mid, inv_rms_mlp, mlp_gain, d_normed_mlp)
    d_resid_mid = cot_rows.astype(jnp.float32) + d_norm_mid
    d_branch = d_resid_mid.astype(jnp.bfloat16)
    branch_whole = gather_edge(d_branch)
    d_mixed = row_partial(branch_whole, out_proj, CONTRACT_COLS)
    mixed_rows = gather_mid(mixed)
    grad_out = weight_grad(mixed_rows, branch_whole)
    d_state = d_mixed * y_act
    (d_y_pre,) = y_pull(d_mixed * states)
    own_sens = jnp.sum(d_state * cum_keep, axis=0)
    outgoing = carried_in(
        (cum_keep[rows_mid - 1], own_sens), "row", adjoint_chain, (ones_row, zeros_row), True
    )
    d_total = d_state + jnp.pad(outgoing[1][None, :], ((rows_mid - 1, 0), (0, 0)))
    d_rec_pre, d_in_pre, d_conv_direct, grad_decay = scan_pull((d_total * state_prev, d_total))
    d_rec_low = d_rec_pre.astype(jnp.bfloat16)
    d_in_low = d_in_pre.astype(jnp.bfloat16)
    d_rec_heads = d_rec_low.reshape(rows_mid, head_count, -1)
    d_in_heads = d_in_low.reshape(rows_mid, head_count, -1)
    d_conv = d_conv_direct + jnp.einsum(
        "thj,hkj->thk", d_rec_heads, rec_gate_w, preferred_element_type=jnp.float32
    ).reshape(rows_mid, rec_width)
    d_conv = d_conv + jnp.einsum(
        "thj,hkj->thk", d_in_heads, in_gate_w, preferred_element_type=jnp.float32
    ).reshape(rows_mid, rec_width)
    grad_rec_w = jnp.einsum(
        "thk,thj->hkj", conv_heads, d_rec_heads, preferred_element_type=jnp.float32
    )
    grad_in_w = jnp.einsum(
        "thk,thj->hkj", conv_heads, d_in_heads, preferred_element_type=jnp.float32
    )
    grad_rec_b = jnp.sum(d_rec_low.astype(jnp.float32), axis=0)
    grad_in_b = jnp.sum(d_in_low.astype(jnp.float32), axis=0)
    d_ext, grad_conv_w, grad_conv_b = conv_pull(d_conv)
    d_from_next = from_behind(d_ext[:margin], "row", -1)
    d_x_pre = d_ext[margin:] + jnp.pad(d_from_next, ((rows_mid - margin, 0), (0, 0)))
    d_pre = jnp.concatenate([d_x_pre, d_y_pre], axis=1).astype(jnp.bfloat16)
    bias_sums = jnp.sum(d_pre.astype(jnp.float32), axis=0)
    d_pre_whole = gather_mid(d_pre)
    d_normed_mix = col_partial(d_pre_whole, mix_weights, CONTRACT_COLS)
    mix_rows = gather_edge(normed_mix)
    grad_mix = weight_grad(mix_rows, d_pre_whole)
    d_norm_in, grad_mix_gain = norm_backward(resid, inv_rms_mix, mix_gain, d_normed_mix)
    inputs_grad = d_resid_mid + d_norm_in
    grad_mix, grad_out, grad_gate_up, grad_down = (
        lax.psum(grad_mix.astype(jnp.bfloat16), "dp").astype(jnp.float32),
        lax.psum(grad_out.astype(jnp.bfloat16), "dp").astype(jnp.float32),
        lax.psum(grad_gate_up.astype(jnp.bfloat16), "dp").astype(jnp.float32),
        lax.psum(grad_down.astype(jnp.bfloat16), "dp").astype(jnp.float32),
    )
    (
        bias_sums,
        grad_conv_w,
        grad_conv_b,
        grad_rec_w,
        grad_in_w,
        grad_rec_b,
        grad_in_b,
        grad_decay,
    ) = (
        lax.psum(bias_sums.astype(jnp.bfloat16), ("dp", "row")).astype(jnp.float32),
        lax.psum(grad_conv_w.astype(jnp.bfloat16), ("dp", "row")).astype(jnp.float32),
        lax.psum(grad_conv_b.astype(jnp.bfloat16), ("dp", "row")).astype(jnp.float32),
        lax.psum(grad_rec_w.astype(jnp.bfloat16), ("dp", "row")).astype(jnp.float32),
        lax.psum(grad_in_w.astype(jnp.bfloat16), ("dp", "row")).astype(jnp.float32),
        lax.psum(grad_rec_b.astype(jnp.bfloat16), ("dp", "row")).astype(jnp.float32),
        lax.psum(grad_in_b.astype(jnp.bfloat16), ("dp", "row")).astype(jnp.float32),
        lax.psum(grad_decay.astype(jnp.bfloat16), ("dp", "row")).astype(jnp.float32),
    )
    grad_mix_gain, grad_mlp_gain = lax.psum((grad_mix_gain, grad_mlp_gain), ("dp", "col"))
    return (
        output.T,
        inputs_grad.T,
        grad_mix[:, :rec_width],
        grad_mix[:, rec_width:],
        grad_out,
        grad_gate_up[:, :ff_width],
        grad_gate_up[:, ff_width:],
        grad_down,
        grad_mix_gain,
        grad_mlp_gain,
        bias_sums[:rec_width],
        bias_sums[rec_width:],
        grad_conv_w,
        grad_conv_b,
        grad_rec_w,
        grad_in_w,
        grad_rec_b,
        grad_in_b,
        grad_decay,
    )


GATHER_ID, FORWARD_ID, BACKWARD_ID = (0, 1, 2)
BLOCK = 128
VMEM_BYTES = 60 << 20


def one_minus_exp(rate):
    series = rate * (1.0 - rate * (0.5 - rate * (1.0 / 6.0 - rate * (1.0 / 24.0 - rate / 120.0))))
    return jnp.where(rate < 0.1, series, 1.0 - jnp.exp(-rate))


GELU_C = 0.7978845608028654


def gelu_both(values):
    squared = values * values
    inner = jnp.tanh(GELU_C * values * (1.0 + 0.044715 * squared))
    value = 0.5 * values * (1.0 + inner)
    slope = 0.5 * (1.0 + inner) + 0.5 * values * (1.0 - inner * inner) * GELU_C * (
        1.0 + 3.0 * 0.044715 * squared
    )
    return (value, slope)


def down_rows(values, by):
    return pltpu.roll(values, by, 0)


def up_rows(values, by):
    return pltpu.roll(values, values.shape[0] - by, 0)


def scan_down(keep, add):
    rows = keep.shape[0]
    position = lax.broadcasted_iota(jnp.int32, keep.shape, 0)
    step = 1
    while step < rows:
        if step < 8:
            inside = position >= step
            before_keep = jnp.where(inside, down_rows(keep, step), 1.0)
            before_add = jnp.where(inside, down_rows(add, step), 0.0)
            add = add + keep * before_add
            keep = keep * before_keep
        else:
            add = jnp.concatenate([add[:step], add[step:] + keep[step:] * add[:-step]], axis=0)
            keep = jnp.concatenate([keep[:step], keep[step:] * keep[:-step]], axis=0)
        step *= 2
    return (keep, add)


def scan_up(keep, add):
    rows = keep.shape[0]
    position = lax.broadcasted_iota(jnp.int32, keep.shape, 0)
    step = 1
    while step < rows:
        if step < 8:
            inside = position < rows - step
            after_keep = jnp.where(inside, up_rows(keep, step), 1.0)
            after_add = jnp.where(inside, up_rows(add, step), 0.0)
            add = add + keep * after_add
            keep = keep * after_keep
        else:
            add = jnp.concatenate([add[:-step] + keep[:-step] * add[step:], add[-step:]], axis=0)
            keep = jnp.concatenate([keep[:-step] * keep[step:], keep[-step:]], axis=0)
        step *= 2
    return (keep, add)


def mixer_forward_step(
    pre, marks, vec, rec_w, in_w, mixed, x_pre, conv, rec_gate, in_gate, states, tail, carry
):
    width = x_pre.shape[1]
    x = pre[:, :width] + vec[0:1, :]
    x_pre[...] = x
    longer = jnp.concatenate([tail[...], x], axis=0)
    tail[...] = x[BLOCK - 8 :]
    total = x * vec[2:3, :] + vec[6:7, :]
    for tap in range(1, 4):
        total = total + marks[:, tap : tap + 1] * down_rows(longer, tap)[8:] * vec[
            2 + tap : 3 + tap, :
        ]
    low = total.astype(jnp.bfloat16)
    conv[...] = low
    rec = jax.nn.sigmoid(
        jnp.dot(low, rec_w[...], preferred_element_type=jnp.float32) + vec[7:8, :]
    )
    inn = jax.nn.sigmoid(
        jnp.dot(low, in_w[...], preferred_element_type=jnp.float32) + vec[8:9, :]
    )
    rec_gate[...] = rec
    in_gate[...] = inn
    log_keep = rec * vec[9:10, :]
    fresh = marks[:, 0:1]
    scale = jnp.where(fresh > 0.5, 1.0, jnp.sqrt(one_minus_exp(-2.0 * log_keep)))
    driven = low.astype(jnp.float32) * inn * scale
    keep, add = scan_down(jnp.exp(log_keep) * (1.0 - fresh), driven)
    state = add + keep * carry[0:1, :]
    carry[...] = jnp.broadcast_to(state[BLOCK - 1 :, :], carry.shape)
    states[...] = state
    y = pre[:, width:] + vec[1:2, :]
    mixed[:, :width] = (state * gelu_both(y)[0]).astype(jnp.bfloat16)
    mixed[:, width:] = jnp.zeros((BLOCK, mixed.shape[1] - width), jnp.bfloat16)


def mixer_backward_step(
    incoming,
    pre,
    marks,
    vec,
    rec_w,
    in_w,
    x_pre,
    x_before,
    conv,
    rec_gate,
    in_gate,
    states,
    state_before,
    d_pre,
    d_gates,
    sums,
    edge,
    carry,
):
    width = x_pre.shape[1]
    position = lax.broadcasted_iota(jnp.int32, (BLOCK, width), 0)
    fresh = marks[:, 0:1]
    stale = 1.0 - fresh
    gelu, slope = gelu_both(pre[:, width:] + vec[1:2, :])
    state = states[...]
    d_y = (incoming * state * slope).astype(jnp.bfloat16)
    rec, inn = (rec_gate[...], in_gate[...])
    conv_vals = conv[...].astype(jnp.float32)
    log_keep = rec * vec[9:10, :]
    keep_rate = jnp.exp(log_keep)
    scale = jnp.where(fresh > 0.5, 1.0, jnp.sqrt(one_minus_exp(-2.0 * log_keep)))
    carried = keep_rate * stale
    after = jnp.where(position == BLOCK - 1, carry[1:2, :], up_rows(carried, 1))
    keep, add = scan_up(after, incoming * gelu)
    adjoint = add + keep * carry[0:1, :]
    carry[0:1, :] = adjoint[0:1]
    carry[1:2, :] = carried[0:1]
    earlier = jnp.where(position == 0, state_before[7:8, :], down_rows(state, 1))
    drive = adjoint * scale
    d_log = stale * (
        adjoint * earlier * keep_rate
        - adjoint * inn * conv_vals * keep_rate * keep_rate / scale
    )
    d_rec = (d_log * vec[9:10, :] * rec * (1.0 - rec)).astype(jnp.bfloat16)
    d_in = (drive * conv_vals * inn * (1.0 - inn)).astype(jnp.bfloat16)
    d_gates[:, :width] = d_rec
    d_gates[:, width:] = d_in
    d_conv = drive * inn
    d_conv = d_conv + lax.dot_general(
        d_rec, rec_w[...], CONTRACT_COLS, preferred_element_type=jnp.float32
    )
    d_conv = d_conv + lax.dot_general(
        d_in, in_w[...], CONTRACT_COLS, preferred_element_type=jnp.float32
    )
    x = x_pre[...]
    longer = jnp.concatenate([x_before[...], x], axis=0)

    def column(values):
        return jnp.sum(values, axis=0, keepdims=True)

    d_x = d_conv * vec[2:3, :]
    taps = [column(d_conv * x)]
    for tap in range(1, 4):
        piece = marks[:, tap : tap + 1] * d_conv
        taps.append(column(piece * down_rows(longer, tap)[8:]))
        beyond = jnp.concatenate([piece, edge[8 * tap - 8 : 8 * tap, :]], axis=0)
        d_x = d_x + vec[2 + tap : 3 + tap, :] * up_rows(beyond, tap)[:BLOCK]
        edge[8 * tap - 8 : 8 * tap, :] = piece[:8]
    d_x = d_x.astype(jnp.bfloat16)
    d_pre[:, :width] = d_x
    d_pre[:, width:] = d_y
    pieces = (
        [column(d_x.astype(jnp.float32)), column(d_y.astype(jnp.float32))]
        + taps
        + [
            column(d_conv),
            column(d_rec.astype(jnp.float32)),
            column(d_in.astype(jnp.float32)),
            column(d_log * rec) * vec[10:11, :],
        ]
    )
    for place, piece in enumerate(pieces):
        sums[place : place + 1, :] += piece


def here():
    return (lax.axis_index("dp"), lax.axis_index("row"), lax.axis_index("col"))


def flip(index):
    return index + 1 - 2 * (index % 2)


def across(row):
    return (row + 2) % 4


def greet(peers):
    barrier = pltpu.get_barrier_semaphore()
    for peer in peers:
        pl.semaphore_signal(barrier, inc=1, device_id=peer, device_id_type=MESH)
    pl.semaphore_wait(barrier, len(peers))


class Copies:
    def __init__(self, send, recv):
        self.send, self.recv, self.used, self.sent = (send, recv, 0, [])

    def make(self, source, target, device):
        place = self.used
        self.used += 1
        if device is None:
            copy = pltpu.make_async_copy(source, target, self.recv.at[place])
        else:
            copy = pltpu.make_async_remote_copy(
                src_ref=source,
                dst_ref=target,
                send_sem=self.send.at[place],
                recv_sem=self.recv.at[place],
                device_id=device,
                device_id_type=MESH,
            )
            self.sent.append(copy)
        return copy

    def go(self, source, target, device):
        copy = self.make(source, target, device)
        copy.start()
        return copy

    def finish(self):
        for copy in self.sent:
            copy.wait_send()
        self.sent = []


def arrived(copy):
    copy.wait_recv()


def spread(copies, own, place, halves, between=lambda: None):
    z, r, c = here()
    twin, side, top = ((z, flip(r), c), (z, across(r), c), (z, r, 1 - c))
    to_side = copies.go(own, place(r, c), side)
    to_top = copies.go(own, place(r, c), top)
    to_twin = copies.go(own, place(r, c), twin)
    between()
    arrived(to_side)
    from_side = place(across(r), c)
    on_top = copies.go(halves(from_side, 0), halves(from_side, 0), top)
    late = [to_twin, copies.go(from_side, from_side, twin)]
    between()
    arrived(to_top)
    from_top = place(r, 1 - c)
    on_side = copies.go(halves(from_top, 1), halves(from_top, 1), side)
    late.append(copies.go(from_top, from_top, twin))
    far = place(across(r), 1 - c)
    between()
    for half, copy in enumerate((on_top, on_side)):
        arrived(copy)
        late.append(copies.go(halves(far, half), halves(far, half), twin))
    return late


def spread_tall(copies, own, place, between=lambda: None):
    z, r, c = here()
    twin, side, top = ((z, flip(r), c), (z, across(r), c), (z, r, 1 - c))
    to_side = copies.go(own, place(r, c), side)
    to_top = copies.go(own, place(r, c), top)
    late = [copies.go(own, place(r, c), twin)]
    between()
    arrived(to_side)
    from_side = place(across(r), c)
    on_top = copies.go(from_side, from_side, top)
    late.append(copies.go(from_side, from_side, twin))
    between()
    arrived(to_top)
    from_top = place(r, 1 - c)
    late.append(copies.go(from_top, from_top, twin))
    between()
    arrived(on_top)
    far = place(across(r), 1 - c)
    late.append(copies.go(far, far, twin))
    return late


def part(start, size, step):
    return pl.ds(pl.multiple_of(start * step, step), size)


class Moves:
    def __init__(self, copies, matrices, cuts):
        z, r, c = here()
        mine = z % 2
        sides = ((z, across(r), c), (z, flip(across(r)), c))
        pair = (flip(z), r, c)
        self.groups, self.locals, self.late = ([], [], [])
        self.begun, self.ended = (0, 0)

        def piece(ref, size, cut):
            length = size // 2 // cuts
            return ref.at[part(mine * cuts + cut, length, length), :]

        for source, target, size in matrices:
            for cut in range(cuts):
                group = []
                for peer in sides:
                    spot = piece(target(peer[1]), size, cut)
                    group.append(
                        (
                            copies.make(
                                piece(source(peer[1]), size, cut), piece(target(r), size, cut), peer
                            ),
                            copies.make(spot, spot, pair),
                        )
                    )
                self.groups.append(group)
        for source, target, size in matrices:
            self.locals.append(copies.go(source(r), target(r), None))
            self.late.append(copies.go(source(flip(r)), target(r), (z, flip(r), c)))

    def step(self):
        if self.begun - self.ended == 2 or self.begun == len(self.groups):
            if self.ended < self.begun:
                for first, second in self.groups[self.ended]:
                    arrived(first)
                    second.start()
                self.ended += 1
        if self.begun < len(self.groups):
            for first, _ in self.groups[self.begun]:
                first.start()
            self.begun += 1

    def finish(self):
        while self.ended < len(self.groups):
            self.step()
        for group in self.groups:
            for _, second in group:
                arrived(second)
        for copy in self.late:
            arrived(copy)
        for copy in self.locals:
            copy.wait()


def block_of(ref, rows, columns):
    return lambda row, col: ref.at[part(col, rows, rows), part(row, columns, columns)]


def halves_of(rows):
    return lambda ref, which: ref.at[pl.ds(which * (rows // 2), rows // 2), :]


def mlp_matrices(sources, targets):
    depth, width = (sources[0].shape[0], sources[0].shape[1] // 4)
    return [
        (
            lambda to, source=source: source.at[:, part(to, width, width)],
            lambda of, target=target: target.at[part(of, depth, depth), :],
            depth,
        )
        for source, target in zip(sources, targets)
    ]


def gather_kernel(
    x_in,
    c_in,
    s_in,
    g_in,
    x_proj,
    y_proj,
    out_in,
    x_all,
    c_all,
    s_all,
    g_all,
    mix_all,
    out_all,
    x_here,
    y_here,
    mix_in,
    load_sem,
    send,
    recv,
):
    z, r, c = here()
    twin, side, cross, top, pair = (
        (z, flip(r), c),
        (z, across(r), c),
        (z, flip(across(r)), c),
        (z, r, 1 - c),
        (flip(z), r, c),
    )
    loads = [
        pltpu.make_async_copy(source, target, load_sem.at[place])
        for place, (source, target) in enumerate(((x_proj, x_here), (y_proj, y_here)))
    ]
    for copy in loads:
        copy.start()
    greet((twin, side, cross, top, pair))
    copies = Copies(send, recv)
    rows, columns = x_in.shape
    depth, rec = (mix_in.shape[1], out_in.shape[0] // 4)
    matrices = [
        (lambda to: mix_in.at[to], lambda of: mix_all.at[part(of, depth, depth), :], depth),
        (
            lambda to: out_in.at[part(to, rec, rec), :],
            lambda of: out_all.at[:, part(of, columns, columns)],
            rec,
        ),
    ]
    moves = []

    def between():
        if not moves:
            for copy in loads:
                copy.wait()

            def body(at):
                strip = pl.ds(at, STRIP)
                x, y = (x_here[strip, :], y_here[strip, :])
                for to in range(4):
                    span = slice(to * rec, (to + 1) * rec)
                    mix_in[to, strip, :] = jnp.concatenate([x[:, span], y[:, span]], axis=1)

            strips(depth, body)
            moves.append(Moves(copies, matrices, 2))
        moves[0].step()

    small = g_all.at[:, part(r, depth, depth)]
    late = spread_tall(copies, x_in, block_of(x_all, rows, columns), between)
    locals_ = [
        copies.go(x_in, block_of(x_all, rows, columns)(r, c), None),
        copies.go(c_in, block_of(c_all, rows, columns)(r, c), None),
        copies.go(s_in, s_all.at[r], None),
        copies.go(g_in, small, None),
    ]
    for peer in (twin, side, cross):
        late.append(copies.go(g_in, small, peer))
    flags_side = copies.go(s_in, s_all.at[r], side)
    late.append(copies.go(s_in, s_all.at[r], twin))
    late.extend(spread_tall(copies, c_in, block_of(c_all, rows, columns), between))
    arrived(flags_side)
    late.append(copies.go(s_all.at[across(r)], s_all.at[across(r)], twin))
    moves[0].finish()
    for copy in late:
        arrived(copy)
    for copy in locals_:
        copy.wait()
    copies.finish()


def gather(x_in, c_in, s_in, g_in, x_proj, y_proj, out_in):
    rows, columns = x_in.shape
    depth, wide = x_proj.shape

    def shape(*dims, kind=jnp.bfloat16):
        return jax.ShapeDtypeStruct(dims, kind)

    outs = [
        shape(2 * rows, 4 * columns),
        shape(2 * rows, 4 * columns),
        shape(4, *s_in.shape, kind=s_in.dtype),
        shape(g_in.shape[0], 4 * depth, kind=g_in.dtype),
        shape(4 * depth, wide // 2),
        shape(out_in.shape[0] // 4, 4 * columns),
    ]
    dma = pltpu.SemaphoreType.DMA
    return pl.pallas_call(
        gather_kernel,
        in_specs=[pl.BlockSpec(memory_space=pltpu.HBM)] * 7,
        out_specs=[pl.BlockSpec(memory_space=pltpu.HBM)] * 6,
        out_shape=outs,
        scratch_shapes=[
            pltpu.VMEM((depth, wide), jnp.bfloat16),
            pltpu.VMEM((depth, wide), jnp.bfloat16),
            pltpu.VMEM((4, depth, wide // 2), jnp.bfloat16),
            dma((2,)),
            dma((64,)),
            dma((64,)),
        ],
        compiler_params=pltpu.CompilerParams(
            collective_id=GATHER_ID, has_side_effects=True, vmem_limit_bytes=60 << 20
        ),
        name="gather",
    )(x_in, c_in, s_in, g_in, x_proj, y_proj, out_in)


STRIP = 16


def strips(count, body):
    def run(index, nothing):
        body(pl.multiple_of(index * STRIP, STRIP))
        return nothing

    lax.fori_loop(0, count // STRIP, run, 0)


def token_shard(row, col):
    return col * 4 + row


def reduce_shards(
    copies, parts, twin_in, sums, side_in, top_in, hop_in, between=lambda: None, tall=False
):
    z, r, c = here()
    twin, side, top = ((z, flip(r), c), (z, across(r), c), (z, r, 1 - c))
    size = side_in.shape[0]
    half = size // 2

    def shard(row, col):
        return pl.multiple_of(token_shard(row, col) * size, size)

    spots = [(across(r), 1 - c), (across(r), c), (r, 1 - c), (r, c)]
    from_twin = [
        copies.go(parts.at[pl.ds(shard(flip(row), col), size), :], twin_in.at[place], twin)
        for place, (row, col) in enumerate(spots)
    ]

    def add_twin(place):
        arrived(from_twin[place])
        start = shard(*spots[place])

        def body(at):
            total = parts[pl.ds(start + at, STRIP), :].astype(jnp.float32) + twin_in[
                place, pl.ds(at, STRIP), :
            ].astype(jnp.float32)
            sums[place, pl.ds(at, STRIP), :] = total.astype(jnp.bfloat16)

        strips(size, body)

    def add_hop(place, which, hop):
        def body(at):
            rows = pl.ds(which * half + at, STRIP)
            total = sums[place, rows, :].astype(jnp.float32) + hop_in[
                hop, pl.ds(at, STRIP), :
            ].astype(jnp.float32)
            sums[place, rows, :] = total.astype(jnp.bfloat16)

        strips(half, body)

    def rows_of(ref, which):
        return ref.at[pl.ds(which * half, half), :]

    def total(at):
        rows = pl.ds(at, STRIP)
        return (
            sums[3, rows, :].astype(jnp.float32)
            + side_in[rows, :].astype(jnp.float32)
            + top_in[rows, :].astype(jnp.float32)
        )

    add_twin(0)
    if tall:
        hops = [copies.go(rows_of(sums.at[0], k), hop_in.at[k], top) for k in (0, 1)]
        add_twin(2)
        to_top = copies.go(sums.at[2], top_in, top)
        add_twin(1)
        add_twin(3)
        between()
        to_side = []
        for k in (0, 1):
            arrived(hops[k])
            add_hop(1, k, k)
            to_side.append(copies.go(rows_of(sums.at[1], k), rows_of(side_in, k), side))
        between()
        for copy in [to_top, *to_side]:
            arrived(copy)
        return total
    hop_side = copies.go(rows_of(sums.at[0], 0), hop_in.at[0], side)
    hop_top = copies.go(rows_of(sums.at[0], 1), hop_in.at[1], top)
    add_twin(1)
    waits = [copies.go(rows_of(sums.at[1], 0), rows_of(side_in, 0), side)]
    add_twin(2)
    waits.append(copies.go(rows_of(sums.at[2], 1), rows_of(top_in, 1), top))
    add_twin(3)
    between()
    arrived(hop_top)
    add_hop(1, 1, 1)
    waits.append(copies.go(rows_of(sums.at[1], 1), rows_of(side_in, 1), side))
    arrived(hop_side)
    add_hop(2, 0, 0)
    waits.append(copies.go(rows_of(sums.at[2], 0), rows_of(top_in, 0), top))
    between()
    for copy in waits:
        arrived(copy)
    return total


def reduce_scratch(size, width):
    return [
        pltpu.VMEM((4, size, width), jnp.bfloat16),
        pltpu.VMEM((4, size, width), jnp.bfloat16),
        pltpu.VMEM((size, width), jnp.bfloat16),
        pltpu.VMEM((size, width), jnp.bfloat16),
        pltpu.VMEM((2, size // 2, width), jnp.bfloat16),
    ]


def near():
    z, r, c = here()
    return ((z, flip(r), c), (z, across(r), c), (z, r, 1 - c))


def spread_rows(copies, mine, full, between=lambda: None, tall=False):
    z, r, c = here()
    size = mine.shape[0]
    half = size // 2

    def place(row, col):
        return full.at[pl.ds(pl.multiple_of(token_shard(row, col) * size, size), size), :]

    local = copies.go(mine, place(r, c), None)
    if tall:
        late = spread_tall(copies, mine, place, between)
    else:
        late = spread(
            copies, mine, place, lambda ref, which: ref.at[pl.ds(which * half, half), :], between
        )
    for copy in late:
        arrived(copy)
    local.wait()


def mark_rows(flags, tail):
    stale = 1.0 - flags
    longer = jnp.concatenate([tail[...], stale], axis=0)
    tail[...] = stale[BLOCK - 8 :]
    pair = stale * down_rows(longer, 1)[8:]
    triple = pair * down_rows(longer, 2)[8:]
    lane = lax.broadcasted_iota(jnp.int32, flags.shape, 1)
    return jnp.where(lane == 0, flags, jnp.where(lane == 1, stale, jnp.where(lane == 2, pair, triple)))


def forward_kernel(vec, rec_w, in_w, gains, *refs):
    x_in, s_in, mix_in, out_in = refs[:4]
    mlp_in, outs, scratch = (refs[4:7], refs[7:21], refs[21:])
    full, resid_mid = outs[:2]
    mlp_all, kept_out = (outs[2:5], outs[5:])
    kept, (tail, carry, parts), (*buffers, mine, kept_sem, send, recv) = (
        scratch[:9],
        scratch[9:12],
        scratch[12:],
    )
    x_all, flags, mix_w, out_w, mark_tail, load_sem, *buffers = buffers
    normed, pre, mixed, *saved, masks = kept
    loads = [
        pltpu.make_async_copy(source, target, load_sem.at[8 + place])
        for place, (source, target) in enumerate(
            ((mix_in, mix_w), (s_in, flags), (out_in, out_w))
        )
    ]

    def load_rows(index):
        rows = pl.ds(pl.multiple_of(index * BLOCK, BLOCK), BLOCK)
        return pltpu.make_async_copy(x_in.at[rows, :], x_all.at[rows, :], load_sem.at[index])

    load_rows(0).start()
    for copy in loads:
        copy.start()
    for index in range(1, x_all.shape[0] // BLOCK):
        load_rows(index).start()
    z, r, c = here()
    greet((*near(), (z, flip(across(r)), c), (flip(z), r, c)))
    copies = Copies(send, recv)
    moves = Moves(copies, mlp_matrices(mlp_in, mlp_all), 2)
    moves.step()
    moves.step()
    for copy in loads:
        copy.wait()
    mark_tail[...] = jnp.zeros_like(mark_tail)
    tail[...] = jnp.zeros_like(tail)
    carry[...] = jnp.zeros_like(carry)

    def block(index, nothing):
        start = pl.multiple_of(index * BLOCK, BLOCK)
        rows = pl.ds(start, BLOCK)
        for turn in (3, 6):

            @pl.when(index == turn)
            def _():
                moves.step()

        load_rows(index).wait()
        marks = mark_rows(flags[rows, :8].astype(jnp.float32), mark_tail)
        masks[rows, :] = marks

        def norm(at):
            strip = pl.ds(start + at, STRIP)
            values = x_all[strip, :].astype(jnp.float32)
            scale = lax.rsqrt(jnp.mean(values * values, axis=1, keepdims=True) + EPS)
            normed[strip, :] = (values * scale * gains[0:1, :]).astype(jnp.bfloat16)

        strips(BLOCK, norm)
        pre[rows, :] = jnp.dot(normed[rows, :], mix_w[...], preferred_element_type=jnp.float32)
        mixer_forward_step(
            pre.at[rows, :],
            marks,
            vec,
            rec_w,
            in_w,
            mixed.at[rows, :],
            *[ref.at[rows, :] for ref in saved],
            tail,
            carry,
        )
        width = rec_w.shape[0]
        parts[rows, :] = jnp.dot(
            mixed[rows, :width], out_w[...], preferred_element_type=jnp.float32
        ).astype(jnp.bfloat16)
        return nothing

    lax.fori_loop(0, x_all.shape[0] // BLOCK, block, 0)
    keeping = [
        pltpu.make_async_copy(source, target, kept_sem.at[place])
        for place, (source, target) in enumerate(zip(kept, kept_out))
    ]
    for copy in keeping:
        copy.start()
    total = reduce_shards(copies, parts, *buffers, between=moves.step, tall=True)
    size = mine.shape[0]
    start = pl.multiple_of(token_shard(r, c) * size, size)

    def body(at):
        rows = pl.ds(at, STRIP)
        values = x_all[pl.ds(start + at, STRIP), :].astype(jnp.float32) + total(at)
        resid_mid[rows, :] = values
        scale = lax.rsqrt(jnp.mean(values * values, axis=1, keepdims=True) + EPS)
        mine[rows, :] = (values * scale * gains[1:2, :]).astype(jnp.bfloat16)

    strips(size, body)
    spread_rows(copies, mine, full, moves.step, tall=True)
    moves.finish()
    for copy in keeping:
        copy.wait()
    copies.finish()


def norm_pull(values, gain, incoming):
    scale = lax.rsqrt(jnp.mean(values * values, axis=1, keepdims=True) + EPS)
    scaled = gain * incoming
    dots = jnp.sum(scaled * values, axis=1, keepdims=True)
    grad = scale * scaled - values * (scale * scale * scale * dots / values.shape[1])
    return (grad, jnp.sum(incoming * values * scale, axis=0, keepdims=True))


def vmem_call(kernel, name, place, arrays, outs, spaces, scratch, count, loose=()):
    return pl.pallas_call(
        kernel,
        in_specs=[pl.BlockSpec(memory_space=pltpu.VMEM)] * len(arrays)
        + [pl.BlockSpec(memory_space=pltpu.HBM)] * len(loose),
        out_specs=[pl.BlockSpec(memory_space=space) for space in spaces],
        out_shape=outs,
        scratch_shapes=scratch
        + [pltpu.SemaphoreType.DMA((count,)), pltpu.SemaphoreType.DMA((count,))],
        compiler_params=pltpu.CompilerParams(
            collective_id=place, has_side_effects=True, vmem_limit_bytes=VMEM_BYTES
        ),
        name=name,
    )(*arrays, *loose)


AHEAD = 3
DEPTH = 4
SUM_LAG = 1
HAND_LAG = 3
LAG = 4
RING = 9
SEGMENTS = 2


def run_loop(first, last, body):
    def run(index, nothing):
        body(index)
        return nothing

    lax.fori_loop(first, last, run, 0)


def remote(source, target, sender, receiver, device):
    return pltpu.make_async_remote_copy(
        src_ref=source,
        dst_ref=target,
        send_sem=sender,
        recv_sem=receiver,
        device_id=device,
        device_id_type=MESH,
    )


class Line:
    def __init__(self, own, left, right, out, sems, lead):
        self.own, self.left, self.right, self.out, self.lead = (own, left, right, out, lead)
        (
            self.end_send,
            self.low_recv,
            self.high_recv,
            self.out_recv,
            self.mid_send,
            self.first_send,
            self.last_send,
            self.hand_send,
            self.on_send,
        ) = sems
        z, r, c = here()
        self.chunk = left.shape[1]
        self.rows = out.shape[1]
        self.half = self.rows // 2
        self.per = self.half // self.chunk
        self.first = 4 * self.per
        self.chunks = 4 * SEGMENTS * self.per + lead
        self.total = self.chunks + LAG
        self.at = 0
        self.ahead = 0
        self.is_end = (z == 0) | (z == 3)
        self.near_z = (jnp.where(z == 0, 1, 2), r, c)
        self.outer = (jnp.where(z == 1, 0, 3), r, c)
        self.other = (3 - z, r, c)

    def extra(self, index):
        return (index >= self.first) & (index < self.first + self.lead)

    def spot(self, index):
        later = index >= self.first + self.lead
        plain = index - jnp.where(later, self.lead, 0)
        step = jnp.where(self.extra(index), 0, plain // self.per)
        strip = jnp.where(self.extra(index), index - self.first, plain % self.per)
        return (step // 4, step % 4, strip)

    def peer_row(self, index):
        r = here()[1]
        step = self.spot(index)[1]
        return (r // 2 + step // 2) % 2 * 2 + (r % 2 + step % 2) % 2

    def stays(self, index):
        return self.spot(index)[1] == 0

    def span(self, index, which):
        segment, _, strip = self.spot(index)
        start = (segment * 4 + self.peer_row(index)) * self.rows + which * self.half
        outside = SEGMENTS * 4 * self.rows + which * self.lead * self.chunk
        start = jnp.where(self.extra(index), outside, start)
        return pl.ds(pl.multiple_of(start + strip * self.chunk, self.chunk), self.chunk)

    def own_at(self, index, which):
        return self.own.at[self.span(index, which), :]

    def out_at(self, index, which, row):
        segment, _, strip = self.spot(index)
        place = jnp.where(self.extra(index), 4 * SEGMENTS, segment * 4 + row)
        start = pl.multiple_of(which * self.half + strip * self.chunk, self.chunk)
        return self.out.at[place, pl.ds(start, self.chunk), :]

    def end_sends(self, index):
        low = here()[0] // 3
        return (
            remote(
                self.own_at(index, low),
                self.left.at[index % RING],
                self.end_send.at[0, index],
                self.low_recv.at[index],
                self.near_z,
            ),
            remote(
                self.own_at(index, 1 - low),
                self.right.at[1, index % RING],
                self.end_send.at[1, index],
                self.high_recv.at[1, index],
                self.near_z,
            ),
        )

    def to_other(self, index):
        low = here()[0] - 1
        return remote(
            self.own_at(index, 1 - low),
            self.right.at[0, index % RING],
            self.mid_send.at[index],
            self.high_recv.at[0, index],
            self.other,
        )

    def from_outer(self, index):
        low = here()[0] - 1
        return (
            remote(
                self.own_at(index, low),
                self.left.at[index % RING],
                self.mid_send.at[index],
                self.low_recv.at[index],
                self.outer,
            ),
            remote(
                self.own_at(index, 1 - low),
                self.right.at[1, index % RING],
                self.mid_send.at[index],
                self.high_recv.at[1, index],
                self.outer,
            ),
        )

    def hand(self, index):
        z, r, c = here()
        low = z - 1
        mine, spot = (self.own_at(index, low), self.out_at(index, low, r))
        return (
            pltpu.make_async_copy(mine, spot, self.out_recv.at[low, index]),
            remote(
                mine,
                spot,
                self.hand_send.at[index],
                self.out_recv.at[low, index],
                (z, self.peer_row(index), c),
            ),
        )

    def along(self, index):
        low = here()[0] - 1
        spot = self.out_at(index, low, self.peer_row(index))
        return (
            remote(
                spot, spot, self.first_send.at[index], self.out_recv.at[low, index], self.outer
            ),
            remote(spot, spot, self.last_send.at[index], self.out_recv.at[low, index], self.other),
        )

    def onward(self, index):
        low = here()[0] - 1
        spot = self.out_at(index, 1 - low, self.peer_row(index))
        return remote(
            spot, spot, self.on_send.at[index], self.out_recv.at[1 - low, index], self.outer
        )

    def came_back(self, index):
        for which in (0, 1):
            spot = self.out_at(index, which, self.peer_row(index))
            remote(
                spot, spot, self.end_send.at[0, index], self.out_recv.at[which, index], self.near_z
            ).wait_recv()

    def end_step(self, index):
        @pl.when(index < self.chunks)
        def _():
            @pl.when(index >= DEPTH)
            def _():
                for copy in self.end_sends(index - DEPTH):
                    copy.wait_send()

            @pl.when(index >= RING)
            def _():
                self.came_back(index - RING)

            for copy in self.end_sends(index):
                copy.start()

    def mid_step(self, index):
        own, left, right, low = (self.own, self.left, self.right, here()[0] - 1)

        @pl.when(index < self.chunks)
        def _():
            self.from_outer(index)[1].wait_recv()
            span = self.span(index, 1 - low)
            total = own[span, :].astype(jnp.float32) + right[1, index % RING].astype(jnp.float32)
            own[span, :] = total.astype(jnp.bfloat16)
            self.to_other(index).start()

        @pl.when((index >= SUM_LAG) & (index < self.chunks + SUM_LAG))
        def _():
            back = index - SUM_LAG
            self.from_outer(back)[0].wait_recv()
            self.to_other(back).wait_recv()
            span = self.span(back, low)
            total = (
                own[span, :].astype(jnp.float32)
                + left[back % RING].astype(jnp.float32)
                + right[0, back % RING].astype(jnp.float32)
            )
            own[span, :] = total.astype(jnp.bfloat16)

            @pl.when(self.stays(back))
            def _():
                self.hand(back)[0].start()

            @pl.when(jnp.logical_not(self.stays(back)))
            def _():
                self.hand(back)[1].start()

        @pl.when((index >= HAND_LAG) & (index < self.chunks + HAND_LAG))
        def _():
            back = index - HAND_LAG

            @pl.when(self.stays(back))
            def _():
                self.hand(back)[0].wait()

            @pl.when(jnp.logical_not(self.stays(back)))
            def _():
                self.hand(back)[1].wait_recv()

            for copy in self.along(back):
                copy.start()

        @pl.when(index >= LAG)
        def _():
            copy = self.onward(index - LAG)
            copy.wait_recv()
            copy.start()

    def prime(self):
        @pl.when(self.is_end)
        def _():
            run_loop(0, AHEAD, self.end_step)

        self.ahead = AHEAD

    def advance(self, count):
        first, last = (self.at, min(self.at + count, self.total))
        self.at = last
        if first == last:
            return

        @pl.when(self.is_end)
        def _():
            run_loop(self.ahead, last + AHEAD, self.end_step)

        self.ahead = last + AHEAD

        @pl.when(jnp.logical_not(self.is_end))
        def _():
            run_loop(first, last, self.mid_step)

    def one(self, index):
        @pl.when(self.is_end)
        def _():
            self.end_step(index + AHEAD)

        @pl.when(jnp.logical_not(self.is_end))
        def _():
            self.mid_step(index)

    def skip(self, count):
        self.at += count
        self.ahead += count

    def end_done(self, index):
        @pl.when(index >= self.chunks - DEPTH)
        def _():
            for copy in self.end_sends(index):
                copy.wait_send()

        @pl.when(index >= self.chunks - RING)
        def _():
            self.came_back(index)

    def mid_done(self, index):
        self.to_other(index).wait_send()

        @pl.when(jnp.logical_not(self.stays(index)))
        def _():
            self.hand(index)[1].wait_send()

        for copy in self.along(index):
            copy.wait_send()
        self.onward(index).wait_send()

    def finish(self):
        self.advance(self.total)

        @pl.when(self.is_end)
        def _():
            run_loop(0, self.chunks, self.end_done)

        @pl.when(jnp.logical_not(self.is_end))
        def _():
            run_loop(0, self.chunks, self.mid_done)


def line_scratch(rows, width, chunk, lead):
    dma = pltpu.SemaphoreType.DMA
    chunks = 4 * SEGMENTS * (rows // 2 // chunk) + lead
    return [
        pltpu.VMEM((4 * SEGMENTS * rows + 2 * lead * chunk, width), jnp.bfloat16),
        pltpu.VMEM((RING, chunk, width), jnp.bfloat16),
        pltpu.VMEM((2, RING, chunk, width), jnp.bfloat16),
        dma((2, chunks)),
        dma((chunks,)),
        dma((2, chunks)),
        dma((2, chunks)),
        dma((chunks,)),
        dma((chunks,)),
        dma((chunks,)),
        dma((chunks,)),
        dma((chunks,)),
    ]


LINE_REFS = 12
PACK = 32
CHUNK = 32
PACE = (2, 3, 3, 1, 1, 2, 2, 3, 3)
BLOCK_STEPS = 1


def z_peers():
    z, r, c = here()
    return [((z + step) % 4, r, c) for step in (1, 2, 3)]


def plane_peers():
    z, r, c = here()
    return [(z, (r + turn % 4) % 4, (c + turn // 4) % 2) for turn in range(1, 8)]


def hand_out(copies, source, target):
    z, r, c = here()
    twin, side, _ = near()
    cross = (z, flip(across(r)), c)
    columns = target.shape[1]
    size = source.shape[0]

    def piece(row):
        return source.at[:, part(row, columns, columns)]

    spot = target.at[part(r, size, size), :]
    waits = [copies.go(piece(peer[1]), spot, peer) for peer in (side, cross, twin)]
    local = copies.go(piece(r), spot, None)

    def done():
        for copy in waits:
            arrived(copy)
        local.wait()

    return done


def gate_tiles(width):
    tiles = []
    for tile in range(5):
        first, rest = (0, width)
        if tile < 4:
            tiles.append((tile, 0, width, tile // 2, tile % 2 * width))
        else:
            tiles.append((tile, 0, 384, 0, 2 * width))
            tiles.append((tile, 384, width - 384, 1, 2 * width))
    return tiles


def backward_kernel(resid_mid, both_gains, masks, vec, rec_w, in_w, mix_w, out_w, *refs):
    parts_in, out_parts, c_all, x_all, *kept_in = refs[:12]
    gate_grad, up_grad, down_grad = refs[12:15]
    grad, output, grads, out_gates, out_vec, out_gain = refs[15:21]
    scratch = refs[21:]
    line_refs, scratch = (scratch[:LINE_REFS], scratch[LINE_REFS:])
    parts, cot, resid, branch, d_resid, d_pre, d_gates, edge, carry = scratch[:9]
    kept, scratch = (scratch[9:17], scratch[17:])
    sums, gains, vec_z, gain_z, vec_sum, gain_sum, vec_in, gain_in = scratch[:8]
    *buffers, mine, mine_out, load_sem, gate_sem, small_send, small_recv, free, send, recv = scratch[8:]
    normed, pre, mixed, x_pre, conv, rec_gate, in_gate, states = kept
    z, r, c = here()
    twin, side, top = near()
    cross = (z, flip(across(r)), c)
    lines, plane = (z_peers(), plane_peers())
    greet(lines + plane)
    copies = Copies(send, recv)
    line = Line(*line_refs[:3], grads, line_refs[3:], PACK // CHUNK)
    own, half, rows_all = (line.own, line.half, 4 * line.rows)
    size = mine.shape[0]
    shard = part(token_shard(r, c), size, size)
    width, ff = (x_pre.shape[1], gate_grad.shape[1])
    head, rest = (own.shape[1] - 2 * ff, 3 * ff - own.shape[1])
    first, second = (pl.ds(0, rows_all), pl.ds(rows_all, rows_all))
    loads = [
        pltpu.make_async_copy(source, target, load_sem.at[place])
        for place, (source, target) in enumerate(
            zip(
                [
                    gate_grad,
                    up_grad,
                    down_grad.at[:, pl.ds(0, head)],
                    parts_in,
                    down_grad.at[:, pl.ds(head, rest)],
                    c_all.at[shard, :],
                    x_all.at[shard, :],
                    *kept_in,
                ],
                [
                    own.at[first, pl.ds(0, ff)],
                    own.at[first, pl.ds(ff, ff)],
                    own.at[first, pl.ds(2 * ff, head)],
                    parts,
                    own.at[second, pl.ds(0, rest)],
                    cot,
                    resid,
                    *kept,
                ],
            )
        )
    ]
    for copy in loads[:4]:
        copy.start()
    for ref in (gains, sums, edge, carry):
        ref[...] = jnp.zeros_like(ref)
    for copy in loads[:3]:
        copy.wait()
    line.prime()
    loads[3].wait()
    for copy in loads[4:]:
        copy.start()
    pace = iter(PACE)

    def between():
        line.advance(next(pace))

    total = reduce_shards(copies, parts, *buffers, between=between)
    for copy in loads[4:]:
        copy.wait()

    def body(at):
        rows = pl.ds(at, STRIP)
        values, piece = norm_pull(resid_mid[rows, :], both_gains[1:2, :], total(at))
        values = values + cot[rows, :].astype(jnp.float32)
        gains[1:2, :] += piece
        d_resid[rows, :] = values
        mine[rows, :] = values.astype(jnp.bfloat16)

    strips(size, body)
    spread_rows(copies, mine, branch, between)
    copies.finish()
    last = branch.shape[0] // BLOCK - 1

    def block(index, base):
        start = pl.multiple_of((last - index) * BLOCK, BLOCK)
        rows = pl.ds(start, BLOCK)
        before = pl.ds(pl.multiple_of(jnp.maximum(start - 8, 0), 8), 8)
        mixer_backward_step(
            lax.dot_general(
                branch[rows, :], out_w[...], CONTRACT_COLS, preferred_element_type=jnp.float32
            ),
            pre.at[rows, :],
            masks[rows, :],
            vec,
            rec_w,
            in_w,
            x_pre.at[rows, :],
            x_pre.at[before, :],
            conv.at[rows, :],
            rec_gate.at[rows, :],
            in_gate.at[rows, :],
            states.at[rows, :],
            states.at[before, :],
            d_pre.at[rows, :],
            d_gates.at[rows, :],
            sums,
            edge,
            carry,
        )
        parts[rows, :] = lax.dot_general(
            d_pre[rows, :], mix_w[...], CONTRACT_COLS, preferred_element_type=jnp.float32
        ).astype(jnp.bfloat16)
        for step in range(BLOCK_STEPS):
            line.one(base + BLOCK_STEPS * index + step)
        return base

    lax.fori_loop(0, last + 1, block, line.at)
    line.skip(BLOCK_STEPS * (last + 1))
    total_back = reduce_shards(copies, parts, *buffers, between=between)

    def body_back(at):
        rows = pl.ds(at, STRIP)
        values, piece = norm_pull(
            resid[rows, :].astype(jnp.float32), both_gains[0:1, :], total_back(at)
        )
        gains[0:1, :] += piece
        mine[rows, :] = (d_resid[rows, :] + values).astype(jnp.bfloat16)

    strips(size, body_back)
    for peer in (twin, side, top):
        pl.semaphore_signal(free, inc=1, device_id=peer, device_id_type=MESH)
    copies.finish()
    load = pltpu.make_async_copy(out_parts, parts, load_sem.at[0])
    load.start()
    grad_done = hand_out(copies, mine, grad)
    small = [
        [
            remote(
                source,
                target.at[3 - step],
                small_send.at[kind, step - 1],
                small_recv.at[kind, 3 - step],
                lines[step - 1],
            )
            for step in (1, 2, 3)
        ]
        for kind, (source, target) in enumerate(((sums, vec_z), (gains, gain_z)))
    ]
    for kind in small:
        for copy in kind:
            copy.start()
    blocks = lax.dot_general(conv[...], d_gates[...], CONTRACT_ROWS, preferred_element_type=jnp.float32)
    rows_half = width // 2
    lane = lax.broadcasted_iota(jnp.int32, (rows_half, 2 * width), 1)
    mingled = jnp.where(
        lane // rows_half % 2 == 0, blocks[:rows_half], blocks[rows_half:]
    ).astype(jnp.bfloat16)
    for tile, begin, length, which, spot in gate_tiles(2 * width):
        own[pl.ds(2 * rows_all + which * PACK, PACK), spot : spot + length] = mingled[
            tile * PACK : (tile + 1) * PACK, begin : begin + length
        ]

    def weights(index, base):
        columns = pl.ds(pl.multiple_of(index * 256, 256), 256)
        rows = pl.ds(pl.multiple_of(rows_all + index * 256, 256), 256)
        own[rows, rest : rest + 2 * width] = lax.dot_general(
            normed[:, columns], d_pre[...], CONTRACT_ROWS, preferred_element_type=jnp.float32
        ).astype(jnp.bfloat16)
        own[rows, rest + 2 * width :] = lax.dot_general(
            branch[:, columns], mixed[...], CONTRACT_ROWS, preferred_element_type=jnp.float32
        ).astype(jnp.bfloat16)
        line.one(base + index)
        return base

    lax.fori_loop(0, rows_all // 256, weights, line.at)
    line.skip(rows_all // 256)
    assert line.at + AHEAD <= line.first + line.lead
    load.wait()
    pl.semaphore_wait(free, 3)
    total_out = reduce_shards(copies, parts, *buffers, between=between)

    def body_out(at):
        rows = pl.ds(at, STRIP)
        mine_out[rows, :] = (resid_mid[rows, :] + total_out(at)).astype(jnp.bfloat16)

    strips(size, body_out)
    output_done = hand_out(copies, mine_out, output)
    spread_out = [
        [
            remote(
                source,
                target.at[6 - step],
                small_send.at[kind, 3 + step],
                small_recv.at[kind, 3 + 6 - step],
                peer,
            )
            for step, peer in enumerate(plane)
        ]
        for kind, (source, target) in enumerate(((vec_sum, vec_in), (gain_sum, gain_in)))
    ]
    for kind in small:
        for copy in kind:
            copy.wait_recv()
    vec_sum[...] = sums[...] + vec_z[0] + vec_z[1] + vec_z[2]
    gain_sum[...] = gains[...] + gain_z[0] + gain_z[1] + gain_z[2]
    for kind in spread_out:
        for copy in kind:
            copy.start()
    line.advance(max(line.first + line.lead + RING + 2 - line.at, 0))
    gate_moves = [
        remote(
            grads.at[4 * SEGMENTS, pl.ds(which * half, PACK), :],
            out_gates.at[r, which],
            small_send.at[0, 10 + 2 * place + which],
            small_recv.at[0, 10 + 2 * place + which],
            peer,
        )
        for place, peer in enumerate((twin, side, cross))
        for which in (0, 1)
    ]
    gate_local = [
        pltpu.make_async_copy(
            grads.at[4 * SEGMENTS, pl.ds(which * half, PACK), :],
            out_gates.at[r, which],
            gate_sem.at[which],
        )
        for which in (0, 1)
    ]
    for copy in gate_moves + gate_local:
        copy.start()
    for kind in spread_out:
        for copy in kind:
            copy.wait_recv()
    all_gains = gain_sum[...]
    for place in range(7):
        all_gains = all_gains + gain_in[place]
    gain_z[0] = all_gains
    out_gain[...] = gain_z[0, :, part(r, out_gain.shape[1], out_gain.shape[1])]
    out_vec[r] = vec_sum[...]
    for step in (0, 1, 2):
        out_vec[(r + 3 - step) % 4] = vec_in[6 - step]
    line.finish()
    grad_done()
    output_done()
    for copy in gate_moves:
        copy.wait_recv()
    for copy in gate_local:
        copy.wait()
    for group in small + spread_out + [gate_moves]:
        for copy in group:
            copy.wait_send()
    copies.finish()


def unpack_kernel(grads, gates, vec, output, grad_in, *outs):
    out_t, grad_t, x_grad, y_grad, out_grad, gate_grad, up_grad, down_grad, rec_w, in_w = outs[:10]
    wide, ff, rec = (grads.shape[2], gate_grad.shape[1] // 4, x_grad.shape[1] // 4)
    head = wide - 2 * ff
    rest = ff - head
    out_t[...] = output[...].astype(jnp.float32).T.astype(out_t.dtype)
    grad_t[...] = grad_in[...].astype(jnp.float32).T
    for row in range(4):
        wide_span, span = (slice(row * ff, (row + 1) * ff), slice(row * rec, (row + 1) * rec))

        def body(at):
            rows = pl.ds(at, 64)
            early = grads[row, rows, :].astype(jnp.float32)
            late = grads[4 + row, rows, :].astype(jnp.float32)
            gate_grad[rows, wide_span] = early[:, :ff]
            up_grad[rows, wide_span] = early[:, ff : 2 * ff]
            down_grad[rows, row * ff : row * ff + head] = early[:, 2 * ff :]
            down_grad[rows, row * ff + head : (row + 1) * ff] = late[:, :rest]
            x_grad[rows, span] = late[:, rest : rest + rec]
            y_grad[rows, span] = late[:, rest + rec : rest + 2 * rec]

        body(0)
        body(64)
        last = grads[4 + row, :, rest + 2 * rec : rest + 3 * rec]
        out_grad[span, :] = last.astype(jnp.float32).T
    heads, width = (rec_w.shape[0], rec_w.shape[1])
    for tile in range(5):
        spots = [item for item in gate_tiles(2 * rec) if item[0] == tile]
        values = jnp.concatenate(
            [gates[0, which, :, spot : spot + length] for _, _, length, which, spot in spots],
            axis=1,
        ).astype(jnp.float32)
        rows = slice(tile * PACK, (tile + 1) * PACK)
        for place in range(heads):
            rec_w[place, rows, :] = values[:, place * width : (place + 1) * width]
            in_w[place, rows, :] = values[:, rec + place * width : rec + (place + 1) * width]
    line = 0
    for ref in outs[10:]:
        for row in range(ref.shape[0]):
            ref[row : row + 1, :] = jnp.concatenate(
                [vec[place, line : line + 1, :] for place in range(4)], axis=1
            )
            line += 1


def unpack(grads, gates, vec, output, grad_in, rec, ff, heads):
    depth, wide = grads.shape[1:]
    tokens, head = (output.shape[0], rec // heads)

    def out(*dims, kind=jnp.float32):
        return jax.ShapeDtypeStruct(dims, kind)

    def rows(columns):
        return pl.BlockSpec((BLOCK, columns), lambda i: (i, 0))

    def columns(length):
        return pl.BlockSpec((length, BLOCK), lambda i: (0, i))

    def whole(*dims):
        return pl.BlockSpec(dims, lambda i: (0,) * len(dims))

    blocks = pl.BlockSpec((heads, head, head), lambda i: (i, 0, 0))
    lines = (1, 1, 4, 1, 1, 1, 1)
    return pl.pallas_call(
        unpack_kernel,
        grid=(depth // BLOCK,),
        in_specs=[
            pl.BlockSpec((8, BLOCK, wide), lambda i: (0, i, 0)),
            pl.BlockSpec((1, 2, PACK, wide), lambda i: (i, 0, 0, 0)),
            whole(*vec.shape),
            columns(tokens),
            columns(tokens),
        ],
        out_specs=[rows(tokens), rows(tokens), rows(4 * rec), rows(4 * rec), columns(4 * rec)]
        + [rows(4 * ff)] * 3
        + [blocks] * 2
        + [whole(count, 4 * rec) for count in lines],
        out_shape=[
            out(depth, tokens, kind=output.dtype),
            out(depth, tokens),
            out(depth, 4 * rec),
            out(depth, 4 * rec),
            out(4 * rec, depth),
        ]
        + [out(depth, 4 * ff)] * 3
        + [out(4 * heads, head, head)] * 2
        + [out(count, 4 * rec) for count in lines],
        compiler_params=pltpu.CompilerParams(vmem_limit_bytes=60 << 20),
        name="unpack",
    )(grads, gates, vec, output, grad_in)


def dot(left, right, dims, kind=jnp.float32):
    return lax.dot_general(left, right, dims, preferred_element_type=jnp.float32).astype(kind)


def local_plane(
    inputs,
    cotangent,
    starts,
    x_proj,
    y_proj,
    out_proj,
    gate_proj,
    up_proj,
    down_proj,
    mix_gain,
    mlp_gain,
    x_bias,
    y_bias,
    conv_w,
    conv_b,
    rec_gate_w,
    in_gate_w,
    rec_gate_b,
    in_gate_b,
    decay_param,
):
    z, r, c = here()
    depth = x_proj.shape[0]
    rec = x_proj.shape[1] // 4
    width = gate_proj.shape[1] // 4
    heads, head = (rec_gate_w.shape[0] // 4, rec_gate_w.shape[1])
    padded = (rec + 127) // 128 * 128
    low = jnp.bfloat16

    def mine(array, size, axis=0):
        return lax.dynamic_slice_in_dim(array, r * size, size, axis)

    flags = jnp.broadcast_to(starts.astype(low)[:, None], (starts.shape[0], 128))
    x_all, c_all, s_all, g_all, mix_w, out_w = gather(
        inputs.T,
        cotangent.T,
        flags,
        jnp.stack([mix_gain, mlp_gain]),
        x_proj,
        y_proj,
        out_proj,
    )
    tokens, model = x_all.shape
    vectors = jnp.concatenate(
        [
            x_bias,
            y_bias,
            conv_w.reshape(-1),
            conv_b,
            rec_gate_b,
            in_gate_b,
            -GATE_C * jax.nn.softplus(decay_param),
            -GATE_C * jax.nn.sigmoid(decay_param),
            jnp.zeros((5 * x_bias.shape[0],), jnp.float32),
        ]
    ).reshape(-1, x_bias.shape[0])
    vec = mine(vectors, rec, 1)

    def diagonal(blocks):
        blocks = mine(blocks, heads)
        rows = [jnp.pad(blocks[i], ((0, 0), (i * head, rec - (i + 1) * head))) for i in range(heads)]
        return jnp.concatenate(rows, axis=0)

    rec_w, in_w = (diagonal(rec_gate_w), diagonal(in_gate_w))
    size = tokens // 8
    full = jax.ShapeDtypeStruct((tokens, model), low)
    part = jax.ShapeDtypeStruct((size, model), jnp.float32)
    piece = pltpu.VMEM((size, model), low)
    block = jax.ShapeDtypeStruct((inputs.shape[1], inputs.shape[0]), low)
    weights = (gate_proj, up_proj, down_proj)
    slices = jax.ShapeDtypeStruct((4 * depth, width), low)
    kept = [((tokens, model), low), ((tokens, 2 * rec), jnp.float32), ((tokens, padded), low)]
    kept += [((tokens, rec), kind) for kind in (jnp.float32, low) + (jnp.float32,) * 3]
    kept.append(((tokens, 8), jnp.float32))
    row8 = pltpu.VMEM((8, rec), jnp.float32)
    (
        normed_mlp,
        resid_mid,
        gate_w,
        up_w,
        down_w,
        normed_mix,
        pre,
        mixed,
        x_pre,
        conv,
        rec_gate,
        in_gate,
        states,
        masks,
    ) = vmem_call(
        forward_kernel,
        "forward",
        FORWARD_ID,
        (vec, rec_w, in_w, g_all),
        [full, part] + [slices] * 3 + [jax.ShapeDtypeStruct(*item) for item in kept],
        [pl.ANY, pltpu.VMEM] + [pl.ANY] * 12,
        [pltpu.VMEM(*item) for item in kept]
        + [row8, row8, pltpu.VMEM((tokens, model), low)]
        + [
            pltpu.VMEM((tokens, model), low),
            pltpu.VMEM((tokens, 128), low),
            pltpu.VMEM(mix_w.shape, low),
            pltpu.VMEM(out_w.shape, low),
            pltpu.VMEM((8, 8), jnp.float32),
            pltpu.SemaphoreType.DMA((11,)),
        ]
        + reduce_scratch(size, model)
        + [piece, pltpu.SemaphoreType.DMA((9,))],
        80,
        (x_all, s_all.reshape(tokens, 128), mix_w, out_w, *weights),
    )
    gate = dot(normed_mlp, gate_w, CONTRACT_PLAIN)
    up = dot(normed_mlp, up_w, CONTRACT_PLAIN)
    d_activ = dot(c_all, down_w, CONTRACT_PLAIN)
    gelu, slope = gelu_both(gate)
    activ = (gelu * up).astype(low)
    d_gate = (d_activ * up * slope).astype(low)
    d_up = (d_activ * gelu).astype(low)
    d_normed = lax.dot_general(
        d_gate, gate_w, CONTRACT_COLS, preferred_element_type=jnp.float32
    ) + lax.dot_general(d_up, up_w, CONTRACT_COLS, preferred_element_type=jnp.float32)
    def kind_of(array):
        return pltpu.VMEM(array.shape, array.dtype)

    def like(array):
        return jax.ShapeDtypeStruct(array.shape, array.dtype)

    both = jax.ShapeDtypeStruct((tokens, 2 * rec), low)
    held = (normed_mix, pre, mixed, x_pre, conv, rec_gate, in_gate, states)
    wide = (3 * width + 2 * rec + padded) // SEGMENTS
    sums = pltpu.VMEM((16, rec), jnp.float32)
    lines = pltpu.VMEM((2, model), jnp.float32)
    dma = pltpu.SemaphoreType.DMA

    def several(count, kind):
        return pltpu.VMEM((count, *kind.shape), kind.dtype)

    grad_in, output, grads, gates, vec_sums, gains = vmem_call(
        backward_kernel,
        "backward",
        BACKWARD_ID,
        (resid_mid, g_all, masks, vec, rec_w, in_w, mix_w, out_w),
        [
            block,
            block,
            jax.ShapeDtypeStruct((4 * SEGMENTS + 1, depth, wide), low),
            jax.ShapeDtypeStruct((4, 2, PACK, wide), low),
            jax.ShapeDtypeStruct((4, 16, rec), jnp.float32),
            jax.ShapeDtypeStruct((2, depth), jnp.float32),
        ],
        [pl.ANY] * 4 + [pltpu.VMEM] * 2,
        line_scratch(depth, wide, CHUNK, PACK // CHUNK)
        + [
            kind_of(full),
            piece,
            piece,
            kind_of(full),
            kind_of(part),
            kind_of(both),
            kind_of(both),
            pltpu.VMEM((24, rec), jnp.float32),
            row8,
        ]
        + [kind_of(item) for item in held]
        + [
            sums,
            lines,
            several(3, sums),
            several(3, lines),
            sums,
            lines,
            several(7, sums),
            several(7, lines),
        ]
        + reduce_scratch(size, model)
        + [
            piece,
            piece,
            dma((15,)),
            dma((2,)),
            dma((2, 16)),
            dma((2, 16)),
            pltpu.SemaphoreType.REGULAR,
        ],
        80,
        (
            d_normed.astype(low),
            dot(activ, down_w, CONTRACT_COLS, low),
            c_all,
            x_all,
            *held,
            dot(normed_mlp, d_gate, CONTRACT_ROWS, low),
            dot(normed_mlp, d_up, CONTRACT_ROWS, low),
            dot(c_all, activ, CONTRACT_ROWS, low),
        ),
    )
    done = unpack(grads, gates, vec_sums, output, grad_in, rec, width, heads)
    lines = [item if item.shape[0] > 1 else item[0] for item in done[10:]]
    return (*done[:8], gains[0], gains[1], *lines[:4], *done[8:10], *lines[4:])


def fits(mesh):
    return mesh.shape["dp"] == 4 and mesh.shape["row"] == 4 and mesh.shape["col"] == 2


def solution(mesh):
    placed = (
        P("row", ("dp", "col")),
        P("row", ("dp", "col")),
        P(("dp", "row")),
        P("row", "col"),
        P("row", "col"),
        P("col", "row"),
        P("row", "col"),
        P("row", "col"),
        P("row", "col"),
        P("row"),
        P("row"),
        P("col"),
        P("col"),
        P(None, "col"),
        P("col"),
        P("col", None, None),
        P("col", None, None),
        P("col"),
        P("col"),
        P("col"),
    )
    return jax.shard_map(
        local_plane if fits(mesh) else local,
        mesh=mesh,
        in_specs=placed,
        out_specs=(
            P("row", ("dp", "col")),
            P("row", ("dp", "col")),
            P("row", "col"),
            P("row", "col"),
            P("col", "row"),
            P("row", "col"),
            P("row", "col"),
            P("row", "col"),
            P("row"),
            P("row"),
            P("col"),
            P("col"),
            P(None, "col"),
            P("col"),
            P("col", None, None),
            P("col", None, None),
            P("col"),
            P("col"),
            P("col"),
        ),
        check_vma=False,
    )
```
